32 devices in a mesh: dp: 4 (over y, x), row: 4 (over z), col: 2 (over core).
Axes of the slice: x: 2, y: 2, z: 4, core: 2. Of those that a mesh axis runs over, the one named last changes fastest.
Arguments:
- patches: bfloat16 [4, 2, 1408, 768], P('dp', None, ('row', 'col')), may hold values from -6 to 6
- picture_ids: int32 [4, 2, 1408], P('dp'), may hold values from 0 to 3, never falling along the last dimension, each value on 1 to 1024 neighbouring positions
- ln1_gain: float32 [768], replicated, may hold values from 0.5 to 1.5
- ln1_bias: float32 [768], replicated, may hold values from -3 to 3
- w_query: bfloat16 [768, 768], P(('dp', 'row'), 'col'), may hold values from -0.21875 to 0.21875
- w_key: bfloat16 [768, 768], P(('dp', 'row'), 'col'), may hold values from -0.21875 to 0.21875
- w_value: bfloat16 [768, 768], P(('dp', 'row'), 'col'), may hold values from -0.21875 to 0.21875
- q_gain: float32 [64], replicated, may hold values from 0.1 to 1.9
- k_gain: float32 [64], replicated, may hold values from 0.1 to 1.9
- w_out: bfloat16 [768, 768], P('col', ('dp', 'row')), may hold values from -2 to 2
- ln2_gain: float32 [768], replicated, may hold values from 0.5 to 1.5
- ln2_bias: float32 [768], replicated, may hold values from -3 to 3
- w_up: bfloat16 [768, 3072], P(('dp', 'row'), 'col'), may hold values from -0.21875 to 0.21875
- w_down: bfloat16 [3072, 768], P('col', ('dp', 'row')), may hold values from -0.109375 to 0.109375
- cotangent: bfloat16 [4, 2, 1408, 768], P('dp', None, ('row', 'col')), may hold values from -6 to 6
Outputs:
- result: bfloat16 [4, 2, 1408, 768], P('dp', None, ('row', 'col'))
- grad_input: float32 [4, 2, 1408, 768], P('dp', None, ('row', 'col'))
- grad_ln1_gain: float32 [768], replicated
- grad_ln1_bias: float32 [768], replicated
- grad_w_query: float32 [768, 768], P(('dp', 'row'), 'col')
- grad_w_key: float32 [768, 768], P(('dp', 'row'), 'col')
- grad_w_value: float32 [768, 768], P(('dp', 'row'), 'col')
- grad_q_gain: float32 [64], replicated
- grad_k_gain: float32 [64], replicated
- grad_w_out: float32 [768, 768], P('col', ('dp', 'row'))
- grad_ln2_gain: float32 [768], replicated
- grad_ln2_bias: float32 [768], replicated
- grad_w_up: float32 [768, 3072], P(('dp', 'row'), 'col')
- grad_w_down: float32 [3072, 768], P('col', ('dp', 'row'))
The draws below stay inside these ranges and needn't reach their ends.
Inputs may be any that keep to these rules, and one draw needn't show every extreme that they name: `picture_ids`: in each packed row the picture ids never fall, every id is used, each picture covers 1 to 1024 patches and one covers exactly 1024.
All inputs are finite; a program needn't handle non-finite values.
Results may differ from the reference program's by a relative error of at most 0.017.
Values may be sent and summed in bfloat16 or wider, within the bound.
No kernel may reach another device: no remote copies, remote signals or barrier semaphores. Data moves between devices by JAX's collectives and lax.ppermute only.
A program may use at most 128 MiB of HBM per device.

```python
import math
import jax
import jax.numpy as jnp
import numpy as np
from jax import lax

D = 768
HEADS = 12
HD = 64
FF = 3072
SEQ = 1408
MOST = 1024
PICS = 4
MICRO = 2
GROUPS = 4


def steps_of(own_key, dims, split, low, high):
    gain = 1.0
    for dim, parts in split:
        draws = jax.random.uniform(jax.random.fold_in(jax.random.fold_in(own_key, 6), dim), (parts,), jnp.float32, low / len(split), high / len(split))
        gain = gain * jnp.repeat(jnp.exp(draws), dims[dim] // parts).reshape((-1,) + (1,) * (len(dims) - 1 - dim))
    return gain


def length_profile(count, total, reach, slope):
    portions = [(1 << 20) // math.isqrt(standing ** slope) + 1 for standing in range(2, count + 1)]
    spare, holding = total - reach - (count - 1), [1] * (count - 1)
    while spare > 0:
        candidates = [i for i in range(count - 1) if holding[i] < reach]
        pool, left = sum([portions[i] for i in candidates]), spare
        for i in candidates:
            extra = min(reach - holding[i], max(1, left * portions[i] // pool), spare)
            holding[i] = holding[i] + extra
            spare = spare - extra
    return np.array([reach] + holding)


def ragged_sizes(key, amount, total, limit, lean):
    if amount == 2:
        one = jax.random.randint(key, (), max(1, total - limit), min(limit, total - 1) + 1)
        return jnp.stack([one, total - one])
    lengths = jnp.asarray(length_profile(amount, total, limit, lean), jnp.int32)
    pairs = (amount - 1) // 2
    donor, receiver = lengths[1:1 + 2 * pairs:2], lengths[2:2 + 2 * pairs:2]
    margin = jnp.minimum(donor - 1, limit - receiver)
    passed = jax.random.randint(jax.random.fold_in(key, 1), (pairs,), 0, 1 << 20) % (margin + 1)
    lengths = lengths.at[1:1 + 2 * pairs:2].set(donor - passed).at[2:2 + 2 * pairs:2].set(receiver + passed)
    return lengths[jax.random.permutation(jax.random.fold_in(key, 2), amount)]


def bell_draw(own_key, dims, spread, limit, pieces=(), dtype=jnp.bfloat16):
    factor_of = steps_of(own_key, dims, pieces, -0.22, 0.18) if pieces else 1.0
    entries = jax.random.normal(own_key, dims, jnp.float32) * spread * factor_of
    return jnp.minimum(jnp.maximum(entries, -limit), limit).astype(dtype)


def setup_inputs(seed: int = 0) -> dict:
    keys = jax.random.split(jax.random.key(seed), 16)
    return {
        "patches": bell_draw(keys[0], (GROUPS, MICRO, SEQ, D), 1.0, 6.0, ((0, 4), (2, 8))),
        "picture_ids": jax.vmap(lambda own: jnp.searchsorted(jnp.cumsum(ragged_sizes(own, PICS, SEQ, MOST, 1)), jnp.arange(SEQ), side="right"))(jax.random.split(keys[1], GROUPS * MICRO)).reshape((GROUPS, MICRO, SEQ)).astype(jnp.int32),
        "ln1_gain": jnp.clip(1.0 + 0.1 * jax.random.normal(keys[2], (D,), jnp.float32), 0.5, 1.5),
        "ln1_bias": bell_draw(keys[3], (D,), 0.3, 3.0, (), jnp.float32),
        "w_query": bell_draw(keys[4], (D, D), D ** -0.5, 0.21875, ((0, 16), (1, 2))),
        "w_key": bell_draw(keys[5], (D, D), D ** -0.5, 0.21875, ((0, 16), (1, 2))),
        "w_value": bell_draw(keys[6], (D, D), D ** -0.5, 0.21875, ((0, 16), (1, 2))),
        "q_gain": jnp.clip(1.0 + 0.18 * jax.random.normal(keys[7], (HD,), jnp.float32), 0.1, 1.9),
        "k_gain": jnp.clip(1.0 + 0.18 * jax.random.normal(keys[8], (HD,), jnp.float32), 0.1, 1.9),
        "w_out": bell_draw(keys[9], (D, D), (D // 96) ** -0.5, 2.0, ((0, 2), (1, 16))),
        "ln2_gain": jnp.clip(1.0 + 0.1 * jax.random.normal(keys[10], (D,), jnp.float32), 0.5, 1.5),
        "ln2_bias": bell_draw(keys[11], (D,), 0.3, 3.0, (), jnp.float32),
        "w_up": bell_draw(keys[12], (D, FF), D ** -0.5, 0.21875, ((0, 16), (1, 2))),
        "w_down": bell_draw(keys[13], (FF, D), FF ** -0.5, 0.109375, ((0, 2), (1, 16))),
        "cotangent": bell_draw(keys[14], (GROUPS, MICRO, SEQ, D), 1.0, 6.0, ((0, 4), (2, 8))),
    }


EPSILON = 1e-06
MASKED_SCORE = -1e+30

@jax.custom_vjp
def low(v):
    return lax.optimization_barrier(v.astype(jnp.bfloat16)).astype(jnp.float32)

@jax.custom_vjp
def low_back(v):
    return v

def low_keep(v):
    return (low(v), None)

def low_pass(kept, grad):
    return (grad,)

def back_keep(v):
    return (v, None)

def back_low(kept, grad):
    return (low(grad),)
low.defvjp(low_keep, low_pass)
low_back.defvjp(back_keep, back_low)

def matmul(left_arr, right_arr):
    return jnp.dot(left_arr, right_arr, precision=lax.Precision.HIGHEST, preferred_element_type=jnp.float32)

def layer_norm(tensor, gain_vec, bias_vec):
    average = lax.optimization_barrier(jnp.mean(tensor, axis=-1, keepdims=True))
    centred = tensor - average
    variance = lax.optimization_barrier(jnp.mean(centred * centred, axis=-1, keepdims=True))
    return centred * lax.rsqrt(variance + EPSILON) * gain_vec + bias_vec

def forward(patch_row, id_row, params):
    ln1_gain, ln1_bias, w_query, w_key, w_value, q_gain, k_gain, w_out, ln2_gain, ln2_bias, w_up, w_down = params
    factor = float(HD) ** (-0.5)
    normed = low(layer_norm(patch_row, ln1_gain, ln1_bias))
    queries_raw = low_back(matmul(normed, w_query)).reshape(SEQ, HEADS, HD)
    keys_raw = low_back(matmul(normed, w_key)).reshape(SEQ, HEADS, HD)
    values_low = low(low_back(matmul(normed, w_value))).reshape(SEQ, HEADS, HD)
    queries_low = low(layer_norm(queries_raw, q_gain, 0.0) * factor)
    keys_low = low(layer_norm(keys_raw, k_gain, 0.0))
    scores = low_back(jnp.einsum('qhd,khd->hqk', queries_low, keys_low, precision=lax.Precision.HIGHEST))
    same_pic = id_row[:, None] == id_row[None, :]
    masked = jnp.where(same_pic[None], scores, MASKED_SCORE)
    prob_full = jax.nn.softmax(masked, axis=-1)
    attended = jnp.einsum('hqk,khd->qhd', low(prob_full), values_low, precision=lax.Precision.HIGHEST)
    attended = low(low_back(attended.reshape(SEQ, D)))
    mixed = patch_row + low_back(matmul(attended, w_out))
    normed_two = low(layer_norm(mixed, ln2_gain, ln2_bias))
    up_proj = low_back(matmul(normed_two, w_up))
    activated = low(jax.nn.gelu(up_proj, approximate=True))
    return mixed + low_back(matmul(activated, w_down))

def reference(patches, picture_ids, ln1_gain, ln1_bias, w_query, w_key, w_value, q_gain, k_gain, w_out, ln2_gain, ln2_bias, w_up, w_down, cotangent):
    params = tuple((source.astype(jnp.float32) for source in (ln1_gain, ln1_bias, w_query, w_key, w_value, q_gain, k_gain, w_out, ln2_gain, ln2_bias, w_up, w_down)))
    rows_total = GROUPS * MICRO
    patch_rows = patches.reshape(rows_total, SEQ, D).astype(jnp.float32)
    id_rows = picture_ids.reshape(rows_total, SEQ)
    cot_rows = cotangent.reshape(rows_total, SEQ, D).astype(jnp.float32)

    def one_row(running, scan_items):
        patch_row, id_row, cot_row = scan_items

        def run(row_in, *weights):
            return forward(row_in, id_row, weights)
        output, pull_back = jax.vjp(run, patch_row, *params)
        gradients = pull_back(cot_row)
        running = tuple((acc + gradient for acc, gradient in zip(running, gradients[1:])))
        return (running, (output.astype(jnp.bfloat16), gradients[0]))
    initial = tuple((jnp.zeros(weight_arr.shape, jnp.float32) for weight_arr in params))
    running, (outputs, grads_in) = lax.scan(one_row, initial, (patch_rows, id_rows, cot_rows))
    shape_out = (GROUPS, MICRO, SEQ, D)
    return (outputs.reshape(shape_out), grads_in.reshape(shape_out), running[0], running[1], running[2], running[3], running[4], running[5], running[6], running[7], running[8], running[9], running[10], running[11])
```

```python
import functools
import math

import jax
import jax.numpy as jnp
from jax import lax
from jax.experimental import pallas as pl
from jax.experimental.pallas import tpu as pltpu
from jax.sharding import PartitionSpec as P

HD = 64
LANES = 128
TILE = 256
EPSILON = 1e-06
BF = jnp.bfloat16
F4 = jnp.float32
VM = pl.BlockSpec(memory_space=pltpu.VMEM)


def ring_order(n):
    return list(range(0, n, 2)) + list(range(n - 1 - (n % 2), 0, -2))


def ring_place(r, n):
    return jnp.where(r % 2 == 0, r // 2, n - 1 - r // 2 - (n % 2) + (n % 2) * 1)


def ring_row(q, n):
    return jnp.where(2 * q < n, 2 * q, 2 * (n - 1 - q) + 1)


def hop(x, n):
    order = ring_order(n)
    pairs = [(order[i], order[(i + 1) % n]) for i in range(n)]
    return lax.ppermute(x, "row", pairs)


def swap_bit(x, axis, n, bit):
    return lax.ppermute(x, axis, [(i, i ^ (1 << bit)) for i in range(n)])


def swap_core(x):
    return lax.ppermute(x, "col", [(0, 1), (1, 0)])


def bit_orders(n):
    bits = list(range(n.bit_length() - 1))
    half = len(bits) // 2
    return bits, bits[half:] + bits[:half]


def regular(block):
    dp = lax.axis_size("dp")
    return dp & (dp - 1) == 0 and block % 16 == 0


def gather_line(shard):
    n = lax.axis_size("row")
    place = ring_place(lax.axis_index("row"), n)
    blocks = [shard]
    for _ in range(n - 1):
        blocks.append(hop(blocks[-1], n))
    parts = []
    for r in range(n):
        slot = (place - ring_order(n).index(r)) % n
        parts.append(lax.select_n(slot, *blocks) if n > 1 else blocks[0])
    return jnp.concatenate(parts, axis=0)


def gather_plane(x, order):
    n = lax.axis_size("dp")
    me = lax.axis_index("dp")
    done = []
    for bit in order:
        other = swap_bit(x, "dp", n, bit)
        at = sum(1 for b in done if b > bit)
        low = (me >> bit) & 1
        first = jnp.where(low == 0, x, other)
        second = jnp.where(low == 0, other, x)
        x = jnp.stack([first, second], axis=at)
        done.append(bit)
    return x.reshape(-1, x.shape[-1])


def gather_weights(shard, cut):
    block = shard.shape[0]
    if not regular(block):
        whole = lax.all_gather(shard, ("dp", "row"), axis=0, tiled=True)
        one, two = whole[:, :cut], whole[:, cut:]
    else:
        line = gather_line(shard)
        a, b = bit_orders(lax.axis_size("dp"))
        one = gather_plane(line[:, :cut], a)
        two = gather_plane(line[:, cut:], b)
    return (one, swap_core(one)), (two, swap_core(two))


def add_low(a, b):
    return (a.astype(F4) + b.astype(F4)).astype(BF)


def scatter_plane(x, order):
    n = lax.axis_size("dp")
    me = lax.axis_index("dp")
    count = n.bit_length() - 1
    x = x.reshape((2,) * count + (-1, x.shape[-1]))
    left = list(range(count - 1, -1, -1))
    for bit in order:
        at = left.index(bit)
        low = (me >> bit) & 1
        send = lax.dynamic_index_in_dim(x, 1 - low, at, keepdims=False)
        keep = lax.dynamic_index_in_dim(x, low, at, keepdims=False)
        x = add_low(keep, swap_bit(send, "dp", n, bit))
        left.remove(bit)
    return x


def scatter_line(x):
    n = lax.axis_size("row")
    place = ring_place(lax.axis_index("row"), n)
    x = x.reshape(n, -1, x.shape[-1])

    def own(q):
        return lax.dynamic_index_in_dim(x, ring_row(q % n, n), 0, keepdims=False)

    if n == 1:
        return x[0].astype(F4)
    acc = own(place - 1 + n)
    for step in range(n - 2):
        acc = add_low(own(place - 2 - step + n), hop(acc, n))
    return own(place).astype(F4) + hop(acc, n).astype(F4)


def scatter_grads(one, two):
    block = one[0].shape[0] // (lax.axis_size("dp") * lax.axis_size("row"))
    one = add_low(one[0], swap_core(one[1]))
    two = add_low(two[0], swap_core(two[1]))
    if not regular(block):
        both = jnp.concatenate([one, two], axis=1)
        return lax.psum_scatter(
            both, ("dp", "row"), scatter_dimension=0, tiled=True
        ).astype(F4)
    a, b = bit_orders(lax.axis_size("dp"))
    both = jnp.concatenate([scatter_plane(one, a), scatter_plane(two, b)], axis=1)
    return scatter_line(both)


def sum_all(x):
    x = x + swap_core(x)
    for axis in ("dp", "row"):
        n = lax.axis_size(axis)
        if n & (n - 1):
            x = lax.psum(x, axis)
        else:
            for bit in range(n.bit_length() - 1):
                x = x + swap_bit(x, axis, n, bit)
    return x


def dot_nn(a, b):
    return jnp.dot(a, b, preferred_element_type=F4)


def dot_nt(a, b):
    return lax.dot_general(a, b, (((1,), (1,)), ((), ())), preferred_element_type=F4)


def dot_tn(a, b):
    return lax.dot_general(a, b, (((0,), (0,)), ((), ())), preferred_element_type=F4)


def mean_last(x):
    return jnp.mean(x, axis=-1, keepdims=True)


def centre(x):
    c = x - mean_last(x)
    return c, lax.rsqrt(mean_last(c * c) + EPSILON)


def group_matrix():
    i = lax.broadcasted_iota(jnp.int32, (TILE, TILE), 0) // HD
    j = lax.broadcasted_iota(jnp.int32, (TILE, TILE), 1) // HD
    return jnp.where(i == j, 1.0 / HD, 0.0).astype(BF)


def group_mean(x, matrix):
    high = x.astype(BF)
    low = (x - high.astype(F4)).astype(BF)
    return dot_nn(high, matrix) + dot_nn(low, matrix)


def head_norm(x, matrix):
    c = x - group_mean(x, matrix)
    return c, lax.rsqrt(group_mean(c * c, matrix) + EPSILON)


def head_norm_back(e, x, gain, matrix):
    c, r = head_norm(x, matrix)
    t = e * gain
    d = r * (t - group_mean(t, matrix) - c * (r * r) * group_mean(t * c, matrix))
    return d, e * c * r


def fold_heads(x):
    return jnp.sum(x, axis=0, keepdims=True)


def tiles(width):
    return width // TILE


def lane(i, width):
    return pl.ds(pl.multiple_of(i * width, width), width)


def call(body, outs, scratch, flops, *args):
    size = sum(a.size * a.dtype.itemsize for a in args)
    size += sum(math.prod(s) * jnp.dtype(d).itemsize for s, d in outs)
    hold = sum(math.prod(s.shape) * jnp.dtype(s.dtype).itemsize for s in scratch)
    limit = min(62 << 20, size + hold + (12 << 20))
    return pl.pallas_call(
        body,
        out_shape=[jax.ShapeDtypeStruct(s, d) for s, d in outs],
        in_specs=[VM] * len(args),
        out_specs=[VM] * len(outs),
        scratch_shapes=scratch,
        compiler_params=pltpu.CompilerParams(vmem_limit_bytes=limit),
        cost_estimate=pl.CostEstimate(
            flops=int(flops), bytes_accessed=int(size), transcendentals=0
        ),
    )(*args)


def qkv_body(with_query, half, *refs):
    p, g1, b1, qg, kg, a1o, a1x, a2o, a2x = refs[:9]
    normed, k_raw, k_low, v_low = refs[9:13]
    x = p[...].astype(F4)
    c, r = centre(x)
    n = (c * r * g1[...] + b1[...]).astype(BF)
    normed[...] = n
    head = 0 if with_query else half
    cut = a1o.shape[1]
    for s, (a1, a2) in enumerate(((a1o, a2o), (a1x, a2x))):
        at = s * half
        one = dot_nn(n, a1[:, head:])
        two = dot_nn(n, a2[...])
        if with_query:
            refs[13][:, at : at + half] = one[:, :half]
        k_raw[:, at : at + cut - half] = one[:, half - head :]
        k_raw[:, at + cut - half : at + half] = two[:, : 2 * half - cut]
        v_low[:, at : at + half] = two[:, 2 * half - cut :].astype(BF)
    matrix = group_matrix()
    for t in range(tiles(2 * half)):
        cols = slice(t * TILE, (t + 1) * TILE)
        c, r = head_norm(k_raw[:, cols], matrix)
        k_low[:, cols] = (c * r * kg[...]).astype(BF)
        if with_query:
            c, r = head_norm(refs[13][:, cols], matrix)
            refs[14][:, cols] = (c * r * qg[...] * (float(HD) ** -0.5)).astype(BF)


def qkv_block(with_query, p, g1, b1, qg, kg, parts):
    tokens, width = p.shape
    half = width // 2
    outs = [((tokens, width), BF), ((tokens, width), F4)] + [((tokens, width), BF)] * 2
    if with_query:
        outs += [((tokens, width), F4), ((tokens, width), BF)]
    flops = 2 * tokens * width * width * (3 if with_query else 2)
    body = functools.partial(qkv_body, with_query, half)
    return call(body, outs, [], flops, p, g1, b1, qg, kg, *parts)


def pair_masks(rows):
    at = lax.broadcasted_iota(jnp.int32, (rows, LANES), 1)
    return (at < HD, at >= HD)


def pick(x, mask):
    return jnp.where(mask, x, jnp.zeros_like(x))


def column(ref, h):
    at = lax.broadcasted_iota(jnp.int32, ref.shape, 1)
    return jnp.sum(jnp.where(at == h, ref[...], 0.0), axis=-1, keepdims=True)


def attend_body(n, *refs):
    q, idq, idk = refs[:3]
    ks, vs = refs[3 : 3 + n], refs[3 + n : 3 + 2 * n]
    att, stat, k_all, v_all, bias = refs[3 + 2 * n :]
    tokens = q.shape[0]
    for b in range(n):
        k_all[b * tokens : (b + 1) * tokens, :] = ks[b][...]
        v_all[b * tokens : (b + 1) * tokens, :] = vs[b][...]
    bias[...] = jnp.where(idq[...] == idk[...], 0.0, -1e30)
    stat[...] = jnp.zeros_like(stat)
    masks = pair_masks(tokens)
    at = lax.broadcasted_iota(jnp.int32, stat.shape, 1)

    @pl.loop(0, q.shape[1] // LANES)
    def _(pair):
        cols = lane(pair, LANES)
        q_pair = q[:, cols]
        k_pair = k_all[:, cols]
        v_pair = v_all[:, cols]
        outs = []
        for s, mask in enumerate(masks):
            e = jnp.exp(dot_nt(pick(q_pair, mask), k_pair) + bias[...])
            total = jnp.sum(e, axis=-1, keepdims=True)
            low = (e * (1.0 / total)).astype(BF)
            outs.append(dot_nn(low, v_pair))
            stat[...] += jnp.where(at == 2 * pair + s, jnp.log(total), 0.0)
        att[:, cols] = jnp.where(masks[0], outs[0], outs[1]).astype(BF)


def attend(q, idq, idk, ks, vs):
    tokens, width = q.shape
    n = len(ks)
    outs = [((tokens, width), BF), ((tokens, LANES), F4)]
    scratch = [
        pltpu.VMEM((n * tokens, width), BF),
        pltpu.VMEM((n * tokens, width), BF),
        pltpu.VMEM((tokens, n * tokens), F4),
    ]
    flops = 4 * tokens * n * tokens * width * 4
    body = functools.partial(attend_body, n)
    return call(body, outs, scratch, flops, q, idq, idk, *ks, *vs)


ROOT = math.sqrt(2.0 / math.pi)
CUBE = 0.044715


def gelu_pair(u):
    square = u * u
    t = jnp.tanh(ROOT * u * (1.0 + CUBE * square))
    half = 0.5 * (1.0 + t)
    slope = half + 0.5 * u * (1.0 - t * t) * (ROOT * (1.0 + 3.0 * CUBE * square))
    return u * half, slope


def up_body(half, p, att, cot, g2, b2, b1o, b1x, b2o, b2x, *outs):
    mixed, n2, act, slope, g1o, g1x, g2o, g2x = outs
    first = b1o.shape[1]
    inner = first + b2o.shape[1] - half
    m = p[...].astype(F4)
    for s, part in enumerate((b2o, b2x)):
        m = m + dot_nt(att[:, s * half : (s + 1) * half], part[:, :half])
    mixed[...] = m
    c, r = centre(m)
    n2[...] = (c * r * g2[...] + b2[...]).astype(BF)
    for s, (one, two) in enumerate(((b1o, b2o), (b1x, b2x))):

        @pl.loop(0, tiles(first))
        def _(i):
            u = dot_nn(n2[...], one[:, lane(i, TILE)])
            to = pl.ds(pl.multiple_of(s * inner + i * TILE, TILE), TILE)
            a, d = gelu_pair(u)
            act[:, to] = a.astype(BF)
            slope[:, to] = d.astype(BF)

        rest = inner - first
        for i in range(tiles(rest)):
            u = dot_nn(n2[...], two[:, half + i * TILE : half + (i + 1) * TILE])
            to = slice(s * inner + first + i * TILE, s * inner + first + (i + 1) * TILE)
            a, d = gelu_pair(u)
            act[:, to] = a.astype(BF)
            slope[:, to] = d.astype(BF)
    mid = g1o.shape[1]
    for s, (one, two) in enumerate(((g1o, g2o), (g1x, g2x))):
        for base, out in ((s * inner, one), (s * inner + mid, two)):

            @pl.loop(0, tiles(mid))
            def _(i):
                frm = pl.ds(pl.multiple_of(base + i * TILE, TILE), TILE)
                out[:, lane(i, TILE)] = dot_tn(cot[...], act[:, frm]).astype(BF)


def down_body(half, *refs):
    mixed, n2, act, slope, att, cot, g2 = refs[:7]
    b1o, b1x, b2o, b2x, c1o, c1x, c2o, c2x = refs[7:15]
    result, d_mixed, d_att, delta, gains, h1o, h1x, h2o, h2x, d_up = refs[15:]
    first = b1o.shape[1]
    inner = first + b2o.shape[1] - half
    mid = c1o.shape[1]
    out = mixed[...]
    for s, (one, two) in enumerate(((c1o, c2o), (c1x, c2x))):
        at = s * inner
        out = out + dot_nt(act[:, at : at + mid], one[...])
        out = out + dot_nt(act[:, at + mid : at + inner], two[...])
        for base, part in ((at, one), (at + mid, two)):

            @pl.loop(0, tiles(mid))
            def _(i):
                to = pl.ds(pl.multiple_of(base + i * TILE, TILE), TILE)
                d = dot_nn(cot[...], part[:, lane(i, TILE)])
                d_up[:, to] = (d * slope[:, to].astype(F4)).astype(BF)

    result[...] = out.astype(BF)
    e = jnp.zeros(mixed.shape, F4)
    for s, (one, two) in enumerate(((b1o, b2o), (b1x, b2x))):
        at = s * inner
        e = e + dot_nt(d_up[:, at : at + first], one[...])
        e = e + dot_nt(d_up[:, at + first : at + inner], two[:, half:])
    c, r = centre(mixed[...])
    t = e * g2[...]
    d_mixed[...] = cot[...].astype(F4) + r * (
        t - mean_last(t) - c * (r * r) * mean_last(t * c)
    )
    gains[0:1, :] = jnp.sum(e * c * r, axis=0, keepdims=True)
    gains[1:2, :] = jnp.sum(e, axis=0, keepdims=True)
    d_branch = d_mixed[...].astype(BF)
    row = lax.broadcasted_iota(jnp.int32, (half, LANES), 0) // HD
    col = lax.broadcasted_iota(jnp.int32, (half, LANES), 1)
    sums = jnp.zeros(delta.shape, F4)
    for s, part in enumerate((b2o, b2x)):
        cols = slice(s * half, (s + 1) * half)
        d = dot_nn(d_branch, part[:, :half]).astype(BF)
        d_att[:, cols] = d
        prod = d.astype(F4) * att[:, cols].astype(F4)
        high = prod.astype(BF)
        low = (prod - high.astype(F4)).astype(BF)
        sel = jnp.where(row + s * (half // HD) == col, 1.0, 0.0).astype(BF)
        sums = sums + dot_nn(high, sel) + dot_nn(low, sel)
    delta[...] = sums
    for s, (one, two) in enumerate(((h1o, h2o), (h1x, h2x))):
        at = s * inner
        two[:, :half] = dot_tn(d_branch, att[:, s * half : (s + 1) * half]).astype(BF)

        @pl.loop(0, tiles(first))
        def _(i):
            frm = pl.ds(pl.multiple_of(at + i * TILE, TILE), TILE)
            one[:, lane(i, TILE)] = dot_tn(n2[...], d_up[:, frm]).astype(BF)

        two[:, half:] = dot_tn(n2[...], d_up[:, at + first : at + inner]).astype(BF)


def back_body(half, *refs):
    q, k, v, d_att, stat, delta, idq, idk, k_raw, p, kg = refs[:11]
    a1o, a1x, a2o, a2x = refs[11:15]
    dk_low, dv_low, dq, part, k_gain, gains, bias, dk = refs[15:]
    tokens = q.shape[0]
    bias[...] = jnp.where(idq[...] == idk[...], 0.0, -1e30)
    masks = pair_masks(tokens)

    @pl.loop(0, q.shape[1] // LANES)
    def _(pair):
        cols = lane(pair, LANES)
        q_pair, k_pair, v_pair, d_pair = q[:, cols], k[:, cols], v[:, cols], d_att[:, cols]
        sum_q = sum_k = sum_v = None
        for s, mask in enumerate(masks):
            q_one, d_one, k_one = pick(q_pair, mask), pick(d_pair, mask), pick(k_pair, mask)
            h = 2 * pair + s
            score = dot_nt(q_one, k_pair) + bias[...]
            prob = jnp.exp(score - column(stat, h))
            d_prob = dot_nt(d_one, v_pair)
            d_score = (prob * (d_prob - column(delta, h))).astype(BF)
            one_v = dot_tn(prob.astype(BF), d_one)
            one_k = dot_tn(d_score, q_one)
            one_q = dot_nn(d_score, k_one)
            sum_v = one_v if s == 0 else sum_v + one_v
            sum_k = one_k if s == 0 else sum_k + one_k
            sum_q = one_q if s == 0 else sum_q + one_q
        dq[:, cols] = sum_q
        dk[:, cols] = sum_k
        dv_low[:, cols] = sum_v.astype(BF)

    matrix = group_matrix()
    total = jnp.zeros((1, TILE), F4)
    for t in range(tiles(2 * half)):
        cols = slice(t * TILE, (t + 1) * TILE)
        d, g = head_norm_back(dk[:, cols], k_raw[:, cols], kg[...], matrix)
        dk_low[:, cols] = d.astype(BF)
        total = total + fold_heads(g)
    k_gain[...] = total
    cut = a1o.shape[1]
    e = jnp.zeros((tokens, 2 * half), F4)
    for s, (one, two) in enumerate(((a1o, a2o), (a1x, a2x))):
        at = s * half
        mid = at + cut - half
        e = e + dot_nt(dk_low[:, at:mid], one[:, half:])
        e = e + dot_nt(dk_low[:, mid : at + half], two[:, : 2 * half - cut])
        e = e + dot_nt(dv_low[:, at : at + half], two[:, 2 * half - cut :])
    part[...] = e.astype(part.dtype)
    c, r = centre(p[...].astype(F4))
    gains[0:1, :] = jnp.sum(e * c * r, axis=0, keepdims=True)
    gains[1:2, :] = jnp.sum(e, axis=0, keepdims=True)


def back_block(last, q, k, v, d_att, stat, delta, idq, idk, k_raw, p, kg, parts):
    tokens, width = q.shape
    half = width // 2
    outs = [
        ((tokens, width), BF),
        ((tokens, width), BF),
        ((tokens, width), F4),
        ((tokens, width), F4 if last else BF),
        ((1, TILE), F4),
        ((2, width), F4),
    ]
    scratch = [pltpu.VMEM((tokens, tokens), F4), pltpu.VMEM((tokens, width), F4)]
    flops = 10 * tokens * tokens * width * 4 + 4 * tokens * width * width
    body = functools.partial(back_body, half)
    return call(
        body, outs, scratch, flops,
        q, k, v, d_att, stat, delta, idq, idk, k_raw, p, kg, *parts,
    )


def weight_body(n, half, *refs):
    q_raw, qg, p, own = refs[:4]
    a1o, a1x = refs[4:6]
    dqs, ns = refs[6 : 6 + n], refs[6 + n : 6 + 2 * n]
    dks, dvs = refs[6 + 2 * n : 6 + 3 * n], refs[6 + 3 * n : 6 + 4 * n]
    part, q_gain, gains, g1o, g1x, g2o, g2x, dq_low, n_all, dk_all, dv_all = refs[6 + 4 * n :]
    tokens = q_raw.shape[0]
    matrix = group_matrix()
    total = jnp.zeros((1, TILE), F4)
    factor = float(HD) ** -0.5
    for t in range(tiles(2 * half)):
        cols = slice(t * TILE, (t + 1) * TILE)
        e = dqs[0][:, cols]
        for other in dqs[1:]:
            e = e + other[:, cols]
        d, g = head_norm_back(e * factor, q_raw[:, cols], qg[...], matrix)
        dq_low[:, cols] = d.astype(BF)
        total = total + fold_heads(g)
    q_gain[...] = total
    e = dot_nt(dq_low[:, :half], a1o[:, :half]) + dot_nt(dq_low[:, half:], a1x[:, :half])
    part[...] = own[...] + e
    c, r = centre(p[...].astype(F4))
    gains[0:1, :] = jnp.sum(e * c * r, axis=0, keepdims=True)
    gains[1:2, :] = jnp.sum(e, axis=0, keepdims=True)
    for b in range(n):
        rows = slice(b * tokens, (b + 1) * tokens)
        n_all[rows, :] = ns[b][...]
        dk_all[rows, :] = dks[b][...]
        dv_all[rows, :] = dvs[b][...]
    cut = g1o.shape[1]
    for s, (one, two) in enumerate(((g1o, g2o), (g1x, g2x))):
        at = s * half
        mid = at + cut - half
        one[:, :half] = dot_tn(ns[0][...], dq_low[:, at : at + half]).astype(BF)
        one[:, half:] = dot_tn(n_all[...], dk_all[:, at:mid]).astype(BF)
        two[:, : 2 * half - cut] = dot_tn(n_all[...], dk_all[:, mid : at + half]).astype(BF)
        two[:, 2 * half - cut :] = dot_tn(n_all[...], dv_all[:, at : at + half]).astype(BF)


def take_micro(x, c):
    mine = jnp.where(c == 0, x[0], x[1])
    other = jnp.where(c == 0, x[1], x[0])
    return mine, other


def per_device(
    patches,
    picture_ids,
    ln1_gain,
    ln1_bias,
    w_query,
    w_key,
    w_value,
    q_gain,
    k_gain,
    w_out,
    ln2_gain,
    ln2_bias,
    w_up,
    w_down,
    cotangent,
):
    n = lax.axis_size("row")
    c = lax.axis_index("col")
    place = ring_place(lax.axis_index("row"), n)
    width = patches.shape[-1]
    half = w_query.shape[1]
    piece = patches.shape[2]
    tokens = 2 * piece
    inner = w_up.shape[1]

    both = jnp.stack([patches[0], cotangent[0]], axis=1)
    mine, other = take_micro(both, c)
    got = swap_core(other)
    low = jnp.where(c == 0, mine, got)
    high = jnp.where(c == 0, got, mine)
    own = jnp.concatenate([low, high], axis=1)
    p_own, cot = own[0], own[1]

    cut_a = half + half * 2 // 3
    first = inner * 2 // 3
    chunk_a = jnp.concatenate([w_query, w_key, w_value], axis=1)
    chunk_b = jnp.concatenate([w_up[:, :first], w_out.T, w_up[:, first:]], axis=1)
    chunk_c = w_down.T
    a_one, a_two = gather_weights(chunk_a, cut_a)
    a_parts = a_one + a_two
    blocks = [p_own]
    for _ in range(n - 1):
        blocks.append(hop(blocks[-1], n))
    b_one, b_two = gather_weights(chunk_b, first)
    b_parts = b_one + b_two
    c_one, c_two = gather_weights(chunk_c, inner // 2)
    c_parts = c_one + c_two

    g1, b1 = ln1_gain[None], ln1_bias[None]
    g2, b2 = ln2_gain[None], ln2_bias[None]
    qg, kg = jnp.tile(q_gain, TILE // HD)[None], jnp.tile(k_gain, TILE // HD)[None]

    ids = jnp.where(c == 0, picture_ids[0, 0], picture_ids[0, 1]).reshape(n, tokens)
    id_blocks = [
        lax.dynamic_index_in_dim(ids, ring_row((place - j + n) % n, n), 0)
        for j in range(n)
    ]
    idq = id_blocks[0].reshape(tokens, 1)
    idk = jnp.concatenate(id_blocks, axis=1)

    made = [qkv_block(j == 0, blocks[j], g1, b1, qg, kg, a_parts) for j in range(n)]
    q_raw, q_low = made[0][4], made[0][5]
    normed = [m[0] for m in made]
    k_raw, k_low, v_low = [m[1] for m in made], [m[2] for m in made], [m[3] for m in made]

    att, stat = attend(q_low, idq, idk, k_low, v_low)

    mid = inner // 2
    mixed, n2, act, slope, *gc = call(
        functools.partial(up_body, half),
        [((tokens, width), F4), ((tokens, width), BF)]
        + [((tokens, 2 * inner), BF)] * 2
        + [((width, mid), BF)] * 4,
        [],
        2 * tokens * width * (width + 4 * inner),
        p_own, att, cot, g2, b2, *b_parts,
    )
    grad_c = scatter_grads((gc[0], gc[1]), (gc[2], gc[3]))

    result, d_mixed, d_att, delta, gains2, *gb = call(
        functools.partial(down_body, half),
        [((tokens, width), BF), ((tokens, width), F4), ((tokens, width), BF)]
        + [((tokens, LANES), F4), ((2, width), F4)]
        + [((width, first), BF)] * 2
        + [((width, half + inner - first), BF)] * 2,
        [pltpu.VMEM((tokens, 2 * inner), BF)],
        2 * tokens * width * (2 * width + 8 * inner),
        mixed, n2, act, slope, att, cot, g2, *b_parts, *c_parts,
    )
    grad_b = scatter_grads((gb[0], gb[1]), (gb[2], gb[3]))

    back = [None] * n
    acc = None
    for j in [*range(1, n), 0]:
        back[j] = back_block(
            j == 0, q_low, k_low[j], v_low[j], d_att, stat, delta, idq,
            id_blocks[j], k_raw[j], blocks[j], kg, a_parts,
        )
        if j:
            part = back[j][3]
            acc = part if acc is None else add_low(part, acc)
            acc = hop(acc, n)

    part, dq_gain, gains_q, *ga = call(
        functools.partial(weight_body, n, half),
        [((tokens, width), F4), ((1, TILE), F4), ((2, width), F4)]
        + [((width, cut_a), BF)] * 2
        + [((width, 3 * half - cut_a), BF)] * 2,
        [pltpu.VMEM((tokens, width), BF)] + [pltpu.VMEM((n * tokens, width), BF)] * 3,
        2 * tokens * width * width * (2 + 2 * n),
        q_raw, qg, p_own, back[0][3], *a_one,
        *[b[2] for b in back], *normed, *[b[0] for b in back], *[b[1] for b in back],
    )
    grad_a = scatter_grads((ga[0], ga[1]), (ga[2], ga[3]))

    gains1 = gains_q
    key_gain = jnp.zeros((1, TILE), F4)
    for b in back:
        gains1 = gains1 + b[5]
        key_gain = key_gain + b[4]
    small = jnp.concatenate(
        [
            gains1.reshape(-1, LANES),
            gains2.reshape(-1, LANES),
            dq_gain.reshape(-1, LANES),
            key_gain.reshape(-1, LANES),
        ],
        axis=0,
    )
    small = sum_all(small)
    step = width // LANES
    grad_g1, grad_b1 = small[:step].reshape(-1), small[step : 2 * step].reshape(-1)
    grad_g2, grad_b2 = (
        small[2 * step : 3 * step].reshape(-1),
        small[3 * step : 4 * step].reshape(-1),
    )
    rest = TILE // LANES
    grad_gq = small[4 * step : 4 * step + rest].reshape(-1, HD).sum(axis=0)
    grad_gk = small[4 * step + rest :].reshape(-1, HD).sum(axis=0)

    e = part if acc is None else part + acc.astype(F4)
    centred, rate = centre(p_own.astype(F4))
    t = e * g1
    grad_in = d_mixed + rate * (
        t - mean_last(t) - centred * (rate * rate) * mean_last(t * centred)
    )

    def back_home(x):
        lower, upper = x[:piece], x[piece:]
        keep = jnp.where(c == 0, lower, upper)
        got = swap_core(jnp.where(c == 0, upper, lower))
        return jnp.stack([jnp.where(c == 0, keep, got), jnp.where(c == 0, got, keep)])

    rest = half + first
    grad_wu = jnp.concatenate([grad_b[:, :first], grad_b[:, rest:]], axis=1)
    return (
        back_home(result)[None],
        back_home(grad_in)[None],
        grad_g1,
        grad_b1,
        grad_a[:, :half],
        grad_a[:, half : 2 * half],
        grad_a[:, 2 * half :],
        grad_gq,
        grad_gk,
        grad_b[:, first:rest].T,
        grad_g2,
        grad_b2,
        grad_wu,
        grad_c.T,
    )


def solution(mesh):
    rows = P("dp", None, ("row", "col"), None)
    inward = P(("dp", "row"), "col")
    outward = P("col", ("dp", "row"))
    return jax.shard_map(
        per_device,
        mesh=mesh,
        in_specs=(
            rows, P("dp", None, None), P(), P(), inward, inward, inward, P(), P(),
            outward, P(), P(), inward, outward, rows,
        ),
        out_specs=(
            rows, rows, P(), P(), inward, inward, inward, P(), P(),
            outward, P(), P(), inward, outward,
        ),
        check_vma=False,
    )
```

```python
import functools
import math

import jax
import jax.numpy as jnp
from jax import lax
from jax.experimental import pallas as pl
from jax.experimental.pallas import tpu as pltpu
from jax.sharding import PartitionSpec as P

HD = 64
LANES = 128
TILE = 256
EPSILON = 1e-06
BF = jnp.bfloat16
F4 = jnp.float32
VM = pl.BlockSpec(memory_space=pltpu.VMEM)


def ring_order(n):
    return list(range(0, n, 2)) + list(range(n - 1 - (n % 2), 0, -2))


def ring_place(r, n):
    return jnp.where(r % 2 == 0, r // 2, n - 1 - r // 2 - (n % 2) + (n % 2) * 1)


def ring_row(q, n):
    return jnp.where(2 * q < n, 2 * q, 2 * (n - 1 - q) + 1)


def hop(x, n):
    order = ring_order(n)
    pairs = [(order[i], order[(i + 1) % n]) for i in range(n)]
    return lax.ppermute(x, "row", pairs)


def swap_bit(x, axis, n, bit):
    return lax.ppermute(x, axis, [(i, i ^ (1 << bit)) for i in range(n)])


def swap_core(x):
    return lax.ppermute(x, "col", [(0, 1), (1, 0)])


def bit_orders(n):
    bits = list(range(n.bit_length() - 1))
    half = len(bits) // 2
    return bits, bits[half:] + bits[:half]


def regular(block):
    dp = lax.axis_size("dp")
    return dp & (dp - 1) == 0 and block % 16 == 0


def after(x, deps):
    if not deps:
        return x
    return lax.optimization_barrier((x, *deps))[0]


class Chain:
    def __init__(self, steps):
        self.steps = steps
        self.last = ()
        self.value = None
        next(steps)

    def step(self, *deps):
        if self.value is None:
            try:
                self.last = self.steps.send(deps)
            except StopIteration as end:
                self.value = end.value
        return self

    def finish(self):
        while self.value is None:
            self.step()
        return self.value


def join_line(blocks):
    n = len(blocks)
    place = ring_place(lax.axis_index("row"), n)
    parts = []
    for r in range(n):
        slot = (place - ring_order(n).index(r)) % n
        parts.append(lax.select_n(slot, *blocks) if n > 1 else blocks[0])
    return jnp.concatenate(parts, axis=0)


def gather_steps(shard, cut):
    deps = yield ()
    if not regular(shard.shape[0]):
        whole = lax.all_gather(after(shard, deps), ("dp", "row"), axis=0, tiled=True)
        parts = [whole[:, :cut], whole[:, cut:]]
        deps = yield (whole,)
    else:
        n, m = lax.axis_size("row"), lax.axis_size("dp")
        me = lax.axis_index("dp")
        blocks = [shard]
        for _ in range(n - 1):
            blocks.append(hop(after(blocks[-1], deps), n))
            deps = yield (blocks[-1],)
        line = join_line(blocks)
        parts = [line[:, :cut], line[:, cut:]]
        orders = bit_orders(m)
        done = ([], [])
        for bits in zip(*orders):
            got = [
                swap_bit(after(x, deps), "dp", m, bit) for x, bit in zip(parts, bits)
            ]
            for i, bit in enumerate(bits):
                at = sum(1 for b in done[i] if b > bit)
                low = (me >> bit) & 1
                first = jnp.where(low == 0, parts[i], got[i])
                second = jnp.where(low == 0, got[i], parts[i])
                parts[i] = jnp.stack([first, second], axis=at)
                done[i].append(bit)
            deps = yield tuple(got)
        parts = [x.reshape(-1, x.shape[-1]) for x in parts]
    got = [swap_core(after(x, deps)) for x in parts]
    yield tuple(got)
    return (parts[0], got[0]), (parts[1], got[1])


def add_low(a, b):
    return (a.astype(F4) + b.astype(F4)).astype(BF)


def scatter_steps(one, two):
    n, m = lax.axis_size("row"), lax.axis_size("dp")
    block = one[0].shape[0] // (m * n)
    deps = yield ()
    got = [swap_core(after(x[1], deps)) for x in (one, two)]
    deps = yield tuple(got)
    parts = [add_low(x[0], y) for x, y in zip((one, two), got)]
    if not regular(block):
        both = after(jnp.concatenate(parts, axis=1), deps)
        total = lax.psum_scatter(both, ("dp", "row"), scatter_dimension=0, tiled=True)
        yield (total,)
        return total.astype(F4)
    me = lax.axis_index("dp")
    count = m.bit_length() - 1
    left = [list(range(count - 1, -1, -1)), list(range(count - 1, -1, -1))]
    parts = [x.reshape((2,) * count + (-1, x.shape[-1])) for x in parts]
    for bits in zip(*bit_orders(m)):
        got, keep = [], []
        for i, bit in enumerate(bits):
            at = left[i].index(bit)
            low = (me >> bit) & 1
            send = lax.dynamic_index_in_dim(parts[i], 1 - low, at, keepdims=False)
            keep.append(lax.dynamic_index_in_dim(parts[i], low, at, keepdims=False))
            got.append(swap_bit(after(send, deps), "dp", m, bit))
            left[i].remove(bit)
        deps = yield tuple(got)
        parts = [add_low(x, y) for x, y in zip(keep, got)]
    both = jnp.concatenate(parts, axis=1)
    place = ring_place(lax.axis_index("row"), n)
    both = both.reshape(n, -1, both.shape[-1])

    def own(q):
        return lax.dynamic_index_in_dim(both, ring_row(q % n, n), 0, keepdims=False)

    if n == 1:
        return both[0].astype(F4)
    acc = own(place - 1 + n)
    for step in range(n - 1):
        got = hop(after(acc, deps), n)
        deps = yield (got,)
        if step < n - 2:
            acc = add_low(own(place - 2 - step + n), got)
    return own(place).astype(F4) + got.astype(F4)


def sum_all(x):
    x = x + swap_core(x)
    for axis in ("dp", "row"):
        n = lax.axis_size(axis)
        if n & (n - 1):
            x = lax.psum(x, axis)
        else:
            for bit in range(n.bit_length() - 1):
                x = x + swap_bit(x, axis, n, bit)
    return x


def dot_nn(a, b):
    return jnp.dot(a, b, preferred_element_type=F4)


def dot_nt(a, b):
    return lax.dot_general(a, b, (((1,), (1,)), ((), ())), preferred_element_type=F4)


def dot_tn(a, b):
    return lax.dot_general(a, b, (((0,), (0,)), ((), ())), preferred_element_type=F4)


def mean_last(x):
    return jnp.mean(x, axis=-1, keepdims=True)


def centre(x):
    c = x - mean_last(x)
    return c, lax.rsqrt(mean_last(c * c) + EPSILON)


def group_matrix():
    i = lax.broadcasted_iota(jnp.int32, (TILE, TILE), 0) // HD
    j = lax.broadcasted_iota(jnp.int32, (TILE, TILE), 1) // HD
    return jnp.where(i == j, 1.0 / HD, 0.0).astype(BF)


def group_mean(x, matrix):
    high = x.astype(BF)
    low = (x - high.astype(F4)).astype(BF)
    return dot_nn(high, matrix) + dot_nn(low, matrix)


def head_norm(x, matrix):
    c = x - group_mean(x, matrix)
    return c, lax.rsqrt(group_mean(c * c, matrix) + EPSILON)


def head_norm_back(e, x, gain, matrix):
    c, r = head_norm(x, matrix)
    t = e * gain
    d = r * (t - group_mean(t, matrix) - c * (r * r) * group_mean(t * c, matrix))
    return d, e * c * r


def fold_heads(x):
    return jnp.sum(x, axis=0, keepdims=True)


def tiles(width):
    return width // TILE


def lane(i, width):
    return pl.ds(pl.multiple_of(i * width, width), width)


def call(body, outs, scratch, room, flops, *args):
    size = sum(a.size * a.dtype.itemsize for a in args)
    size += sum(math.prod(s) * jnp.dtype(d).itemsize for s, d in outs)
    hold = sum(math.prod(s.shape) * jnp.dtype(s.dtype).itemsize for s in scratch)
    return pl.pallas_call(
        body,
        out_shape=[jax.ShapeDtypeStruct(s, d) for s, d in outs],
        in_specs=[VM] * len(args),
        out_specs=[VM] * len(outs),
        scratch_shapes=scratch,
        compiler_params=pltpu.CompilerParams(vmem_limit_bytes=hold + (room << 20)),
        cost_estimate=pl.CostEstimate(
            flops=int(flops) * 4, bytes_accessed=int(size), transcendentals=0
        ),
    )(*args)


def pair_masks(rows):
    at = lax.broadcasted_iota(jnp.int32, (rows, LANES), 1)
    return (at < HD, at >= HD)


def pick(x, mask):
    return jnp.where(mask, x, jnp.zeros_like(x))


def column(ref, h):
    at = lax.broadcasted_iota(jnp.int32, ref.shape, 1)
    return jnp.sum(jnp.where(at == h, ref[...], 0.0), axis=-1, keepdims=True)


def look_body(first, last, half, *refs):
    p, g1, b1, kg, idq, idk, a1o, a1x, a2o, a2x = refs[:10]
    refs = refs[10:]
    if first:
        qg, normed, k_raw, k_low, v_low, out, stat, q_raw, q, bias = refs
    else:
        q, acc, total_in, normed, k_raw, k_low, v_low, out, stat, bias = refs
    x = p[...].astype(F4)
    c, r = centre(x)
    n = (c * r * g1[...] + b1[...]).astype(BF)
    normed[...] = n
    head = 0 if first else half
    cut = a1o.shape[1]
    for s, (a1, a2) in enumerate(((a1o, a2o), (a1x, a2x))):
        at = s * half
        one = dot_nn(n, a1[:, head:])
        two = dot_nn(n, a2[...])
        if first:
            q_raw[:, at : at + half] = one[:, :half]
        k_raw[:, at : at + cut - half] = one[:, half - head :]
        k_raw[:, at + cut - half : at + half] = two[:, : 2 * half - cut]
        v_low[:, at : at + half] = two[:, 2 * half - cut :].astype(BF)
    matrix = group_matrix()
    for t in range(tiles(2 * half)):
        cols = slice(t * TILE, (t + 1) * TILE)
        c, r = head_norm(k_raw[:, cols], matrix)
        k_low[:, cols] = (c * r * kg[...]).astype(BF)
        if first:
            c, r = head_norm(q_raw[:, cols], matrix)
            q[:, cols] = (c * r * qg[...] * (float(HD) ** -0.5)).astype(BF)

    bias[...] = jnp.where(idq[...] == idk[...], 0.0, -1e30)
    stat[...] = jnp.zeros_like(stat) if first else total_in[...]
    masks = pair_masks(p.shape[0])
    lanes = lax.broadcasted_iota(jnp.int32, stat.shape, 1)

    @pl.loop(0, 2 * half // LANES)
    def _(pair):
        cols = lane(pair, LANES)
        q_pair, k_pair, v_pair = q[:, cols], k_low[:, cols], v_low[:, cols]
        outs = []
        for s, mask in enumerate(masks):
            e = jnp.exp(dot_nt(pick(q_pair, mask), k_pair) + bias[...])
            total = jnp.sum(e, axis=-1, keepdims=True)
            got = dot_nn(e.astype(BF), v_pair)
            if not first:
                got = got + acc[:, cols]
            h = 2 * pair + s
            if last:
                total = total + column(stat, h)
                got = got * (1.0 / total)
                stat[...] = jnp.where(lanes == h, jnp.log(total), stat[...])
            else:
                stat[...] += jnp.where(lanes == h, total, 0.0)
            outs.append(got)
        out[:, cols] = jnp.where(masks[0], outs[0], outs[1]).astype(out.dtype)


def look(first, last, p, g1, b1, qg, kg, idq, idk, parts, before):
    tokens, width = p.shape
    half = width // 2
    wide = (tokens, width)
    outs = [(wide, BF), (wide, F4), (wide, BF), (wide, BF)]
    outs += [(wide, BF if last else F4), ((tokens, LANES), F4)]
    if first:
        outs += [(wide, F4), (wide, BF)]
    flops = 2 * tokens * width * (width * (3 if first else 2) + 4 * tokens)
    body = functools.partial(look_body, first, last, half)
    scratch = [pltpu.VMEM((tokens, tokens), F4)]
    extra = (qg,) if first else before
    return call(
        body, outs, scratch, 6, flops, p, g1, b1, kg, idq, idk, *parts, *extra
    )


ROOT = math.sqrt(2.0 / math.pi)
CUBE = 0.044715


def gelu_pair(u):
    square = u * u
    t = jnp.tanh(ROOT * u * (1.0 + CUBE * square))
    half = 0.5 * (1.0 + t)
    slope = half + 0.5 * u * (1.0 - t * t) * (ROOT * (1.0 + 3.0 * CUBE * square))
    return u * half, slope


def up_body(half, p, att, cot, g2, b2, b1o, b1x, b2o, b2x, *outs):
    mixed, n2, act, slope, g1o, g1x, g2o, g2x = outs
    first = b1o.shape[1]
    inner = first + b2o.shape[1] - half
    m = p[...].astype(F4)
    for s, part in enumerate((b2o, b2x)):
        m = m + dot_nt(att[:, s * half : (s + 1) * half], part[:, :half])
    mixed[...] = m
    c, r = centre(m)
    n2[...] = (c * r * g2[...] + b2[...]).astype(BF)
    for s, (one, two) in enumerate(((b1o, b2o), (b1x, b2x))):

        @pl.loop(0, tiles(first))
        def _(i):
            u = dot_nn(n2[...], one[:, lane(i, TILE)])
            to = pl.ds(pl.multiple_of(s * inner + i * TILE, TILE), TILE)
            a, d = gelu_pair(u)
            act[:, to] = a.astype(BF)
            slope[:, to] = d.astype(BF)

        rest = inner - first
        for i in range(tiles(rest)):
            u = dot_nn(n2[...], two[:, half + i * TILE : half + (i + 1) * TILE])
            to = slice(s * inner + first + i * TILE, s * inner + first + (i + 1) * TILE)
            a, d = gelu_pair(u)
            act[:, to] = a.astype(BF)
            slope[:, to] = d.astype(BF)
    mid = g1o.shape[1]
    for s, (one, two) in enumerate(((g1o, g2o), (g1x, g2x))):
        for base, out in ((s * inner, one), (s * inner + mid, two)):

            @pl.loop(0, tiles(mid))
            def _(i):
                frm = pl.ds(pl.multiple_of(base + i * TILE, TILE), TILE)
                out[:, lane(i, TILE)] = dot_tn(cot[...], act[:, frm]).astype(BF)


def slope_body(half, *refs):
    mixed, slope, att, cot, g2 = refs[:5]
    b1o, b1x, b2o, b2x, c1o, c1x, c2o, c2x = refs[5:13]
    d_up, d_mixed, d_att, delta, gains = refs[13:]
    first = b1o.shape[1]
    inner = first + b2o.shape[1] - half
    mid = c1o.shape[1]
    for s, (one, two) in enumerate(((c1o, c2o), (c1x, c2x))):
        at = s * inner
        for base, part in ((at, one), (at + mid, two)):

            @pl.loop(0, tiles(mid))
            def _(i):
                to = pl.ds(pl.multiple_of(base + i * TILE, TILE), TILE)
                d = dot_nn(cot[...], part[:, lane(i, TILE)])
                d_up[:, to] = (d * slope[:, to].astype(F4)).astype(BF)

    e = jnp.zeros(mixed.shape, F4)
    for s, (one, two) in enumerate(((b1o, b2o), (b1x, b2x))):
        at = s * inner
        e = e + dot_nt(d_up[:, at : at + first], one[...])
        e = e + dot_nt(d_up[:, at + first : at + inner], two[:, half:])
    c, r = centre(mixed[...])
    t = e * g2[...]
    d_mixed[...] = cot[...].astype(F4) + r * (
        t - mean_last(t) - c * (r * r) * mean_last(t * c)
    )
    gains[0:1, :] = jnp.sum(e * c * r, axis=0, keepdims=True)
    gains[1:2, :] = jnp.sum(e, axis=0, keepdims=True)
    d_branch = d_mixed[...].astype(BF)
    row = lax.broadcasted_iota(jnp.int32, (half, LANES), 0) // HD
    col = lax.broadcasted_iota(jnp.int32, (half, LANES), 1)
    sums = jnp.zeros(delta.shape, F4)
    for s, part in enumerate((b2o, b2x)):
        cols = slice(s * half, (s + 1) * half)
        d = dot_nn(d_branch, part[:, :half]).astype(BF)
        d_att[:, cols] = d
        prod = d.astype(F4) * att[:, cols].astype(F4)
        high = prod.astype(BF)
        low = (prod - high.astype(F4)).astype(BF)
        sel = jnp.where(row + s * (half // HD) == col, 1.0, 0.0).astype(BF)
        sums = sums + dot_nn(high, sel) + dot_nn(low, sel)
    delta[...] = sums


def inner_body(half, *refs):
    mixed, n2, act, att, d_up, d_mixed, c1o, c1x, c2o, c2x = refs[:10]
    result, h1o, h1x, h2o, h2x = refs[10:]
    first = h1o.shape[1]
    inner = first + h2o.shape[1] - half
    mid = c1o.shape[1]
    out = mixed[...]
    for s, (one, two) in enumerate(((c1o, c2o), (c1x, c2x))):
        at = s * inner
        out = out + dot_nt(act[:, at : at + mid], one[...])
        out = out + dot_nt(act[:, at + mid : at + inner], two[...])
    result[...] = out.astype(BF)
    d_branch = d_mixed[...].astype(BF)
    for s, (one, two) in enumerate(((h1o, h2o), (h1x, h2x))):
        at = s * inner
        two[:, :half] = dot_tn(d_branch, att[:, s * half : (s + 1) * half]).astype(BF)

        @pl.loop(0, tiles(first))
        def _(i):
            frm = pl.ds(pl.multiple_of(at + i * TILE, TILE), TILE)
            one[:, lane(i, TILE)] = dot_tn(n2[...], d_up[:, frm]).astype(BF)

        two[:, half:] = dot_tn(n2[...], d_up[:, at + first : at + inner]).astype(BF)


def back_body(half, *refs):
    q, k, v, d_att, stat, delta, idq, idk, k_raw, p, kg = refs[:11]
    a1o, a1x, a2o, a2x = refs[11:15]
    dk_low, dv_low, dq, part, k_gain, gains, bias, dk = refs[15:]
    tokens = q.shape[0]
    bias[...] = jnp.where(idq[...] == idk[...], 0.0, -1e30)
    masks = pair_masks(tokens)

    @pl.loop(0, q.shape[1] // LANES)
    def _(pair):
        cols = lane(pair, LANES)
        q_pair, k_pair, v_pair, d_pair = q[:, cols], k[:, cols], v[:, cols], d_att[:, cols]
        sum_q = sum_k = sum_v = None
        for s, mask in enumerate(masks):
            q_one, d_one, k_one = pick(q_pair, mask), pick(d_pair, mask), pick(k_pair, mask)
            h = 2 * pair + s
            score = dot_nt(q_one, k_pair) + bias[...]
            prob = jnp.exp(score - column(stat, h))
            d_prob = dot_nt(d_one, v_pair)
            d_score = (prob * (d_prob - column(delta, h))).astype(BF)
            one_v = dot_tn(prob.astype(BF), d_one)
            one_k = dot_tn(d_score, q_one)
            one_q = dot_nn(d_score, k_one)
            sum_v = one_v if s == 0 else sum_v + one_v
            sum_k = one_k if s == 0 else sum_k + one_k
            sum_q = one_q if s == 0 else sum_q + one_q
        dq[:, cols] = sum_q
        dk[:, cols] = sum_k
        dv_low[:, cols] = sum_v.astype(BF)

    matrix = group_matrix()
    total = jnp.zeros((1, TILE), F4)
    for t in range(tiles(2 * half)):
        cols = slice(t * TILE, (t + 1) * TILE)
        d, g = head_norm_back(dk[:, cols], k_raw[:, cols], kg[...], matrix)
        dk_low[:, cols] = d.astype(BF)
        total = total + fold_heads(g)
    k_gain[...] = total
    cut = a1o.shape[1]
    e = jnp.zeros((tokens, 2 * half), F4)
    for s, (one, two) in enumerate(((a1o, a2o), (a1x, a2x))):
        at = s * half
        mid = at + cut - half
        e = e + dot_nt(dk_low[:, at:mid], one[:, half:])
        e = e + dot_nt(dk_low[:, mid : at + half], two[:, : 2 * half - cut])
        e = e + dot_nt(dv_low[:, at : at + half], two[:, 2 * half - cut :])
    part[...] = e.astype(part.dtype)
    c, r = centre(p[...].astype(F4))
    gains[0:1, :] = jnp.sum(e * c * r, axis=0, keepdims=True)
    gains[1:2, :] = jnp.sum(e, axis=0, keepdims=True)


def back_block(last, q, k, v, d_att, stat, delta, idq, idk, k_raw, p, kg, parts):
    tokens, width = q.shape
    half = width // 2
    outs = [
        ((tokens, width), BF),
        ((tokens, width), BF),
        ((tokens, width), F4),
        ((tokens, width), F4 if last else BF),
        ((1, TILE), F4),
        ((2, width), F4),
    ]
    scratch = [pltpu.VMEM((tokens, tokens), F4), pltpu.VMEM((tokens, width), F4)]
    flops = 10 * tokens * tokens * width * 4 + 4 * tokens * width * width
    body = functools.partial(back_body, half)
    return call(
        body, outs, scratch, 7, flops,
        q, k, v, d_att, stat, delta, idq, idk, k_raw, p, kg, *parts,
    )


def weight_body(n, half, *refs):
    q_raw, qg, p, own = refs[:4]
    a1o, a1x = refs[4:6]
    dqs, ns = refs[6 : 6 + n], refs[6 + n : 6 + 2 * n]
    dks, dvs = refs[6 + 2 * n : 6 + 3 * n], refs[6 + 3 * n : 6 + 4 * n]
    part, q_gain, gains, g1o, g1x, g2o, g2x, dq_low, n_all, dk_all, dv_all = refs[6 + 4 * n :]
    tokens = q_raw.shape[0]
    matrix = group_matrix()
    total = jnp.zeros((1, TILE), F4)
    factor = float(HD) ** -0.5
    for t in range(tiles(2 * half)):
        cols = slice(t * TILE, (t + 1) * TILE)
        e = dqs[0][:, cols]
        for other in dqs[1:]:
            e = e + other[:, cols]
        d, g = head_norm_back(e * factor, q_raw[:, cols], qg[...], matrix)
        dq_low[:, cols] = d.astype(BF)
        total = total + fold_heads(g)
    q_gain[...] = total
    e = dot_nt(dq_low[:, :half], a1o[:, :half]) + dot_nt(dq_low[:, half:], a1x[:, :half])
    part[...] = own[...] + e
    c, r = centre(p[...].astype(F4))
    gains[0:1, :] = jnp.sum(e * c * r, axis=0, keepdims=True)
    gains[1:2, :] = jnp.sum(e, axis=0, keepdims=True)
    for b in range(n):
        rows = slice(b * tokens, (b + 1) * tokens)
        n_all[rows, :] = ns[b][...]
        dk_all[rows, :] = dks[b][...]
        dv_all[rows, :] = dvs[b][...]
    cut = g1o.shape[1]
    for s, (one, two) in enumerate(((g1o, g2o), (g1x, g2x))):
        at = s * half
        mid = at + cut - half
        one[:, :half] = dot_tn(ns[0][...], dq_low[:, at : at + half]).astype(BF)
        one[:, half:] = dot_tn(n_all[...], dk_all[:, at:mid]).astype(BF)
        two[:, : 2 * half - cut] = dot_tn(n_all[...], dk_all[:, mid : at + half]).astype(BF)
        two[:, 2 * half - cut :] = dot_tn(n_all[...], dv_all[:, at : at + half]).astype(BF)


def take_micro(x, c):
    mine = jnp.where(c == 0, x[0], x[1])
    other = jnp.where(c == 0, x[1], x[0])
    return mine, other


def per_device(
    patches,
    picture_ids,
    ln1_gain,
    ln1_bias,
    w_query,
    w_key,
    w_value,
    q_gain,
    k_gain,
    w_out,
    ln2_gain,
    ln2_bias,
    w_up,
    w_down,
    cotangent,
):
    n = lax.axis_size("row")
    c = lax.axis_index("col")
    place = ring_place(lax.axis_index("row"), n)
    width = patches.shape[-1]
    half = w_query.shape[1]
    piece = patches.shape[2]
    tokens = 2 * piece
    inner = w_up.shape[1]

    cut_a = half + half * 2 // 3
    first = inner * 2 // 3
    mid = inner // 2
    chunk_a = jnp.concatenate([w_query, w_key, w_value], axis=1)
    chunk_b = jnp.concatenate([w_up[:, :first], w_out.T, w_up[:, first:]], axis=1)
    chain_a = Chain(gather_steps(chunk_a, cut_a))
    chain_b = Chain(gather_steps(chunk_b, first))
    chain_c = Chain(gather_steps(w_down.T, mid))

    def take(x):
        mine = jnp.where(c == 0, x[0], x[1])
        got = swap_core(jnp.where(c == 0, x[1], x[0]))
        return jnp.concatenate(
            [jnp.where(c == 0, mine, got), jnp.where(c == 0, got, mine)], axis=0
        )

    p_own = take(patches[0])
    for _ in range(n - 1):
        chain_a.step()
    line_a = chain_a.last
    chain_a.step()
    chain_b.step(*line_a)
    blocks = [p_own, hop(after(p_own, line_a), n)]
    chain_a.step()
    for _ in range(n - 2):
        chain_b.step()
    a_one, a_two = chain_a.finish()
    a_parts = a_one + a_two
    cot = take(cotangent[0])

    g1, b1 = ln1_gain[None], ln1_bias[None]
    g2, b2 = ln2_gain[None], ln2_bias[None]
    qg, kg = jnp.tile(q_gain, TILE // HD)[None], jnp.tile(k_gain, TILE // HD)[None]

    ids = jnp.where(c == 0, picture_ids[0, 0], picture_ids[0, 1]).reshape(n, tokens)
    id_blocks = [
        lax.dynamic_index_in_dim(ids, ring_row((place - j + n) % n, n), 0)
        for j in range(n)
    ]
    idq = id_blocks[0].reshape(tokens, 1)

    made = []
    before = ()
    for j in range(n):
        if j == 0:
            deps = chain_b.last
            chain_b.step()
        elif j == 1:
            deps = chain_b.last
            chain_b.step()
            chain_c.step(*deps)
        elif j == n - 1:
            for _ in range(n - 2):
                deps = chain_b.last + chain_c.last
                chain_c.step()
            chain_b.step()
            deps = chain_c.last
            chain_c.step()
        else:
            deps = chain_c.last
        if 0 < j < n - 1:
            blocks.append(hop(blocks[-1], n))
        made.append(
            look(
                j == 0, j == n - 1, after(blocks[j], deps), g1, b1, qg, kg, idq,
                id_blocks[j], a_parts, before,
            )
        )
        if j == 0:
            q_raw, q_low = made[0][6:]
        before = (q_low, *made[j][4:6])
    normed = [m[0] for m in made]
    k_raw, k_low, v_low = [m[1] for m in made], [m[2] for m in made], [m[3] for m in made]
    att, stat = made[-1][4:6]

    deps = chain_c.last
    b_one, b_two = chain_b.finish()
    b_parts = b_one + b_two
    chain_c.step()
    mixed, n2, act, slope, *gc = call(
        functools.partial(up_body, half),
        [((tokens, width), F4), ((tokens, width), BF)]
        + [((tokens, 2 * inner), BF)] * 2
        + [((width, mid), BF)] * 4,
        [], 10,
        2 * tokens * width * (width + 4 * inner),
        p_own, after(att, deps), cot, g2, b2, *b_parts,
    )
    c_one, c_two = chain_c.finish()
    c_parts = c_one + c_two

    back_c = Chain(scatter_steps((gc[0], gc[1]), (gc[2], gc[3]))).step()
    deps = back_c.last
    back_c.step()
    d_up, d_mixed, d_att, delta, gains2 = call(
        functools.partial(slope_body, half),
        [((tokens, 2 * inner), BF), ((tokens, width), F4), ((tokens, width), BF)]
        + [((tokens, LANES), F4), ((2, width), F4)],
        [], 14,
        2 * tokens * width * (width + 4 * inner),
        after(mixed, deps), slope, att, cot, g2, *b_parts, *c_parts,
    )
    deps = back_c.last
    back_c.step()
    result, *gb = call(
        functools.partial(inner_body, half),
        [((tokens, width), BF)]
        + [((width, first), BF)] * 2
        + [((width, half + inner - first), BF)] * 2,
        [], 14,
        2 * tokens * width * (width + 4 * inner),
        mixed, n2, act, att, d_up, after(d_mixed, deps), *c_parts,
    )
    deps = back_c.last
    back_c.step()
    back_b = Chain(scatter_steps((gb[0], gb[1]), (gb[2], gb[3]))).step()

    back = [None] * n
    acc = None
    for j in [*range(1, n), 0]:
        back[j] = back_block(
            j == 0, q_low, k_low[j], v_low[j], after(d_att, deps), stat, delta, idq,
            id_blocks[j], k_raw[j], blocks[j], kg, a_parts,
        )
        deps = back_c.last + back_b.last
        back_c.step()
        back_b.step()
        if j:
            part = back[j][3]
            if acc is None:
                acc = part
            else:
                deps = deps + (acc,)
                acc = add_low(part, acc)
            acc = hop(acc, n)

    part, dq_gain, gains_q, *ga = call(
        functools.partial(weight_body, n, half),
        [((tokens, width), F4), ((1, TILE), F4), ((2, width), F4)]
        + [((width, cut_a), BF)] * 2
        + [((width, 3 * half - cut_a), BF)] * 2,
        [pltpu.VMEM((tokens, width), BF)] + [pltpu.VMEM((n * tokens, width), BF)] * 3,
        14,
        2 * tokens * width * width * (2 + 2 * n),
        after(q_raw, deps), qg, p_own, back[0][3], *a_one,
        *[b[2] for b in back], *normed, *[b[0] for b in back], *[b[1] for b in back],
    )
    grad_a = Chain(scatter_steps((ga[0], ga[1]), (ga[2], ga[3]))).finish()
    grad_b, grad_c = back_b.finish(), back_c.finish()

    gains1 = gains_q
    key_gain = jnp.zeros((1, TILE), F4)
    for b in back:
        gains1 = gains1 + b[5]
        key_gain = key_gain + b[4]
    small = jnp.concatenate(
        [
            gains1.reshape(-1, LANES),
            gains2.reshape(-1, LANES),
            dq_gain.reshape(-1, LANES),
            key_gain.reshape(-1, LANES),
        ],
        axis=0,
    )
    small = sum_all(small)
    step = width // LANES
    grad_g1, grad_b1 = small[:step].reshape(-1), small[step : 2 * step].reshape(-1)
    grad_g2, grad_b2 = (
        small[2 * step : 3 * step].reshape(-1),
        small[3 * step : 4 * step].reshape(-1),
    )
    rest = TILE // LANES
    grad_gq = small[4 * step : 4 * step + rest].reshape(-1, HD).sum(axis=0)
    grad_gk = small[4 * step + rest :].reshape(-1, HD).sum(axis=0)

    e = part if acc is None else part + acc.astype(F4)
    centred, rate = centre(p_own.astype(F4))
    t = e * g1
    grad_in = d_mixed + rate * (
        t - mean_last(t) - centred * (rate * rate) * mean_last(t * centred)
    )

    def back_home(x):
        lower, upper = x[:piece], x[piece:]
        keep = jnp.where(c == 0, lower, upper)
        got = swap_core(jnp.where(c == 0, upper, lower))
        return jnp.stack([jnp.where(c == 0, keep, got), jnp.where(c == 0, got, keep)])

    rest = half + first
    grad_wu = jnp.concatenate([grad_b[:, :first], grad_b[:, rest:]], axis=1)
    return (
        back_home(result)[None],
        back_home(grad_in)[None],
        grad_g1,
        grad_b1,
        grad_a[:, :half],
        grad_a[:, half : 2 * half],
        grad_a[:, 2 * half :],
        grad_gq,
        grad_gk,
        grad_b[:, first:rest].T,
        grad_g2,
        grad_b2,
        grad_wu,
        grad_c.T,
    )


def solution(mesh):
    rows = P("dp", None, ("row", "col"), None)
    inward = P(("dp", "row"), "col")
    outward = P("col", ("dp", "row"))
    return jax.shard_map(
        per_device,
        mesh=mesh,
        in_specs=(
            rows, P("dp", None, None), P(), P(), inward, inward, inward, P(), P(),
            outward, P(), P(), inward, outward, rows,
        ),
        out_specs=(
            rows, rows, P(), P(), inward, inward, inward, P(), P(),
            outward, P(), P(), inward, outward,
        ),
        check_vma=False,
    )
```

```python
import functools
import math

import jax
import jax.numpy as jnp
from jax import lax
from jax.experimental import pallas as pl
from jax.experimental.pallas import tpu as pltpu
from jax.sharding import PartitionSpec as P

HD = 64
LANES = 128
TILE = 256
EPSILON = 1e-06
BF = jnp.bfloat16
F4 = jnp.float32
VM = pl.BlockSpec(memory_space=pltpu.VMEM)


def ring_order(n):
    return list(range(0, n, 2)) + list(range(n - 1 - (n % 2), 0, -2))


def ring_place(r, n):
    return jnp.where(r % 2 == 0, r // 2, n - 1 - r // 2 - (n % 2) + (n % 2) * 1)


def ring_row(q, n):
    return jnp.where(2 * q < n, 2 * q, 2 * (n - 1 - q) + 1)


class Place:
    def __init__(self):
        n, m = lax.axis_size("row"), lax.axis_size("dp")
        place = ring_place(lax.axis_index("row"), n)
        me = lax.axis_index("dp")
        made = {("c",): lax.axis_index("col") == 0}
        for bit in range(m.bit_length() - 1):
            one = (me >> bit) & 1
            made["low", bit] = one == 0
            made["one", bit] = one
            made["zero", bit] = 1 - one
        for r in range(n):
            slot = (place - ring_order(n).index(r) + n) % n
            for k in range(n - 1):
                made["slot", r, k] = slot == k
        for step in range(n):
            made["row", step] = ring_row((place - step + n) % n, n)
        names = list(made)
        self.made = dict(zip(names, lax.optimization_barrier(tuple(made.values()))))

    def __call__(self, *name):
        return self.made[name]


def index(x, i, axis=0, keepdims=False):
    return lax.dynamic_index_in_dim(
        x, i, axis, keepdims=keepdims, allow_negative_indices=False
    )


def hop(x, n):
    order = ring_order(n)
    pairs = [(order[i], order[(i + 1) % n]) for i in range(n)]
    return lax.ppermute(x, "row", pairs)


def swap_bit(x, axis, n, bit):
    return lax.ppermute(x, axis, [(i, i ^ (1 << bit)) for i in range(n)])


def swap_core(x):
    return lax.ppermute(x, "col", [(0, 1), (1, 0)])


def bit_orders(n):
    bits = list(range(n.bit_length() - 1))
    half = len(bits) // 2
    return bits, bits[half:] + bits[:half]


def regular(block):
    dp = lax.axis_size("dp")
    return dp & (dp - 1) == 0 and block % 16 == 0


def after(x, deps):
    if not deps:
        return x
    return lax.optimization_barrier((x, *deps))[0]


def all_after(xs, deps):
    if not deps:
        return tuple(xs)
    return lax.optimization_barrier((*xs, *deps))[: len(xs)]


class Chain:
    def __init__(self, steps):
        self.steps = steps
        self.last = ()
        self.value = None
        next(steps)

    def step(self, *deps):
        if self.value is None:
            try:
                self.last = self.steps.send(deps)
            except StopIteration as end:
                self.value = end.value
        return self

    def finish(self):
        while self.value is None:
            self.step()
        return self.value


def join_line(blocks, at):
    n = len(blocks)
    parts = []
    for r in range(n):
        x = blocks[-1]
        for k in range(n - 1):
            x = jnp.where(at("slot", r, k), blocks[k], x)
        parts.append(x)
    return jnp.concatenate(parts, axis=0)


def gather_steps(shard, cut, at):
    deps = yield ()
    shard = after(shard, deps)
    if not regular(shard.shape[0]):
        whole = lax.all_gather(shard, ("dp", "row"), axis=0, tiled=True)
        deps = yield (whole,)
        whole = after(whole, deps)
        parts = [whole[:, :cut], whole[:, cut:]]
    else:
        n, m = lax.axis_size("row"), lax.axis_size("dp")
        blocks = [shard]
        for _ in range(n - 1):
            got = hop(blocks[-1], n)
            deps = yield (got,)
            blocks.append(after(got, deps))
        line = join_line(blocks, at)
        parts = [line[:, :cut], line[:, cut:]]
        orders = bit_orders(m)
        done = ([], [])
        for bits in zip(*orders):
            got = [swap_bit(x, "dp", m, bit) for x, bit in zip(parts, bits)]
            deps = yield tuple(got)
            got = all_after(got, deps)
            for i, bit in enumerate(bits):
                axis = sum(1 for b in done[i] if b > bit)
                low = at("low", bit)
                first = jnp.where(low, parts[i], got[i])
                second = jnp.where(low, got[i], parts[i])
                parts[i] = jnp.stack([first, second], axis=axis)
                done[i].append(bit)
        parts = [x.reshape(-1, x.shape[-1]) for x in parts]
    got = [swap_core(x) for x in parts]
    yield tuple(got)
    return (parts[0], got[0]), (parts[1], got[1])


def add_low(a, b):
    return (a.astype(F4) + b.astype(F4)).astype(BF)


def scatter_steps(one, two, at):
    n, m = lax.axis_size("row"), lax.axis_size("dp")
    block = one[0].shape[0] // (m * n)
    deps = yield ()
    got = [swap_core(x) for x in all_after((one[1], two[1]), deps)]
    deps = yield tuple(got)
    parts = [add_low(x[0], y) for x, y in zip((one, two), all_after(got, deps))]
    if not regular(block):
        both = jnp.concatenate(parts, axis=1)
        total = lax.psum_scatter(both, ("dp", "row"), scatter_dimension=0, tiled=True)
        yield (total,)
        return total.astype(F4)
    count = m.bit_length() - 1
    left = [list(range(count - 1, -1, -1)), list(range(count - 1, -1, -1))]
    parts = [x.reshape((2,) * count + (-1, x.shape[-1])) for x in parts]
    for bits in zip(*bit_orders(m)):
        got, keep = [], []
        for i, bit in enumerate(bits):
            axis = left[i].index(bit)
            got.append(swap_bit(index(parts[i], at("zero", bit), axis), "dp", m, bit))
            keep.append(index(parts[i], at("one", bit), axis))
            left[i].remove(bit)
        deps = yield tuple(got)
        parts = [add_low(x, y) for x, y in zip(keep, all_after(got, deps))]
    both = jnp.concatenate(parts, axis=1)
    both = both.reshape(n, -1, both.shape[-1])
    if n == 1:
        return both[0].astype(F4)
    acc = index(both, at("row", 1))
    for step in range(n - 1):
        got = hop(acc, n)
        deps = yield (got,)
        got = after(got, deps)
        if step < n - 2:
            acc = add_low(index(both, at("row", step + 2)), got)
    return index(both, at("row", 0)).astype(F4) + got.astype(F4)


def sum_steps(x):
    deps = yield ()
    got = swap_core(after(x, deps))
    deps = yield (got,)
    x = x + after(got, deps)
    for axis in ("dp", "row"):
        n = lax.axis_size(axis)
        for bit in range(n.bit_length() - 1) if n & (n - 1) == 0 else (None,):
            got = lax.psum(x, axis) - x if bit is None else swap_bit(x, axis, n, bit)
            deps = yield (got,)
            x = x + after(got, deps)
    return x


def dot_nn(a, b):
    return jnp.dot(a, b, preferred_element_type=F4)


def dot_nt(a, b):
    return lax.dot_general(a, b, (((1,), (1,)), ((), ())), preferred_element_type=F4)


def dot_tn(a, b):
    return lax.dot_general(a, b, (((0,), (0,)), ((), ())), preferred_element_type=F4)


def mean_last(x):
    return jnp.mean(x, axis=-1, keepdims=True)


def centre(x):
    c = x - mean_last(x)
    return c, lax.rsqrt(mean_last(c * c) + EPSILON)


def group_matrix():
    i = lax.broadcasted_iota(jnp.int32, (TILE, TILE), 0) // HD
    j = lax.broadcasted_iota(jnp.int32, (TILE, TILE), 1) // HD
    return jnp.where(i == j, 1.0 / HD, 0.0).astype(BF)


def group_mean(x, matrix):
    high = x.astype(BF)
    low = (x - high.astype(F4)).astype(BF)
    return dot_nn(high, matrix) + dot_nn(low, matrix)


def head_norm(x, matrix):
    c = x - group_mean(x, matrix)
    return c, lax.rsqrt(group_mean(c * c, matrix) + EPSILON)


def head_norm_back(e, x, gain, matrix):
    c, r = head_norm(x, matrix)
    t = e * gain
    d = r * (t - group_mean(t, matrix) - c * (r * r) * group_mean(t * c, matrix))
    return d, e * c * r


def fold_heads(x):
    return jnp.sum(x, axis=0, keepdims=True)


def tiles(width):
    return width // TILE


def lane(i, width):
    return pl.ds(pl.multiple_of(i * width, width), width)


def call(body, outs, scratch, room, flops, *args):
    size = sum(a.size * a.dtype.itemsize for a in args)
    size += sum(math.prod(s) * jnp.dtype(d).itemsize for s, d in outs)
    hold = sum(math.prod(s.shape) * jnp.dtype(s.dtype).itemsize for s in scratch)
    return pl.pallas_call(
        body,
        out_shape=[jax.ShapeDtypeStruct(s, d) for s, d in outs],
        in_specs=[VM] * len(args),
        out_specs=[VM] * len(outs),
        scratch_shapes=scratch,
        compiler_params=pltpu.CompilerParams(vmem_limit_bytes=hold + (room << 20)),
        cost_estimate=pl.CostEstimate(
            flops=int(flops) * 4, bytes_accessed=int(size), transcendentals=0
        ),
    )(*args)


def pair_masks(rows):
    at = lax.broadcasted_iota(jnp.int32, (rows, LANES), 1)
    return (at < HD, at >= HD)


def pick(x, mask):
    return jnp.where(mask, x, jnp.zeros_like(x))


def column(ref, h):
    at = lax.broadcasted_iota(jnp.int32, ref.shape, 1)
    return jnp.sum(jnp.where(at == h, ref[...], 0.0), axis=-1, keepdims=True)


def look_body(first, last, half, *refs):
    p, g1, b1, kg, idq, idk, a1o, a1x, a2o, a2x = refs[:10]
    refs = refs[10:]
    if first:
        qg, normed, k_raw, k_low, v_low, out, stat, q_raw, q, bias = refs
    else:
        q, acc, total_in, normed, k_raw, k_low, v_low, out, stat, bias = refs
    x = p[...].astype(F4)
    c, r = centre(x)
    n = (c * r * g1[...] + b1[...]).astype(BF)
    normed[...] = n
    head = 0 if first else half
    cut = a1o.shape[1]
    for s, (a1, a2) in enumerate(((a1o, a2o), (a1x, a2x))):
        at = s * half
        one = dot_nn(n, a1[:, head:])
        two = dot_nn(n, a2[...])
        if first:
            q_raw[:, at : at + half] = one[:, :half]
        k_raw[:, at : at + cut - half] = one[:, half - head :]
        k_raw[:, at + cut - half : at + half] = two[:, : 2 * half - cut]
        v_low[:, at : at + half] = two[:, 2 * half - cut :].astype(BF)
    matrix = group_matrix()
    for t in range(tiles(2 * half)):
        cols = slice(t * TILE, (t + 1) * TILE)
        c, r = head_norm(k_raw[:, cols], matrix)
        k_low[:, cols] = (c * r * kg[...]).astype(BF)
        if first:
            c, r = head_norm(q_raw[:, cols], matrix)
            q[:, cols] = (c * r * qg[...] * (float(HD) ** -0.5)).astype(BF)

    bias[...] = jnp.where(idq[...] == idk[...], 0.0, -1e30)
    stat[...] = jnp.zeros_like(stat) if first else total_in[...]
    masks = pair_masks(p.shape[0])
    lanes = lax.broadcasted_iota(jnp.int32, stat.shape, 1)

    @pl.loop(0, 2 * half // LANES)
    def _(pair):
        cols = lane(pair, LANES)
        q_pair, k_pair, v_pair = q[:, cols], k_low[:, cols], v_low[:, cols]
        outs = []
        for s, mask in enumerate(masks):
            e = jnp.exp(dot_nt(pick(q_pair, mask), k_pair) + bias[...])
            total = jnp.sum(e, axis=-1, keepdims=True)
            got = dot_nn(e.astype(BF), v_pair)
            if not first:
                got = got + acc[:, cols]
            h = 2 * pair + s
            if last:
                total = total + column(stat, h)
                got = got * (1.0 / total)
                stat[...] = jnp.where(lanes == h, jnp.log(total), stat[...])
            else:
                stat[...] += jnp.where(lanes == h, total, 0.0)
            outs.append(got)
        out[:, cols] = jnp.where(masks[0], outs[0], outs[1]).astype(out.dtype)


def look(first, last, p, g1, b1, qg, kg, idq, idk, parts, before):
    tokens, width = p.shape
    half = width // 2
    wide = (tokens, width)
    outs = [(wide, BF), (wide, F4), (wide, BF), (wide, BF)]
    outs += [(wide, BF if last else F4), ((tokens, LANES), F4)]
    if first:
        outs += [(wide, F4), (wide, BF)]
    flops = 2 * tokens * width * (width * (3 if first else 2) + 4 * tokens)
    body = functools.partial(look_body, first, last, half)
    scratch = [pltpu.VMEM((tokens, tokens), F4)]
    extra = (qg,) if first else before
    return call(
        body, outs, scratch, 6, flops, p, g1, b1, kg, idq, idk, *parts, *extra
    )


ROOT = math.sqrt(2.0 / math.pi)
CUBE = 0.044715


def gelu_pair(u):
    square = u * u
    t = jnp.tanh(ROOT * u * (1.0 + CUBE * square))
    half = 0.5 * (1.0 + t)
    slope = half + 0.5 * u * (1.0 - t * t) * (ROOT * (1.0 + 3.0 * CUBE * square))
    return u * half, slope


def up_body(half, p, att, cot, g2, b2, b1o, b1x, b2o, b2x, *outs):
    mixed, n2, act, slope, g1o, g1x, g2o, g2x = outs
    first = b1o.shape[1]
    inner = first + b2o.shape[1] - half
    m = p[...].astype(F4)
    for s, part in enumerate((b2o, b2x)):
        m = m + dot_nt(att[:, s * half : (s + 1) * half], part[:, :half])
    mixed[...] = m
    c, r = centre(m)
    n2[...] = (c * r * g2[...] + b2[...]).astype(BF)
    for s, (one, two) in enumerate(((b1o, b2o), (b1x, b2x))):

        @pl.loop(0, tiles(first))
        def _(i):
            u = dot_nn(n2[...], one[:, lane(i, TILE)])
            to = pl.ds(pl.multiple_of(s * inner + i * TILE, TILE), TILE)
            a, d = gelu_pair(u)
            act[:, to] = a.astype(BF)
            slope[:, to] = d.astype(BF)

        rest = inner - first
        for i in range(tiles(rest)):
            u = dot_nn(n2[...], two[:, half + i * TILE : half + (i + 1) * TILE])
            to = slice(s * inner + first + i * TILE, s * inner + first + (i + 1) * TILE)
            a, d = gelu_pair(u)
            act[:, to] = a.astype(BF)
            slope[:, to] = d.astype(BF)
    mid = g1o.shape[1]
    for s, (one, two) in enumerate(((g1o, g2o), (g1x, g2x))):
        for base, out in ((s * inner, one), (s * inner + mid, two)):

            @pl.loop(0, tiles(mid))
            def _(i):
                frm = pl.ds(pl.multiple_of(base + i * TILE, TILE), TILE)
                out[:, lane(i, TILE)] = dot_tn(cot[...], act[:, frm]).astype(BF)


def slope_body(half, *refs):
    mixed, slope, att, cot, g2 = refs[:5]
    b1o, b1x, b2o, b2x, c1o, c1x, c2o, c2x = refs[5:13]
    d_up, d_mixed, d_att, delta, gains = refs[13:]
    first = b1o.shape[1]
    inner = first + b2o.shape[1] - half
    mid = c1o.shape[1]
    for s, (one, two) in enumerate(((c1o, c2o), (c1x, c2x))):
        at = s * inner
        for base, part in ((at, one), (at + mid, two)):

            @pl.loop(0, tiles(mid))
            def _(i):
                to = pl.ds(pl.multiple_of(base + i * TILE, TILE), TILE)
                d = dot_nn(cot[...], part[:, lane(i, TILE)])
                d_up[:, to] = (d * slope[:, to].astype(F4)).astype(BF)

    e = jnp.zeros(mixed.shape, F4)
    for s, (one, two) in enumerate(((b1o, b2o), (b1x, b2x))):
        at = s * inner
        e = e + dot_nt(d_up[:, at : at + first], one[...])
        e = e + dot_nt(d_up[:, at + first : at + inner], two[:, half:])
    c, r = centre(mixed[...])
    t = e * g2[...]
    d_mixed[...] = cot[...].astype(F4) + r * (
        t - mean_last(t) - c * (r * r) * mean_last(t * c)
    )
    gains[0:1, :] = jnp.sum(e * c * r, axis=0, keepdims=True)
    gains[1:2, :] = jnp.sum(e, axis=0, keepdims=True)
    d_branch = d_mixed[...].astype(BF)
    row = lax.broadcasted_iota(jnp.int32, (half, LANES), 0) // HD
    col = lax.broadcasted_iota(jnp.int32, (half, LANES), 1)
    sums = jnp.zeros(delta.shape, F4)
    for s, part in enumerate((b2o, b2x)):
        cols = slice(s * half, (s + 1) * half)
        d = dot_nn(d_branch, part[:, :half]).astype(BF)
        d_att[:, cols] = d
        prod = d.astype(F4) * att[:, cols].astype(F4)
        high = prod.astype(BF)
        low = (prod - high.astype(F4)).astype(BF)
        sel = jnp.where(row + s * (half // HD) == col, 1.0, 0.0).astype(BF)
        sums = sums + dot_nn(high, sel) + dot_nn(low, sel)
    delta[...] = sums


def inner_body(half, *refs):
    mixed, n2, act, att, d_up, d_mixed, c1o, c1x, c2o, c2x = refs[:10]
    result, h1o, h1x, h2o, h2x = refs[10:]
    first = h1o.shape[1]
    inner = first + h2o.shape[1] - half
    mid = c1o.shape[1]
    out = mixed[...]
    for s, (one, two) in enumerate(((c1o, c2o), (c1x, c2x))):
        at = s * inner
        out = out + dot_nt(act[:, at : at + mid], one[...])
        out = out + dot_nt(act[:, at + mid : at + inner], two[...])
    result[...] = out.astype(BF)
    d_branch = d_mixed[...].astype(BF)
    for s, (one, two) in enumerate(((h1o, h2o), (h1x, h2x))):
        at = s * inner
        two[:, :half] = dot_tn(d_branch, att[:, s * half : (s + 1) * half]).astype(BF)

        @pl.loop(0, tiles(first))
        def _(i):
            frm = pl.ds(pl.multiple_of(at + i * TILE, TILE), TILE)
            one[:, lane(i, TILE)] = dot_tn(n2[...], d_up[:, frm]).astype(BF)

        two[:, half:] = dot_tn(n2[...], d_up[:, at + first : at + inner]).astype(BF)


def back_body(half, *refs):
    q, k, v, d_att, stat, delta, idq, idk, k_raw, p, kg = refs[:11]
    a1o, a1x, a2o, a2x = refs[11:15]
    dk_low, dv_low, dq, part, k_gain, gains, bias, dk = refs[15:]
    tokens = q.shape[0]
    bias[...] = jnp.where(idq[...] == idk[...], 0.0, -1e30)
    masks = pair_masks(tokens)

    @pl.loop(0, q.shape[1] // LANES)
    def _(pair):
        cols = lane(pair, LANES)
        q_pair, k_pair, v_pair, d_pair = q[:, cols], k[:, cols], v[:, cols], d_att[:, cols]
        sum_q = sum_k = sum_v = None
        for s, mask in enumerate(masks):
            q_one, d_one, k_one = pick(q_pair, mask), pick(d_pair, mask), pick(k_pair, mask)
            h = 2 * pair + s
            score = dot_nt(q_one, k_pair) + bias[...]
            prob = jnp.exp(score - column(stat, h))
            d_prob = dot_nt(d_one, v_pair)
            d_score = (prob * (d_prob - column(delta, h))).astype(BF)
            one_v = dot_tn(prob.astype(BF), d_one)
            one_k = dot_tn(d_score, q_one)
            one_q = dot_nn(d_score, k_one)
            sum_v = one_v if s == 0 else sum_v + one_v
            sum_k = one_k if s == 0 else sum_k + one_k
            sum_q = one_q if s == 0 else sum_q + one_q
        dq[:, cols] = sum_q
        dk[:, cols] = sum_k
        dv_low[:, cols] = sum_v.astype(BF)

    matrix = group_matrix()
    total = jnp.zeros((1, TILE), F4)
    for t in range(tiles(2 * half)):
        cols = slice(t * TILE, (t + 1) * TILE)
        d, g = head_norm_back(dk[:, cols], k_raw[:, cols], kg[...], matrix)
        dk_low[:, cols] = d.astype(BF)
        total = total + fold_heads(g)
    k_gain[...] = total
    cut = a1o.shape[1]
    e = jnp.zeros((tokens, 2 * half), F4)
    for s, (one, two) in enumerate(((a1o, a2o), (a1x, a2x))):
        at = s * half
        mid = at + cut - half
        e = e + dot_nt(dk_low[:, at:mid], one[:, half:])
        e = e + dot_nt(dk_low[:, mid : at + half], two[:, : 2 * half - cut])
        e = e + dot_nt(dv_low[:, at : at + half], two[:, 2 * half - cut :])
    part[...] = e.astype(part.dtype)
    c, r = centre(p[...].astype(F4))
    gains[0:1, :] = jnp.sum(e * c * r, axis=0, keepdims=True)
    gains[1:2, :] = jnp.sum(e, axis=0, keepdims=True)


def back_block(last, q, k, v, d_att, stat, delta, idq, idk, k_raw, p, kg, parts):
    tokens, width = q.shape
    half = width // 2
    outs = [
        ((tokens, width), BF),
        ((tokens, width), BF),
        ((tokens, width), F4),
        ((tokens, width), F4 if last else BF),
        ((1, TILE), F4),
        ((2, width), F4),
    ]
    scratch = [pltpu.VMEM((tokens, tokens), F4), pltpu.VMEM((tokens, width), F4)]
    flops = 10 * tokens * tokens * width * 4 + 4 * tokens * width * width
    body = functools.partial(back_body, half)
    return call(
        body, outs, scratch, 9, flops,
        q, k, v, d_att, stat, delta, idq, idk, k_raw, p, kg, *parts,
    )


def weight_body(n, half, *refs):
    q_raw, qg, p, own = refs[:4]
    a1o, a1x = refs[4:6]
    dqs, ns = refs[6 : 6 + n], refs[6 + n : 6 + 2 * n]
    dks, dvs = refs[6 + 2 * n : 6 + 3 * n], refs[6 + 3 * n : 6 + 4 * n]
    part, q_gain, gains, g1o, g1x, g2o, g2x, dq_low, n_all, dk_all, dv_all = refs[6 + 4 * n :]
    tokens = q_raw.shape[0]
    matrix = group_matrix()
    total = jnp.zeros((1, TILE), F4)
    factor = float(HD) ** -0.5
    for t in range(tiles(2 * half)):
        cols = slice(t * TILE, (t + 1) * TILE)
        e = dqs[0][:, cols]
        for other in dqs[1:]:
            e = e + other[:, cols]
        d, g = head_norm_back(e * factor, q_raw[:, cols], qg[...], matrix)
        dq_low[:, cols] = d.astype(BF)
        total = total + fold_heads(g)
    q_gain[...] = total
    e = dot_nt(dq_low[:, :half], a1o[:, :half]) + dot_nt(dq_low[:, half:], a1x[:, :half])
    part[...] = own[...] + e
    c, r = centre(p[...].astype(F4))
    gains[0:1, :] = jnp.sum(e * c * r, axis=0, keepdims=True)
    gains[1:2, :] = jnp.sum(e, axis=0, keepdims=True)
    for b in range(n):
        rows = slice(b * tokens, (b + 1) * tokens)
        n_all[rows, :] = ns[b][...]
        dk_all[rows, :] = dks[b][...]
        dv_all[rows, :] = dvs[b][...]
    cut = g1o.shape[1]
    for s, (one, two) in enumerate(((g1o, g2o), (g1x, g2x))):
        at = s * half
        mid = at + cut - half
        one[:, :half] = dot_tn(ns[0][...], dq_low[:, at : at + half]).astype(BF)
        one[:, half:] = dot_tn(n_all[...], dk_all[:, at:mid]).astype(BF)
        two[:, : 2 * half - cut] = dot_tn(n_all[...], dk_all[:, mid : at + half]).astype(BF)
        two[:, 2 * half - cut :] = dot_tn(n_all[...], dv_all[:, at : at + half]).astype(BF)


def input_body(own, rest, p, g1, d_mixed, out):
    e = own[...] + rest[...].astype(F4)
    c, r = centre(p[...].astype(F4))
    t = e * g1[...]
    out[...] = d_mixed[...] + r * (t - mean_last(t) - c * (r * r) * mean_last(t * c))


def small_body(n, *refs):
    first, second, query, keys = refs[: n + 1], refs[n + 1], refs[n + 2], refs[n + 3 : -1]
    out = refs[-1]
    out[...] = jnp.zeros_like(out)
    total = first[0][...]
    for x in first[1:]:
        total = total + x[...]
    out[0:2, :] = total
    out[2:4, :] = second[...]
    out[4:5, :TILE] = query[...]
    total = keys[0][...]
    for x in keys[1:]:
        total = total + x[...]
    out[5:6, :TILE] = total


def take_micro(x, c):
    mine = jnp.where(c0, x[0], x[1])
    other = jnp.where(c0, x[1], x[0])
    return mine, other


def per_device(
    patches,
    picture_ids,
    ln1_gain,
    ln1_bias,
    w_query,
    w_key,
    w_value,
    q_gain,
    k_gain,
    w_out,
    ln2_gain,
    ln2_bias,
    w_up,
    w_down,
    cotangent,
):
    n = lax.axis_size("row")
    at = Place()
    c0 = at("c")
    width = patches.shape[-1]
    half = w_query.shape[1]
    piece = patches.shape[2]
    tokens = 2 * piece
    inner = w_up.shape[1]

    cut_a = half + half * 2 // 3
    first = inner * 2 // 3
    mid = inner // 2
    chunk_a = jnp.concatenate([w_query, w_key, w_value], axis=1)
    chunk_b = jnp.concatenate([w_up[:, :first], w_out.T, w_up[:, first:]], axis=1)
    chain_a = Chain(gather_steps(chunk_a, cut_a, at))
    chain_b = Chain(gather_steps(chunk_b, first, at))
    chain_c = Chain(gather_steps(w_down.T, mid, at))

    def take(x):
        mine = jnp.where(c0, x[0], x[1])
        got = swap_core(jnp.where(c0, x[1], x[0]))
        return jnp.concatenate(
            [jnp.where(c0, mine, got), jnp.where(c0, got, mine)], axis=0
        )

    g1, b1 = ln1_gain[None], ln1_bias[None]
    g2, b2 = ln2_gain[None], ln2_bias[None]
    qg, kg = jnp.tile(q_gain, TILE // HD)[None], jnp.tile(k_gain, TILE // HD)[None]
    ids = jnp.where(c0, picture_ids[0, 0], picture_ids[0, 1]).reshape(n, tokens)
    id_blocks = [index(ids, at("row", j), keepdims=True) for j in range(n)]
    idq = id_blocks[0].reshape(tokens, 1)
    ready = lax.optimization_barrier((g1, b1, g2, b2, qg, kg, idq, *id_blocks))
    g1, b1, g2, b2, qg, kg, idq, *id_blocks = ready

    chain_a.step()
    p_own = take(patches[0])
    for _ in range(n - 2):
        chain_a.step(*ready)
        ready = ()
    line_a = chain_a.last
    chain_a.step()
    chain_b.step(*line_a)
    blocks = [p_own, hop(after(p_own, line_a), n)]
    chain_a.step()
    for _ in range(n - 2):
        chain_b.step()
    line_b = chain_b.last
    a_one, a_two = chain_a.finish()
    a_parts = a_one + a_two
    cot = take(cotangent[0])

    made = []
    before = token = ()
    deps = line_b + (blocks[1],)
    for j in range(n):
        if 0 < j < n - 1:
            blocks.append(hop(after(blocks[j], line_b), n))
        chain_b.step(*token)
        chain_c.step(*(token or line_b))
        made.append(
            look(
                j == 0, j == n - 1, after(blocks[j], deps), g1, b1, qg, kg, idq,
                id_blocks[j], a_parts, before,
            )
        )
        if j == 0:
            q_raw, q_low = made[0][6:]
        before = (q_low, *made[j][4:6])
        token = (made[j][5],)
        deps = chain_b.last + chain_c.last
    normed = [m[0] for m in made]
    k_raw, k_low, v_low = [m[1] for m in made], [m[2] for m in made], [m[3] for m in made]
    att, stat = made[-1][4:6]

    b_one, b_two = chain_b.finish()
    b_parts = b_one + b_two
    chain_c.step(*token)
    mixed, n2, act, slope, *gc = call(
        functools.partial(up_body, half),
        [((tokens, width), F4), ((tokens, width), BF)]
        + [((tokens, 2 * inner), BF)] * 2
        + [((width, mid), BF)] * 4,
        [], 7,
        2 * tokens * width * (width + 4 * inner),
        p_own, after(att, deps), cot, g2, b2, *b_parts,
    )
    c_one, c_two = chain_c.finish()
    c_parts = c_one + c_two

    back_c = Chain(scatter_steps((gc[0], gc[1]), (gc[2], gc[3]), at)).step()
    deps = back_c.last
    back_c.step()
    d_up, d_mixed, d_att, delta, gains2 = call(
        functools.partial(slope_body, half),
        [((tokens, 2 * inner), BF), ((tokens, width), F4), ((tokens, width), BF)]
        + [((tokens, LANES), F4), ((2, width), F4)],
        [], 11,
        2 * tokens * width * (width + 4 * inner),
        after(mixed, deps), slope, att, cot, g2, *b_parts, *c_parts,
    )
    deps = back_c.last
    back_c.step(delta)
    result, *gb = call(
        functools.partial(inner_body, half),
        [((tokens, width), BF)]
        + [((width, first), BF)] * 2
        + [((width, half + inner - first), BF)] * 2,
        [], 10,
        2 * tokens * width * (width + 4 * inner),
        mixed, n2, act, att, d_up, after(d_mixed, deps), *c_parts,
    )
    deps = back_c.last
    back_c.step(result)
    back_b = Chain(scatter_steps((gb[0], gb[1]), (gb[2], gb[3]), at)).step()

    back = [None] * n
    acc = None
    order = [*range(1, n), 0]
    for turn, j in enumerate(order):
        back[j] = back_block(
            j == 0, q_low, k_low[j], v_low[j], after(d_att, deps), stat, delta, idq,
            id_blocks[j], k_raw[j], blocks[j], kg, a_parts,
        )
        token = back[j][4]
        deps = back_c.last + (token,)
        back_c.step(token)
        if turn != 1:
            deps = deps + back_b.last
            back_b.step(token)
        if j:
            part = back[j][3]
            if acc is None:
                acc = part
            else:
                deps = deps + (acc,)
                acc = add_low(part, acc)
            acc = hop(acc, n)

    part, dq_gain, gains_q, *ga = call(
        functools.partial(weight_body, n, half),
        [((tokens, width), F4), ((1, TILE), F4), ((2, width), F4)]
        + [((width, cut_a), BF)] * 2
        + [((width, 3 * half - cut_a), BF)] * 2,
        [pltpu.VMEM((tokens, width), BF)] + [pltpu.VMEM((n * tokens, width), BF)] * 3,
        12,
        2 * tokens * width * width * (2 + 2 * n),
        after(q_raw, deps), qg, p_own, back[0][3], *a_one,
        *[b[2] for b in back], *normed, *[b[0] for b in back], *[b[1] for b in back],
    )
    back_a = Chain(scatter_steps((ga[0], ga[1]), (ga[2], ga[3]), at)).step()
    back_b.step(dq_gain)
    (small,) = call(
        functools.partial(small_body, n), [((8, width), F4)], [], 1, 0,
        *[b[5] for b in back], gains_q, gains2, dq_gain, *[b[4] for b in back],
    )
    sums = Chain(sum_steps(small))
    while back_a.value is None or sums.value is None:
        deps = back_a.last
        back_a.step()
        sums.step(*deps)
    grad_a, grad_b, grad_c = back_a.value, back_b.finish(), back_c.finish()
    small = sums.value
    grad_g1, grad_b1, grad_g2, grad_b2 = small[0], small[1], small[2], small[3]
    grad_gq = small[4, :TILE].reshape(-1, HD).sum(axis=0)
    grad_gk = small[5, :TILE].reshape(-1, HD).sum(axis=0)

    (grad_in,) = call(
        input_body, [((tokens, width), F4)], [], 6, 0, part, acc, p_own, g1, d_mixed
    )

    def back_home(x):
        lower, upper = x[:piece], x[piece:]
        keep = jnp.where(c0, lower, upper)
        got = swap_core(jnp.where(c0, upper, lower))
        return jnp.stack([jnp.where(c0, keep, got), jnp.where(c0, got, keep)])

    rest = half + first
    grad_wu = jnp.concatenate([grad_b[:, :first], grad_b[:, rest:]], axis=1)
    return (
        back_home(result)[None],
        back_home(grad_in)[None],
        grad_g1,
        grad_b1,
        grad_a[:, :half],
        grad_a[:, half : 2 * half],
        grad_a[:, 2 * half :],
        grad_gq,
        grad_gk,
        grad_b[:, first:rest].T,
        grad_g2,
        grad_b2,
        grad_wu,
        grad_c.T,
    )


def solution(mesh):
    rows = P("dp", None, ("row", "col"), None)
    inward = P(("dp", "row"), "col")
    outward = P("col", ("dp", "row"))
    return jax.shard_map(
        per_device,
        mesh=mesh,
        in_specs=(
            rows, P("dp", None, None), P(), P(), inward, inward, inward, P(), P(),
            outward, P(), P(), inward, outward, rows,
        ),
        out_specs=(
            rows, rows, P(), P(), inward, inward, inward, P(), P(),
            outward, P(), P(), inward, outward,
        ),
        check_vma=False,
    )
```

```python
import functools
import math

import jax
import jax.numpy as jnp
from jax import lax
from jax.experimental import pallas as pl
from jax.experimental.pallas import tpu as pltpu
from jax.sharding import PartitionSpec as P

HD = 64
LANES = 128
TILE = 256
EPSILON = 1e-06
BF = jnp.bfloat16
F4 = jnp.float32
VM = pl.BlockSpec(memory_space=pltpu.VMEM)


def ring_order(n):
    return list(range(0, n, 2)) + list(range(n - 1 - (n % 2), 0, -2))


def ring_place(r, n):
    return jnp.where(r % 2 == 0, r // 2, n - 1 - r // 2 - (n % 2) + (n % 2) * 1)


def ring_row(q, n):
    return jnp.where(2 * q < n, 2 * q, 2 * (n - 1 - q) + 1)


class Place:
    def __init__(self):
        n, m = lax.axis_size("row"), lax.axis_size("dp")
        place = ring_place(lax.axis_index("row"), n)
        me = lax.axis_index("dp")
        made = {("c",): lax.axis_index("col") == 0}
        for bit in range(m.bit_length() - 1):
            one = (me >> bit) & 1
            made["low", bit] = one == 0
            made["one", bit] = one
            made["zero", bit] = 1 - one
        for r in range(n):
            slot = (place - ring_order(n).index(r) + n) % n
            for k in range(n - 1):
                made["slot", r, k] = slot == k
        for step in range(n):
            made["row", step] = ring_row((place - step + n) % n, n)
        names = list(made)
        self.made = dict(zip(names, lax.optimization_barrier(tuple(made.values()))))

    def __call__(self, *name):
        return self.made[name]


def index(x, i, axis=0, keepdims=False):
    return lax.dynamic_index_in_dim(
        x, i, axis, keepdims=keepdims, allow_negative_indices=False
    )


def hop(x, n):
    order = ring_order(n)
    pairs = [(order[i], order[(i + 1) % n]) for i in range(n)]
    return lax.ppermute(x, "row", pairs)


def swap_bit(x, axis, n, bit):
    return lax.ppermute(x, axis, [(i, i ^ (1 << bit)) for i in range(n)])


def swap_core(x):
    return lax.ppermute(x, "col", [(0, 1), (1, 0)])


def bit_orders(n):
    bits = list(range(n.bit_length() - 1))
    half = len(bits) // 2
    return bits, bits[half:] + bits[:half]


def regular(block):
    dp = lax.axis_size("dp")
    return dp & (dp - 1) == 0 and block % 16 == 0


def after(x, deps):
    if not deps:
        return x
    return lax.optimization_barrier((x, *deps))[0]


def all_after(xs, deps):
    if not deps:
        return tuple(xs)
    return lax.optimization_barrier((*xs, *deps))[: len(xs)]


class Chain:
    def __init__(self, steps):
        self.steps = steps
        self.last = ()
        self.value = None
        next(steps)

    def step(self, *deps):
        if self.value is None:
            try:
                self.last = self.steps.send(deps)
            except StopIteration as end:
                self.value = end.value
        return self

    def finish(self):
        while self.value is None:
            self.step()
        return self.value


def join_line(blocks, at):
    n = len(blocks)
    parts = []
    for r in range(n):
        x = blocks[-1]
        for k in range(n - 1):
            x = jnp.where(at("slot", r, k), blocks[k], x)
        parts.append(x)
    return jnp.concatenate(parts, axis=0)


def line_steps(shard, at):
    deps = yield ()
    shard = after(shard, deps)
    if not regular(shard.shape[0]):
        return shard
    n = lax.axis_size("row")
    blocks = [shard]
    for _ in range(n - 1):
        got = hop(blocks[-1], n)
        deps = yield (got,)
        blocks.append(after(got, deps))
    return join_line(blocks, at)


def plane_steps(parts, whole, at):
    deps = yield ()
    m = lax.axis_size("dp")
    parts = list(parts)
    if whole:
        both = lax.all_gather(
            jnp.concatenate(parts, axis=1), ("dp", "row"), axis=0, tiled=True
        )
        deps = yield (both,)
        both, cut = after(both, deps), parts[0].shape[1]
        parts = [both[:, :cut], both[:, cut:]]
    else:
        done = ([], [])
        for bits in zip(*bit_orders(m)):
            got = [swap_bit(x, "dp", m, bit) for x, bit in zip(parts, bits)]
            deps = yield tuple(got)
            got = all_after(got, deps)
            for i, bit in enumerate(bits):
                axis = sum(1 for b in done[i] if b > bit)
                low = at("low", bit)
                first = jnp.where(low, parts[i], got[i])
                second = jnp.where(low, got[i], parts[i])
                parts[i] = jnp.stack([first, second], axis=axis)
                done[i].append(bit)
        parts = [x.reshape(-1, x.shape[-1]) for x in parts]
    got = [swap_core(x) for x in parts]
    yield tuple(got)
    return (parts[0], got[0]), (parts[1], got[1])


def add_low(a, b):
    return (a.astype(F4) + b.astype(F4)).astype(BF)


def plane_sums(one, two, whole, at):
    m = lax.axis_size("dp")
    deps = yield ()
    got = [swap_core(x) for x in all_after((one[1], two[1]), deps)]
    deps = yield tuple(got)
    parts = [add_low(x[0], y) for x, y in zip((one, two), all_after(got, deps))]
    if whole:
        return jnp.concatenate(parts, axis=1)
    count = m.bit_length() - 1
    left = [list(range(count - 1, -1, -1)), list(range(count - 1, -1, -1))]
    parts = [x.reshape((2,) * count + (-1, x.shape[-1])) for x in parts]
    for bits in zip(*bit_orders(m)):
        got, keep = [], []
        for i, bit in enumerate(bits):
            axis = left[i].index(bit)
            got.append(swap_bit(index(parts[i], at("zero", bit), axis), "dp", m, bit))
            keep.append(index(parts[i], at("one", bit), axis))
            left[i].remove(bit)
        deps = yield tuple(got)
        parts = [add_low(x, y) for x, y in zip(keep, all_after(got, deps))]
    return jnp.concatenate(parts, axis=1)


def line_sums(both, whole, at):
    deps = yield ()
    both = after(both, deps)
    if whole:
        total = lax.psum_scatter(both, ("dp", "row"), scatter_dimension=0, tiled=True)
        yield (total,)
        return total.astype(F4)
    n = lax.axis_size("row")
    both = both.reshape(n, -1, both.shape[-1])
    acc = index(both, at("row", 1))
    for step in range(n - 1):
        got = hop(acc, n)
        deps = yield (got,)
        got = after(got, deps)
        if step < n - 2:
            acc = add_low(index(both, at("row", step + 2)), got)
    return index(both, at("row", 0)).astype(F4) + got.astype(F4)


def sum_steps(x):
    deps = yield ()
    got = swap_core(after(x, deps))
    deps = yield (got,)
    x = x + after(got, deps)
    for axis in ("dp", "row"):
        n = lax.axis_size(axis)
        for bit in range(n.bit_length() - 1) if n & (n - 1) == 0 else (None,):
            got = lax.psum(x, axis) - x if bit is None else swap_bit(x, axis, n, bit)
            deps = yield (got,)
            x = x + after(got, deps)
    return x


def dot_nn(a, b):
    return jnp.dot(a, b, preferred_element_type=F4)


def dot_nt(a, b):
    return lax.dot_general(a, b, (((1,), (1,)), ((), ())), preferred_element_type=F4)


def dot_tn(a, b):
    return lax.dot_general(a, b, (((0,), (0,)), ((), ())), preferred_element_type=F4)


def mean_last(x):
    return jnp.mean(x, axis=-1, keepdims=True)


def centre(x):
    c = x - mean_last(x)
    return c, lax.rsqrt(mean_last(c * c) + EPSILON)


def group_matrix():
    i = lax.broadcasted_iota(jnp.int32, (TILE, TILE), 0) // HD
    j = lax.broadcasted_iota(jnp.int32, (TILE, TILE), 1) // HD
    return jnp.where(i == j, 1.0 / HD, 0.0).astype(BF)


def group_mean(x, matrix):
    high = x.astype(BF)
    low = (x - high.astype(F4)).astype(BF)
    return dot_nn(high, matrix) + dot_nn(low, matrix)


def head_norm(x, matrix):
    c = x - group_mean(x, matrix)
    return c, lax.rsqrt(group_mean(c * c, matrix) + EPSILON)


def head_norm_back(e, x, gain, matrix):
    c, r = head_norm(x, matrix)
    t = e * gain
    d = r * (t - group_mean(t, matrix) - c * (r * r) * group_mean(t * c, matrix))
    return d, e * c * r


def fold_heads(x):
    return jnp.sum(x, axis=0, keepdims=True)


def tiles(width):
    return width // TILE


def lane(i, width):
    return pl.ds(pl.multiple_of(i * width, width), width)


def call(body, outs, scratch, room, flops, *args):
    size = sum(a.size * a.dtype.itemsize for a in args)
    size += sum(math.prod(s) * jnp.dtype(d).itemsize for s, d in outs)
    hold = sum(math.prod(s.shape) * jnp.dtype(s.dtype).itemsize for s in scratch)
    return pl.pallas_call(
        body,
        out_shape=[jax.ShapeDtypeStruct(s, d) for s, d in outs],
        in_specs=[VM] * len(args),
        out_specs=[VM] * len(outs),
        scratch_shapes=scratch,
        compiler_params=pltpu.CompilerParams(vmem_limit_bytes=hold + (room << 20)),
        cost_estimate=pl.CostEstimate(
            flops=int(flops) * 4, bytes_accessed=int(size), transcendentals=0
        ),
    )(*args)


def pair_masks(rows):
    at = lax.broadcasted_iota(jnp.int32, (rows, LANES), 1)
    return (at < HD, at >= HD)


def pick(x, mask):
    return jnp.where(mask, x, jnp.zeros_like(x))


def column(ref, h):
    at = lax.broadcasted_iota(jnp.int32, ref.shape, 1)
    return jnp.sum(jnp.where(at == h, ref[...], 0.0), axis=-1, keepdims=True)


def look_body(first, last, half, *refs):
    p, g1, b1, kg, idq, idk, a1o, a1x, a2o, a2x = refs[:10]
    refs = refs[10:]
    if first:
        qg, normed, k_raw, k_low, v_low, out, stat, q_raw, q, bias = refs
    else:
        q, acc, total_in, normed, k_raw, k_low, v_low, out, stat, bias = refs
    x = p[...].astype(F4)
    c, r = centre(x)
    n = (c * r * g1[...] + b1[...]).astype(BF)
    normed[...] = n
    head = 0 if first else half
    cut = a1o.shape[1]
    for s, (a1, a2) in enumerate(((a1o, a2o), (a1x, a2x))):
        at = s * half
        one = dot_nn(n, a1[:, head:])
        two = dot_nn(n, a2[...])
        if first:
            q_raw[:, at : at + half] = one[:, :half]
        k_raw[:, at : at + cut - half] = one[:, half - head :]
        k_raw[:, at + cut - half : at + half] = two[:, : 2 * half - cut]
        v_low[:, at : at + half] = two[:, 2 * half - cut :].astype(BF)
    matrix = group_matrix()
    for t in range(tiles(2 * half)):
        cols = slice(t * TILE, (t + 1) * TILE)
        c, r = head_norm(k_raw[:, cols], matrix)
        k_low[:, cols] = (c * r * kg[...]).astype(BF)
        if first:
            c, r = head_norm(q_raw[:, cols], matrix)
            q[:, cols] = (c * r * qg[...] * (float(HD) ** -0.5)).astype(BF)

    bias[...] = jnp.where(idq[...] == idk[...], 0.0, -1e30)
    stat[...] = jnp.zeros_like(stat) if first else total_in[...]
    masks = pair_masks(p.shape[0])
    lanes = lax.broadcasted_iota(jnp.int32, stat.shape, 1)

    @pl.loop(0, 2 * half // LANES)
    def _(pair):
        cols = lane(pair, LANES)
        q_pair, k_pair, v_pair = q[:, cols], k_low[:, cols], v_low[:, cols]
        outs = []
        for s, mask in enumerate(masks):
            e = jnp.exp(dot_nt(pick(q_pair, mask), k_pair) + bias[...])
            total = jnp.sum(e, axis=-1, keepdims=True)
            got = dot_nn(e.astype(BF), v_pair)
            if not first:
                got = got + acc[:, cols]
            h = 2 * pair + s
            if last:
                total = total + column(stat, h)
                got = got * (1.0 / total)
                stat[...] = jnp.where(lanes == h, jnp.log(total), stat[...])
            else:
                stat[...] += jnp.where(lanes == h, total, 0.0)
            outs.append(got)
        out[:, cols] = jnp.where(masks[0], outs[0], outs[1]).astype(out.dtype)


def look(first, last, p, g1, b1, qg, kg, idq, idk, parts, before):
    tokens, width = p.shape
    half = width // 2
    wide = (tokens, width)
    outs = [(wide, BF), (wide, F4), (wide, BF), (wide, BF)]
    outs += [(wide, BF if last else F4), ((tokens, LANES), F4)]
    if first:
        outs += [(wide, F4), (wide, BF)]
    flops = 2 * tokens * width * (width * (3 if first else 2) + 4 * tokens)
    body = functools.partial(look_body, first, last, half)
    scratch = [pltpu.VMEM((tokens, tokens), F4)]
    extra = (qg,) if first else before
    return call(
        body, outs, scratch, 6, flops, p, g1, b1, kg, idq, idk, *parts, *extra
    )


ROOT = math.sqrt(2.0 / math.pi)
CUBE = 0.044715


def gelu_pair(u):
    square = u * u
    t = jnp.tanh(ROOT * u * (1.0 + CUBE * square))
    half = 0.5 * (1.0 + t)
    slope = half + 0.5 * u * (1.0 - t * t) * (ROOT * (1.0 + 3.0 * CUBE * square))
    return u * half, slope


def up_body(half, p, att, cot, g2, b2, b1o, b1x, b2o, b2x, *outs):
    mixed, n2, act, slope, g1o, g1x, g2o, g2x = outs
    first = b1o.shape[1]
    inner = first + b2o.shape[1] - half
    m = p[...].astype(F4)
    for s, part in enumerate((b2o, b2x)):
        m = m + dot_nt(att[:, s * half : (s + 1) * half], part[:, :half])
    mixed[...] = m
    c, r = centre(m)
    n2[...] = (c * r * g2[...] + b2[...]).astype(BF)
    for s, (one, two) in enumerate(((b1o, b2o), (b1x, b2x))):

        @pl.loop(0, tiles(first))
        def _(i):
            u = dot_nn(n2[...], one[:, lane(i, TILE)])
            to = pl.ds(pl.multiple_of(s * inner + i * TILE, TILE), TILE)
            a, d = gelu_pair(u)
            act[:, to] = a.astype(BF)
            slope[:, to] = d.astype(BF)

        rest = inner - first
        for i in range(tiles(rest)):
            u = dot_nn(n2[...], two[:, half + i * TILE : half + (i + 1) * TILE])
            to = slice(s * inner + first + i * TILE, s * inner + first + (i + 1) * TILE)
            a, d = gelu_pair(u)
            act[:, to] = a.astype(BF)
            slope[:, to] = d.astype(BF)
    mid = g1o.shape[1]
    for s, (one, two) in enumerate(((g1o, g2o), (g1x, g2x))):
        for base, out in ((s * inner, one), (s * inner + mid, two)):

            @pl.loop(0, tiles(mid))
            def _(i):
                frm = pl.ds(pl.multiple_of(base + i * TILE, TILE), TILE)
                out[:, lane(i, TILE)] = dot_tn(cot[...], act[:, frm]).astype(BF)


def slope_body(half, *refs):
    mixed, slope, att, cot, g2 = refs[:5]
    b1o, b1x, b2o, b2x, c1o, c1x, c2o, c2x = refs[5:13]
    d_up, d_mixed, d_att, delta, gains = refs[13:]
    first = b1o.shape[1]
    inner = first + b2o.shape[1] - half
    mid = c1o.shape[1]
    for s, (one, two) in enumerate(((c1o, c2o), (c1x, c2x))):
        at = s * inner
        for base, part in ((at, one), (at + mid, two)):

            @pl.loop(0, tiles(mid))
            def _(i):
                to = pl.ds(pl.multiple_of(base + i * TILE, TILE), TILE)
                d = dot_nn(cot[...], part[:, lane(i, TILE)])
                d_up[:, to] = (d * slope[:, to].astype(F4)).astype(BF)

    e = jnp.zeros(mixed.shape, F4)
    for s, (one, two) in enumerate(((b1o, b2o), (b1x, b2x))):
        at = s * inner
        e = e + dot_nt(d_up[:, at : at + first], one[...])
        e = e + dot_nt(d_up[:, at + first : at + inner], two[:, half:])
    c, r = centre(mixed[...])
    t = e * g2[...]
    d_mixed[...] = cot[...].astype(F4) + r * (
        t - mean_last(t) - c * (r * r) * mean_last(t * c)
    )
    gains[0:1, :] = jnp.sum(e * c * r, axis=0, keepdims=True)
    gains[1:2, :] = jnp.sum(e, axis=0, keepdims=True)
    d_branch = d_mixed[...].astype(BF)
    row = lax.broadcasted_iota(jnp.int32, (half, LANES), 0) // HD
    col = lax.broadcasted_iota(jnp.int32, (half, LANES), 1)
    sums = jnp.zeros(delta.shape, F4)
    for s, part in enumerate((b2o, b2x)):
        cols = slice(s * half, (s + 1) * half)
        d = dot_nn(d_branch, part[:, :half]).astype(BF)
        d_att[:, cols] = d
        prod = d.astype(F4) * att[:, cols].astype(F4)
        high = prod.astype(BF)
        low = (prod - high.astype(F4)).astype(BF)
        sel = jnp.where(row + s * (half // HD) == col, 1.0, 0.0).astype(BF)
        sums = sums + dot_nn(high, sel) + dot_nn(low, sel)
    delta[...] = sums


def inner_body(half, *refs):
    mixed, n2, act, att, d_up, d_mixed, c1o, c1x, c2o, c2x = refs[:10]
    result, h1o, h1x, h2o, h2x = refs[10:]
    first = h1o.shape[1]
    inner = first + h2o.shape[1] - half
    mid = c1o.shape[1]
    out = mixed[...]
    for s, (one, two) in enumerate(((c1o, c2o), (c1x, c2x))):
        at = s * inner
        out = out + dot_nt(act[:, at : at + mid], one[...])
        out = out + dot_nt(act[:, at + mid : at + inner], two[...])
    result[...] = out.astype(BF)
    d_branch = d_mixed[...].astype(BF)
    for s, (one, two) in enumerate(((h1o, h2o), (h1x, h2x))):
        at = s * inner
        two[:, :half] = dot_tn(d_branch, att[:, s * half : (s + 1) * half]).astype(BF)

        @pl.loop(0, tiles(first))
        def _(i):
            frm = pl.ds(pl.multiple_of(at + i * TILE, TILE), TILE)
            one[:, lane(i, TILE)] = dot_tn(n2[...], d_up[:, frm]).astype(BF)

        two[:, half:] = dot_tn(n2[...], d_up[:, at + first : at + inner]).astype(BF)


def back_body(half, *refs):
    q, k, v, d_att, stat, delta, idq, idk, k_raw, p, kg = refs[:11]
    a1o, a1x, a2o, a2x = refs[11:15]
    dk_low, dv_low, dq, part, k_gain, gains, bias, dk = refs[15:]
    tokens = q.shape[0]
    bias[...] = jnp.where(idq[...] == idk[...], 0.0, -1e30)
    masks = pair_masks(tokens)

    @pl.loop(0, q.shape[1] // LANES)
    def _(pair):
        cols = lane(pair, LANES)
        q_pair, k_pair, v_pair, d_pair = q[:, cols], k[:, cols], v[:, cols], d_att[:, cols]
        sum_q = sum_k = sum_v = None
        for s, mask in enumerate(masks):
            q_one, d_one, k_one = pick(q_pair, mask), pick(d_pair, mask), pick(k_pair, mask)
            h = 2 * pair + s
            score = dot_nt(q_one, k_pair) + bias[...]
            prob = jnp.exp(score - column(stat, h))
            d_prob = dot_nt(d_one, v_pair)
            d_score = (prob * (d_prob - column(delta, h))).astype(BF)
            one_v = dot_tn(prob.astype(BF), d_one)
            one_k = dot_tn(d_score, q_one)
            one_q = dot_nn(d_score, k_one)
            sum_v = one_v if s == 0 else sum_v + one_v
            sum_k = one_k if s == 0 else sum_k + one_k
            sum_q = one_q if s == 0 else sum_q + one_q
        dq[:, cols] = sum_q
        dk[:, cols] = sum_k
        dv_low[:, cols] = sum_v.astype(BF)

    matrix = group_matrix()
    total = jnp.zeros((1, TILE), F4)
    for t in range(tiles(2 * half)):
        cols = slice(t * TILE, (t + 1) * TILE)
        d, g = head_norm_back(dk[:, cols], k_raw[:, cols], kg[...], matrix)
        dk_low[:, cols] = d.astype(BF)
        total = total + fold_heads(g)
    k_gain[...] = total
    cut = a1o.shape[1]
    e = jnp.zeros((tokens, 2 * half), F4)
    for s, (one, two) in enumerate(((a1o, a2o), (a1x, a2x))):
        at = s * half
        mid = at + cut - half
        e = e + dot_nt(dk_low[:, at:mid], one[:, half:])
        e = e + dot_nt(dk_low[:, mid : at + half], two[:, : 2 * half - cut])
        e = e + dot_nt(dv_low[:, at : at + half], two[:, 2 * half - cut :])
    part[...] = e.astype(part.dtype)
    c, r = centre(p[...].astype(F4))
    gains[0:1, :] = jnp.sum(e * c * r, axis=0, keepdims=True)
    gains[1:2, :] = jnp.sum(e, axis=0, keepdims=True)


def back_block(last, q, k, v, d_att, stat, delta, idq, idk, k_raw, p, kg, parts):
    tokens, width = q.shape
    half = width // 2
    outs = [
        ((tokens, width), BF),
        ((tokens, width), BF),
        ((tokens, width), F4),
        ((tokens, width), F4 if last else BF),
        ((1, TILE), F4),
        ((2, width), F4),
    ]
    scratch = [pltpu.VMEM((tokens, tokens), F4), pltpu.VMEM((tokens, width), F4)]
    flops = 10 * tokens * tokens * width * 4 + 4 * tokens * width * width
    body = functools.partial(back_body, half)
    return call(
        body, outs, scratch, 9, flops,
        q, k, v, d_att, stat, delta, idq, idk, k_raw, p, kg, *parts,
    )


def weight_body(n, half, *refs):
    q_raw, qg, p, own = refs[:4]
    a1o, a1x = refs[4:6]
    dqs, ns = refs[6 : 6 + n], refs[6 + n : 6 + 2 * n]
    dks, dvs = refs[6 + 2 * n : 6 + 3 * n], refs[6 + 3 * n : 6 + 4 * n]
    part, q_gain, gains, g1o, g1x, g2o, g2x, dq_low, n_all, dk_all, dv_all = refs[6 + 4 * n :]
    tokens = q_raw.shape[0]
    matrix = group_matrix()
    total = jnp.zeros((1, TILE), F4)
    factor = float(HD) ** -0.5
    for t in range(tiles(2 * half)):
        cols = slice(t * TILE, (t + 1) * TILE)
        e = dqs[0][:, cols]
        for other in dqs[1:]:
            e = e + other[:, cols]
        d, g = head_norm_back(e * factor, q_raw[:, cols], qg[...], matrix)
        dq_low[:, cols] = d.astype(BF)
        total = total + fold_heads(g)
    q_gain[...] = total
    e = dot_nt(dq_low[:, :half], a1o[:, :half]) + dot_nt(dq_low[:, half:], a1x[:, :half])
    part[...] = own[...] + e
    c, r = centre(p[...].astype(F4))
    gains[0:1, :] = jnp.sum(e * c * r, axis=0, keepdims=True)
    gains[1:2, :] = jnp.sum(e, axis=0, keepdims=True)
    for b in range(n):
        rows = slice(b * tokens, (b + 1) * tokens)
        n_all[rows, :] = ns[b][...]
        dk_all[rows, :] = dks[b][...]
        dv_all[rows, :] = dvs[b][...]
    cut = g1o.shape[1]
    for s, (one, two) in enumerate(((g1o, g2o), (g1x, g2x))):
        at = s * half
        mid = at + cut - half
        one[:, :half] = dot_tn(ns[0][...], dq_low[:, at : at + half]).astype(BF)
        one[:, half:] = dot_tn(n_all[...], dk_all[:, at:mid]).astype(BF)
        two[:, : 2 * half - cut] = dot_tn(n_all[...], dk_all[:, mid : at + half]).astype(BF)
        two[:, 2 * half - cut :] = dot_tn(n_all[...], dv_all[:, at : at + half]).astype(BF)


def input_body(own, rest, p, g1, d_mixed, out):
    e = own[...] + rest[...].astype(F4)
    c, r = centre(p[...].astype(F4))
    t = e * g1[...]
    out[...] = d_mixed[...] + r * (t - mean_last(t) - c * (r * r) * mean_last(t * c))


def small_body(n, *refs):
    first, second, query, keys = refs[: n + 1], refs[n + 1], refs[n + 2], refs[n + 3 : -1]
    out = refs[-1]
    out[...] = jnp.zeros_like(out)
    total = first[0][...]
    for x in first[1:]:
        total = total + x[...]
    out[0:2, :] = total
    out[2:4, :] = second[...]
    out[4:5, :TILE] = query[...]
    total = keys[0][...]
    for x in keys[1:]:
        total = total + x[...]
    out[5:6, :TILE] = total


def take_micro(x, c):
    mine = jnp.where(c0, x[0], x[1])
    other = jnp.where(c0, x[1], x[0])
    return mine, other


def per_device(
    patches,
    picture_ids,
    ln1_gain,
    ln1_bias,
    w_query,
    w_key,
    w_value,
    q_gain,
    k_gain,
    w_out,
    ln2_gain,
    ln2_bias,
    w_up,
    w_down,
    cotangent,
):
    n = lax.axis_size("row")
    at = Place()
    c0 = at("c")
    width = patches.shape[-1]
    half = w_query.shape[1]
    piece = patches.shape[2]
    tokens = 2 * piece
    inner = w_up.shape[1]

    cut_a = half + half * 2 // 3
    first = inner * 2 // 3
    mid = inner // 2
    width_b = inner + half
    whole = not regular(w_query.shape[0])
    chunk_a = jnp.concatenate([w_query, w_key, w_value], axis=1)
    chunk_b = [w_up[:, :first], w_out.T, w_up[:, first:], w_down.T]
    line_a = Chain(line_steps(chunk_a, at))
    line_b = Chain(line_steps(jnp.concatenate(chunk_b, axis=1), at))

    def take(x):
        mine = jnp.where(c0, x[0], x[1])
        got = swap_core(jnp.where(c0, x[1], x[0]))
        return jnp.concatenate(
            [jnp.where(c0, mine, got), jnp.where(c0, got, mine)], axis=0
        )

    g1, b1 = ln1_gain[None], ln1_bias[None]
    g2, b2 = ln2_gain[None], ln2_bias[None]
    qg, kg = jnp.tile(q_gain, TILE // HD)[None], jnp.tile(k_gain, TILE // HD)[None]
    ids = jnp.where(c0, picture_ids[0, 0], picture_ids[0, 1]).reshape(n, tokens)
    id_blocks = [index(ids, at("row", j), keepdims=True) for j in range(n)]
    idq = id_blocks[0].reshape(tokens, 1)
    ready = lax.optimization_barrier((g1, b1, g2, b2, qg, kg, idq, *id_blocks))
    g1, b1, g2, b2, qg, kg, idq, *id_blocks = ready

    line_a.step()
    p_own = take(patches[0])
    for _ in range(n - 2):
        line_a.step(*ready)
        ready = ()
    got_a = line_a.last
    rows_a = line_a.finish()
    chain_a = Chain(plane_steps((rows_a[:, :cut_a], rows_a[:, cut_a:]), whole, at))
    chain_a.step()
    line_b.step(*got_a)
    chain_a.step()
    for _ in range(n - 3):
        line_b.step()
    blocks = [p_own, hop(after(p_own, line_b.last), n)]
    line_b.step()
    got_b = line_b.last
    rows_b = line_b.finish()
    a_one, a_two = chain_a.finish()
    a_parts = a_one + a_two
    cot = take(cotangent[0])
    parts_b = (rows_b[:, :first], rows_b[:, first:width_b])
    parts_c = (rows_b[:, width_b : width_b + mid], rows_b[:, width_b + mid :])
    chain_b = Chain(plane_steps(parts_b, whole, at))
    chain_c = Chain(plane_steps(parts_c, whole, at))

    made = []
    before = token = ()
    deps = got_b
    for j in range(n):
        if 0 < j < n - 1:
            blocks.append(hop(blocks[j], n))
        if j in (0, 1, n - 1):
            chain_b.step(*token)
        if j == n - 1:
            chain_c.step(*deps)
        made.append(
            look(
                j == 0, j == n - 1, after(blocks[j], deps), g1, b1, qg, kg, idq,
                id_blocks[j], a_parts, before,
            )
        )
        if j == 0:
            q_raw, q_low = made[0][6:]
        before = (q_low, *made[j][4:6])
        token = (made[j][5],)
        deps = token
        if j != 1 or n < 4:
            deps = deps + chain_b.last + chain_c.last
    normed = [m[0] for m in made]
    k_raw, k_low, v_low = [m[1] for m in made], [m[2] for m in made], [m[3] for m in made]
    att, stat = made[-1][4:6]

    b_one, b_two = chain_b.finish()
    b_parts = b_one + b_two
    chain_c.step(*token)
    mixed, n2, act, slope, *gc = call(
        functools.partial(up_body, half),
        [((tokens, width), F4), ((tokens, width), BF)]
        + [((tokens, 2 * inner), BF)] * 2
        + [((width, mid), BF)] * 4,
        [], 7,
        2 * tokens * width * (width + 4 * inner),
        p_own, after(att, deps), cot, g2, b2, *b_parts,
    )
    c_one, c_two = chain_c.finish()
    c_parts = c_one + c_two

    back_c = Chain(plane_sums((gc[0], gc[1]), (gc[2], gc[3]), whole, at)).step()
    deps = back_c.last
    back_c.step()
    d_up, d_mixed, d_att, delta, gains2 = call(
        functools.partial(slope_body, half),
        [((tokens, 2 * inner), BF), ((tokens, width), F4), ((tokens, width), BF)]
        + [((tokens, LANES), F4), ((2, width), F4)],
        [], 11,
        2 * tokens * width * (width + 4 * inner),
        after(mixed, deps), slope, att, cot, g2, *b_parts, *c_parts,
    )
    deps = back_c.last
    back_c.step(delta)
    result, *gb = call(
        functools.partial(inner_body, half),
        [((tokens, width), BF)]
        + [((width, first), BF)] * 2
        + [((width, half + inner - first), BF)] * 2,
        [], 10,
        2 * tokens * width * (width + 4 * inner),
        mixed, n2, act, att, d_up, after(d_mixed, deps), *c_parts,
    )
    sum_c = back_c.step(result).finish()
    back_b = Chain(plane_sums((gb[0], gb[1]), (gb[2], gb[3]), whole, at)).step()
    deps = (result,)

    back = [None] * n
    acc = None
    order = [*range(1, n), 0]
    for turn, j in enumerate(order):
        back[j] = back_block(
            j == 0, q_low, k_low[j], v_low[j], after(d_att, deps), stat, delta, idq,
            id_blocks[j], k_raw[j], blocks[j], kg, a_parts,
        )
        token = back[j][4]
        deps = (token,)
        if turn != 1 or n < 4:
            deps = deps + back_b.last
            back_b.step(token)
        if j:
            part = back[j][3]
            if acc is None:
                acc = part
            else:
                deps = deps + (acc,)
                acc = add_low(part, acc)
            acc = hop(acc, n)

    sum_b = back_b.finish()
    line = Chain(line_sums(jnp.concatenate([sum_b, sum_c], axis=1), whole, at)).step()
    part, dq_gain, gains_q, *ga = call(
        functools.partial(weight_body, n, half),
        [((tokens, width), F4), ((1, TILE), F4), ((2, width), F4)]
        + [((width, cut_a), BF)] * 2
        + [((width, 3 * half - cut_a), BF)] * 2,
        [pltpu.VMEM((tokens, width), BF)] + [pltpu.VMEM((n * tokens, width), BF)] * 3,
        12,
        2 * tokens * width * width * (2 + 2 * n),
        after(q_raw, deps), qg, p_own, back[0][3], *a_one,
        *[b[2] for b in back], *normed, *[b[0] for b in back], *[b[1] for b in back],
    )
    back_a = Chain(plane_sums((ga[0], ga[1]), (ga[2], ga[3]), whole, at))
    back_a.step(*line.last)
    (small,) = call(
        functools.partial(small_body, n), [((8, width), F4)], [], 1, 0,
        *[b[5] for b in back], gains_q, gains2, dq_gain, *[b[4] for b in back],
    )
    sums = Chain(sum_steps(small))
    while back_a.value is None:
        deps = back_a.last
        back_a.step(*deps)
        line.step(*deps)
        sums.step(*deps)
    last_a = Chain(line_sums(back_a.value, whole, at)).step()
    while last_a.value is None or sums.value is None:
        deps = last_a.last
        last_a.step(*deps)
        sums.step(*deps)
    grad_a, grad_bc = last_a.value, line.finish()
    grad_b, grad_c = grad_bc[:, :width_b], grad_bc[:, width_b:]
    small = sums.value
    grad_g1, grad_b1, grad_g2, grad_b2 = small[0], small[1], small[2], small[3]
    grad_gq = small[4, :TILE].reshape(-1, HD).sum(axis=0)
    grad_gk = small[5, :TILE].reshape(-1, HD).sum(axis=0)

    (grad_in,) = call(
        input_body, [((tokens, width), F4)], [], 6, 0, part, acc, p_own, g1, d_mixed
    )

    def back_home(x):
        lower, upper = x[:piece], x[piece:]
        keep = jnp.where(c0, lower, upper)
        got = swap_core(jnp.where(c0, upper, lower))
        return jnp.stack([jnp.where(c0, keep, got), jnp.where(c0, got, keep)])

    rest = half + first
    grad_wu = jnp.concatenate([grad_b[:, :first], grad_b[:, rest:]], axis=1)
    return (
        back_home(result)[None],
        back_home(grad_in)[None],
        grad_g1,
        grad_b1,
        grad_a[:, :half],
        grad_a[:, half : 2 * half],
        grad_a[:, 2 * half :],
        grad_gq,
        grad_gk,
        grad_b[:, first:rest].T,
        grad_g2,
        grad_b2,
        grad_wu,
        grad_c.T,
    )


def solution(mesh):
    rows = P("dp", None, ("row", "col"), None)
    inward = P(("dp", "row"), "col")
    outward = P("col", ("dp", "row"))
    return jax.shard_map(
        per_device,
        mesh=mesh,
        in_specs=(
            rows, P("dp", None, None), P(), P(), inward, inward, inward, P(), P(),
            outward, P(), P(), inward, outward, rows,
        ),
        out_specs=(
            rows, rows, P(), P(), inward, inward, inward, P(), P(),
            outward, P(), P(), inward, outward,
        ),
        check_vma=False,
    )
```

```python
import functools
import math

import jax
import jax.numpy as jnp
from jax import lax
from jax.experimental import pallas as pl
from jax.experimental.pallas import tpu as pltpu
from jax.sharding import PartitionSpec as P

HD = 64
LANES = 128
TILE = 256
EPSILON = 1e-06
BF = jnp.bfloat16
F4 = jnp.float32
VM = pl.BlockSpec(memory_space=pltpu.VMEM)


def ring_order(n):
    return list(range(0, n, 2)) + list(range(n - 1 - (n % 2), 0, -2))


def ring_place(r, n):
    return jnp.where(r % 2 == 0, r // 2, n - 1 - r // 2 - (n % 2) + (n % 2) * 1)


def ring_row(q, n):
    return jnp.where(2 * q < n, 2 * q, 2 * (n - 1 - q) + 1)


class Place:
    def __init__(self):
        n, m = lax.axis_size("row"), lax.axis_size("dp")
        place = ring_place(lax.axis_index("row"), n)
        me = lax.axis_index("dp")
        made = {("c",): lax.axis_index("col") == 0}
        for bit in range(m.bit_length() - 1):
            one = (me >> bit) & 1
            made["low", bit] = one == 0
            made["one", bit] = one
            made["zero", bit] = 1 - one
        for r in range(n):
            slot = (place - ring_order(n).index(r) + n) % n
            for k in range(n - 1):
                made["slot", r, k] = slot == k
        for step in range(n):
            made["row", step] = ring_row((place - step + n) % n, n)
        names = list(made)
        self.made = dict(zip(names, lax.optimization_barrier(tuple(made.values()))))

    def __call__(self, *name):
        return self.made[name]


def index(x, i, axis=0, keepdims=False):
    return lax.dynamic_index_in_dim(
        x, i, axis, keepdims=keepdims, allow_negative_indices=False
    )


def hop(x, n):
    order = ring_order(n)
    pairs = [(order[i], order[(i + 1) % n]) for i in range(n)]
    return lax.ppermute(x, "row", pairs)


def swap_bit(x, axis, n, bit):
    return lax.ppermute(x, axis, [(i, i ^ (1 << bit)) for i in range(n)])


def swap_core(x):
    return lax.ppermute(x, "col", [(0, 1), (1, 0)])


def bit_orders(n):
    bits = list(range(n.bit_length() - 1))
    half = len(bits) // 2
    return bits, bits[half:] + bits[:half]


def regular(block):
    dp = lax.axis_size("dp")
    return dp & (dp - 1) == 0 and block % 16 == 0


def after(x, deps):
    if not deps:
        return x
    return lax.optimization_barrier((x, *deps))[0]


def all_after(xs, deps):
    if not deps:
        return tuple(xs)
    return lax.optimization_barrier((*xs, *deps))[: len(xs)]


class Chain:
    def __init__(self, steps):
        self.steps = steps
        self.last = ()
        self.value = None
        next(steps)

    def step(self, *deps):
        if self.value is None:
            try:
                self.last = self.steps.send(deps)
            except StopIteration as end:
                self.value = end.value
        return self

    def finish(self):
        while self.value is None:
            self.step()
        return self.value


def join_line(blocks, at):
    n = len(blocks)
    parts = []
    for r in range(n):
        x = blocks[-1]
        for k in range(n - 1):
            x = jnp.where(at("slot", r, k), blocks[k], x)
        parts.append(x)
    return jnp.concatenate(parts, axis=0)


def line_steps(shard, at):
    deps = yield ()
    shard = after(shard, deps)
    if not regular(shard.shape[0]):
        return shard
    n = lax.axis_size("row")
    blocks = [shard]
    for _ in range(n - 1):
        got = hop(blocks[-1], n)
        deps = yield (got,)
        blocks.append(after(got, deps))
    return join_line(blocks, at)


def plane_steps(parts, whole, at):
    deps = yield ()
    m = lax.axis_size("dp")
    parts = list(parts)
    if whole:
        both = lax.all_gather(
            jnp.concatenate(parts, axis=1), ("dp", "row"), axis=0, tiled=True
        )
        deps = yield (both,)
        both, cut = after(both, deps), parts[0].shape[1]
        parts = [both[:, :cut], both[:, cut:]]
    else:
        done = ([], [])
        for bits in zip(*bit_orders(m)):
            got = [swap_bit(x, "dp", m, bit) for x, bit in zip(parts, bits)]
            deps = yield tuple(got)
            got = all_after(got, deps)
            for i, bit in enumerate(bits):
                axis = sum(1 for b in done[i] if b > bit)
                low = at("low", bit)
                first = jnp.where(low, parts[i], got[i])
                second = jnp.where(low, got[i], parts[i])
                parts[i] = jnp.stack([first, second], axis=axis)
                done[i].append(bit)
        parts = [x.reshape(-1, x.shape[-1]) for x in parts]
    got = [swap_core(x) for x in parts]
    yield tuple(got)
    return (parts[0], got[0]), (parts[1], got[1])


def add_low(a, b):
    return (a.astype(F4) + b.astype(F4)).astype(BF)


def plane_sums(one, two, whole, at):
    m = lax.axis_size("dp")
    deps = yield ()
    got = [swap_core(x) for x in all_after((one[1], two[1]), deps)]
    deps = yield tuple(got)
    parts = [add_low(x[0], y) for x, y in zip((one, two), all_after(got, deps))]
    if whole:
        return jnp.concatenate(parts, axis=1)
    count = m.bit_length() - 1
    left = [list(range(count - 1, -1, -1)), list(range(count - 1, -1, -1))]
    parts = [x.reshape((2,) * count + (-1, x.shape[-1])) for x in parts]
    for bits in zip(*bit_orders(m)):
        got, keep = [], []
        for i, bit in enumerate(bits):
            axis = left[i].index(bit)
            got.append(swap_bit(index(parts[i], at("zero", bit), axis), "dp", m, bit))
            keep.append(index(parts[i], at("one", bit), axis))
            left[i].remove(bit)
        deps = yield tuple(got)
        parts = [add_low(x, y) for x, y in zip(keep, all_after(got, deps))]
    return jnp.concatenate(parts, axis=1)


def line_sums(both, whole, at):
    deps = yield ()
    both = after(both, deps)
    if whole:
        total = lax.psum_scatter(both, ("dp", "row"), scatter_dimension=0, tiled=True)
        yield (total,)
        return total.astype(F4)
    n = lax.axis_size("row")
    both = both.reshape(n, -1, both.shape[-1])
    acc = index(both, at("row", 1))
    for step in range(n - 1):
        got = hop(acc, n)
        deps = yield (got,)
        got = after(got, deps)
        if step < n - 2:
            acc = add_low(index(both, at("row", step + 2)), got)
    return index(both, at("row", 0)).astype(F4) + got.astype(F4)


def sum_steps(x):
    deps = yield ()
    got = swap_core(after(x, deps))
    deps = yield (got,)
    x = x + after(got, deps)
    for axis in ("dp", "row"):
        n = lax.axis_size(axis)
        for bit in range(n.bit_length() - 1) if n & (n - 1) == 0 else (None,):
            got = lax.psum(x, axis) - x if bit is None else swap_bit(x, axis, n, bit)
            deps = yield (got,)
            x = x + after(got, deps)
    return x


def dot_nn(a, b):
    return jnp.dot(a, b, preferred_element_type=F4)


def dot_nt(a, b):
    return lax.dot_general(a, b, (((1,), (1,)), ((), ())), preferred_element_type=F4)


def dot_tn(a, b):
    return lax.dot_general(a, b, (((0,), (0,)), ((), ())), preferred_element_type=F4)


def mean_last(x):
    return jnp.mean(x, axis=-1, keepdims=True)


def centre(x):
    c = x - mean_last(x)
    return c, lax.rsqrt(mean_last(c * c) + EPSILON)


def group_matrix():
    i = lax.broadcasted_iota(jnp.int32, (TILE, TILE), 0) // HD
    j = lax.broadcasted_iota(jnp.int32, (TILE, TILE), 1) // HD
    return jnp.where(i == j, 1.0 / HD, 0.0).astype(BF)


def group_mean(x, matrix):
    high = x.astype(BF)
    low = (x - high.astype(F4)).astype(BF)
    return dot_nn(high, matrix) + dot_nn(low, matrix)


def head_norm(x, matrix):
    c = x - group_mean(x, matrix)
    return c, lax.rsqrt(group_mean(c * c, matrix) + EPSILON)


def head_norm_back(e, x, gain, matrix):
    c, r = head_norm(x, matrix)
    t = e * gain
    d = r * (t - group_mean(t, matrix) - c * (r * r) * group_mean(t * c, matrix))
    return d, e * c * r


def fold_heads(x):
    return jnp.sum(x, axis=0, keepdims=True)


def tiles(width):
    return width // TILE


def lane(i, width):
    return pl.ds(pl.multiple_of(i * width, width), width)


def call(body, outs, scratch, room, flops, *args):
    size = sum(a.size * a.dtype.itemsize for a in args)
    size += sum(math.prod(s) * jnp.dtype(d).itemsize for s, d in outs)
    hold = sum(math.prod(s.shape) * jnp.dtype(s.dtype).itemsize for s in scratch)
    return pl.pallas_call(
        body,
        out_shape=[jax.ShapeDtypeStruct(s, d) for s, d in outs],
        in_specs=[VM] * len(args),
        out_specs=[VM] * len(outs),
        scratch_shapes=scratch,
        compiler_params=pltpu.CompilerParams(vmem_limit_bytes=hold + (room << 20)),
        cost_estimate=pl.CostEstimate(
            flops=int(flops) * 4, bytes_accessed=int(size), transcendentals=0
        ),
    )(*args)


def pair_masks(rows):
    at = lax.broadcasted_iota(jnp.int32, (rows, LANES), 1)
    return (at < HD, at >= HD)


def pick(x, mask):
    return jnp.where(mask, x, jnp.zeros_like(x))


def column(ref, h):
    at = lax.broadcasted_iota(jnp.int32, ref.shape, 1)
    return jnp.sum(jnp.where(at == h, ref[...], 0.0), axis=-1, keepdims=True)


def look_body(first, last, half, *refs):
    p, g1, b1, kg, idq, idk, a1o, a1x, a2o, a2x = refs[:10]
    refs = refs[10:]
    if first:
        qg, normed, k_raw, k_low, v_low, out, stat, q_raw, q, bias = refs
    else:
        q, acc, total_in, normed, k_raw, k_low, v_low, out, stat, bias = refs
    x = p[...].astype(F4)
    c, r = centre(x)
    n = (c * r * g1[...] + b1[...]).astype(BF)
    normed[...] = n
    head = 0 if first else half
    cut = a1o.shape[1]
    for s, (a1, a2) in enumerate(((a1o, a2o), (a1x, a2x))):
        at = s * half
        one = dot_nn(n, a1[:, head:])
        two = dot_nn(n, a2[...])
        if first:
            q_raw[:, at : at + half] = one[:, :half]
        k_raw[:, at : at + cut - half] = one[:, half - head :]
        k_raw[:, at + cut - half : at + half] = two[:, : 2 * half - cut]
        v_low[:, at : at + half] = two[:, 2 * half - cut :].astype(BF)
    matrix = group_matrix()
    for t in range(tiles(2 * half)):
        cols = slice(t * TILE, (t + 1) * TILE)
        c, r = head_norm(k_raw[:, cols], matrix)
        k_low[:, cols] = (c * r * kg[...]).astype(BF)
        if first:
            c, r = head_norm(q_raw[:, cols], matrix)
            q[:, cols] = (c * r * qg[...] * (float(HD) ** -0.5)).astype(BF)

    bias[...] = jnp.where(idq[...] == idk[...], 0.0, -1e30)
    stat[...] = jnp.zeros_like(stat) if first else total_in[...]
    masks = pair_masks(p.shape[0])
    lanes = lax.broadcasted_iota(jnp.int32, stat.shape, 1)

    @pl.loop(0, 2 * half // LANES)
    def _(pair):
        cols = lane(pair, LANES)
        q_pair, k_pair, v_pair = q[:, cols], k_low[:, cols], v_low[:, cols]
        outs = []
        for s, mask in enumerate(masks):
            e = jnp.exp(dot_nt(pick(q_pair, mask), k_pair) + bias[...])
            total = jnp.sum(e, axis=-1, keepdims=True)
            got = dot_nn(e.astype(BF), v_pair)
            if not first:
                got = got + acc[:, cols]
            h = 2 * pair + s
            if last:
                total = total + column(stat, h)
                got = got * (1.0 / total)
                stat[...] = jnp.where(lanes == h, jnp.log(total), stat[...])
            else:
                stat[...] += jnp.where(lanes == h, total, 0.0)
            outs.append(got)
        out[:, cols] = jnp.where(masks[0], outs[0], outs[1]).astype(out.dtype)


def look(first, last, p, g1, b1, qg, kg, idq, idk, parts, before):
    tokens, width = p.shape
    half = width // 2
    wide = (tokens, width)
    outs = [(wide, BF), (wide, F4), (wide, BF), (wide, BF)]
    outs += [(wide, BF if last else F4), ((tokens, LANES), F4)]
    if first:
        outs += [(wide, F4), (wide, BF)]
    flops = 2 * tokens * width * (width * (3 if first else 2) + 4 * tokens)
    body = functools.partial(look_body, first, last, half)
    scratch = [pltpu.VMEM((tokens, tokens), F4)]
    extra = (qg,) if first else before
    return call(
        body, outs, scratch, 6, flops, p, g1, b1, kg, idq, idk, *parts, *extra
    )


ROOT = math.sqrt(2.0 / math.pi)
CUBE = 0.044715


def gelu_pair(u):
    square = u * u
    t = jnp.tanh(ROOT * u * (1.0 + CUBE * square))
    half = 0.5 * (1.0 + t)
    slope = half + 0.5 * u * (1.0 - t * t) * (ROOT * (1.0 + 3.0 * CUBE * square))
    return u * half, slope


def up_body(half, p, att, cot, g2, b2, b1o, b1x, b2o, b2x, *outs):
    mixed, n2, act, slope, g1o, g1x, g2o, g2x = outs
    first = b1o.shape[1]
    inner = first + b2o.shape[1] - half
    m = p[...].astype(F4)
    for s, part in enumerate((b2o, b2x)):
        m = m + dot_nt(att[:, s * half : (s + 1) * half], part[:, :half])
    mixed[...] = m
    c, r = centre(m)
    n2[...] = (c * r * g2[...] + b2[...]).astype(BF)
    for s, (one, two) in enumerate(((b1o, b2o), (b1x, b2x))):

        @pl.loop(0, tiles(first))
        def _(i):
            u = dot_nn(n2[...], one[:, lane(i, TILE)])
            to = pl.ds(pl.multiple_of(s * inner + i * TILE, TILE), TILE)
            a, d = gelu_pair(u)
            act[:, to] = a.astype(BF)
            slope[:, to] = d.astype(BF)

        rest = inner - first
        for i in range(tiles(rest)):
            u = dot_nn(n2[...], two[:, half + i * TILE : half + (i + 1) * TILE])
            to = slice(s * inner + first + i * TILE, s * inner + first + (i + 1) * TILE)
            a, d = gelu_pair(u)
            act[:, to] = a.astype(BF)
            slope[:, to] = d.astype(BF)
    mid = g1o.shape[1]
    for s, (one, two) in enumerate(((g1o, g2o), (g1x, g2x))):
        for base, out in ((s * inner, one), (s * inner + mid, two)):

            @pl.loop(0, tiles(mid))
            def _(i):
                frm = pl.ds(pl.multiple_of(base + i * TILE, TILE), TILE)
                out[:, lane(i, TILE)] = dot_tn(cot[...], act[:, frm]).astype(BF)


def slope_body(half, *refs):
    mixed, slope, att, cot, g2 = refs[:5]
    b1o, b1x, b2o, b2x, c1o, c1x, c2o, c2x = refs[5:13]
    d_up, d_mixed, d_att, delta, gains = refs[13:]
    first = b1o.shape[1]
    inner = first + b2o.shape[1] - half
    mid = c1o.shape[1]
    for s, (one, two) in enumerate(((c1o, c2o), (c1x, c2x))):
        at = s * inner
        for base, part in ((at, one), (at + mid, two)):

            @pl.loop(0, tiles(mid))
            def _(i):
                to = pl.ds(pl.multiple_of(base + i * TILE, TILE), TILE)
                d = dot_nn(cot[...], part[:, lane(i, TILE)])
                d_up[:, to] = (d * slope[:, to].astype(F4)).astype(BF)

    e = jnp.zeros(mixed.shape, F4)
    for s, (one, two) in enumerate(((b1o, b2o), (b1x, b2x))):
        at = s * inner
        e = e + dot_nt(d_up[:, at : at + first], one[...])
        e = e + dot_nt(d_up[:, at + first : at + inner], two[:, half:])
    c, r = centre(mixed[...])
    t = e * g2[...]
    d_mixed[...] = cot[...].astype(F4) + r * (
        t - mean_last(t) - c * (r * r) * mean_last(t * c)
    )
    gains[0:1, :] = jnp.sum(e * c * r, axis=0, keepdims=True)
    gains[1:2, :] = jnp.sum(e, axis=0, keepdims=True)
    d_branch = d_mixed[...].astype(BF)
    row = lax.broadcasted_iota(jnp.int32, (half, LANES), 0) // HD
    col = lax.broadcasted_iota(jnp.int32, (half, LANES), 1)
    sums = jnp.zeros(delta.shape, F4)
    for s, part in enumerate((b2o, b2x)):
        cols = slice(s * half, (s + 1) * half)
        d = dot_nn(d_branch, part[:, :half]).astype(BF)
        d_att[:, cols] = d
        prod = d.astype(F4) * att[:, cols].astype(F4)
        high = prod.astype(BF)
        low = (prod - high.astype(F4)).astype(BF)
        sel = jnp.where(row + s * (half // HD) == col, 1.0, 0.0).astype(BF)
        sums = sums + dot_nn(high, sel) + dot_nn(low, sel)
    delta[...] = sums


def inner_body(half, *refs):
    mixed, n2, act, att, d_up, d_mixed, c1o, c1x, c2o, c2x = refs[:10]
    result, h1o, h1x, h2o, h2x = refs[10:]
    first = h1o.shape[1]
    inner = first + h2o.shape[1] - half
    mid = c1o.shape[1]
    out = mixed[...]
    for s, (one, two) in enumerate(((c1o, c2o), (c1x, c2x))):
        at = s * inner
        out = out + dot_nt(act[:, at : at + mid], one[...])
        out = out + dot_nt(act[:, at + mid : at + inner], two[...])
    result[...] = out.astype(BF)
    d_branch = d_mixed[...].astype(BF)
    for s, (one, two) in enumerate(((h1o, h2o), (h1x, h2x))):
        at = s * inner
        two[:, :half] = dot_tn(d_branch, att[:, s * half : (s + 1) * half]).astype(BF)

        @pl.loop(0, tiles(first))
        def _(i):
            frm = pl.ds(pl.multiple_of(at + i * TILE, TILE), TILE)
            one[:, lane(i, TILE)] = dot_tn(n2[...], d_up[:, frm]).astype(BF)

        two[:, half:] = dot_tn(n2[...], d_up[:, at + first : at + inner]).astype(BF)


def back_body(half, *refs):
    q, k, v, d_att, stat, delta, idq, idk, k_raw, p, kg = refs[:11]
    a1o, a1x, a2o, a2x = refs[11:15]
    dk_low, dv_low, dq, part, k_gain, gains, bias, dk = refs[15:]
    tokens = q.shape[0]
    bias[...] = jnp.where(idq[...] == idk[...], 0.0, -1e30)
    masks = pair_masks(tokens)

    @pl.loop(0, q.shape[1] // LANES)
    def _(pair):
        cols = lane(pair, LANES)
        q_pair, k_pair, v_pair, d_pair = q[:, cols], k[:, cols], v[:, cols], d_att[:, cols]
        sum_q = sum_k = sum_v = None
        for s, mask in enumerate(masks):
            q_one, d_one, k_one = pick(q_pair, mask), pick(d_pair, mask), pick(k_pair, mask)
            h = 2 * pair + s
            score = dot_nt(q_one, k_pair) + bias[...]
            prob = jnp.exp(score - column(stat, h))
            d_prob = dot_nt(d_one, v_pair)
            d_score = (prob * (d_prob - column(delta, h))).astype(BF)
            one_v = dot_tn(prob.astype(BF), d_one)
            one_k = dot_tn(d_score, q_one)
            one_q = dot_nn(d_score, k_one)
            sum_v = one_v if s == 0 else sum_v + one_v
            sum_k = one_k if s == 0 else sum_k + one_k
            sum_q = one_q if s == 0 else sum_q + one_q
        dq[:, cols] = sum_q
        dk[:, cols] = sum_k
        dv_low[:, cols] = sum_v.astype(BF)

    matrix = group_matrix()
    total = jnp.zeros((1, TILE), F4)
    for t in range(tiles(2 * half)):
        cols = slice(t * TILE, (t + 1) * TILE)
        d, g = head_norm_back(dk[:, cols], k_raw[:, cols], kg[...], matrix)
        dk_low[:, cols] = d.astype(BF)
        total = total + fold_heads(g)
    k_gain[...] = total
    cut = a1o.shape[1]
    e = jnp.zeros((tokens, 2 * half), F4)
    for s, (one, two) in enumerate(((a1o, a2o), (a1x, a2x))):
        at = s * half
        mid = at + cut - half
        e = e + dot_nt(dk_low[:, at:mid], one[:, half:])
        e = e + dot_nt(dk_low[:, mid : at + half], two[:, : 2 * half - cut])
        e = e + dot_nt(dv_low[:, at : at + half], two[:, 2 * half - cut :])
    part[...] = e.astype(part.dtype)
    c, r = centre(p[...].astype(F4))
    gains[0:1, :] = jnp.sum(e * c * r, axis=0, keepdims=True)
    gains[1:2, :] = jnp.sum(e, axis=0, keepdims=True)


def back_block(last, q, k, v, d_att, stat, delta, idq, idk, k_raw, p, kg, parts):
    tokens, width = q.shape
    half = width // 2
    outs = [
        ((tokens, width), BF),
        ((tokens, width), BF),
        ((tokens, width), F4),
        ((tokens, width), F4 if last else BF),
        ((1, TILE), F4),
        ((2, width), F4),
    ]
    scratch = [pltpu.VMEM((tokens, tokens), F4), pltpu.VMEM((tokens, width), F4)]
    flops = 10 * tokens * tokens * width * 4 + 4 * tokens * width * width
    body = functools.partial(back_body, half)
    return call(
        body, outs, scratch, 9, flops,
        q, k, v, d_att, stat, delta, idq, idk, k_raw, p, kg, *parts,
    )


def weight_body(n, half, *refs):
    q_raw, qg, p, own = refs[:4]
    a1o, a1x = refs[4:6]
    dqs, ns = refs[6 : 6 + n], refs[6 + n : 6 + 2 * n]
    dks, dvs = refs[6 + 2 * n : 6 + 3 * n], refs[6 + 3 * n : 6 + 4 * n]
    part, q_gain, gains, g1o, g1x, g2o, g2x, dq_low, n_all, dk_all, dv_all = refs[6 + 4 * n :]
    tokens = q_raw.shape[0]
    matrix = group_matrix()
    total = jnp.zeros((1, TILE), F4)
    factor = float(HD) ** -0.5
    for t in range(tiles(2 * half)):
        cols = slice(t * TILE, (t + 1) * TILE)
        e = dqs[0][:, cols]
        for other in dqs[1:]:
            e = e + other[:, cols]
        d, g = head_norm_back(e * factor, q_raw[:, cols], qg[...], matrix)
        dq_low[:, cols] = d.astype(BF)
        total = total + fold_heads(g)
    q_gain[...] = total
    e = dot_nt(dq_low[:, :half], a1o[:, :half]) + dot_nt(dq_low[:, half:], a1x[:, :half])
    part[...] = own[...] + e
    c, r = centre(p[...].astype(F4))
    gains[0:1, :] = jnp.sum(e * c * r, axis=0, keepdims=True)
    gains[1:2, :] = jnp.sum(e, axis=0, keepdims=True)
    for b in range(n):
        rows = slice(b * tokens, (b + 1) * tokens)
        n_all[rows, :] = ns[b][...]
        dk_all[rows, :] = dks[b][...]
        dv_all[rows, :] = dvs[b][...]
    cut = g1o.shape[1]
    for s, (one, two) in enumerate(((g1o, g2o), (g1x, g2x))):
        at = s * half
        mid = at + cut - half
        one[:, :half] = dot_tn(ns[0][...], dq_low[:, at : at + half]).astype(BF)
        one[:, half:] = dot_tn(n_all[...], dk_all[:, at:mid]).astype(BF)
        two[:, : 2 * half - cut] = dot_tn(n_all[...], dk_all[:, mid : at + half]).astype(BF)
        two[:, 2 * half - cut :] = dot_tn(n_all[...], dv_all[:, at : at + half]).astype(BF)


def input_body(own, rest, p, g1, d_mixed, out):
    e = own[...] + rest[...].astype(F4)
    c, r = centre(p[...].astype(F4))
    t = e * g1[...]
    out[...] = d_mixed[...] + r * (t - mean_last(t) - c * (r * r) * mean_last(t * c))


def small_body(n, *refs):
    first, second, query, keys = refs[: n + 1], refs[n + 1], refs[n + 2], refs[n + 3 : -1]
    out = refs[-1]
    out[...] = jnp.zeros_like(out)
    total = first[0][...]
    for x in first[1:]:
        total = total + x[...]
    out[0:2, :] = total
    out[2:4, :] = second[...]
    out[4:5, :TILE] = query[...]
    total = keys[0][...]
    for x in keys[1:]:
        total = total + x[...]
    out[5:6, :TILE] = total


def take_micro(x, c):
    mine = jnp.where(c0, x[0], x[1])
    other = jnp.where(c0, x[1], x[0])
    return mine, other


def per_device(
    patches,
    picture_ids,
    ln1_gain,
    ln1_bias,
    w_query,
    w_key,
    w_value,
    q_gain,
    k_gain,
    w_out,
    ln2_gain,
    ln2_bias,
    w_up,
    w_down,
    cotangent,
):
    n = lax.axis_size("row")
    at = Place()
    c0 = at("c")
    width = patches.shape[-1]
    half = w_query.shape[1]
    piece = patches.shape[2]
    tokens = 2 * piece
    inner = w_up.shape[1]

    cut_a = half + half * 2 // 3
    first = inner * 2 // 3
    mid = inner // 2
    width_b = inner + half
    whole = not regular(w_query.shape[0])
    chunk_a = jnp.concatenate([w_query, w_key, w_value], axis=1)
    chunk_b = [w_up[:, :first], w_out.T, w_up[:, first:], w_down.T]
    line_a = Chain(line_steps(chunk_a, at))
    line_b = Chain(line_steps(jnp.concatenate(chunk_b, axis=1), at))

    def take(x):
        mine = jnp.where(c0, x[0], x[1])
        got = swap_core(jnp.where(c0, x[1], x[0]))
        return jnp.concatenate(
            [jnp.where(c0, mine, got), jnp.where(c0, got, mine)], axis=0
        )

    g1, b1 = ln1_gain[None], ln1_bias[None]
    g2, b2 = ln2_gain[None], ln2_bias[None]
    qg, kg = jnp.tile(q_gain, TILE // HD)[None], jnp.tile(k_gain, TILE // HD)[None]
    ids = jnp.where(c0, picture_ids[0, 0], picture_ids[0, 1]).reshape(n, tokens)
    id_blocks = [index(ids, at("row", j), keepdims=True) for j in range(n)]
    idq = id_blocks[0].reshape(tokens, 1)
    ready = lax.optimization_barrier((g1, b1, g2, b2, qg, kg, idq, *id_blocks))
    g1, b1, g2, b2, qg, kg, idq, *id_blocks = ready

    line_a.step()
    p_own = take(patches[0])
    blocks = [p_own, hop(p_own, n)]
    for _ in range(n - 2):
        line_a.step(*ready)
        ready = ()
    got_a = line_a.last
    rows_a = line_a.finish()
    chain_a = Chain(plane_steps((rows_a[:, :cut_a], rows_a[:, cut_a:]), whole, at))
    chain_a.step()
    line_b.step(*got_a)
    chain_a.step()
    for _ in range(n - 3):
        line_b.step()
    line_b.step()
    got_b = line_b.last
    rows_b = line_b.finish()
    a_one, a_two = chain_a.finish()
    a_parts = a_one + a_two
    cot = take(cotangent[0])
    parts_b = (rows_b[:, :first], rows_b[:, first:width_b])
    parts_c = (rows_b[:, width_b : width_b + mid], rows_b[:, width_b + mid :])
    chain_b = Chain(plane_steps(parts_b, whole, at))
    chain_c = Chain(plane_steps(parts_c, whole, at))

    made, marks = [], []
    before = token = ()
    deps = got_b
    for j in range(n):
        if 0 < j < n - 1:
            blocks.append(hop(after(blocks[j], marks[j - 2] if j > 1 else got_b), n))
        if j in (0, 1, n - 1):
            chain_b.step(*token)
        if j == n - 1:
            chain_c.step(*deps)
        made.append(
            look(
                j == 0, j == n - 1, after(blocks[j], deps), g1, b1, qg, kg, idq,
                id_blocks[j], a_parts, before,
            )
        )
        if j == 0:
            q_raw, q_low = made[0][6:]
        before = (q_low, *made[j][4:6])
        token = (made[j][5],)
        marks.append(token)
        deps = token
        if j != 1 or n < 4:
            deps = deps + chain_b.last + chain_c.last
    normed = [m[0] for m in made]
    k_raw, k_low, v_low = [m[1] for m in made], [m[2] for m in made], [m[3] for m in made]
    att, stat = made[-1][4:6]

    b_one, b_two = chain_b.finish()
    b_parts = b_one + b_two
    chain_c.step(*token)
    mixed, n2, act, slope, *gc = call(
        functools.partial(up_body, half),
        [((tokens, width), F4), ((tokens, width), BF)]
        + [((tokens, 2 * inner), BF)] * 2
        + [((width, mid), BF)] * 4,
        [], 7,
        2 * tokens * width * (width + 4 * inner),
        p_own, after(att, deps), cot, g2, b2, *b_parts,
    )
    c_one, c_two = chain_c.finish()
    c_parts = c_one + c_two

    back_c = Chain(plane_sums((gc[0], gc[1]), (gc[2], gc[3]), whole, at)).step()
    deps = back_c.last
    back_c.step()
    d_up, d_mixed, d_att, delta, gains2 = call(
        functools.partial(slope_body, half),
        [((tokens, 2 * inner), BF), ((tokens, width), F4), ((tokens, width), BF)]
        + [((tokens, LANES), F4), ((2, width), F4)],
        [], 11,
        2 * tokens * width * (width + 4 * inner),
        after(mixed, deps), slope, att, cot, g2, *b_parts, *c_parts,
    )
    result, *gb = call(
        functools.partial(inner_body, half),
        [((tokens, width), BF)]
        + [((width, first), BF)] * 2
        + [((width, half + inner - first), BF)] * 2,
        [], 10,
        2 * tokens * width * (width + 4 * inner),
        mixed, n2, act, att, d_up, d_mixed, *c_parts,
    )
    back_c.step(result)
    back_b = Chain(plane_sums((gb[0], gb[1]), (gb[2], gb[3]), whole, at)).step()
    deps = (result,)

    back = [None] * n
    acc = None
    order = [*range(1, n), 0]
    for turn, j in enumerate(order):
        back[j] = back_block(
            j == 0, q_low, k_low[j], v_low[j], after(d_att, deps), stat, delta, idq,
            id_blocks[j], k_raw[j], blocks[j], kg, a_parts,
        )
        token = back[j][4]
        deps = (token, *back_b.last, *back_c.last)
        back_b.step(token)
        back_c.step(token)
        if j:
            part = back[j][3]
            if acc is None:
                acc = part
            else:
                deps = deps + (acc,)
                acc = add_low(part, acc)
            acc = hop(acc, n)
    deps = deps + (acc,)
    sum_b, sum_c = back_b.finish(), back_c.finish()
    line = Chain(line_sums(jnp.concatenate([sum_b, sum_c], axis=1), whole, at)).step()
    part, dq_gain, gains_q, *ga = call(
        functools.partial(weight_body, n, half),
        [((tokens, width), F4), ((1, TILE), F4), ((2, width), F4)]
        + [((width, cut_a), BF)] * 2
        + [((width, 3 * half - cut_a), BF)] * 2,
        [pltpu.VMEM((tokens, width), BF)] + [pltpu.VMEM((n * tokens, width), BF)] * 3,
        12,
        2 * tokens * width * width * (2 + 2 * n),
        after(q_raw, deps), qg, p_own, back[0][3], *a_one,
        *[b[2] for b in back], *normed, *[b[0] for b in back], *[b[1] for b in back],
    )
    back_a = Chain(plane_sums((ga[0], ga[1]), (ga[2], ga[3]), whole, at))
    back_a.step(*line.last)
    (small,) = call(
        functools.partial(small_body, n), [((8, width), F4)], [], 1, 0,
        *[b[5] for b in back], gains_q, gains2, dq_gain, *[b[4] for b in back],
    )
    sums = Chain(sum_steps(small))
    while back_a.value is None:
        deps = back_a.last
        back_a.step(*deps)
        line.step(*deps)
        sums.step(*deps)
    last_a = Chain(line_sums(back_a.value, whole, at)).step()
    while last_a.value is None or sums.value is None:
        deps = last_a.last
        last_a.step(*deps)
        sums.step(*deps)
    grad_a, grad_bc = last_a.value, line.finish()
    grad_b, grad_c = grad_bc[:, :width_b], grad_bc[:, width_b:]
    small = sums.value
    grad_g1, grad_b1, grad_g2, grad_b2 = small[0], small[1], small[2], small[3]
    grad_gq = small[4, :TILE].reshape(-1, HD).sum(axis=0)
    grad_gk = small[5, :TILE].reshape(-1, HD).sum(axis=0)

    (grad_in,) = call(
        input_body, [((tokens, width), F4)], [], 6, 0, part, acc, p_own, g1, d_mixed
    )

    def back_home(x):
        lower, upper = x[:piece], x[piece:]
        keep = jnp.where(c0, lower, upper)
        got = swap_core(jnp.where(c0, upper, lower))
        return jnp.stack([jnp.where(c0, keep, got), jnp.where(c0, got, keep)])

    rest = half + first
    grad_wu = jnp.concatenate([grad_b[:, :first], grad_b[:, rest:]], axis=1)
    return (
        back_home(result)[None],
        back_home(grad_in)[None],
        grad_g1,
        grad_b1,
        grad_a[:, :half],
        grad_a[:, half : 2 * half],
        grad_a[:, 2 * half :],
        grad_gq,
        grad_gk,
        grad_b[:, first:rest].T,
        grad_g2,
        grad_b2,
        grad_wu,
        grad_c.T,
    )


def solution(mesh):
    rows = P("dp", None, ("row", "col"), None)
    inward = P(("dp", "row"), "col")
    outward = P("col", ("dp", "row"))
    return jax.shard_map(
        per_device,
        mesh=mesh,
        in_specs=(
            rows, P("dp", None, None), P(), P(), inward, inward, inward, P(), P(),
            outward, P(), P(), inward, outward, rows,
        ),
        out_specs=(
            rows, rows, P(), P(), inward, inward, inward, P(), P(),
            outward, P(), P(), inward, outward,
        ),
        check_vma=False,
    )
```

```python
import functools
import math

import jax
import jax.numpy as jnp
from jax import lax
from jax.experimental import pallas as pl
from jax.experimental.pallas import tpu as pltpu
from jax.sharding import PartitionSpec as P

HD = 64
LANES = 128
TILE = 256
EPSILON = 1e-06
BF = jnp.bfloat16
F4 = jnp.float32
VM = pl.BlockSpec(memory_space=pltpu.VMEM)


def ring_order(n):
    return list(range(0, n, 2)) + list(range(n - 1 - (n % 2), 0, -2))


def ring_place(r, n):
    return jnp.where(r % 2 == 0, r // 2, n - 1 - r // 2 - (n % 2) + (n % 2) * 1)


def ring_row(q, n):
    return jnp.where(2 * q < n, 2 * q, 2 * (n - 1 - q) + 1)


class Place:
    def __init__(self):
        n, m = lax.axis_size("row"), lax.axis_size("dp")
        place = ring_place(lax.axis_index("row"), n)
        me = lax.axis_index("dp")
        made = {("c",): lax.axis_index("col") == 0}
        for bit in range(m.bit_length() - 1):
            one = (me >> bit) & 1
            made["low", bit] = one == 0
            made["one", bit] = one
            made["zero", bit] = 1 - one
        for r in range(n):
            slot = (place - ring_order(n).index(r) + n) % n
            for k in range(n - 1):
                made["slot", r, k] = slot == k
        for step in range(n):
            made["row", step] = ring_row((place - step + n) % n, n)
        names = list(made)
        self.made = dict(zip(names, lax.optimization_barrier(tuple(made.values()))))

    def __call__(self, *name):
        return self.made[name]


def index(x, i, axis=0, keepdims=False):
    return lax.dynamic_index_in_dim(
        x, i, axis, keepdims=keepdims, allow_negative_indices=False
    )


def hop(x, n):
    order = ring_order(n)
    pairs = [(order[i], order[(i + 1) % n]) for i in range(n)]
    return lax.ppermute(x, "row", pairs)


def swap_bit(x, axis, n, bit):
    return lax.ppermute(x, axis, [(i, i ^ (1 << bit)) for i in range(n)])


def swap_core(x):
    return lax.ppermute(x, "col", [(0, 1), (1, 0)])


def bit_orders(n):
    bits = list(range(n.bit_length() - 1))
    half = len(bits) // 2
    return bits, bits[half:] + bits[:half]


def regular(block):
    dp = lax.axis_size("dp")
    return dp & (dp - 1) == 0 and block % 16 == 0


def after(x, deps):
    if not deps:
        return x
    return lax.optimization_barrier((x, *deps))[0]


def all_after(xs, deps):
    if not deps:
        return tuple(xs)
    return lax.optimization_barrier((*xs, *deps))[: len(xs)]


class Chain:
    def __init__(self, steps):
        self.steps = steps
        self.last = ()
        self.value = None
        next(steps)

    def step(self, *deps):
        if self.value is None:
            try:
                self.last = self.steps.send(deps)
            except StopIteration as end:
                self.value = end.value
        return self

    def finish(self):
        while self.value is None:
            self.step()
        return self.value


def join_line(blocks, at):
    n = len(blocks)
    parts = []
    for r in range(n):
        x = blocks[-1]
        for k in range(n - 1):
            x = jnp.where(at("slot", r, k), blocks[k], x)
        parts.append(x)
    return jnp.concatenate(parts, axis=0)


def line_steps(shard, at):
    deps = yield ()
    shard = after(shard, deps)
    if not regular(shard.shape[0]):
        return shard
    n = lax.axis_size("row")
    blocks = [shard]
    for _ in range(n - 1):
        got = hop(blocks[-1], n)
        deps = yield (got,)
        blocks.append(after(got, deps))
    return join_line(blocks, at)


def plane_steps(parts, whole, at):
    deps = yield ()
    m = lax.axis_size("dp")
    parts = list(parts)
    if whole:
        both = lax.all_gather(
            jnp.concatenate(parts, axis=1), ("dp", "row"), axis=0, tiled=True
        )
        deps = yield (both,)
        both, cut = after(both, deps), parts[0].shape[1]
        parts = [both[:, :cut], both[:, cut:]]
    else:
        done = ([], [])
        for bits in zip(*bit_orders(m)):
            got = [swap_bit(x, "dp", m, bit) for x, bit in zip(parts, bits)]
            deps = yield tuple(got)
            got = all_after(got, deps)
            for i, bit in enumerate(bits):
                axis = sum(1 for b in done[i] if b > bit)
                low = at("low", bit)
                first = jnp.where(low, parts[i], got[i])
                second = jnp.where(low, got[i], parts[i])
                parts[i] = jnp.stack([first, second], axis=axis)
                done[i].append(bit)
        parts = [x.reshape(-1, x.shape[-1]) for x in parts]
    got = [swap_core(x) for x in parts]
    yield tuple(got)
    return (parts[0], got[0]), (parts[1], got[1])


def add_low(a, b):
    return (a.astype(F4) + b.astype(F4)).astype(BF)


def plane_sums(one, two, whole, at):
    m = lax.axis_size("dp")
    deps = yield ()
    got = [swap_core(x) for x in all_after((one[1], two[1]), deps)]
    deps = yield tuple(got)
    parts = [add_low(x[0], y) for x, y in zip((one, two), all_after(got, deps))]
    if whole:
        return jnp.concatenate(parts, axis=1)
    count = m.bit_length() - 1
    left = [list(range(count - 1, -1, -1)), list(range(count - 1, -1, -1))]
    parts = [x.reshape((2,) * count + (-1, x.shape[-1])) for x in parts]
    for bits in zip(*bit_orders(m)):
        got, keep = [], []
        for i, bit in enumerate(bits):
            axis = left[i].index(bit)
            got.append(swap_bit(index(parts[i], at("zero", bit), axis), "dp", m, bit))
            keep.append(index(parts[i], at("one", bit), axis))
            left[i].remove(bit)
        deps = yield tuple(got)
        parts = [add_low(x, y) for x, y in zip(keep, all_after(got, deps))]
    return jnp.concatenate(parts, axis=1)


def line_sums(both, whole, at):
    deps = yield ()
    both = after(both, deps)
    if whole:
        total = lax.psum_scatter(both, ("dp", "row"), scatter_dimension=0, tiled=True)
        yield (total,)
        return total.astype(F4)
    n = lax.axis_size("row")
    both = both.reshape(n, -1, both.shape[-1])
    acc = index(both, at("row", 1))
    for step in range(n - 1):
        got = hop(acc, n)
        deps = yield (got,)
        got = after(got, deps)
        if step < n - 2:
            acc = add_low(index(both, at("row", step + 2)), got)
    return index(both, at("row", 0)).astype(F4) + got.astype(F4)


def sum_steps(x):
    deps = yield ()
    got = swap_core(after(x, deps))
    deps = yield (got,)
    x = x + after(got, deps)
    for axis in ("dp", "row"):
        n = lax.axis_size(axis)
        for bit in range(n.bit_length() - 1) if n & (n - 1) == 0 else (None,):
            got = lax.psum(x, axis) - x if bit is None else swap_bit(x, axis, n, bit)
            deps = yield (got,)
            x = x + after(got, deps)
    return x


def dot_nn(a, b):
    return jnp.dot(a, b, preferred_element_type=F4)


def dot_nt(a, b):
    return lax.dot_general(a, b, (((1,), (1,)), ((), ())), preferred_element_type=F4)


def dot_tn(a, b):
    return lax.dot_general(a, b, (((0,), (0,)), ((), ())), preferred_element_type=F4)


def mean_last(x):
    return jnp.mean(x, axis=-1, keepdims=True)


def centre(x):
    c = x - mean_last(x)
    return c, lax.rsqrt(mean_last(c * c) + EPSILON)


def group_matrix():
    i = lax.broadcasted_iota(jnp.int32, (TILE, TILE), 0) // HD
    j = lax.broadcasted_iota(jnp.int32, (TILE, TILE), 1) // HD
    return jnp.where(i == j, 1.0 / HD, 0.0).astype(BF)


def group_mean(x, matrix):
    high = x.astype(BF)
    low = (x - high.astype(F4)).astype(BF)
    return dot_nn(high, matrix) + dot_nn(low, matrix)


def head_norm(x, matrix):
    c = x - group_mean(x, matrix)
    return c, lax.rsqrt(group_mean(c * c, matrix) + EPSILON)


def low_mean(x, matrix):
    return dot_nn(x.astype(BF), matrix)


def head_norm_back(e, hat, rate, gain, matrix):
    t = e * gain
    d = rate * (t - low_mean(t, matrix) - hat * low_mean(t * hat, matrix))
    return d, e * hat


def fold_heads(x):
    return jnp.sum(x, axis=0, keepdims=True)


def padded(rows):
    return -(-rows // LANES) * LANES


def head_rows(columns):
    rows = columns.shape[0]
    pair = lax.broadcasted_iota(jnp.int32, (8, LANES), 0)
    at = lax.broadcasted_iota(jnp.int32, (8, LANES), 1)
    parts = []
    for s in (0, 1):
        sel = jnp.where(at == 2 * pair + s, 1.0, 0.0)
        parts.append(
            lax.dot_general(
                sel, columns, (((1,), (1,)), ((), ())),
                precision=lax.Precision.HIGHEST, preferred_element_type=F4,
            )
        )
    return parts, padded(rows)


def tiles(width):
    return width // TILE


def lane(i, width):
    return pl.ds(pl.multiple_of(i * width, width), width)


def call(body, outs, scratch, room, flops, *args):
    size = sum(a.size * a.dtype.itemsize for a in args)
    size += sum(math.prod(s) * jnp.dtype(d).itemsize for s, d in outs)
    hold = sum(math.prod(s.shape) * jnp.dtype(s.dtype).itemsize for s in scratch)
    return pl.pallas_call(
        body,
        out_shape=[jax.ShapeDtypeStruct(s, d) for s, d in outs],
        in_specs=[VM] * len(args),
        out_specs=[VM] * len(outs),
        scratch_shapes=scratch,
        compiler_params=pltpu.CompilerParams(vmem_limit_bytes=hold + (room << 20)),
        cost_estimate=pl.CostEstimate(
            flops=int(flops) * 4, bytes_accessed=int(size), transcendentals=0
        ),
    )(*args)


def pair_masks(rows):
    at = lax.broadcasted_iota(jnp.int32, (rows, LANES), 1)
    return (at < HD, at >= HD)


def pick(x, mask):
    return jnp.where(mask, x, jnp.zeros_like(x))


def write_rows(ref, columns):
    parts, step = head_rows(columns)
    ref[...] = jnp.zeros_like(ref)
    for s, x in enumerate(parts):
        ref[:, s * step : s * step + x.shape[1]] = x


def column(ref, h):
    at = lax.broadcasted_iota(jnp.int32, ref.shape, 1)
    return jnp.sum(jnp.where(at == h, ref[...], 0.0), axis=-1, keepdims=True)


def look_body(first, last, half, *refs):
    p, g1, b1, kg, ids, idk, a1o, a1x, a2o, a2x = refs[:10]
    idq = ids[: p.shape[0], :]
    refs = refs[10:]
    if first:
        qg, normed, k_raw, k_rate, k_low, v_low, out, total_out = refs[:8]
        q_raw, q_rate, q, bias, stat = refs[8:]
    else:
        q, acc, total_in, normed, k_raw, k_rate, k_low, v_low, out, total_out = refs[:10]
        bias, stat = refs[10:]
    x = p[...].astype(F4)
    c, r = centre(x)
    n = (c * r * g1[...] + b1[...]).astype(BF)
    normed[...] = n
    head = 0 if first else half
    cut = a1o.shape[1]
    for s, (a1, a2) in enumerate(((a1o, a2o), (a1x, a2x))):
        at = s * half
        one = dot_nn(n, a1[:, head:])
        two = dot_nn(n, a2[...])
        if first:
            q_raw[:, at : at + half] = one[:, :half]
        k_raw[:, at : at + cut - half] = one[:, half - head :]
        k_raw[:, at + cut - half : at + half] = two[:, : 2 * half - cut]
        v_low[:, at : at + half] = two[:, 2 * half - cut :].astype(BF)
    matrix = group_matrix()
    for t in range(tiles(2 * half)):
        cols = slice(t * TILE, (t + 1) * TILE)
        c, r = head_norm(k_raw[:, cols], matrix)
        k_raw[:, cols] = c * r
        k_rate[:, cols] = r
        k_low[:, cols] = (c * r * kg[...]).astype(BF)
        if first:
            c, r = head_norm(q_raw[:, cols], matrix)
            q_raw[:, cols] = c * r
            q_rate[:, cols] = r
            q[:, cols] = (c * r * qg[...] * (float(HD) ** -0.5)).astype(BF)

    bias[...] = jnp.where(idq == idk[...], 0.0, -1e30)
    stat[...] = jnp.zeros_like(stat) if first else total_in[...]
    masks = pair_masks(p.shape[0])
    lanes = lax.broadcasted_iota(jnp.int32, stat.shape, 1)

    @pl.loop(0, 2 * half // LANES)
    def _(pair):
        cols = lane(pair, LANES)
        q_pair, k_pair, v_pair = q[:, cols], k_low[:, cols], v_low[:, cols]
        outs = []
        for s, mask in enumerate(masks):
            e = jnp.exp(dot_nt(pick(q_pair, mask), k_pair) + bias[...])
            total = jnp.sum(e, axis=-1, keepdims=True)
            got = dot_nn(e.astype(BF), v_pair)
            if not first:
                got = got + acc[:, cols]
            h = 2 * pair + s
            if last:
                total = total + column(stat, h)
                got = got * (1.0 / total)
                stat[...] = jnp.where(lanes == h, jnp.log(total), stat[...])
            else:
                stat[...] += jnp.where(lanes == h, total, 0.0)
            outs.append(got)
        out[:, cols] = jnp.where(masks[0], outs[0], outs[1]).astype(out.dtype)

    if last:
        write_rows(total_out, stat[...])
    else:
        total_out[...] = stat[...]


def look(first, last, p, g1, b1, qg, kg, idq, idk, parts, before):
    tokens, width = p.shape
    half = width // 2
    wide = (tokens, width)
    outs = [(wide, BF), (wide, F4), (wide, F4), (wide, BF), (wide, BF)]
    outs += [(wide, BF if last else F4)]
    outs += [((8, 2 * padded(tokens)) if last else (tokens, LANES), F4)]
    if first:
        outs += [(wide, F4), (wide, F4), (wide, BF)]
    flops = 2 * tokens * width * (width * (3 if first else 2) + 4 * tokens)
    body = functools.partial(look_body, first, last, half)
    scratch = [pltpu.VMEM((tokens, tokens), F4), pltpu.VMEM((tokens, LANES), F4)]
    extra = (qg,) if first else before
    return call(
        body, outs, scratch, 6, flops, p, g1, b1, kg, idq, idk, *parts, *extra
    )


ROOT = math.sqrt(2.0 / math.pi)
CUBE = 0.044715


def gelu_pair(u):
    square = u * u
    t = jnp.tanh(ROOT * u * (1.0 + CUBE * square))
    half = 0.5 * (1.0 + t)
    slope = half + 0.5 * u * (1.0 - t * t) * (ROOT * (1.0 + 3.0 * CUBE * square))
    return u * half, slope


def up_body(half, p, att, cot, g2, b2, b1o, b1x, b2o, b2x, *outs):
    mixed, n2, act, slope, g1o, g1x, g2o, g2x = outs
    first = b1o.shape[1]
    inner = first + b2o.shape[1] - half
    m = p[...].astype(F4)
    for s, part in enumerate((b2o, b2x)):
        m = m + dot_nt(att[:, s * half : (s + 1) * half], part[:, :half])
    mixed[...] = m
    c, r = centre(m)
    n2[...] = (c * r * g2[...] + b2[...]).astype(BF)
    for s, (one, two) in enumerate(((b1o, b2o), (b1x, b2x))):

        @pl.loop(0, tiles(first))
        def _(i):
            u = dot_nn(n2[...], one[:, lane(i, TILE)])
            to = pl.ds(pl.multiple_of(s * inner + i * TILE, TILE), TILE)
            a, d = gelu_pair(u)
            act[:, to] = a.astype(BF)
            slope[:, to] = d.astype(BF)

        rest = inner - first
        for i in range(tiles(rest)):
            u = dot_nn(n2[...], two[:, half + i * TILE : half + (i + 1) * TILE])
            to = slice(s * inner + first + i * TILE, s * inner + first + (i + 1) * TILE)
            a, d = gelu_pair(u)
            act[:, to] = a.astype(BF)
            slope[:, to] = d.astype(BF)
    mid = g1o.shape[1]
    for s, (one, two) in enumerate(((g1o, g2o), (g1x, g2x))):
        for base, out in ((s * inner, one), (s * inner + mid, two)):

            @pl.loop(0, tiles(mid))
            def _(i):
                frm = pl.ds(pl.multiple_of(base + i * TILE, TILE), TILE)
                out[:, lane(i, TILE)] = dot_tn(cot[...], act[:, frm]).astype(BF)


def slope_body(half, *refs):
    mixed, slope, att, cot, g2 = refs[:5]
    b1o, b1x, b2o, b2x, c1o, c1x, c2o, c2x = refs[5:13]
    d_up, d_mixed, d_att, delta, gains = refs[13:]
    first = b1o.shape[1]
    inner = first + b2o.shape[1] - half
    mid = c1o.shape[1]
    for s, (one, two) in enumerate(((c1o, c2o), (c1x, c2x))):
        at = s * inner
        for base, part in ((at, one), (at + mid, two)):

            @pl.loop(0, tiles(mid))
            def _(i):
                to = pl.ds(pl.multiple_of(base + i * TILE, TILE), TILE)
                d = dot_nn(cot[...], part[:, lane(i, TILE)])
                d_up[:, to] = (d * slope[:, to].astype(F4)).astype(BF)

    e = jnp.zeros(mixed.shape, F4)
    for s, (one, two) in enumerate(((b1o, b2o), (b1x, b2x))):
        at = s * inner
        e = e + dot_nt(d_up[:, at : at + first], one[...])
        e = e + dot_nt(d_up[:, at + first : at + inner], two[:, half:])
    c, r = centre(mixed[...])
    t = e * g2[...]
    d_mixed[...] = cot[...].astype(F4) + r * (
        t - mean_last(t) - c * (r * r) * mean_last(t * c)
    )
    gains[0:1, :] = jnp.sum(e * c * r, axis=0, keepdims=True)
    gains[1:2, :] = jnp.sum(e, axis=0, keepdims=True)
    d_branch = d_mixed[...].astype(BF)
    row = lax.broadcasted_iota(jnp.int32, (half, LANES), 0) // HD
    col = lax.broadcasted_iota(jnp.int32, (half, LANES), 1)
    sums = jnp.zeros((mixed.shape[0], LANES), F4)
    for s, part in enumerate((b2o, b2x)):
        cols = slice(s * half, (s + 1) * half)
        d = dot_nn(d_branch, part[:, :half]).astype(BF)
        d_att[:, cols] = d
        prod = d.astype(F4) * att[:, cols].astype(F4)
        high = prod.astype(BF)
        low = (prod - high.astype(F4)).astype(BF)
        sel = jnp.where(row + s * (half // HD) == col, 1.0, 0.0).astype(BF)
        sums = sums + dot_nn(high, sel) + dot_nn(low, sel)
    write_rows(delta, sums)


def inner_body(half, *refs):
    mixed, n2, act, att, d_up, d_mixed, c1o, c1x, c2o, c2x = refs[:10]
    result, h1o, h1x, h2o, h2x = refs[10:]
    first = h1o.shape[1]
    inner = first + h2o.shape[1] - half
    mid = c1o.shape[1]
    out = mixed[...]
    for s, (one, two) in enumerate(((c1o, c2o), (c1x, c2x))):
        at = s * inner
        out = out + dot_nt(act[:, at : at + mid], one[...])
        out = out + dot_nt(act[:, at + mid : at + inner], two[...])
    result[...] = out.astype(BF)
    d_branch = d_mixed[...].astype(BF)
    for s, (one, two) in enumerate(((h1o, h2o), (h1x, h2x))):
        at = s * inner
        two[:, :half] = dot_tn(d_branch, att[:, s * half : (s + 1) * half]).astype(BF)

        @pl.loop(0, tiles(first))
        def _(i):
            frm = pl.ds(pl.multiple_of(at + i * TILE, TILE), TILE)
            one[:, lane(i, TILE)] = dot_tn(n2[...], d_up[:, frm]).astype(BF)

        two[:, half:] = dot_tn(n2[...], d_up[:, at + first : at + inner]).astype(BF)


def back_body(half, j, *refs):
    q, k, v, d_att, stat, delta, idq, ids, k_hat, k_rate, kg = refs[:11]
    a1o, a1x, a2o, a2x = refs[11:15]
    dk_low, dv_low, dq, part, k_gain, bias, dk, q_cat, d_cat = refs[15:]
    tokens = q.shape[0]
    step = padded(tokens)
    bias[...] = jnp.where(ids[j * tokens : (j + 1) * tokens, :] == idq[...], 0.0, -1e30)
    q_cat[...] = jnp.zeros_like(q_cat)
    d_cat[...] = jnp.zeros_like(d_cat)
    masks = pair_masks(tokens)

    @pl.loop(0, q.shape[1] // LANES)
    def _(pair):
        cols = lane(pair, LANES)
        k_pair, v_pair = k[:, cols], v[:, cols]
        for s, mask in enumerate(masks):
            q_cat[s * step : s * step + tokens, :] = pick(q[:, cols], mask)
            d_cat[s * step : s * step + tokens, :] = pick(d_att[:, cols], mask)
        row = pl.ds(pair, 1)
        prob = jnp.exp(dot_nt(k_pair, q_cat[...]) + bias[...] - stat[row, :])
        d_prob = dot_nt(v_pair, d_cat[...])
        d_score = (prob * (d_prob - delta[row, :])).astype(BF)
        dv_low[:, cols] = dot_nn(prob.astype(BF), d_cat[...]).astype(BF)
        dk[:, cols] = dot_nn(d_score, q_cat[...])
        both = dot_tn(d_score, k_pair)
        dq[:, cols] = jnp.where(masks[0], both[:tokens], both[step : step + tokens])

    matrix = group_matrix()
    total = jnp.zeros((1, TILE), F4)
    for t in range(tiles(2 * half)):
        cols = slice(t * TILE, (t + 1) * TILE)
        d, g = head_norm_back(
            dk[:, cols], k_hat[:, cols], k_rate[:, cols], kg[...], matrix
        )
        dk_low[:, cols] = d.astype(BF)
        total = total + fold_heads(g)
    k_gain[...] = total
    cut = a1o.shape[1]
    e = jnp.zeros((tokens, 2 * half), F4)
    for s, (one, two) in enumerate(((a1o, a2o), (a1x, a2x))):
        at = s * half
        mid = at + cut - half
        e = e + dot_nt(dk_low[:, at:mid], one[:, half:])
        e = e + dot_nt(dk_low[:, mid : at + half], two[:, : 2 * half - cut])
        e = e + dot_nt(dv_low[:, at : at + half], two[:, 2 * half - cut :])
    part[...] = e.astype(part.dtype)


def back_block(j, q, k, v, d_att, stat, delta, idq, ids, k_hat, k_rate, kg, parts):
    tokens, width = q.shape
    wide, step = (tokens, width), padded(tokens)
    outs = [(wide, BF), (wide, BF), (wide, F4), (wide, F4 if j == 0 else BF)]
    outs += [((1, TILE), F4)]
    scratch = [pltpu.VMEM((tokens, 2 * step), F4), pltpu.VMEM(wide, F4)]
    scratch += [pltpu.VMEM((2 * step, LANES), BF)] * 2
    flops = 10 * tokens * tokens * width * 4 + 4 * tokens * width * width
    body = functools.partial(back_body, width // 2, j)
    return call(
        body, outs, scratch, 10, flops,
        q, k, v, d_att, stat, delta, idq, ids, k_hat, k_rate, kg, *parts,
    )


def weight_body(n, half, *refs):
    q_hat, q_rate, qg, own = refs[:4]
    a1o, a1x = refs[4:6]
    dqs, ns = refs[6 : 6 + n], refs[6 + n : 6 + 2 * n]
    dks, dvs = refs[6 + 2 * n : 6 + 3 * n], refs[6 + 3 * n : 6 + 4 * n]
    part, q_gain, g1o, g1x, g2o, g2x, dq_low, n_all, dk_all, dv_all = refs[6 + 4 * n :]
    tokens = q_hat.shape[0]
    matrix = group_matrix()
    total = jnp.zeros((1, TILE), F4)
    factor = float(HD) ** -0.5
    for t in range(tiles(2 * half)):
        cols = slice(t * TILE, (t + 1) * TILE)
        e = dqs[0][:, cols]
        for other in dqs[1:]:
            e = e + other[:, cols]
        d, g = head_norm_back(
            e * factor, q_hat[:, cols], q_rate[:, cols], qg[...], matrix
        )
        dq_low[:, cols] = d.astype(BF)
        total = total + fold_heads(g)
    q_gain[...] = total
    e = dot_nt(dq_low[:, :half], a1o[:, :half]) + dot_nt(dq_low[:, half:], a1x[:, :half])
    part[...] = own[...] + e
    for b in range(n):
        rows = slice(b * tokens, (b + 1) * tokens)
        n_all[rows, :] = ns[b][...]
        dk_all[rows, :] = dks[b][...]
        dv_all[rows, :] = dvs[b][...]
    cut = g1o.shape[1]
    for s, (one, two) in enumerate(((g1o, g2o), (g1x, g2x))):
        at = s * half
        mid = at + cut - half
        one[:, :half] = dot_tn(ns[0][...], dq_low[:, at : at + half]).astype(BF)
        one[:, half:] = dot_tn(n_all[...], dk_all[:, at:mid]).astype(BF)
        two[:, : 2 * half - cut] = dot_tn(n_all[...], dk_all[:, mid : at + half]).astype(BF)
        two[:, 2 * half - cut :] = dot_tn(n_all[...], dv_all[:, at : at + half]).astype(BF)


def input_body(own, rest, p, g1, d_mixed, second, query, *refs):
    keys, (out, small) = refs[:-2], refs[-2:]
    e = own[...] + rest[...].astype(F4)
    c, r = centre(p[...].astype(F4))
    hat = c * r
    t = e * g1[...]
    out[...] = d_mixed[...] + r * (t - mean_last(t) - hat * mean_last(t * hat))
    small[...] = jnp.zeros_like(small)
    small[0:1, :] = jnp.sum(e * hat, axis=0, keepdims=True)
    small[1:2, :] = jnp.sum(e, axis=0, keepdims=True)
    small[2:4, :] = second[...]
    small[4:5, :TILE] = query[...]
    total = keys[0][...]
    for x in keys[1:]:
        total = total + x[...]
    small[5:6, :TILE] = total


def take_micro(x, c):
    mine = jnp.where(c0, x[0], x[1])
    other = jnp.where(c0, x[1], x[0])
    return mine, other


def per_device(
    patches,
    picture_ids,
    ln1_gain,
    ln1_bias,
    w_query,
    w_key,
    w_value,
    q_gain,
    k_gain,
    w_out,
    ln2_gain,
    ln2_bias,
    w_up,
    w_down,
    cotangent,
):
    n = lax.axis_size("row")
    at = Place()
    c0 = at("c")
    width = patches.shape[-1]
    half = w_query.shape[1]
    piece = patches.shape[2]
    tokens = 2 * piece
    inner = w_up.shape[1]

    cut_a = half + half * 2 // 3
    first = inner * 2 // 3
    mid = inner // 2
    width_b = inner + half
    whole = not regular(w_query.shape[0])
    chunk_a = jnp.concatenate([w_query, w_key, w_value], axis=1)
    chunk_b = [w_up[:, :first], w_out.T, w_up[:, first:], w_down.T]
    line_a = Chain(line_steps(chunk_a, at))
    line_b = Chain(line_steps(jnp.concatenate(chunk_b, axis=1), at))

    def take(x):
        mine = jnp.where(c0, x[0], x[1])
        got = swap_core(jnp.where(c0, x[1], x[0]))
        return jnp.concatenate(
            [jnp.where(c0, mine, got), jnp.where(c0, got, mine)], axis=0
        )

    g1, b1 = ln1_gain[None], ln1_bias[None]
    g2, b2 = ln2_gain[None], ln2_bias[None]
    qg, kg = jnp.tile(q_gain, TILE // HD)[None], jnp.tile(k_gain, TILE // HD)[None]
    ids = jnp.where(c0, picture_ids[0, 0], picture_ids[0, 1]).reshape(n, tokens)
    id_blocks = [index(ids, at("row", j), keepdims=True) for j in range(n)]
    ids = jnp.concatenate(id_blocks, axis=1).reshape(n * tokens, 1)
    spare = jnp.full((1, padded(tokens) - tokens), -1, jnp.int32)
    idq = jnp.concatenate([id_blocks[0], spare] * 2, axis=1)
    ready = lax.optimization_barrier((g1, b1, g2, b2, qg, kg, ids, idq, *id_blocks))
    g1, b1, g2, b2, qg, kg, ids, idq, *id_blocks = ready

    line_a.step()
    p_own = take(patches[0])
    blocks = [p_own, hop(p_own, n)]
    for _ in range(n - 2):
        line_a.step(*ready)
        ready = ()
    got_a = line_a.last
    rows_a = line_a.finish()
    chain_a = Chain(plane_steps((rows_a[:, :cut_a], rows_a[:, cut_a:]), whole, at))
    chain_a.step()
    line_b.step(*got_a)
    chain_a.step()
    for _ in range(n - 3):
        line_b.step()
    line_b.step()
    got_b = line_b.last
    rows_b = line_b.finish()
    a_one, a_two = chain_a.finish()
    a_parts = a_one + a_two
    cot = take(cotangent[0])
    parts_b = (rows_b[:, :first], rows_b[:, first:width_b])
    parts_c = (rows_b[:, width_b : width_b + mid], rows_b[:, width_b + mid :])
    chain_b = Chain(plane_steps(parts_b, whole, at))
    chain_c = Chain(plane_steps(parts_c, whole, at))

    made, marks = [], []
    before = token = ()
    deps = got_b
    for j in range(n):
        if 0 < j < n - 1:
            blocks.append(hop(after(blocks[j], marks[j - 2] if j > 1 else got_b), n))
        if j in (0, 1, n - 1):
            chain_b.step(*token)
        if j == n - 1:
            chain_c.step(*deps)
        made.append(
            look(
                j == 0, j == n - 1, after(blocks[j], deps), g1, b1, qg, kg, ids,
                id_blocks[j], a_parts, before,
            )
        )
        if j == 0:
            q_hat, q_rate, q_low = made[0][7:]
        before = (q_low, *made[j][5:7])
        token = (made[j][6],)
        marks.append(token)
        deps = token
        if j != 1 or n < 4:
            deps = deps + chain_b.last + chain_c.last
    normed = [m[0] for m in made]
    k_hat, k_rate, k_low, v_low = [[m[i] for m in made] for i in (1, 2, 3, 4)]
    att, stat = made[-1][5:7]

    b_one, b_two = chain_b.finish()
    b_parts = b_one + b_two
    chain_c.step(*token)
    mixed, n2, act, slope, *gc = call(
        functools.partial(up_body, half),
        [((tokens, width), F4), ((tokens, width), BF)]
        + [((tokens, 2 * inner), BF)] * 2
        + [((width, mid), BF)] * 4,
        [], 7,
        2 * tokens * width * (width + 4 * inner),
        p_own, after(att, deps), cot, g2, b2, *b_parts,
    )
    c_one, c_two = chain_c.finish()
    c_parts = c_one + c_two

    back_c = Chain(plane_sums((gc[0], gc[1]), (gc[2], gc[3]), whole, at)).step()
    deps = back_c.last
    back_c.step()
    d_up, d_mixed, d_att, delta, gains2 = call(
        functools.partial(slope_body, half),
        [((tokens, 2 * inner), BF), ((tokens, width), F4), ((tokens, width), BF)]
        + [((8, 2 * padded(tokens)), F4), ((2, width), F4)],
        [], 11,
        2 * tokens * width * (width + 4 * inner),
        after(mixed, deps), slope, att, cot, g2, *b_parts, *c_parts,
    )
    result, *gb = call(
        functools.partial(inner_body, half),
        [((tokens, width), BF)]
        + [((width, first), BF)] * 2
        + [((width, half + inner - first), BF)] * 2,
        [], 10,
        2 * tokens * width * (width + 4 * inner),
        mixed, n2, act, att, d_up, d_mixed, *c_parts,
    )
    back_c.step(result)
    back_b = Chain(plane_sums((gb[0], gb[1]), (gb[2], gb[3]), whole, at)).step()
    deps = (result,)

    back = [None] * n
    acc = None
    order = [*range(1, n), 0]
    for turn, j in enumerate(order):
        back[j] = back_block(
            j, q_low, k_low[j], v_low[j], after(d_att, deps), stat, delta, idq, ids,
            k_hat[j], k_rate[j], kg, a_parts,
        )
        token = back[j][4]
        deps = (token, *back_b.last, *back_c.last)
        back_b.step(token)
        back_c.step(token)
        if j:
            part = back[j][3]
            if acc is None:
                acc = part
            else:
                deps = deps + (acc,)
                acc = add_low(part, acc)
            acc = hop(acc, n)
    sum_b, sum_c = back_b.finish(), back_c.finish()
    line = Chain(line_sums(jnp.concatenate([sum_b, sum_c], axis=1), whole, at)).step()
    part, dq_gain, *ga = call(
        functools.partial(weight_body, n, half),
        [((tokens, width), F4), ((1, TILE), F4)]
        + [((width, cut_a), BF)] * 2
        + [((width, 3 * half - cut_a), BF)] * 2,
        [pltpu.VMEM((tokens, width), BF)] + [pltpu.VMEM((n * tokens, width), BF)] * 3,
        12,
        2 * tokens * width * width * (2 + 2 * n),
        after(q_hat, deps), q_rate, qg, back[0][3], *a_one,
        *[b[2] for b in back], *normed, *[b[0] for b in back], *[b[1] for b in back],
    )
    back_a = Chain(plane_sums((ga[0], ga[1]), (ga[2], ga[3]), whole, at))
    back_a.step(*line.last)
    deps = back_a.last
    back_a.step(*deps)
    line.step(*deps)
    deps = back_a.last
    back_a.step(*deps)
    line.step(*deps)
    grad_in, small = call(
        input_body, [((tokens, width), F4), ((8, width), F4)], [], 6, 0,
        part, after(acc, deps), p_own, g1, d_mixed, gains2, dq_gain,
        *[b[4] for b in back],
    )
    sums = Chain(sum_steps(small)).step()
    back_a.finish()
    last_a = Chain(line_sums(back_a.value, whole, at)).step()
    last_a.finish()
    sums.finish()
    grad_a, grad_bc = last_a.value, line.finish()
    grad_b, grad_c = grad_bc[:, :width_b], grad_bc[:, width_b:]
    small = sums.value
    grad_g1, grad_b1, grad_g2, grad_b2 = small[0], small[1], small[2], small[3]
    grad_gq = small[4, :TILE].reshape(-1, HD).sum(axis=0)
    grad_gk = small[5, :TILE].reshape(-1, HD).sum(axis=0)

    def back_home(x):
        lower, upper = x[:piece], x[piece:]
        keep = jnp.where(c0, lower, upper)
        got = swap_core(jnp.where(c0, upper, lower))
        return jnp.stack([jnp.where(c0, keep, got), jnp.where(c0, got, keep)])

    rest = half + first
    grad_wu = jnp.concatenate([grad_b[:, :first], grad_b[:, rest:]], axis=1)
    return (
        back_home(result)[None],
        back_home(grad_in)[None],
        grad_g1,
        grad_b1,
        grad_a[:, :half],
        grad_a[:, half : 2 * half],
        grad_a[:, 2 * half :],
        grad_gq,
        grad_gk,
        grad_b[:, first:rest].T,
        grad_g2,
        grad_b2,
        grad_wu,
        grad_c.T,
    )


def solution(mesh):
    rows = P("dp", None, ("row", "col"), None)
    inward = P(("dp", "row"), "col")
    outward = P("col", ("dp", "row"))
    return jax.shard_map(
        per_device,
        mesh=mesh,
        in_specs=(
            rows, P("dp", None, None), P(), P(), inward, inward, inward, P(), P(),
            outward, P(), P(), inward, outward, rows,
        ),
        out_specs=(
            rows, rows, P(), P(), inward, inward, inward, P(), P(),
            outward, P(), P(), inward, outward,
        ),
        check_vma=False,
    )
```

```python
import functools
import math

import jax
import jax.numpy as jnp
from jax import lax
from jax.experimental import pallas as pl
from jax.experimental.pallas import tpu as pltpu
from jax.sharding import PartitionSpec as P

HD = 64
LANES = 128
TILE = 256
EPSILON = 1e-06
BF = jnp.bfloat16
F4 = jnp.float32
VM = pl.BlockSpec(memory_space=pltpu.VMEM)


def ring_order(n):
    return list(range(0, n, 2)) + list(range(n - 1 - (n % 2), 0, -2))


def ring_place(r, n):
    return jnp.where(r % 2 == 0, r // 2, n - 1 - r // 2 - (n % 2) + (n % 2) * 1)


def ring_row(q, n):
    return jnp.where(2 * q < n, 2 * q, 2 * (n - 1 - q) + 1)


class Place:
    def __init__(self):
        n, m = lax.axis_size("row"), lax.axis_size("dp")
        place = ring_place(lax.axis_index("row"), n)
        me = lax.axis_index("dp")
        made = {("c",): lax.axis_index("col") == 0}
        for bit in range(m.bit_length() - 1):
            one = (me >> bit) & 1
            made["low", bit] = one == 0
            made["one", bit] = one
            made["zero", bit] = 1 - one
        for r in range(n):
            slot = (place - ring_order(n).index(r) + n) % n
            for k in range(n - 1):
                made["slot", r, k] = slot == k
        for r in range(n):
            for k in range(n - 1):
                made["far", r, k] = lax.axis_index("row") == r ^ k
        for k in range(n):
            made["pair", k] = lax.axis_index("row") ^ k
        for step in range(n):
            made["row", step] = ring_row((place - step + n) % n, n)
        names = list(made)
        self.made = dict(zip(names, lax.optimization_barrier(tuple(made.values()))))

    def __call__(self, *name):
        return self.made[name]


def index(x, i, axis=0, keepdims=False):
    return lax.dynamic_index_in_dim(
        x, i, axis, keepdims=keepdims, allow_negative_indices=False
    )


def hop(x, n):
    order = ring_order(n)
    pairs = [(order[i], order[(i + 1) % n]) for i in range(n)]
    return lax.ppermute(x, "row", pairs)


def swap_bit(x, axis, n, bit):
    return lax.ppermute(x, axis, [(i, i ^ (1 << bit)) for i in range(n)])


def swap_core(x):
    return lax.ppermute(x, "col", [(0, 1), (1, 0)])


def bit_orders(n):
    bits = list(range(n.bit_length() - 1))
    half = len(bits) // 2
    return bits, bits[half:] + bits[:half]


def regular(block):
    dp = lax.axis_size("dp")
    return dp & (dp - 1) == 0 and block % 16 == 0


def after(x, deps):
    if not deps:
        return x
    return lax.optimization_barrier((x, *deps))[0]


def all_after(xs, deps):
    if not deps:
        return tuple(xs)
    return lax.optimization_barrier((*xs, *deps))[: len(xs)]


class Chain:
    def __init__(self, steps):
        self.steps = steps
        self.last = ()
        self.value = None
        next(steps)

    def step(self, *deps):
        if self.value is None:
            try:
                self.last = self.steps.send(deps)
            except StopIteration as end:
                self.value = end.value
        return self

    def finish(self):
        while self.value is None:
            self.step()
        return self.value


def join_line(blocks, at, kind="slot"):
    n = len(blocks)
    parts = []
    for r in range(n):
        x = blocks[-1]
        for k in range(n - 1):
            x = jnp.where(at(kind, r, k), blocks[k], x)
        parts.append(x)
    return jnp.concatenate(parts, axis=0)


def straight(n):
    return n & (n - 1) == 0 and n <= 4


def line_steps(shard, at, at_once=False):
    deps = yield ()
    shard = after(shard, deps)
    if not regular(shard.shape[0]):
        return shard
    n = lax.axis_size("row")
    blocks = [shard]
    if at_once and straight(n):
        for k in range(1, n):
            pairs = [(i, i ^ k) for i in range(n)]
            blocks.append(lax.ppermute(shard, "row", pairs))
        deps = yield tuple(blocks[1:])
        blocks[1:] = all_after(blocks[1:], deps)
        return join_line(blocks, at, "far")
    for _ in range(n - 1):
        got = hop(blocks[-1], n)
        deps = yield (got,)
        blocks.append(after(got, deps))
    return join_line(blocks, at)


def plane_steps(parts, whole, at):
    deps = yield ()
    m = lax.axis_size("dp")
    parts = list(parts)
    if whole:
        both = lax.all_gather(
            jnp.concatenate(parts, axis=1), ("dp", "row"), axis=0, tiled=True
        )
        deps = yield (both,)
        both, cut = after(both, deps), parts[0].shape[1]
        parts = [both[:, :cut], both[:, cut:]]
    else:
        done = ([], [])
        for bits in zip(*bit_orders(m)):
            got = [swap_bit(x, "dp", m, bit) for x, bit in zip(parts, bits)]
            deps = yield tuple(got)
            got = all_after(got, deps)
            for i, bit in enumerate(bits):
                axis = sum(1 for b in done[i] if b > bit)
                low = at("low", bit)
                first = jnp.where(low, parts[i], got[i])
                second = jnp.where(low, got[i], parts[i])
                parts[i] = jnp.stack([first, second], axis=axis)
                done[i].append(bit)
        parts = [x.reshape(-1, x.shape[-1]) for x in parts]
    got = [swap_core(x) for x in parts]
    yield tuple(got)
    return (parts[0], got[0]), (parts[1], got[1])


def add_low(a, b):
    return (a.astype(F4) + b.astype(F4)).astype(BF)


def plane_sums(one, two, whole, at):
    m = lax.axis_size("dp")
    deps = yield ()
    got = [swap_core(x) for x in all_after((one[1], two[1]), deps)]
    deps = yield tuple(got)
    parts = [add_low(x[0], y) for x, y in zip((one, two), all_after(got, deps))]
    if whole:
        return jnp.concatenate(parts, axis=1)
    count = m.bit_length() - 1
    left = [list(range(count - 1, -1, -1)), list(range(count - 1, -1, -1))]
    parts = [x.reshape((2,) * count + (-1, x.shape[-1])) for x in parts]
    for bits in zip(*bit_orders(m)):
        got, keep = [], []
        for i, bit in enumerate(bits):
            axis = left[i].index(bit)
            got.append(swap_bit(index(parts[i], at("zero", bit), axis), "dp", m, bit))
            keep.append(index(parts[i], at("one", bit), axis))
            left[i].remove(bit)
        deps = yield tuple(got)
        parts = [add_low(x, y) for x, y in zip(keep, all_after(got, deps))]
    return jnp.concatenate(parts, axis=1)


def line_sums(both, whole, at, at_once=False):
    deps = yield ()
    both = after(both, deps)
    if whole:
        total = lax.psum_scatter(both, ("dp", "row"), scatter_dimension=0, tiled=True)
        yield (total,)
        return total.astype(F4)
    n = lax.axis_size("row")
    both = both.reshape(n, -1, both.shape[-1])
    if at_once and straight(n):
        got = [
            lax.ppermute(index(both, at("pair", k)), "row", [(i, i ^ k) for i in range(n)])
            for k in range(1, n)
        ]
        deps = yield tuple(got)
        total = index(both, at("pair", 0)).astype(F4)
        for x in all_after(got, deps):
            total = total + x.astype(F4)
        return total
    acc = index(both, at("row", 1))
    for step in range(n - 1):
        got = hop(acc, n)
        deps = yield (got,)
        got = after(got, deps)
        if step < n - 2:
            acc = add_low(index(both, at("row", step + 2)), got)
    return index(both, at("row", 0)).astype(F4) + got.astype(F4)


def sum_steps(x):
    deps = yield ()
    got = swap_core(after(x, deps))
    deps = yield (got,)
    x = x + after(got, deps)
    for axis in ("dp", "row"):
        n = lax.axis_size(axis)
        for bit in range(n.bit_length() - 1) if n & (n - 1) == 0 else (None,):
            got = lax.psum(x, axis) - x if bit is None else swap_bit(x, axis, n, bit)
            deps = yield (got,)
            x = x + after(got, deps)
    return x


def dot_nn(a, b):
    return jnp.dot(a, b, preferred_element_type=F4)


def dot_nt(a, b):
    return lax.dot_general(a, b, (((1,), (1,)), ((), ())), preferred_element_type=F4)


def dot_tn(a, b):
    return lax.dot_general(a, b, (((0,), (0,)), ((), ())), preferred_element_type=F4)


def mean_last(x):
    return jnp.mean(x, axis=-1, keepdims=True)


def centre(x):
    c = x - mean_last(x)
    return c, lax.rsqrt(mean_last(c * c) + EPSILON)


def group_matrix():
    i = lax.broadcasted_iota(jnp.int32, (TILE, TILE), 0) // HD
    j = lax.broadcasted_iota(jnp.int32, (TILE, TILE), 1) // HD
    return jnp.where(i == j, 1.0 / HD, 0.0).astype(BF)


def group_mean(x, matrix):
    high = x.astype(BF)
    low = (x - high.astype(F4)).astype(BF)
    return dot_nn(high, matrix) + dot_nn(low, matrix)


def head_norm(x, matrix):
    c = x - group_mean(x, matrix)
    return c, lax.rsqrt(group_mean(c * c, matrix) + EPSILON)


def low_mean(x, matrix):
    return dot_nn(x.astype(BF), matrix)


def head_norm_back(e, hat, rate, gain, matrix):
    t = e * gain
    hat, rate = hat.astype(F4), rate.astype(F4)
    d = rate * (t - low_mean(t, matrix) - hat * low_mean(t * hat, matrix))
    return d, e * hat


def fold_heads(x):
    return jnp.sum(x, axis=0, keepdims=True)


def padded(rows):
    return -(-rows // LANES) * LANES


def head_rows(columns):
    rows = columns.shape[0]
    pair = lax.broadcasted_iota(jnp.int32, (8, LANES), 0)
    at = lax.broadcasted_iota(jnp.int32, (8, LANES), 1)
    parts = []
    for s in (0, 1):
        sel = jnp.where(at == 2 * pair + s, 1.0, 0.0)
        parts.append(
            lax.dot_general(
                sel, columns, (((1,), (1,)), ((), ())),
                precision=lax.Precision.HIGHEST, preferred_element_type=F4,
            )
        )
    return parts, padded(rows)


def tiles(width):
    return width // TILE


def lane(i, width):
    return pl.ds(pl.multiple_of(i * width, width), width)


def call(body, outs, scratch, room, flops, *args):
    size = sum(a.size * a.dtype.itemsize for a in args)
    size += sum(math.prod(s) * jnp.dtype(d).itemsize for s, d in outs)
    hold = sum(math.prod(s.shape) * jnp.dtype(s.dtype).itemsize for s in scratch)
    return pl.pallas_call(
        body,
        out_shape=[jax.ShapeDtypeStruct(s, d) for s, d in outs],
        in_specs=[VM] * len(args),
        out_specs=[VM] * len(outs),
        scratch_shapes=scratch,
        compiler_params=pltpu.CompilerParams(vmem_limit_bytes=hold + (room << 20)),
        cost_estimate=pl.CostEstimate(
            flops=int(flops) * 4, bytes_accessed=int(size), transcendentals=0
        ),
    )(*args)


def pair_masks(rows):
    at = lax.broadcasted_iota(jnp.int32, (rows, LANES), 1)
    return (at < HD, at >= HD)


def pick(x, mask):
    return jnp.where(mask, x, jnp.zeros_like(x))


def write_rows(ref, columns):
    parts, step = head_rows(columns)
    ref[...] = jnp.zeros_like(ref)
    for s, x in enumerate(parts):
        ref[:, s * step : s * step + x.shape[1]] = x


def column(ref, h):
    at = lax.broadcasted_iota(jnp.int32, ref.shape, 1)
    return jnp.sum(jnp.where(at == h, ref[...], 0.0), axis=-1, keepdims=True)


def look_body(first, last, half, *refs):
    p, g1, b1, kg, ids, idk, a1o, a1x, a2o, a2x = refs[:10]
    idq = ids[: p.shape[0], :]
    refs = refs[10:]
    if first:
        qg, normed, k_hat, k_rate, k_low, v_low, out, total_out = refs[:8]
        q_hat, q_rate, q, bias, stat, k_raw, q_raw = refs[8:]
    else:
        q, acc, total_in, normed, k_hat, k_rate, k_low, v_low, out, total_out = refs[:10]
        bias, stat, k_raw = refs[10:]
    x = p[...].astype(F4)
    c, r = centre(x)
    n = (c * r * g1[...] + b1[...]).astype(BF)
    normed[...] = n
    head = 0 if first else half
    cut = a1o.shape[1]
    for s, (a1, a2) in enumerate(((a1o, a2o), (a1x, a2x))):
        at = s * half
        one = dot_nn(n, a1[:, head:])
        two = dot_nn(n, a2[...])
        if first:
            q_raw[:, at : at + half] = one[:, :half]
        k_raw[:, at : at + cut - half] = one[:, half - head :]
        k_raw[:, at + cut - half : at + half] = two[:, : 2 * half - cut]
        v_low[:, at : at + half] = two[:, 2 * half - cut :].astype(BF)
    matrix = group_matrix()
    for t in range(tiles(2 * half)):
        cols = slice(t * TILE, (t + 1) * TILE)
        c, r = head_norm(k_raw[:, cols], matrix)
        k_hat[:, cols] = (c * r).astype(BF)
        k_rate[:, cols] = r.astype(BF)
        k_low[:, cols] = (c * r * kg[...]).astype(BF)
        if first:
            c, r = head_norm(q_raw[:, cols], matrix)
            q_hat[:, cols] = (c * r).astype(BF)
            q_rate[:, cols] = r.astype(BF)
            q[:, cols] = (c * r * qg[...] * (float(HD) ** -0.5)).astype(BF)

    bias[...] = jnp.where(idq == idk[...], 0.0, -1e30)
    stat[...] = jnp.zeros_like(stat) if first else total_in[...]
    masks = pair_masks(p.shape[0])
    lanes = lax.broadcasted_iota(jnp.int32, stat.shape, 1)

    @pl.loop(0, 2 * half // LANES)
    def _(pair):
        cols = lane(pair, LANES)
        q_pair, k_pair, v_pair = q[:, cols], k_low[:, cols], v_low[:, cols]
        outs = []
        for s, mask in enumerate(masks):
            e = jnp.exp(dot_nt(pick(q_pair, mask), k_pair) + bias[...])
            total = jnp.sum(e, axis=-1, keepdims=True)
            got = dot_nn(e.astype(BF), v_pair)
            if not first:
                got = got + acc[:, cols]
            h = 2 * pair + s
            if last:
                total = total + column(stat, h)
                got = got * (1.0 / total)
                stat[...] = jnp.where(lanes == h, jnp.log(total), stat[...])
            else:
                stat[...] += jnp.where(lanes == h, total, 0.0)
            outs.append(got)
        out[:, cols] = jnp.where(masks[0], outs[0], outs[1]).astype(out.dtype)

    if last:
        write_rows(total_out, stat[...])
    else:
        total_out[...] = stat[...]


def look(first, last, p, g1, b1, qg, kg, idq, idk, parts, before):
    tokens, width = p.shape
    half = width // 2
    wide = (tokens, width)
    outs = [(wide, BF)] * 5
    outs += [(wide, BF if last else F4)]
    outs += [((8, 2 * padded(tokens)) if last else (tokens, LANES), F4)]
    if first:
        outs += [(wide, BF)] * 3
    flops = 2 * tokens * width * (width * (3 if first else 2) + 4 * tokens)
    body = functools.partial(look_body, first, last, half)
    scratch = [pltpu.VMEM((tokens, tokens), F4), pltpu.VMEM((tokens, LANES), F4)]
    scratch += [pltpu.VMEM(wide, F4)] * (2 if first else 1)
    extra = (qg,) if first else before
    return call(
        body, outs, scratch, 6, flops, p, g1, b1, kg, idq, idk, *parts, *extra
    )


ROOT = math.sqrt(2.0 / math.pi)
CUBE = 0.044715


def gelu_pair(u):
    square = u * u
    t = jnp.tanh(ROOT * u * (1.0 + CUBE * square))
    half = 0.5 * (1.0 + t)
    slope = half + 0.5 * u * (1.0 - t * t) * (ROOT * (1.0 + 3.0 * CUBE * square))
    return u * half, slope


def up_body(half, p, att, cot, g2, b2, b1o, b1x, b2o, b2x, *outs):
    mixed, n2, act, slope, g1o, g1x, g2o, g2x = outs
    first = b1o.shape[1]
    inner = first + b2o.shape[1] - half
    m = p[...].astype(F4)
    for s, part in enumerate((b2o, b2x)):
        m = m + dot_nt(att[:, s * half : (s + 1) * half], part[:, :half])
    mixed[...] = m
    c, r = centre(m)
    n2[...] = (c * r * g2[...] + b2[...]).astype(BF)
    for s, (one, two) in enumerate(((b1o, b2o), (b1x, b2x))):

        @pl.loop(0, tiles(first))
        def _(i):
            u = dot_nn(n2[...], one[:, lane(i, TILE)])
            to = pl.ds(pl.multiple_of(s * inner + i * TILE, TILE), TILE)
            a, d = gelu_pair(u)
            act[:, to] = a.astype(BF)
            slope[:, to] = d.astype(BF)

        rest = inner - first
        for i in range(tiles(rest)):
            u = dot_nn(n2[...], two[:, half + i * TILE : half + (i + 1) * TILE])
            to = slice(s * inner + first + i * TILE, s * inner + first + (i + 1) * TILE)
            a, d = gelu_pair(u)
            act[:, to] = a.astype(BF)
            slope[:, to] = d.astype(BF)
    mid = g1o.shape[1]
    for s, (one, two) in enumerate(((g1o, g2o), (g1x, g2x))):
        for base, out in ((s * inner, one), (s * inner + mid, two)):

            @pl.loop(0, tiles(mid))
            def _(i):
                frm = pl.ds(pl.multiple_of(base + i * TILE, TILE), TILE)
                out[:, lane(i, TILE)] = dot_tn(cot[...], act[:, frm]).astype(BF)


def slope_body(half, *refs):
    mixed, slope, att, cot, g2 = refs[:5]
    b1o, b1x, b2o, b2x, c1o, c1x, c2o, c2x = refs[5:13]
    d_up, d_mixed, d_att, delta, gains = refs[13:]
    first = b1o.shape[1]
    inner = first + b2o.shape[1] - half
    mid = c1o.shape[1]
    for s, (one, two) in enumerate(((c1o, c2o), (c1x, c2x))):
        at = s * inner
        for base, part in ((at, one), (at + mid, two)):

            @pl.loop(0, tiles(mid))
            def _(i):
                to = pl.ds(pl.multiple_of(base + i * TILE, TILE), TILE)
                d = dot_nn(cot[...], part[:, lane(i, TILE)])
                d_up[:, to] = (d * slope[:, to].astype(F4)).astype(BF)

    e = jnp.zeros(mixed.shape, F4)
    for s, (one, two) in enumerate(((b1o, b2o), (b1x, b2x))):
        at = s * inner
        e = e + dot_nt(d_up[:, at : at + first], one[...])
        e = e + dot_nt(d_up[:, at + first : at + inner], two[:, half:])
    c, r = centre(mixed[...])
    t = e * g2[...]
    d_mixed[...] = cot[...].astype(F4) + r * (
        t - mean_last(t) - c * (r * r) * mean_last(t * c)
    )
    gains[0:1, :] = jnp.sum(e * c * r, axis=0, keepdims=True)
    gains[1:2, :] = jnp.sum(e, axis=0, keepdims=True)
    d_branch = d_mixed[...].astype(BF)
    row = lax.broadcasted_iota(jnp.int32, (half, LANES), 0) // HD
    col = lax.broadcasted_iota(jnp.int32, (half, LANES), 1)
    sums = jnp.zeros((mixed.shape[0], LANES), F4)
    for s, part in enumerate((b2o, b2x)):
        cols = slice(s * half, (s + 1) * half)
        d = dot_nn(d_branch, part[:, :half]).astype(BF)
        d_att[:, cols] = d
        prod = d.astype(F4) * att[:, cols].astype(F4)
        high = prod.astype(BF)
        low = (prod - high.astype(F4)).astype(BF)
        sel = jnp.where(row + s * (half // HD) == col, 1.0, 0.0).astype(BF)
        sums = sums + dot_nn(high, sel) + dot_nn(low, sel)
    write_rows(delta, sums)


def inner_body(half, *refs):
    mixed, n2, act, att, d_up, d_mixed, c1o, c1x, c2o, c2x = refs[:10]
    result, h1o, h1x, h2o, h2x = refs[10:]
    first = h1o.shape[1]
    inner = first + h2o.shape[1] - half
    mid = c1o.shape[1]
    out = mixed[...]
    for s, (one, two) in enumerate(((c1o, c2o), (c1x, c2x))):
        at = s * inner
        out = out + dot_nt(act[:, at : at + mid], one[...])
        out = out + dot_nt(act[:, at + mid : at + inner], two[...])
    result[...] = out.astype(BF)
    d_branch = d_mixed[...].astype(BF)
    for s, (one, two) in enumerate(((h1o, h2o), (h1x, h2x))):
        at = s * inner
        two[:, :half] = dot_tn(d_branch, att[:, s * half : (s + 1) * half]).astype(BF)

        @pl.loop(0, tiles(first))
        def _(i):
            frm = pl.ds(pl.multiple_of(at + i * TILE, TILE), TILE)
            one[:, lane(i, TILE)] = dot_tn(n2[...], d_up[:, frm]).astype(BF)

        two[:, half:] = dot_tn(n2[...], d_up[:, at + first : at + inner]).astype(BF)


def back_body(half, j, *refs):
    q, k, v, d_att, stat, delta, idq, ids, k_hat, k_rate, kg = refs[:11]
    a1o, a1x, a2o, a2x = refs[11:15]
    dk_low, dv_low, dq, part, k_gain, bias, dk, q_cat, d_cat = refs[15:]
    tokens = q.shape[0]
    step = padded(tokens)
    bias[...] = jnp.where(ids[j * tokens : (j + 1) * tokens, :] == idq[...], 0.0, -1e30)
    q_cat[...] = jnp.zeros_like(q_cat)
    d_cat[...] = jnp.zeros_like(d_cat)
    masks = pair_masks(tokens)

    @pl.loop(0, q.shape[1] // LANES)
    def _(pair):
        cols = lane(pair, LANES)
        k_pair, v_pair = k[:, cols], v[:, cols]
        for s, mask in enumerate(masks):
            q_cat[s * step : s * step + tokens, :] = pick(q[:, cols], mask)
            d_cat[s * step : s * step + tokens, :] = pick(d_att[:, cols], mask)
        row = pl.ds(pair, 1)
        prob = jnp.exp(dot_nt(k_pair, q_cat[...]) + bias[...] - stat[row, :])
        d_prob = dot_nt(v_pair, d_cat[...])
        d_score = (prob * (d_prob - delta[row, :])).astype(BF)
        dv_low[:, cols] = dot_nn(prob.astype(BF), d_cat[...]).astype(BF)
        dk[:, cols] = dot_nn(d_score, q_cat[...])
        both = dot_tn(d_score, k_pair)
        dq[:, cols] = jnp.where(masks[0], both[:tokens], both[step : step + tokens])

    matrix = group_matrix()
    total = jnp.zeros((1, TILE), F4)
    for t in range(tiles(2 * half)):
        cols = slice(t * TILE, (t + 1) * TILE)
        d, g = head_norm_back(
            dk[:, cols], k_hat[:, cols], k_rate[:, cols], kg[...], matrix
        )
        dk_low[:, cols] = d.astype(BF)
        total = total + fold_heads(g)
    k_gain[...] = total
    cut = a1o.shape[1]
    e = jnp.zeros((tokens, 2 * half), F4)
    for s, (one, two) in enumerate(((a1o, a2o), (a1x, a2x))):
        at = s * half
        mid = at + cut - half
        e = e + dot_nt(dk_low[:, at:mid], one[:, half:])
        e = e + dot_nt(dk_low[:, mid : at + half], two[:, : 2 * half - cut])
        e = e + dot_nt(dv_low[:, at : at + half], two[:, 2 * half - cut :])
    part[...] = e.astype(part.dtype)


def back_block(j, q, k, v, d_att, stat, delta, idq, ids, k_hat, k_rate, kg, parts):
    tokens, width = q.shape
    wide, step = (tokens, width), padded(tokens)
    outs = [(wide, BF), (wide, BF), (wide, F4), (wide, F4 if j == 0 else BF)]
    outs += [((1, TILE), F4)]
    scratch = [pltpu.VMEM((tokens, 2 * step), F4), pltpu.VMEM(wide, F4)]
    scratch += [pltpu.VMEM((2 * step, LANES), BF)] * 2
    flops = 10 * tokens * tokens * width * 4 + 4 * tokens * width * width
    body = functools.partial(back_body, width // 2, j)
    return call(
        body, outs, scratch, 10, flops,
        q, k, v, d_att, stat, delta, idq, ids, k_hat, k_rate, kg, *parts,
    )


def weight_body(n, half, *refs):
    q_hat, q_rate, qg, own = refs[:4]
    a1o, a1x = refs[4:6]
    dqs, ns = refs[6 : 6 + n], refs[6 + n : 6 + 2 * n]
    dks, dvs = refs[6 + 2 * n : 6 + 3 * n], refs[6 + 3 * n : 6 + 4 * n]
    part, q_gain, g1o, g1x, g2o, g2x, dq_low, n_all, dk_all, dv_all = refs[6 + 4 * n :]
    tokens = q_hat.shape[0]
    matrix = group_matrix()
    total = jnp.zeros((1, TILE), F4)
    factor = float(HD) ** -0.5
    for t in range(tiles(2 * half)):
        cols = slice(t * TILE, (t + 1) * TILE)
        e = dqs[0][:, cols]
        for other in dqs[1:]:
            e = e + other[:, cols]
        d, g = head_norm_back(
            e * factor, q_hat[:, cols], q_rate[:, cols], qg[...], matrix
        )
        dq_low[:, cols] = d.astype(BF)
        total = total + fold_heads(g)
    q_gain[...] = total
    e = dot_nt(dq_low[:, :half], a1o[:, :half]) + dot_nt(dq_low[:, half:], a1x[:, :half])
    part[...] = own[...] + e
    for b in range(n):
        rows = slice(b * tokens, (b + 1) * tokens)
        n_all[rows, :] = ns[b][...]
        dk_all[rows, :] = dks[b][...]
        dv_all[rows, :] = dvs[b][...]
    cut = g1o.shape[1]
    for s, (one, two) in enumerate(((g1o, g2o), (g1x, g2x))):
        at = s * half
        mid = at + cut - half
        one[:, :half] = dot_tn(ns[0][...], dq_low[:, at : at + half]).astype(BF)
        one[:, half:] = dot_tn(n_all[...], dk_all[:, at:mid]).astype(BF)
        two[:, : 2 * half - cut] = dot_tn(n_all[...], dk_all[:, mid : at + half]).astype(BF)
        two[:, 2 * half - cut :] = dot_tn(n_all[...], dv_all[:, at : at + half]).astype(BF)


def input_body(own, rest, p, g1, d_mixed, second, query, *refs):
    keys, (out, small) = refs[:-2], refs[-2:]
    e = own[...] + rest[...].astype(F4)
    c, r = centre(p[...].astype(F4))
    hat = c * r
    t = e * g1[...]
    out[...] = d_mixed[...] + r * (t - mean_last(t) - hat * mean_last(t * hat))
    small[...] = jnp.zeros_like(small)
    small[0:1, :] = jnp.sum(e * hat, axis=0, keepdims=True)
    small[1:2, :] = jnp.sum(e, axis=0, keepdims=True)
    small[2:4, :] = second[...]
    small[4:5, :TILE] = query[...]
    total = keys[0][...]
    for x in keys[1:]:
        total = total + x[...]
    small[5:6, :TILE] = total


def take_micro(x, c):
    mine = jnp.where(c0, x[0], x[1])
    other = jnp.where(c0, x[1], x[0])
    return mine, other


def per_device(
    patches,
    picture_ids,
    ln1_gain,
    ln1_bias,
    w_query,
    w_key,
    w_value,
    q_gain,
    k_gain,
    w_out,
    ln2_gain,
    ln2_bias,
    w_up,
    w_down,
    cotangent,
):
    n = lax.axis_size("row")
    at = Place()
    c0 = at("c")
    width = patches.shape[-1]
    half = w_query.shape[1]
    piece = patches.shape[2]
    tokens = 2 * piece
    inner = w_up.shape[1]

    cut_a = half + half * 2 // 3
    first = inner * 2 // 3
    mid = inner // 2
    width_b = inner + half
    whole = not regular(w_query.shape[0])
    chunk_a = jnp.concatenate([w_query, w_key, w_value], axis=1)
    chunk_b = jnp.concatenate([w_up[:, :first], w_out.T, w_up[:, first:]], axis=1)
    line_a = Chain(line_steps(chunk_a, at, True))
    line_b = Chain(line_steps(chunk_b, at))

    def back_home(x):
        lower, upper = x[:piece], x[piece:]
        keep = jnp.where(c0, lower, upper)
        got = swap_core(jnp.where(c0, upper, lower))
        whole = jnp.stack([jnp.where(c0, keep, got), jnp.where(c0, got, keep)])
        return whole[None], got

    def take(x):
        mine = jnp.where(c0, x[0], x[1])
        got = swap_core(jnp.where(c0, x[1], x[0]))
        return jnp.concatenate(
            [jnp.where(c0, mine, got), jnp.where(c0, got, mine)], axis=0
        )

    g1, b1 = ln1_gain[None], ln1_bias[None]
    g2, b2 = ln2_gain[None], ln2_bias[None]
    qg, kg = jnp.tile(q_gain, TILE // HD)[None], jnp.tile(k_gain, TILE // HD)[None]
    ids = jnp.where(c0, picture_ids[0, 0], picture_ids[0, 1]).reshape(n, tokens)
    id_blocks = [index(ids, at("row", j), keepdims=True) for j in range(n)]
    ids = jnp.concatenate(id_blocks, axis=1).reshape(n * tokens, 1)
    spare = jnp.full((1, padded(tokens) - tokens), -1, jnp.int32)
    idq = jnp.concatenate([id_blocks[0], spare] * 2, axis=1)
    ready = lax.optimization_barrier((g1, b1, g2, b2, qg, kg, ids, idq, *id_blocks))
    g1, b1, g2, b2, qg, kg, ids, idq, *id_blocks = ready

    line_a.step()
    p_own = take(patches[0])
    blocks = [p_own, hop(p_own, n)]
    got_a = line_a.last
    rows_a = line_a.step(*ready).finish()
    chain_a = Chain(plane_steps((rows_a[:, :cut_a], rows_a[:, cut_a:]), whole, at))
    chain_a.step()
    line_b.step(*got_a)
    chain_a.step()
    for _ in range(n - 2):
        line_b.step()
    got_b = line_b.last
    rows_b = line_b.finish()
    a_one, a_two = chain_a.finish()
    a_parts = a_one + a_two
    cot = take(cotangent[0])
    line_c = Chain(line_steps(after(w_down.T, got_b), at)).step()
    chain_b = Chain(plane_steps((rows_b[:, :first], rows_b[:, first:]), whole, at))

    made, marks = [], []
    before = token = ()
    deps = got_b
    for j in range(n):
        if 0 < j < n - 1:
            blocks.append(hop(after(blocks[j], marks[j - 2] if j > 1 else got_b), n))
        if j in (0, 1, n - 1):
            chain_b.step(*token)
        if 0 < j < n - 1:
            line_c.step(*token)
        if j == n - 1:
            rows_c = line_c.finish()
            chain_c = Chain(plane_steps((rows_c[:, :mid], rows_c[:, mid:]), whole, at))
            chain_c.step()
        made.append(
            look(
                j == 0, j == n - 1, after(blocks[j], deps), g1, b1, qg, kg, ids,
                id_blocks[j], a_parts, before,
            )
        )
        if j == 0:
            q_hat, q_rate, q_low = made[0][7:]
        before = (q_low, *made[j][5:7])
        token = (made[j][6],)
        marks.append(token)
        deps = token + (chain_c.last if j == n - 1 else line_c.last)
        if j != 1 or n < 4:
            deps = deps + chain_b.last
    normed = [m[0] for m in made]
    k_hat, k_rate, k_low, v_low = [[m[i] for m in made] for i in (1, 2, 3, 4)]
    att, stat = made[-1][5:7]

    b_one, b_two = chain_b.finish()
    b_parts = b_one + b_two
    chain_c.step(*token)
    mixed, n2, act, slope, *gc = call(
        functools.partial(up_body, half),
        [((tokens, width), F4), ((tokens, width), BF)]
        + [((tokens, 2 * inner), BF)] * 2
        + [((width, mid), BF)] * 4,
        [], 7,
        2 * tokens * width * (width + 4 * inner),
        p_own, after(att, deps), cot, g2, b2, *b_parts,
    )
    c_one, c_two = chain_c.finish()
    c_parts = c_one + c_two

    back_c = Chain(plane_sums((gc[0], gc[1]), (gc[2], gc[3]), whole, at)).step()
    deps = back_c.last
    back_c.step()
    d_up, d_mixed, d_att, delta, gains2 = call(
        functools.partial(slope_body, half),
        [((tokens, 2 * inner), BF), ((tokens, width), F4), ((tokens, width), BF)]
        + [((8, 2 * padded(tokens)), F4), ((2, width), F4)],
        [], 11,
        2 * tokens * width * (width + 4 * inner),
        after(mixed, deps), slope, att, cot, g2, *b_parts, *c_parts,
    )
    result, *gb = call(
        functools.partial(inner_body, half),
        [((tokens, width), BF)]
        + [((width, first), BF)] * 2
        + [((width, half + inner - first), BF)] * 2,
        [], 10,
        2 * tokens * width * (width + 4 * inner),
        mixed, n2, act, att, d_up, d_mixed, *c_parts,
    )
    back_c.step(result)
    result, got = back_home(result)
    back_b = Chain(plane_sums((gb[0], gb[1]), (gb[2], gb[3]), whole, at)).step()
    deps = (d_mixed,)

    back = [None] * n
    acc = None
    order = [*range(1, n), 0]
    for turn, j in enumerate(order):
        back[j] = back_block(
            j, q_low, k_low[j], v_low[j], after(d_att, deps), stat, delta, idq, ids,
            k_hat[j], k_rate[j], kg, a_parts,
        )
        token = back[j][4]
        deps = (token, *back_b.last, *back_c.last, got)
        back_b.step(token)
        back_c.step(token)
        if j:
            part = back[j][3]
            if acc is None:
                acc = part
            else:
                deps = deps + (acc,)
                acc = add_low(part, acc)
            acc = hop(acc, n)
    deps = deps + (acc,)
    sum_b, sum_c = back_b.finish(), back_c.finish()
    line = Chain(line_sums(jnp.concatenate([sum_b, sum_c], axis=1), whole, at)).step()
    part, dq_gain, *ga = call(
        functools.partial(weight_body, n, half),
        [((tokens, width), F4), ((1, TILE), F4)]
        + [((width, cut_a), BF)] * 2
        + [((width, 3 * half - cut_a), BF)] * 2,
        [pltpu.VMEM((tokens, width), BF)] + [pltpu.VMEM((n * tokens, width), BF)] * 3,
        12,
        2 * tokens * width * width * (2 + 2 * n),
        after(q_hat, deps), q_rate, qg, back[0][3], *a_one,
        *[b[2] for b in back], *normed, *[b[0] for b in back], *[b[1] for b in back],
    )
    back_a = Chain(plane_sums((ga[0], ga[1]), (ga[2], ga[3]), whole, at))
    back_a.step(*line.last)
    grad_in, small = call(
        input_body, [((tokens, width), F4), ((8, width), F4)], [], 6, 0,
        part, acc, p_own, g1, d_mixed, gains2, dq_gain, *[b[4] for b in back],
    )
    sums = Chain(sum_steps(small)).step()
    while back_a.value is None:
        deps = back_a.last
        back_a.step(*deps)
        line.step(*deps)
        sums.step(*deps)
    last_a = Chain(line_sums(back_a.value, whole, at, True)).step()
    sums.step(*last_a.last)
    last_a.finish()
    sums.finish()
    grad_a, grad_bc = last_a.value, line.finish()
    grad_b, grad_c = grad_bc[:, :width_b], grad_bc[:, width_b:]
    small = sums.value
    grad_g1, grad_b1, grad_g2, grad_b2 = small[0], small[1], small[2], small[3]
    grad_gq = small[4, :TILE].reshape(-1, HD).sum(axis=0)
    grad_gk = small[5, :TILE].reshape(-1, HD).sum(axis=0)

    rest = half + first
    grad_wu = jnp.concatenate([grad_b[:, :first], grad_b[:, rest:]], axis=1)
    return (
        result,
        back_home(grad_in)[0],
        grad_g1,
        grad_b1,
        grad_a[:, :half],
        grad_a[:, half : 2 * half],
        grad_a[:, 2 * half :],
        grad_gq,
        grad_gk,
        grad_b[:, first:rest].T,
        grad_g2,
        grad_b2,
        grad_wu,
        grad_c.T,
    )


def solution(mesh):
    rows = P("dp", None, ("row", "col"), None)
    inward = P(("dp", "row"), "col")
    outward = P("col", ("dp", "row"))
    return jax.shard_map(
        per_device,
        mesh=mesh,
        in_specs=(
            rows, P("dp", None, None), P(), P(), inward, inward, inward, P(), P(),
            outward, P(), P(), inward, outward, rows,
        ),
        out_specs=(
            rows, rows, P(), P(), inward, inward, inward, P(), P(),
            outward, P(), P(), inward, outward,
        ),
        check_vma=False,
    )
```

```python
import functools
import math

import jax
import jax.numpy as jnp
from jax import lax
from jax.experimental import pallas as pl
from jax.experimental.pallas import tpu as pltpu
from jax.sharding import PartitionSpec as P

HD = 64
LANES = 128
TILE = 256
EPSILON = 1e-06
BF = jnp.bfloat16
F4 = jnp.float32
VM = pl.BlockSpec(memory_space=pltpu.VMEM)


def ring_order(n):
    return list(range(0, n, 2)) + list(range(n - 1 - (n % 2), 0, -2))


def ring_place(r, n):
    return jnp.where(r % 2 == 0, r // 2, n - 1 - r // 2 - (n % 2) + (n % 2) * 1)


def ring_row(q, n):
    return jnp.where(2 * q < n, 2 * q, 2 * (n - 1 - q) + 1)


class Place:
    def __init__(self):
        n, m = lax.axis_size("row"), lax.axis_size("dp")
        place = ring_place(lax.axis_index("row"), n)
        me = lax.axis_index("dp")
        made = {("c",): lax.axis_index("col") == 0}
        for bit in range(m.bit_length() - 1):
            one = (me >> bit) & 1
            made["low", bit] = one == 0
            made["one", bit] = one
            made["zero", bit] = 1 - one
        for r in range(n):
            slot = (place - ring_order(n).index(r) + n) % n
            for k in range(n - 1):
                made["slot", r, k] = slot == k
        for r in range(n):
            for k in range(n - 1):
                made["far", r, k] = lax.axis_index("row") == r ^ k
        for k in range(n):
            made["pair", k] = lax.axis_index("row") ^ k
        for step in range(n):
            made["row", step] = ring_row((place - step + n) % n, n)
        names = list(made)
        self.made = dict(zip(names, lax.optimization_barrier(tuple(made.values()))))

    def __call__(self, *name):
        return self.made[name]


def index(x, i, axis=0, keepdims=False):
    return lax.dynamic_index_in_dim(
        x, i, axis, keepdims=keepdims, allow_negative_indices=False
    )


def hop(x, n):
    order = ring_order(n)
    pairs = [(order[i], order[(i + 1) % n]) for i in range(n)]
    return lax.ppermute(x, "row", pairs)


def swap_bit(x, axis, n, bit):
    return lax.ppermute(x, axis, [(i, i ^ (1 << bit)) for i in range(n)])


def swap_core(x):
    return lax.ppermute(x, "col", [(0, 1), (1, 0)])


def bit_orders(n):
    bits = list(range(n.bit_length() - 1))
    half = len(bits) // 2
    return bits, bits[half:] + bits[:half]


def regular(block):
    dp = lax.axis_size("dp")
    return dp & (dp - 1) == 0 and block % 16 == 0


def after(x, deps):
    if not deps:
        return x
    return lax.optimization_barrier((x, *deps))[0]


def all_after(xs, deps):
    if not deps:
        return tuple(xs)
    return lax.optimization_barrier((*xs, *deps))[: len(xs)]


class Chain:
    def __init__(self, steps):
        self.steps = steps
        self.last = ()
        self.value = None
        next(steps)

    def step(self, *deps):
        if self.value is None:
            try:
                self.last = self.steps.send(deps)
            except StopIteration as end:
                self.value = end.value
        return self

    def finish(self):
        while self.value is None:
            self.step()
        return self.value


def join_line(blocks, at, kind="slot"):
    n = len(blocks)
    parts = []
    for r in range(n):
        x = blocks[-1]
        for k in range(n - 1):
            x = jnp.where(at(kind, r, k), blocks[k], x)
        parts.append(x)
    return jnp.concatenate(parts, axis=0)


def straight(n):
    return n & (n - 1) == 0 and n <= 4


def line_steps(shard, at, at_once=False):
    deps = yield ()
    shard = after(shard, deps)
    if not regular(shard.shape[0]):
        return shard
    n = lax.axis_size("row")
    blocks = [shard]
    if at_once and straight(n):
        for k in range(1, n):
            pairs = [(i, i ^ k) for i in range(n)]
            blocks.append(lax.ppermute(shard, "row", pairs))
        deps = yield tuple(blocks[1:])
        blocks[1:] = all_after(blocks[1:], deps)
        return join_line(blocks, at, "far")
    for _ in range(n - 1):
        got = hop(blocks[-1], n)
        deps = yield (got,)
        blocks.append(after(got, deps))
    return join_line(blocks, at)


def plane_steps(parts, whole, at):
    deps = yield ()
    m = lax.axis_size("dp")
    parts = list(parts)
    if whole:
        both = lax.all_gather(
            jnp.concatenate(parts, axis=1), ("dp", "row"), axis=0, tiled=True
        )
        deps = yield (both,)
        both, cut = after(both, deps), parts[0].shape[1]
        parts = [both[:, :cut], both[:, cut:]]
    else:
        done = ([], [])
        for bits in zip(*bit_orders(m)):
            got = [swap_bit(x, "dp", m, bit) for x, bit in zip(parts, bits)]
            deps = yield tuple(got)
            got = all_after(got, deps)
            for i, bit in enumerate(bits):
                axis = sum(1 for b in done[i] if b > bit)
                low = at("low", bit)
                first = jnp.where(low, parts[i], got[i])
                second = jnp.where(low, got[i], parts[i])
                parts[i] = jnp.stack([first, second], axis=axis)
                done[i].append(bit)
        parts = [x.reshape(-1, x.shape[-1]) for x in parts]
    got = [swap_core(x) for x in parts]
    yield tuple(got)
    return (parts[0], got[0]), (parts[1], got[1])


def add_low(a, b):
    return (a.astype(F4) + b.astype(F4)).astype(BF)


def plane_sums(one, two, whole, at):
    m = lax.axis_size("dp")
    deps = yield ()
    got = [swap_core(x) for x in all_after((one[1], two[1]), deps)]
    deps = yield tuple(got)
    parts = [add_low(x[0], y) for x, y in zip((one, two), all_after(got, deps))]
    if whole:
        return jnp.concatenate(parts, axis=1)
    count = m.bit_length() - 1
    left = [list(range(count - 1, -1, -1)), list(range(count - 1, -1, -1))]
    parts = [x.reshape((2,) * count + (-1, x.shape[-1])) for x in parts]
    for bits in zip(*bit_orders(m)):
        got, keep = [], []
        for i, bit in enumerate(bits):
            axis = left[i].index(bit)
            got.append(swap_bit(index(parts[i], at("zero", bit), axis), "dp", m, bit))
            keep.append(index(parts[i], at("one", bit), axis))
            left[i].remove(bit)
        deps = yield tuple(got)
        parts = [add_low(x, y) for x, y in zip(keep, all_after(got, deps))]
    return jnp.concatenate(parts, axis=1)


def line_sums(both, whole, at, at_once=False):
    deps = yield ()
    both = after(both, deps)
    if whole:
        total = lax.psum_scatter(both, ("dp", "row"), scatter_dimension=0, tiled=True)
        yield (total,)
        return total.astype(F4)
    n = lax.axis_size("row")
    both = both.reshape(n, -1, both.shape[-1])
    if at_once and straight(n):
        got = [
            lax.ppermute(index(both, at("pair", k)), "row", [(i, i ^ k) for i in range(n)])
            for k in range(1, n)
        ]
        deps = yield tuple(got)
        total = index(both, at("pair", 0)).astype(F4)
        for x in all_after(got, deps):
            total = total + x.astype(F4)
        return total
    acc = index(both, at("row", 1))
    for step in range(n - 1):
        got = hop(acc, n)
        deps = yield (got,)
        got = after(got, deps)
        if step < n - 2:
            acc = add_low(index(both, at("row", step + 2)), got)
    return index(both, at("row", 0)).astype(F4) + got.astype(F4)


def sum_steps(x):
    deps = yield ()
    got = swap_core(after(x, deps))
    deps = yield (got,)
    x = x + after(got, deps)
    for axis in ("dp", "row"):
        n = lax.axis_size(axis)
        for bit in range(n.bit_length() - 1) if n & (n - 1) == 0 else (None,):
            got = lax.psum(x, axis) - x if bit is None else swap_bit(x, axis, n, bit)
            deps = yield (got,)
            x = x + after(got, deps)
    return x


def dot_nn(a, b):
    return jnp.dot(a, b, preferred_element_type=F4)


def dot_nt(a, b):
    return lax.dot_general(a, b, (((1,), (1,)), ((), ())), preferred_element_type=F4)


def dot_tn(a, b):
    return lax.dot_general(a, b, (((0,), (0,)), ((), ())), preferred_element_type=F4)


def mean_last(x):
    return jnp.mean(x, axis=-1, keepdims=True)


def centre(x):
    c = x - mean_last(x)
    return c, lax.rsqrt(mean_last(c * c) + EPSILON)


def group_matrix():
    i = lax.broadcasted_iota(jnp.int32, (TILE, TILE), 0) // HD
    j = lax.broadcasted_iota(jnp.int32, (TILE, TILE), 1) // HD
    return jnp.where(i == j, 1.0 / HD, 0.0).astype(BF)


def group_mean(x, matrix):
    high = x.astype(BF)
    low = (x - high.astype(F4)).astype(BF)
    return dot_nn(high, matrix) + dot_nn(low, matrix)


def head_norm(x, matrix):
    c = x - group_mean(x, matrix)
    return c, lax.rsqrt(group_mean(c * c, matrix) + EPSILON)


def low_mean(x, matrix):
    return dot_nn(x.astype(BF), matrix)


def head_norm_back(e, hat, rate, gain, matrix):
    t = e * gain
    hat, rate = hat.astype(F4), rate.astype(F4)
    d = rate * (t - low_mean(t, matrix) - hat * low_mean(t * hat, matrix))
    return d, e * hat


def fold_heads(x):
    return jnp.sum(x, axis=0, keepdims=True)


def padded(rows):
    return -(-rows // LANES) * LANES


def head_rows(columns):
    rows = columns.shape[0]
    pair = lax.broadcasted_iota(jnp.int32, (8, LANES), 0)
    at = lax.broadcasted_iota(jnp.int32, (8, LANES), 1)
    parts = []
    for s in (0, 1):
        sel = jnp.where(at == 2 * pair + s, 1.0, 0.0)
        parts.append(
            lax.dot_general(
                sel, columns, (((1,), (1,)), ((), ())),
                precision=lax.Precision.HIGHEST, preferred_element_type=F4,
            )
        )
    return parts, padded(rows)


def tiles(width):
    return width // TILE


def lane(i, width):
    return pl.ds(pl.multiple_of(i * width, width), width)


def call(body, outs, scratch, room, flops, *args):
    size = sum(a.size * a.dtype.itemsize for a in args)
    size += sum(math.prod(s) * jnp.dtype(d).itemsize for s, d in outs)
    hold = sum(math.prod(s.shape) * jnp.dtype(s.dtype).itemsize for s in scratch)
    return pl.pallas_call(
        body,
        out_shape=[jax.ShapeDtypeStruct(s, d) for s, d in outs],
        in_specs=[VM] * len(args),
        out_specs=[VM] * len(outs),
        scratch_shapes=scratch,
        compiler_params=pltpu.CompilerParams(vmem_limit_bytes=hold + (room << 20)),
        cost_estimate=pl.CostEstimate(
            flops=int(flops) * 4, bytes_accessed=int(size), transcendentals=0
        ),
    )(*args)


def pair_masks(rows):
    at = lax.broadcasted_iota(jnp.int32, (rows, LANES), 1)
    return (at < HD, at >= HD)


def pick(x, mask):
    return jnp.where(mask, x, jnp.zeros_like(x))


def write_rows(ref, columns):
    parts, step = head_rows(columns)
    ref[...] = jnp.zeros_like(ref)
    for s, x in enumerate(parts):
        ref[:, s * step : s * step + x.shape[1]] = x


def column(ref, h):
    at = lax.broadcasted_iota(jnp.int32, ref.shape, 1)
    return jnp.sum(jnp.where(at == h, ref[...], 0.0), axis=-1, keepdims=True)


def look_body(first, last, half, *refs):
    p, g1, b1, kg, ids, idk, a1o, a1x, a2o, a2x = refs[:10]
    idq = ids[: p.shape[0], :]
    refs = refs[10:]
    if first:
        qg, normed, k_hat, k_rate, k_low, v_low, out, total_out = refs[:8]
        q_hat, q_rate, q, bias, stat, k_raw, q_raw = refs[8:]
    else:
        q, acc, total_in, normed, k_hat, k_rate, k_low, v_low, out, total_out = refs[:10]
        bias, stat, k_raw = refs[10:]
    x = p[...].astype(F4)
    c, r = centre(x)
    n = (c * r * g1[...] + b1[...]).astype(BF)
    normed[...] = n
    head = 0 if first else half
    cut = a1o.shape[1]
    for s, (a1, a2) in enumerate(((a1o, a2o), (a1x, a2x))):
        at = s * half
        one = dot_nn(n, a1[:, head:])
        two = dot_nn(n, a2[...])
        if first:
            q_raw[:, at : at + half] = one[:, :half]
        k_raw[:, at : at + cut - half] = one[:, half - head :]
        k_raw[:, at + cut - half : at + half] = two[:, : 2 * half - cut]
        v_low[:, at : at + half] = two[:, 2 * half - cut :].astype(BF)
    matrix = group_matrix()
    for t in range(tiles(2 * half)):
        cols = slice(t * TILE, (t + 1) * TILE)
        c, r = head_norm(k_raw[:, cols], matrix)
        k_hat[:, cols] = (c * r).astype(BF)
        k_rate[:, cols] = r.astype(BF)
        k_low[:, cols] = (c * r * kg[...]).astype(BF)
        if first:
            c, r = head_norm(q_raw[:, cols], matrix)
            q_hat[:, cols] = (c * r).astype(BF)
            q_rate[:, cols] = r.astype(BF)
            q[:, cols] = (c * r * qg[...] * (float(HD) ** -0.5)).astype(BF)

    bias[...] = jnp.where(idq == idk[...], 0.0, -1e30)
    stat[...] = jnp.zeros_like(stat) if first else total_in[...]
    masks = pair_masks(p.shape[0])
    lanes = lax.broadcasted_iota(jnp.int32, stat.shape, 1)

    @pl.loop(0, 2 * half // LANES)
    def _(pair):
        cols = lane(pair, LANES)
        q_pair, k_pair, v_pair = q[:, cols], k_low[:, cols], v_low[:, cols]
        outs = []
        for s, mask in enumerate(masks):
            e = jnp.exp(dot_nt(pick(q_pair, mask), k_pair) + bias[...])
            total = jnp.sum(e, axis=-1, keepdims=True)
            got = dot_nn(e.astype(BF), v_pair)
            if not first:
                got = got + acc[:, cols]
            h = 2 * pair + s
            if last:
                total = total + column(stat, h)
                got = got * (1.0 / total)
                stat[...] = jnp.where(lanes == h, jnp.log(total), stat[...])
            else:
                stat[...] += jnp.where(lanes == h, total, 0.0)
            outs.append(got)
        out[:, cols] = jnp.where(masks[0], outs[0], outs[1]).astype(out.dtype)

    if last:
        write_rows(total_out, stat[...])
    else:
        total_out[...] = stat[...]


def look(first, last, p, g1, b1, qg, kg, idq, idk, parts, before):
    tokens, width = p.shape
    half = width // 2
    wide = (tokens, width)
    outs = [(wide, BF)] * 5
    outs += [(wide, BF if last else F4)]
    outs += [((8, 2 * padded(tokens)) if last else (tokens, LANES), F4)]
    if first:
        outs += [(wide, BF)] * 3
    flops = 2 * tokens * width * (width * (3 if first else 2) + 4 * tokens)
    body = functools.partial(look_body, first, last, half)
    scratch = [pltpu.VMEM((tokens, tokens), F4), pltpu.VMEM((tokens, LANES), F4)]
    scratch += [pltpu.VMEM(wide, F4)] * (2 if first else 1)
    extra = (qg,) if first else before
    return call(
        body, outs, scratch, 6, flops, p, g1, b1, kg, idq, idk, *parts, *extra
    )


ROOT = math.sqrt(2.0 / math.pi)
CUBE = 0.044715


def gelu_pair(u):
    square = u * u
    t = jnp.tanh(ROOT * u * (1.0 + CUBE * square))
    half = 0.5 * (1.0 + t)
    slope = half + 0.5 * u * (1.0 - t * t) * (ROOT * (1.0 + 3.0 * CUBE * square))
    return u * half, slope


def up_body(half, p, att, cot, g2, b2, b1o, b1x, b2o, b2x, *outs):
    mixed, n2, act, slope, g1o, g1x, g2o, g2x = outs
    first = b1o.shape[1]
    inner = first + b2o.shape[1] - half
    m = p[...].astype(F4)
    for s, part in enumerate((b2o, b2x)):
        m = m + dot_nt(att[:, s * half : (s + 1) * half], part[:, :half])
    mixed[...] = m
    c, r = centre(m)
    n2[...] = (c * r * g2[...] + b2[...]).astype(BF)
    for s, (one, two) in enumerate(((b1o, b2o), (b1x, b2x))):

        @pl.loop(0, tiles(first))
        def _(i):
            u = dot_nn(n2[...], one[:, lane(i, TILE)])
            to = pl.ds(pl.multiple_of(s * inner + i * TILE, TILE), TILE)
            a, d = gelu_pair(u)
            act[:, to] = a.astype(BF)
            slope[:, to] = d.astype(BF)

        rest = inner - first
        for i in range(tiles(rest)):
            u = dot_nn(n2[...], two[:, half + i * TILE : half + (i + 1) * TILE])
            to = slice(s * inner + first + i * TILE, s * inner + first + (i + 1) * TILE)
            a, d = gelu_pair(u)
            act[:, to] = a.astype(BF)
            slope[:, to] = d.astype(BF)
    mid = g1o.shape[1]
    for s, (one, two) in enumerate(((g1o, g2o), (g1x, g2x))):
        for base, out in ((s * inner, one), (s * inner + mid, two)):

            @pl.loop(0, tiles(mid))
            def _(i):
                frm = pl.ds(pl.multiple_of(base + i * TILE, TILE), TILE)
                out[:, lane(i, TILE)] = dot_tn(cot[...], act[:, frm]).astype(BF)


def slope_body(half, *refs):
    mixed, slope, att, cot, g2 = refs[:5]
    b1o, b1x, b2o, b2x, c1o, c1x, c2o, c2x = refs[5:13]
    d_up, d_mixed, d_att, delta, gains = refs[13:]
    first = b1o.shape[1]
    inner = first + b2o.shape[1] - half
    mid = c1o.shape[1]
    for s, (one, two) in enumerate(((c1o, c2o), (c1x, c2x))):
        at = s * inner
        for base, part in ((at, one), (at + mid, two)):

            @pl.loop(0, tiles(mid))
            def _(i):
                to = pl.ds(pl.multiple_of(base + i * TILE, TILE), TILE)
                d = dot_nn(cot[...], part[:, lane(i, TILE)])
                d_up[:, to] = (d * slope[:, to].astype(F4)).astype(BF)

    e = jnp.zeros(mixed.shape, F4)
    for s, (one, two) in enumerate(((b1o, b2o), (b1x, b2x))):
        at = s * inner
        e = e + dot_nt(d_up[:, at : at + first], one[...])
        e = e + dot_nt(d_up[:, at + first : at + inner], two[:, half:])
    c, r = centre(mixed[...])
    t = e * g2[...]
    d_mixed[...] = cot[...].astype(F4) + r * (
        t - mean_last(t) - c * (r * r) * mean_last(t * c)
    )
    gains[0:1, :] = jnp.sum(e * c * r, axis=0, keepdims=True)
    gains[1:2, :] = jnp.sum(e, axis=0, keepdims=True)
    d_branch = d_mixed[...].astype(BF)
    row = lax.broadcasted_iota(jnp.int32, (half, LANES), 0) // HD
    col = lax.broadcasted_iota(jnp.int32, (half, LANES), 1)
    sums = jnp.zeros((mixed.shape[0], LANES), F4)
    for s, part in enumerate((b2o, b2x)):
        cols = slice(s * half, (s + 1) * half)
        d = dot_nn(d_branch, part[:, :half]).astype(BF)
        d_att[:, cols] = d
        prod = d.astype(F4) * att[:, cols].astype(F4)
        high = prod.astype(BF)
        low = (prod - high.astype(F4)).astype(BF)
        sel = jnp.where(row + s * (half // HD) == col, 1.0, 0.0).astype(BF)
        sums = sums + dot_nn(high, sel) + dot_nn(low, sel)
    write_rows(delta, sums)


def inner_body(half, *refs):
    mixed, n2, act, att, d_up, d_mixed, c1o, c1x, c2o, c2x = refs[:10]
    result, h1o, h1x, h2o, h2x = refs[10:]
    first = h1o.shape[1]
    inner = first + h2o.shape[1] - half
    mid = c1o.shape[1]
    out = mixed[...]
    for s, (one, two) in enumerate(((c1o, c2o), (c1x, c2x))):
        at = s * inner
        out = out + dot_nt(act[:, at : at + mid], one[...])
        out = out + dot_nt(act[:, at + mid : at + inner], two[...])
    result[...] = out.astype(BF)
    d_branch = d_mixed[...].astype(BF)
    for s, (one, two) in enumerate(((h1o, h2o), (h1x, h2x))):
        at = s * inner
        two[:, :half] = dot_tn(d_branch, att[:, s * half : (s + 1) * half]).astype(BF)

        @pl.loop(0, tiles(first))
        def _(i):
            frm = pl.ds(pl.multiple_of(at + i * TILE, TILE), TILE)
            one[:, lane(i, TILE)] = dot_tn(n2[...], d_up[:, frm]).astype(BF)

        two[:, half:] = dot_tn(n2[...], d_up[:, at + first : at + inner]).astype(BF)


def back_body(half, j, *refs):
    q, k, v, d_att, stat, delta, idq, ids, k_hat, k_rate, kg = refs[:11]
    a1o, a1x, a2o, a2x = refs[11:15]
    dk_low, dv_low, dq, part, k_gain, bias, dk, q_cat, d_cat = refs[15:]
    tokens = q.shape[0]
    step = padded(tokens)
    bias[...] = jnp.where(ids[j * tokens : (j + 1) * tokens, :] == idq[...], 0.0, -1e30)
    q_cat[...] = jnp.zeros_like(q_cat)
    d_cat[...] = jnp.zeros_like(d_cat)
    masks = pair_masks(tokens)

    @pl.loop(0, q.shape[1] // LANES)
    def _(pair):
        cols = lane(pair, LANES)
        k_pair, v_pair = k[:, cols], v[:, cols]
        for s, mask in enumerate(masks):
            q_cat[s * step : s * step + tokens, :] = pick(q[:, cols], mask)
            d_cat[s * step : s * step + tokens, :] = pick(d_att[:, cols], mask)
        row = pl.ds(pair, 1)
        prob = jnp.exp(dot_nt(k_pair, q_cat[...]) + bias[...] - stat[row, :])
        d_prob = dot_nt(v_pair, d_cat[...])
        d_score = (prob * (d_prob - delta[row, :])).astype(BF)
        dv_low[:, cols] = dot_nn(prob.astype(BF), d_cat[...]).astype(BF)
        dk[:, cols] = dot_nn(d_score, q_cat[...])
        both = dot_tn(d_score, k_pair)
        dq[:, cols] = jnp.where(masks[0], both[:tokens], both[step : step + tokens])

    matrix = group_matrix()
    total = jnp.zeros((1, TILE), F4)
    for t in range(tiles(2 * half)):
        cols = slice(t * TILE, (t + 1) * TILE)
        d, g = head_norm_back(
            dk[:, cols], k_hat[:, cols], k_rate[:, cols], kg[...], matrix
        )
        dk_low[:, cols] = d.astype(BF)
        total = total + fold_heads(g)
    k_gain[...] = total
    cut = a1o.shape[1]
    e = jnp.zeros((tokens, 2 * half), F4)
    for s, (one, two) in enumerate(((a1o, a2o), (a1x, a2x))):
        at = s * half
        mid = at + cut - half
        e = e + dot_nt(dk_low[:, at:mid], one[:, half:])
        e = e + dot_nt(dk_low[:, mid : at + half], two[:, : 2 * half - cut])
        e = e + dot_nt(dv_low[:, at : at + half], two[:, 2 * half - cut :])
    part[...] = e.astype(part.dtype)


def back_block(j, q, k, v, d_att, stat, delta, idq, ids, k_hat, k_rate, kg, parts):
    tokens, width = q.shape
    wide, step = (tokens, width), padded(tokens)
    outs = [(wide, BF), (wide, BF), (wide, F4), (wide, F4 if j == 0 else BF)]
    outs += [((1, TILE), F4)]
    scratch = [pltpu.VMEM((tokens, 2 * step), F4), pltpu.VMEM(wide, F4)]
    scratch += [pltpu.VMEM((2 * step, LANES), BF)] * 2
    flops = 10 * tokens * tokens * width * 4 + 4 * tokens * width * width
    body = functools.partial(back_body, width // 2, j)
    return call(
        body, outs, scratch, 10, flops,
        q, k, v, d_att, stat, delta, idq, ids, k_hat, k_rate, kg, *parts,
    )


def weight_body(n, half, *refs):
    q_hat, q_rate, qg, own = refs[:4]
    a1o, a1x = refs[4:6]
    dqs, ns = refs[6 : 6 + n], refs[6 + n : 6 + 2 * n]
    dks, dvs = refs[6 + 2 * n : 6 + 3 * n], refs[6 + 3 * n : 6 + 4 * n]
    part, q_gain, g1o, g1x, g2o, g2x, dq_low, n_all, dk_all, dv_all = refs[6 + 4 * n :]
    tokens = q_hat.shape[0]
    matrix = group_matrix()
    total = jnp.zeros((1, TILE), F4)
    factor = float(HD) ** -0.5
    for t in range(tiles(2 * half)):
        cols = slice(t * TILE, (t + 1) * TILE)
        e = dqs[0][:, cols]
        for other in dqs[1:]:
            e = e + other[:, cols]
        d, g = head_norm_back(
            e * factor, q_hat[:, cols], q_rate[:, cols], qg[...], matrix
        )
        dq_low[:, cols] = d.astype(BF)
        total = total + fold_heads(g)
    q_gain[...] = total
    e = dot_nt(dq_low[:, :half], a1o[:, :half]) + dot_nt(dq_low[:, half:], a1x[:, :half])
    part[...] = own[...] + e
    for b in range(n):
        rows = slice(b * tokens, (b + 1) * tokens)
        n_all[rows, :] = ns[b][...]
        dk_all[rows, :] = dks[b][...]
        dv_all[rows, :] = dvs[b][...]
    cut = g1o.shape[1]
    for s, (one, two) in enumerate(((g1o, g2o), (g1x, g2x))):
        at = s * half
        mid = at + cut - half
        one[:, :half] = dot_tn(ns[0][...], dq_low[:, at : at + half]).astype(BF)
        one[:, half:] = dot_tn(n_all[...], dk_all[:, at:mid]).astype(BF)
        two[:, : 2 * half - cut] = dot_tn(n_all[...], dk_all[:, mid : at + half]).astype(BF)
        two[:, 2 * half - cut :] = dot_tn(n_all[...], dv_all[:, at : at + half]).astype(BF)


def input_body(own, rest, p, g1, d_mixed, second, query, *refs):
    keys, (out, small) = refs[:-2], refs[-2:]
    e = own[...] + rest[...].astype(F4)
    c, r = centre(p[...].astype(F4))
    hat = c * r
    t = e * g1[...]
    out[...] = d_mixed[...] + r * (t - mean_last(t) - hat * mean_last(t * hat))
    small[...] = jnp.zeros_like(small)
    small[0:1, :] = jnp.sum(e * hat, axis=0, keepdims=True)
    small[1:2, :] = jnp.sum(e, axis=0, keepdims=True)
    small[2:4, :] = second[...]
    small[4:5, :TILE] = query[...]
    total = keys[0][...]
    for x in keys[1:]:
        total = total + x[...]
    small[5:6, :TILE] = total


def take_micro(x, c):
    mine = jnp.where(c0, x[0], x[1])
    other = jnp.where(c0, x[1], x[0])
    return mine, other


def per_device(
    patches,
    picture_ids,
    ln1_gain,
    ln1_bias,
    w_query,
    w_key,
    w_value,
    q_gain,
    k_gain,
    w_out,
    ln2_gain,
    ln2_bias,
    w_up,
    w_down,
    cotangent,
):
    n = lax.axis_size("row")
    at = Place()
    c0 = at("c")
    width = patches.shape[-1]
    half = w_query.shape[1]
    piece = patches.shape[2]
    tokens = 2 * piece
    inner = w_up.shape[1]

    cut_a = half + half * 2 // 3
    first = inner * 2 // 3
    mid = inner // 2
    width_b = inner + half
    whole = not regular(w_query.shape[0])
    chunk_a = jnp.concatenate([w_query, w_key, w_value], axis=1)
    chunk_b = jnp.concatenate([w_up[:, :first], w_out.T, w_up[:, first:]], axis=1)
    line_a = Chain(line_steps(chunk_a, at, True))
    line_b = Chain(line_steps(chunk_b, at))

    def back_home(x):
        lower, upper = x[:piece], x[piece:]
        keep = jnp.where(c0, lower, upper)
        got = swap_core(jnp.where(c0, upper, lower))
        whole = jnp.stack([jnp.where(c0, keep, got), jnp.where(c0, got, keep)])
        return whole[None], got

    def take(x):
        mine = jnp.where(c0, x[0], x[1])
        got = swap_core(jnp.where(c0, x[1], x[0]))
        return jnp.concatenate(
            [jnp.where(c0, mine, got), jnp.where(c0, got, mine)], axis=0
        )

    g1, b1 = ln1_gain[None], ln1_bias[None]
    g2, b2 = ln2_gain[None], ln2_bias[None]
    qg, kg = jnp.tile(q_gain, TILE // HD)[None], jnp.tile(k_gain, TILE // HD)[None]
    ids = jnp.where(c0, picture_ids[0, 0], picture_ids[0, 1]).reshape(n, tokens)
    id_blocks = [index(ids, at("row", j), keepdims=True) for j in range(n)]
    ids = jnp.concatenate(id_blocks, axis=1).reshape(n * tokens, 1)
    spare = jnp.full((1, padded(tokens) - tokens), -1, jnp.int32)
    idq = jnp.concatenate([id_blocks[0], spare] * 2, axis=1)
    ready = lax.optimization_barrier((g1, b1, g2, b2, qg, kg, ids, idq, *id_blocks))
    g1, b1, g2, b2, qg, kg, ids, idq, *id_blocks = ready

    line_a.step()
    p_own = take(patches[0])
    blocks = [p_own, hop(p_own, n)]
    got_a = line_a.last
    rows_a = line_a.step(*ready).finish()
    chain_a = Chain(plane_steps((rows_a[:, :cut_a], rows_a[:, cut_a:]), whole, at))
    chain_a.step()
    line_b.step(*got_a)
    chain_a.step()
    for _ in range(n - 2):
        line_b.step()
    got_b = line_b.last
    rows_b = line_b.finish()
    a_one, a_two = chain_a.finish()
    a_parts = a_one + a_two
    cot = take(cotangent[0])
    line_c = Chain(line_steps(after(w_down.T, got_b), at)).step()
    chain_b = Chain(plane_steps((rows_b[:, :first], rows_b[:, first:]), whole, at))

    made, marks = [], []
    before = token = ()
    deps = got_b
    for j in range(n):
        if 0 < j < n - 1:
            blocks.append(hop(after(blocks[j], marks[-1] if j > 1 else got_b), n))
        if j in (0, 1, n - 1):
            chain_b.step(*token)
        if 0 < j < n - 1:
            line_c.step(*token)
        if j == n - 1:
            rows_c = line_c.finish()
            chain_c = Chain(plane_steps((rows_c[:, :mid], rows_c[:, mid:]), whole, at))
            chain_c.step()
        made.append(
            look(
                j == 0, j == n - 1, after(blocks[j], deps), g1, b1, qg, kg, ids,
                id_blocks[j], a_parts, before,
            )
        )
        if j == 0:
            q_hat, q_rate, q_low = made[0][7:]
        before = (q_low, *made[j][5:7])
        token = (made[j][6],)
        marks.append(token)
        deps = token + (chain_c.last if j == n - 1 else line_c.last)
        if j != 1 or n < 4:
            deps = deps + chain_b.last
    normed = [m[0] for m in made]
    k_hat, k_rate, k_low, v_low = [[m[i] for m in made] for i in (1, 2, 3, 4)]
    att, stat = made[-1][5:7]

    b_one, b_two = chain_b.finish()
    b_parts = b_one + b_two
    chain_c.step(*token)
    mixed, n2, act, slope, *gc = call(
        functools.partial(up_body, half),
        [((tokens, width), F4), ((tokens, width), BF)]
        + [((tokens, 2 * inner), BF)] * 2
        + [((width, mid), BF)] * 4,
        [], 7,
        2 * tokens * width * (width + 4 * inner),
        p_own, after(att, deps), cot, g2, b2, *b_parts,
    )
    c_one, c_two = chain_c.finish()
    c_parts = c_one + c_two

    back_c = Chain(plane_sums((gc[0], gc[1]), (gc[2], gc[3]), whole, at)).step()
    deps = back_c.last
    back_c.step()
    d_up, d_mixed, d_att, delta, gains2 = call(
        functools.partial(slope_body, half),
        [((tokens, 2 * inner), BF), ((tokens, width), F4), ((tokens, width), BF)]
        + [((8, 2 * padded(tokens)), F4), ((2, width), F4)],
        [], 11,
        2 * tokens * width * (width + 4 * inner),
        after(mixed, deps), slope, att, cot, g2, *b_parts, *c_parts,
    )
    back = [None] * n
    back_b = acc = None
    deps = (delta,)
    for turn, j in enumerate([*range(1, n), 0]):
        back[j] = back_block(
            j, q_low, k_low[j], v_low[j], after(d_att, deps), stat, delta, idq, ids,
            k_hat[j], k_rate[j], kg, a_parts,
        )
        token = back[j][4]
        deps = (token, *back_c.last)
        back_c.step(token)
        if back_b is not None:
            deps = deps + back_b.last
            back_b.step(token)
        if turn == min(1, n - 1):
            result, *gb = call(
                functools.partial(inner_body, half),
                [((tokens, width), BF)]
                + [((width, first), BF)] * 2
                + [((width, half + inner - first), BF)] * 2,
                [], 10,
                2 * tokens * width * (width + 4 * inner),
                mixed, n2, act, att, d_up, after(d_mixed, deps), *c_parts,
            )
            deps = (result,)
            result, got = back_home(result)
            back_b = Chain(plane_sums((gb[0], gb[1]), (gb[2], gb[3]), whole, at)).step()
        elif turn > 1:
            deps = deps + (got,)
        if j:
            part = back[j][3]
            if acc is None:
                acc = part
            else:
                deps = deps + (acc,)
                acc = add_low(part, acc)
            acc = hop(acc, n)
    deps = deps + (acc,)
    part, dq_gain, *ga = call(
        functools.partial(weight_body, n, half),
        [((tokens, width), F4), ((1, TILE), F4)]
        + [((width, cut_a), BF)] * 2
        + [((width, 3 * half - cut_a), BF)] * 2,
        [pltpu.VMEM((tokens, width), BF)] + [pltpu.VMEM((n * tokens, width), BF)] * 3,
        12,
        2 * tokens * width * width * (2 + 2 * n),
        after(q_hat, deps), q_rate, qg, back[0][3], *a_one,
        *[b[2] for b in back], *normed, *[b[0] for b in back], *[b[1] for b in back],
    )
    sum_b, sum_c = back_b.step(dq_gain).finish(), back_c.finish()
    line = Chain(line_sums(jnp.concatenate([sum_b, sum_c], axis=1), whole, at)).step()
    back_a = Chain(plane_sums((ga[0], ga[1]), (ga[2], ga[3]), whole, at)).step()
    grad_in, small = call(
        input_body, [((tokens, width), F4), ((8, width), F4)], [], 6, 0,
        part, acc, p_own, g1, d_mixed, gains2, dq_gain, *[b[4] for b in back],
    )
    sums = Chain(sum_steps(small)).step()
    deps = back_a.last
    back_a.step(*deps)
    sums.step(*deps)
    while back_a.value is None:
        deps = back_a.last
        back_a.step(*deps)
        line.step(*deps)
        sums.step(*deps)
    last_a = Chain(line_sums(back_a.value, whole, at, True)).step()
    last_a.finish()
    sums.finish()
    grad_a, grad_bc = last_a.value, line.finish()
    grad_b, grad_c = grad_bc[:, :width_b], grad_bc[:, width_b:]
    small = sums.value
    grad_g1, grad_b1, grad_g2, grad_b2 = small[0], small[1], small[2], small[3]
    grad_gq = small[4, :TILE].reshape(-1, HD).sum(axis=0)
    grad_gk = small[5, :TILE].reshape(-1, HD).sum(axis=0)

    rest = half + first
    grad_wu = jnp.concatenate([grad_b[:, :first], grad_b[:, rest:]], axis=1)
    return (
        result,
        back_home(grad_in)[0],
        grad_g1,
        grad_b1,
        grad_a[:, :half],
        grad_a[:, half : 2 * half],
        grad_a[:, 2 * half :],
        grad_gq,
        grad_gk,
        grad_b[:, first:rest].T,
        grad_g2,
        grad_b2,
        grad_wu,
        grad_c.T,
    )


def solution(mesh):
    rows = P("dp", None, ("row", "col"), None)
    inward = P(("dp", "row"), "col")
    outward = P("col", ("dp", "row"))
    return jax.shard_map(
        per_device,
        mesh=mesh,
        in_specs=(
            rows, P("dp", None, None), P(), P(), inward, inward, inward, P(), P(),
            outward, P(), P(), inward, outward, rows,
        ),
        out_specs=(
            rows, rows, P(), P(), inward, inward, inward, P(), P(),
            outward, P(), P(), inward, outward,
        ),
        check_vma=False,
    )
```

```python
import functools
import math

import jax
import jax.numpy as jnp
from jax import lax
from jax.experimental import pallas as pl
from jax.experimental.pallas import tpu as pltpu
from jax.sharding import PartitionSpec as P

HD = 64
LANES = 128
TILE = 256
EPSILON = 1e-06
BF = jnp.bfloat16
F4 = jnp.float32
VM = pl.BlockSpec(memory_space=pltpu.VMEM)


def ring_order(n):
    return list(range(0, n, 2)) + list(range(n - 1 - (n % 2), 0, -2))


def ring_place(r, n):
    return jnp.where(r % 2 == 0, r // 2, n - 1 - r // 2 - (n % 2) + (n % 2) * 1)


def ring_row(q, n):
    return jnp.where(2 * q < n, 2 * q, 2 * (n - 1 - q) + 1)


class Place:
    def __init__(self):
        n, m = lax.axis_size("row"), lax.axis_size("dp")
        place = ring_place(lax.axis_index("row"), n)
        me = lax.axis_index("dp")
        made = {("c",): lax.axis_index("col") == 0}
        for bit in range(m.bit_length() - 1):
            one = (me >> bit) & 1
            made["low", bit] = one == 0
            made["one", bit] = one
            made["zero", bit] = 1 - one
        for r in range(n):
            slot = (place - ring_order(n).index(r) + n) % n
            for k in range(n - 1):
                made["slot", r, k] = slot == k
        for r in range(n):
            for k in range(n - 1):
                made["far", r, k] = lax.axis_index("row") == r ^ k
        for k in range(n):
            made["pair", k] = lax.axis_index("row") ^ k
        for step in range(n):
            made["row", step] = ring_row((place - step + n) % n, n)
        names = list(made)
        self.made = dict(zip(names, lax.optimization_barrier(tuple(made.values()))))

    def __call__(self, *name):
        return self.made[name]


def index(x, i, axis=0, keepdims=False):
    return lax.dynamic_index_in_dim(
        x, i, axis, keepdims=keepdims, allow_negative_indices=False
    )


def hop(x, n):
    order = ring_order(n)
    pairs = [(order[i], order[(i + 1) % n]) for i in range(n)]
    return lax.ppermute(x, "row", pairs)


def swap_bit(x, axis, n, bit):
    return lax.ppermute(x, axis, [(i, i ^ (1 << bit)) for i in range(n)])


def swap_core(x):
    return lax.ppermute(x, "col", [(0, 1), (1, 0)])


def bit_orders(n):
    bits = list(range(n.bit_length() - 1))
    half = len(bits) // 2
    return bits, bits[half:] + bits[:half]


def regular(block):
    dp = lax.axis_size("dp")
    return dp & (dp - 1) == 0 and block % 16 == 0


def after(x, deps):
    if not deps:
        return x
    return lax.optimization_barrier((x, *deps))[0]


def all_after(xs, deps):
    if not deps:
        return tuple(xs)
    return lax.optimization_barrier((*xs, *deps))[: len(xs)]


class Chain:
    def __init__(self, steps):
        self.steps = steps
        self.last = ()
        self.value = None
        next(steps)

    def step(self, *deps):
        if self.value is None:
            try:
                self.last = self.steps.send(deps)
            except StopIteration as end:
                self.value = end.value
        return self

    def finish(self):
        while self.value is None:
            self.step()
        return self.value


def join_line(blocks, at, kind="slot"):
    n = len(blocks)
    parts = []
    for r in range(n):
        x = blocks[-1]
        for k in range(n - 1):
            x = jnp.where(at(kind, r, k), blocks[k], x)
        parts.append(x)
    return jnp.concatenate(parts, axis=0)


def straight(n):
    return n & (n - 1) == 0 and n <= 4


def line_steps(shard, at, at_once=False):
    deps = yield ()
    shard = after(shard, deps)
    if not regular(shard.shape[0]):
        return shard
    n = lax.axis_size("row")
    blocks = [shard]
    if at_once and straight(n):
        for k in range(1, n):
            pairs = [(i, i ^ k) for i in range(n)]
            blocks.append(lax.ppermute(shard, "row", pairs))
        deps = yield tuple(blocks[1:])
        blocks[1:] = all_after(blocks[1:], deps)
        return join_line(blocks, at, "far")
    for _ in range(n - 1):
        got = hop(blocks[-1], n)
        deps = yield (got,)
        blocks.append(after(got, deps))
    return join_line(blocks, at)


def plane_steps(parts, whole, at):
    deps = yield ()
    m = lax.axis_size("dp")
    parts = list(parts)
    if whole:
        both = lax.all_gather(
            jnp.concatenate(parts, axis=1), ("dp", "row"), axis=0, tiled=True
        )
        deps = yield (both,)
        both, cut = after(both, deps), parts[0].shape[1]
        parts = [both[:, :cut], both[:, cut:]]
    else:
        done = ([], [])
        for bits in zip(*bit_orders(m)):
            got = [swap_bit(x, "dp", m, bit) for x, bit in zip(parts, bits)]
            deps = yield tuple(got)
            got = all_after(got, deps)
            for i, bit in enumerate(bits):
                axis = sum(1 for b in done[i] if b > bit)
                low = at("low", bit)
                first = jnp.where(low, parts[i], got[i])
                second = jnp.where(low, got[i], parts[i])
                parts[i] = jnp.stack([first, second], axis=axis)
                done[i].append(bit)
        parts = [x.reshape(-1, x.shape[-1]) for x in parts]
    got = [swap_core(x) for x in parts]
    yield tuple(got)
    return (parts[0], got[0]), (parts[1], got[1])


def add_low(a, b):
    return (a.astype(F4) + b.astype(F4)).astype(BF)


def plane_sums(one, two, whole, at):
    m = lax.axis_size("dp")
    deps = yield ()
    got = [swap_core(x) for x in all_after((one[1], two[1]), deps)]
    deps = yield tuple(got)
    parts = [add_low(x[0], y) for x, y in zip((one, two), all_after(got, deps))]
    if whole:
        return jnp.concatenate(parts, axis=1)
    count = m.bit_length() - 1
    left = [list(range(count - 1, -1, -1)), list(range(count - 1, -1, -1))]
    parts = [x.reshape((2,) * count + (-1, x.shape[-1])) for x in parts]
    for bits in zip(*bit_orders(m)):
        got, keep = [], []
        for i, bit in enumerate(bits):
            axis = left[i].index(bit)
            got.append(swap_bit(index(parts[i], at("zero", bit), axis), "dp", m, bit))
            keep.append(index(parts[i], at("one", bit), axis))
            left[i].remove(bit)
        deps = yield tuple(got)
        parts = [add_low(x, y) for x, y in zip(keep, all_after(got, deps))]
    return jnp.concatenate(parts, axis=1)


def line_sums(both, whole, at, at_once=False):
    deps = yield ()
    both = after(both, deps)
    if whole:
        total = lax.psum_scatter(both, ("dp", "row"), scatter_dimension=0, tiled=True)
        yield (total,)
        return total.astype(F4)
    n = lax.axis_size("row")
    both = both.reshape(n, -1, both.shape[-1])
    if at_once and straight(n):
        got = [
            lax.ppermute(index(both, at("pair", k)), "row", [(i, i ^ k) for i in range(n)])
            for k in range(1, n)
        ]
        deps = yield tuple(got)
        total = index(both, at("pair", 0)).astype(F4)
        for x in all_after(got, deps):
            total = total + x.astype(F4)
        return total
    acc = index(both, at("row", 1))
    for step in range(n - 1):
        got = hop(acc, n)
        deps = yield (got,)
        got = after(got, deps)
        if step < n - 2:
            acc = add_low(index(both, at("row", step + 2)), got)
    return index(both, at("row", 0)).astype(F4) + got.astype(F4)


def sum_steps(x):
    deps = yield ()
    got = swap_core(after(x, deps))
    deps = yield (got,)
    x = x + after(got, deps)
    for axis in ("dp", "row"):
        n = lax.axis_size(axis)
        for bit in range(n.bit_length() - 1) if n & (n - 1) == 0 else (None,):
            got = lax.psum(x, axis) - x if bit is None else swap_bit(x, axis, n, bit)
            deps = yield (got,)
            x = x + after(got, deps)
    return x


def dot_nn(a, b):
    return jnp.dot(a, b, preferred_element_type=F4)


def dot_nt(a, b):
    return lax.dot_general(a, b, (((1,), (1,)), ((), ())), preferred_element_type=F4)


def dot_tn(a, b):
    return lax.dot_general(a, b, (((0,), (0,)), ((), ())), preferred_element_type=F4)


def mean_last(x):
    return jnp.mean(x, axis=-1, keepdims=True)


def centre(x):
    c = x - mean_last(x)
    return c, lax.rsqrt(mean_last(c * c) + EPSILON)


def group_matrix():
    i = lax.broadcasted_iota(jnp.int32, (TILE, TILE), 0) // HD
    j = lax.broadcasted_iota(jnp.int32, (TILE, TILE), 1) // HD
    return jnp.where(i == j, 1.0 / HD, 0.0).astype(BF)


def group_mean(x, matrix):
    high = x.astype(BF)
    low = (x - high.astype(F4)).astype(BF)
    return dot_nn(high, matrix) + dot_nn(low, matrix)


def head_norm(x, matrix):
    c = x - group_mean(x, matrix)
    return c, lax.rsqrt(group_mean(c * c, matrix) + EPSILON)


def low_mean(x, matrix):
    return dot_nn(x.astype(BF), matrix)


def head_norm_back(e, hat, rate, gain, matrix):
    t = e * gain
    hat, rate = hat.astype(F4), rate.astype(F4)
    d = rate * (t - low_mean(t, matrix) - hat * low_mean(t * hat, matrix))
    return d, e * hat


def fold_heads(x):
    return jnp.sum(x, axis=0, keepdims=True)


def padded(rows):
    return -(-rows // LANES) * LANES


def head_rows(columns):
    rows = columns.shape[0]
    pair = lax.broadcasted_iota(jnp.int32, (8, LANES), 0)
    at = lax.broadcasted_iota(jnp.int32, (8, LANES), 1)
    parts = []
    for s in (0, 1):
        sel = jnp.where(at == 2 * pair + s, 1.0, 0.0)
        parts.append(
            lax.dot_general(
                sel, columns, (((1,), (1,)), ((), ())),
                precision=lax.Precision.HIGHEST, preferred_element_type=F4,
            )
        )
    return parts, padded(rows)


def tiles(width):
    return width // TILE


def lane(i, width):
    return pl.ds(pl.multiple_of(i * width, width), width)


def call(body, outs, scratch, room, flops, *args):
    size = sum(a.size * a.dtype.itemsize for a in args)
    size += sum(math.prod(s) * jnp.dtype(d).itemsize for s, d in outs)
    hold = sum(math.prod(s.shape) * jnp.dtype(s.dtype).itemsize for s in scratch)
    return pl.pallas_call(
        body,
        out_shape=[jax.ShapeDtypeStruct(s, d) for s, d in outs],
        in_specs=[VM] * len(args),
        out_specs=[VM] * len(outs),
        scratch_shapes=scratch,
        compiler_params=pltpu.CompilerParams(vmem_limit_bytes=hold + (room << 20)),
        cost_estimate=pl.CostEstimate(
            flops=int(flops) * 4, bytes_accessed=int(size), transcendentals=0
        ),
    )(*args)


def pair_masks(rows):
    at = lax.broadcasted_iota(jnp.int32, (rows, LANES), 1)
    return (at < HD, at >= HD)


def pick(x, mask):
    return jnp.where(mask, x, jnp.zeros_like(x))


def write_rows(ref, columns):
    parts, step = head_rows(columns)
    ref[...] = jnp.zeros_like(ref)
    for s, x in enumerate(parts):
        ref[:, s * step : s * step + x.shape[1]] = x


def column(ref, h):
    at = lax.broadcasted_iota(jnp.int32, ref.shape, 1)
    return jnp.sum(jnp.where(at == h, ref[...], 0.0), axis=-1, keepdims=True)


def look_body(first, last, half, *refs):
    p, g1, b1, kg, ids, idk, a1o, a1x, a2o, a2x = refs[:10]
    idq = ids[: p.shape[0], :]
    refs = refs[10:]
    if first:
        qg, normed, k_hat, k_rate, k_low, v_low, out, total_out = refs[:8]
        q_hat, q_rate, q, bias, stat, k_raw, q_raw = refs[8:]
    else:
        q, acc, total_in, normed, k_hat, k_rate, k_low, v_low, out, total_out = refs[:10]
        bias, stat, k_raw = refs[10:]
    x = p[...].astype(F4)
    c, r = centre(x)
    n = (c * r * g1[...] + b1[...]).astype(BF)
    normed[...] = n
    head = 0 if first else half
    cut = a1o.shape[1]
    for s, (a1, a2) in enumerate(((a1o, a2o), (a1x, a2x))):
        at = s * half
        one = dot_nn(n, a1[:, head:])
        two = dot_nn(n, a2[...])
        if first:
            q_raw[:, at : at + half] = one[:, :half]
        k_raw[:, at : at + cut - half] = one[:, half - head :]
        k_raw[:, at + cut - half : at + half] = two[:, : 2 * half - cut]
        v_low[:, at : at + half] = two[:, 2 * half - cut :].astype(BF)
    matrix = group_matrix()
    for t in range(tiles(2 * half)):
        cols = slice(t * TILE, (t + 1) * TILE)
        c, r = head_norm(k_raw[:, cols], matrix)
        k_hat[:, cols] = (c * r).astype(BF)
        k_rate[:, cols] = r.astype(BF)
        k_low[:, cols] = (c * r * kg[...]).astype(BF)
        if first:
            c, r = head_norm(q_raw[:, cols], matrix)
            q_hat[:, cols] = (c * r).astype(BF)
            q_rate[:, cols] = r.astype(BF)
            q[:, cols] = (c * r * qg[...] * (float(HD) ** -0.5)).astype(BF)

    bias[...] = jnp.where(idq == idk[...], 0.0, -1e30)
    stat[...] = jnp.zeros_like(stat) if first else total_in[...]
    masks = pair_masks(p.shape[0])
    lanes = lax.broadcasted_iota(jnp.int32, stat.shape, 1)

    @pl.loop(0, 2 * half // LANES)
    def _(pair):
        cols = lane(pair, LANES)
        q_pair, k_pair, v_pair = q[:, cols], k_low[:, cols], v_low[:, cols]
        outs = []
        for s, mask in enumerate(masks):
            e = jnp.exp(dot_nt(pick(q_pair, mask), k_pair) + bias[...])
            total = jnp.sum(e, axis=-1, keepdims=True)
            got = dot_nn(e.astype(BF), v_pair)
            if not first:
                got = got + acc[:, cols]
            h = 2 * pair + s
            if last:
                total = total + column(stat, h)
                got = got * (1.0 / total)
                stat[...] = jnp.where(lanes == h, jnp.log(total), stat[...])
            else:
                stat[...] += jnp.where(lanes == h, total, 0.0)
            outs.append(got)
        out[:, cols] = jnp.where(masks[0], outs[0], outs[1]).astype(out.dtype)

    if last:
        write_rows(total_out, stat[...])
    else:
        total_out[...] = stat[...]


def look(first, last, p, g1, b1, qg, kg, idq, idk, parts, before):
    tokens, width = p.shape
    half = width // 2
    wide = (tokens, width)
    outs = [(wide, BF)] * 5
    outs += [(wide, BF if last else F4)]
    outs += [((8, 2 * padded(tokens)) if last else (tokens, LANES), F4)]
    if first:
        outs += [(wide, BF)] * 3
    flops = 2 * tokens * width * (width * (3 if first else 2) + 4 * tokens)
    body = functools.partial(look_body, first, last, half)
    scratch = [pltpu.VMEM((tokens, tokens), F4), pltpu.VMEM((tokens, LANES), F4)]
    scratch += [pltpu.VMEM(wide, F4)] * (2 if first else 1)
    extra = (qg,) if first else before
    return call(
        body, outs, scratch, 5, flops, p, g1, b1, kg, idq, idk, *parts, *extra
    )


ROOT = math.sqrt(2.0 / math.pi)
CUBE = 0.044715


def gelu_pair(u):
    square = u * u
    t = jnp.tanh(ROOT * u * (1.0 + CUBE * square))
    half = 0.5 * (1.0 + t)
    slope = half + 0.5 * u * (1.0 - t * t) * (ROOT * (1.0 + 3.0 * CUBE * square))
    return u * half, slope


def up_body(half, p, att, cot, g2, b2, b1o, b1x, b2o, b2x, *outs):
    mixed, n2, act, slope, g1o, g1x, g2o, g2x = outs
    first = b1o.shape[1]
    inner = first + b2o.shape[1] - half
    m = p[...].astype(F4)
    for s, part in enumerate((b2o, b2x)):
        m = m + dot_nt(att[:, s * half : (s + 1) * half], part[:, :half])
    mixed[...] = m
    c, r = centre(m)
    n2[...] = (c * r * g2[...] + b2[...]).astype(BF)
    for s, (one, two) in enumerate(((b1o, b2o), (b1x, b2x))):

        @pl.loop(0, tiles(first))
        def _(i):
            u = dot_nn(n2[...], one[:, lane(i, TILE)])
            to = pl.ds(pl.multiple_of(s * inner + i * TILE, TILE), TILE)
            a, d = gelu_pair(u)
            act[:, to] = a.astype(BF)
            slope[:, to] = d.astype(BF)

        rest = inner - first
        for i in range(tiles(rest)):
            u = dot_nn(n2[...], two[:, half + i * TILE : half + (i + 1) * TILE])
            to = slice(s * inner + first + i * TILE, s * inner + first + (i + 1) * TILE)
            a, d = gelu_pair(u)
            act[:, to] = a.astype(BF)
            slope[:, to] = d.astype(BF)
    mid = g1o.shape[1]
    for s, (one, two) in enumerate(((g1o, g2o), (g1x, g2x))):
        for base, out in ((s * inner, one), (s * inner + mid, two)):

            @pl.loop(0, tiles(mid))
            def _(i):
                frm = pl.ds(pl.multiple_of(base + i * TILE, TILE), TILE)
                out[:, lane(i, TILE)] = dot_tn(cot[...], act[:, frm]).astype(BF)


def slope_body(half, *refs):
    mixed, slope, att, cot, g2 = refs[:5]
    b1o, b1x, b2o, b2x, c1o, c1x, c2o, c2x = refs[5:13]
    d_up, d_mixed, d_att, delta, gains = refs[13:]
    first = b1o.shape[1]
    inner = first + b2o.shape[1] - half
    mid = c1o.shape[1]
    for s, (one, two) in enumerate(((c1o, c2o), (c1x, c2x))):
        at = s * inner
        for base, part in ((at, one), (at + mid, two)):

            @pl.loop(0, tiles(mid))
            def _(i):
                to = pl.ds(pl.multiple_of(base + i * TILE, TILE), TILE)
                d = dot_nn(cot[...], part[:, lane(i, TILE)])
                d_up[:, to] = (d * slope[:, to].astype(F4)).astype(BF)

    e = jnp.zeros(mixed.shape, F4)
    for s, (one, two) in enumerate(((b1o, b2o), (b1x, b2x))):
        at = s * inner
        e = e + dot_nt(d_up[:, at : at + first], one[...])
        e = e + dot_nt(d_up[:, at + first : at + inner], two[:, half:])
    c, r = centre(mixed[...])
    t = e * g2[...]
    d_mixed[...] = cot[...].astype(F4) + r * (
        t - mean_last(t) - c * (r * r) * mean_last(t * c)
    )
    gains[0:1, :] = jnp.sum(e * c * r, axis=0, keepdims=True)
    gains[1:2, :] = jnp.sum(e, axis=0, keepdims=True)
    d_branch = d_mixed[...].astype(BF)
    row = lax.broadcasted_iota(jnp.int32, (half, LANES), 0) // HD
    col = lax.broadcasted_iota(jnp.int32, (half, LANES), 1)
    sums = jnp.zeros((mixed.shape[0], LANES), F4)
    for s, part in enumerate((b2o, b2x)):
        cols = slice(s * half, (s + 1) * half)
        d = dot_nn(d_branch, part[:, :half]).astype(BF)
        d_att[:, cols] = d
        prod = d.astype(F4) * att[:, cols].astype(F4)
        high = prod.astype(BF)
        low = (prod - high.astype(F4)).astype(BF)
        sel = jnp.where(row + s * (half // HD) == col, 1.0, 0.0).astype(BF)
        sums = sums + dot_nn(high, sel) + dot_nn(low, sel)
    write_rows(delta, sums)


def inner_body(half, *refs):
    mixed, n2, act, att, d_up, d_mixed, c1o, c1x, c2o, c2x = refs[:10]
    result, h1o, h1x, h2o, h2x = refs[10:]
    first = h1o.shape[1]
    inner = first + h2o.shape[1] - half
    mid = c1o.shape[1]
    out = mixed[...]
    for s, (one, two) in enumerate(((c1o, c2o), (c1x, c2x))):
        at = s * inner
        out = out + dot_nt(act[:, at : at + mid], one[...])
        out = out + dot_nt(act[:, at + mid : at + inner], two[...])
    result[...] = out.astype(BF)
    d_branch = d_mixed[...].astype(BF)
    for s, (one, two) in enumerate(((h1o, h2o), (h1x, h2x))):
        at = s * inner
        two[:, :half] = dot_tn(d_branch, att[:, s * half : (s + 1) * half]).astype(BF)

        @pl.loop(0, tiles(first))
        def _(i):
            frm = pl.ds(pl.multiple_of(at + i * TILE, TILE), TILE)
            one[:, lane(i, TILE)] = dot_tn(n2[...], d_up[:, frm]).astype(BF)

        two[:, half:] = dot_tn(n2[...], d_up[:, at + first : at + inner]).astype(BF)


def back_body(half, j, *refs):
    q, k, v, d_att, stat, delta, idq, ids, k_hat, k_rate, kg = refs[:11]
    a1o, a1x, a2o, a2x = refs[11:15]
    dk_low, dv_low, dq, part, k_gain, bias, dk, q_cat, d_cat = refs[15:]
    tokens = q.shape[0]
    step = padded(tokens)
    bias[...] = jnp.where(ids[j * tokens : (j + 1) * tokens, :] == idq[...], 0.0, -1e30)
    q_cat[...] = jnp.zeros_like(q_cat)
    d_cat[...] = jnp.zeros_like(d_cat)
    masks = pair_masks(tokens)

    @pl.loop(0, q.shape[1] // LANES)
    def _(pair):
        cols = lane(pair, LANES)
        k_pair, v_pair = k[:, cols], v[:, cols]
        for s, mask in enumerate(masks):
            q_cat[s * step : s * step + tokens, :] = pick(q[:, cols], mask)
            d_cat[s * step : s * step + tokens, :] = pick(d_att[:, cols], mask)
        row = pl.ds(pair, 1)
        prob = jnp.exp(dot_nt(k_pair, q_cat[...]) + bias[...] - stat[row, :])
        d_prob = dot_nt(v_pair, d_cat[...])
        d_score = (prob * (d_prob - delta[row, :])).astype(BF)
        dv_low[:, cols] = dot_nn(prob.astype(BF), d_cat[...]).astype(BF)
        dk[:, cols] = dot_nn(d_score, q_cat[...])
        both = dot_tn(d_score, k_pair)
        dq[:, cols] = jnp.where(masks[0], both[:tokens], both[step : step + tokens])

    matrix = group_matrix()
    total = jnp.zeros((1, TILE), F4)
    for t in range(tiles(2 * half)):
        cols = slice(t * TILE, (t + 1) * TILE)
        d, g = head_norm_back(
            dk[:, cols], k_hat[:, cols], k_rate[:, cols], kg[...], matrix
        )
        dk_low[:, cols] = d.astype(BF)
        total = total + fold_heads(g)
    k_gain[...] = total
    cut = a1o.shape[1]
    e = jnp.zeros((tokens, 2 * half), F4)
    for s, (one, two) in enumerate(((a1o, a2o), (a1x, a2x))):
        at = s * half
        mid = at + cut - half
        e = e + dot_nt(dk_low[:, at:mid], one[:, half:])
        e = e + dot_nt(dk_low[:, mid : at + half], two[:, : 2 * half - cut])
        e = e + dot_nt(dv_low[:, at : at + half], two[:, 2 * half - cut :])
    part[...] = e.astype(part.dtype)


def back_block(j, q, k, v, d_att, stat, delta, idq, ids, k_hat, k_rate, kg, parts):
    tokens, width = q.shape
    wide, step = (tokens, width), padded(tokens)
    outs = [(wide, BF), (wide, BF), (wide, F4), (wide, F4 if j == 0 else BF)]
    outs += [((1, TILE), F4)]
    scratch = [pltpu.VMEM((tokens, 2 * step), F4), pltpu.VMEM(wide, F4)]
    scratch += [pltpu.VMEM((2 * step, LANES), BF)] * 2
    flops = 10 * tokens * tokens * width * 4 + 4 * tokens * width * width
    body = functools.partial(back_body, width // 2, j)
    return call(
        body, outs, scratch, 8, flops,
        q, k, v, d_att, stat, delta, idq, ids, k_hat, k_rate, kg, *parts,
    )


def weight_body(n, half, *refs):
    q_hat, q_rate, qg, own = refs[:4]
    a1o, a1x = refs[4:6]
    dqs, ns = refs[6 : 6 + n], refs[6 + n : 6 + 2 * n]
    dks, dvs = refs[6 + 2 * n : 6 + 3 * n], refs[6 + 3 * n : 6 + 4 * n]
    part, q_gain, g1o, g1x, g2o, g2x, dq_low, n_all, dk_all, dv_all = refs[6 + 4 * n :]
    tokens = q_hat.shape[0]
    matrix = group_matrix()
    total = jnp.zeros((1, TILE), F4)
    factor = float(HD) ** -0.5
    for t in range(tiles(2 * half)):
        cols = slice(t * TILE, (t + 1) * TILE)
        e = dqs[0][:, cols]
        for other in dqs[1:]:
            e = e + other[:, cols]
        d, g = head_norm_back(
            e * factor, q_hat[:, cols], q_rate[:, cols], qg[...], matrix
        )
        dq_low[:, cols] = d.astype(BF)
        total = total + fold_heads(g)
    q_gain[...] = total
    e = dot_nt(dq_low[:, :half], a1o[:, :half]) + dot_nt(dq_low[:, half:], a1x[:, :half])
    part[...] = own[...] + e
    for b in range(n):
        rows = slice(b * tokens, (b + 1) * tokens)
        n_all[rows, :] = ns[b][...]
        dk_all[rows, :] = dks[b][...]
        dv_all[rows, :] = dvs[b][...]
    cut = g1o.shape[1]
    for s, (one, two) in enumerate(((g1o, g2o), (g1x, g2x))):
        at = s * half
        mid = at + cut - half
        one[:, :half] = dot_tn(ns[0][...], dq_low[:, at : at + half]).astype(BF)
        one[:, half:] = dot_tn(n_all[...], dk_all[:, at:mid]).astype(BF)
        two[:, : 2 * half - cut] = dot_tn(n_all[...], dk_all[:, mid : at + half]).astype(BF)
        two[:, 2 * half - cut :] = dot_tn(n_all[...], dv_all[:, at : at + half]).astype(BF)


def input_body(own, rest, p, g1, d_mixed, second, query, *refs):
    keys, (out, small) = refs[:-2], refs[-2:]
    e = own[...] + rest[...].astype(F4)
    c, r = centre(p[...].astype(F4))
    hat = c * r
    t = e * g1[...]
    out[...] = d_mixed[...] + r * (t - mean_last(t) - hat * mean_last(t * hat))
    small[...] = jnp.zeros_like(small)
    small[0:1, :] = jnp.sum(e * hat, axis=0, keepdims=True)
    small[1:2, :] = jnp.sum(e, axis=0, keepdims=True)
    small[2:4, :] = second[...]
    small[4:5, :TILE] = query[...]
    total = keys[0][...]
    for x in keys[1:]:
        total = total + x[...]
    small[5:6, :TILE] = total


def take_micro(x, c):
    mine = jnp.where(c0, x[0], x[1])
    other = jnp.where(c0, x[1], x[0])
    return mine, other


def per_device(
    patches,
    picture_ids,
    ln1_gain,
    ln1_bias,
    w_query,
    w_key,
    w_value,
    q_gain,
    k_gain,
    w_out,
    ln2_gain,
    ln2_bias,
    w_up,
    w_down,
    cotangent,
):
    n = lax.axis_size("row")
    at = Place()
    c0 = at("c")
    width = patches.shape[-1]
    half = w_query.shape[1]
    piece = patches.shape[2]
    tokens = 2 * piece
    inner = w_up.shape[1]

    cut_a = half + half * 2 // 3
    first = inner * 2 // 3
    mid = inner // 2
    width_b = inner + half
    whole = not regular(w_query.shape[0])
    chunk_a = jnp.concatenate([w_query, w_key, w_value], axis=1)
    chunk_b = jnp.concatenate([w_up[:, :first], w_out.T, w_up[:, first:]], axis=1)
    line_a = Chain(line_steps(chunk_a, at, True))
    line_b = Chain(line_steps(chunk_b, at))

    def back_home(x):
        lower, upper = x[:piece], x[piece:]
        keep = jnp.where(c0, lower, upper)
        got = swap_core(jnp.where(c0, upper, lower))
        whole = jnp.stack([jnp.where(c0, keep, got), jnp.where(c0, got, keep)])
        return whole[None], got

    def take(x):
        mine = jnp.where(c0, x[0], x[1])
        got = swap_core(jnp.where(c0, x[1], x[0]))
        return jnp.concatenate(
            [jnp.where(c0, mine, got), jnp.where(c0, got, mine)], axis=0
        )

    g1, b1 = ln1_gain[None], ln1_bias[None]
    g2, b2 = ln2_gain[None], ln2_bias[None]
    qg, kg = jnp.tile(q_gain, TILE // HD)[None], jnp.tile(k_gain, TILE // HD)[None]
    ids = jnp.where(c0, picture_ids[0, 0], picture_ids[0, 1]).reshape(n, tokens)
    id_blocks = [index(ids, at("row", j), keepdims=True) for j in range(n)]
    ids = jnp.concatenate(id_blocks, axis=1).reshape(n * tokens, 1)
    spare = jnp.full((1, padded(tokens) - tokens), -1, jnp.int32)
    idq = jnp.concatenate([id_blocks[0], spare] * 2, axis=1)
    ready = lax.optimization_barrier((g1, b1, g2, b2, qg, kg, ids, idq, *id_blocks))
    g1, b1, g2, b2, qg, kg, ids, idq, *id_blocks = ready

    line_a.step()
    p_own = take(patches[0])
    blocks = [p_own, hop(p_own, n)]
    got_a = line_a.last
    rows_a = line_a.step(*ready).finish()
    chain_a = Chain(plane_steps((rows_a[:, :cut_a], rows_a[:, cut_a:]), whole, at))
    chain_a.step()
    line_b.step(*got_a)
    chain_a.step()
    for _ in range(n - 2):
        line_b.step()
    got_b = line_b.last
    rows_b = line_b.finish()
    a_one, a_two = chain_a.finish()
    swap_a = chain_a.last
    a_parts = a_one + a_two
    cot = take(cotangent[0])
    line_c = Chain(line_steps(after(w_down.T, got_b), at)).step()
    chain_b = Chain(plane_steps((rows_b[:, :first], rows_b[:, first:]), whole, at))

    made, marks = [], []
    before = token = ()
    deps = got_b
    for j in range(n):
        if 0 < j < n - 1:
            blocks.append(hop(after(blocks[j], marks[-1] if j > 1 else swap_a), n))
        if j in (0, 1, n - 1):
            chain_b.step(*token)
        if 0 < j < n - 1:
            line_c.step(*token)
        if j == n - 1:
            rows_c = line_c.finish()
            chain_c = Chain(plane_steps((rows_c[:, :mid], rows_c[:, mid:]), whole, at))
            chain_c.step()
        made.append(
            look(
                j == 0, j == n - 1, after(blocks[j], deps), g1, b1, qg, kg, ids,
                id_blocks[j], a_parts, before,
            )
        )
        if j == 0:
            q_hat, q_rate, q_low = made[0][7:]
        before = (q_low, *made[j][5:7])
        token = (made[j][6],)
        marks.append(token)
        deps = token + (chain_c.last if j == n - 1 else line_c.last)
        if j != 1 or n < 4:
            deps = deps + chain_b.last
    normed = [m[0] for m in made]
    k_hat, k_rate, k_low, v_low = [[m[i] for m in made] for i in (1, 2, 3, 4)]
    att, stat = made[-1][5:7]

    b_one, b_two = chain_b.finish()
    b_parts = b_one + b_two
    chain_c.step(*token)
    mixed, n2, act, slope, *gc = call(
        functools.partial(up_body, half),
        [((tokens, width), F4), ((tokens, width), BF)]
        + [((tokens, 2 * inner), BF)] * 2
        + [((width, mid), BF)] * 4,
        [], 6,
        2 * tokens * width * (width + 4 * inner),
        p_own, after(att, deps), cot, g2, b2, *b_parts,
    )
    c_one, c_two = chain_c.step(mixed).finish()
    c_parts = c_one + c_two

    back_c = Chain(plane_sums((gc[0], gc[1]), (gc[2], gc[3]), whole, at)).step()
    deps = back_c.last
    back_c.step()
    d_up, d_mixed, d_att, delta, gains2 = call(
        functools.partial(slope_body, half),
        [((tokens, 2 * inner), BF), ((tokens, width), F4), ((tokens, width), BF)]
        + [((8, 2 * padded(tokens)), F4), ((2, width), F4)],
        [], 9,
        2 * tokens * width * (width + 4 * inner),
        after(mixed, deps), slope, att, cot, g2, *b_parts, *c_parts,
    )
    back = [None] * n
    back_b = acc = None
    deps = (delta,)
    for turn, j in enumerate([*range(1, n), 0]):
        back[j] = back_block(
            j, q_low, k_low[j], v_low[j], after(d_att, deps), stat, delta, idq, ids,
            k_hat[j], k_rate[j], kg, a_parts,
        )
        token = back[j][4]
        deps = (token, *back_c.last)
        back_c.step(token)
        if back_b is not None:
            deps = deps + back_b.last
            back_b.step(token)
        if turn == 0:
            result, *gb = call(
                functools.partial(inner_body, half),
                [((tokens, width), BF)]
                + [((width, first), BF)] * 2
                + [((width, half + inner - first), BF)] * 2,
                [], 8,
                2 * tokens * width * (width + 4 * inner),
                mixed, n2, act, att, d_up, after(d_mixed, deps), *c_parts,
            )
            deps = (result,)
            result, got = back_home(result)
            back_b = Chain(plane_sums((gb[0], gb[1]), (gb[2], gb[3]), whole, at)).step()
        elif turn > 0:
            deps = deps + (got,)
        if j:
            part = back[j][3]
            if acc is None:
                acc = part
            else:
                deps = deps + (acc,)
                acc = add_low(part, acc)
            acc = hop(acc, n)
    sum_b, sum_c = back_b.finish(), back_c.finish()
    both = jnp.concatenate([sum_b, sum_c], axis=1)
    line = Chain(line_sums(both, whole, at)).step()
    part, dq_gain, *ga = call(
        functools.partial(weight_body, n, half),
        [((tokens, width), F4), ((1, TILE), F4)]
        + [((width, cut_a), BF)] * 2
        + [((width, 3 * half - cut_a), BF)] * 2,
        [pltpu.VMEM((tokens, width), BF)] + [pltpu.VMEM((n * tokens, width), BF)] * 3,
        10,
        2 * tokens * width * width * (2 + 2 * n),
        after(q_hat, deps), q_rate, qg, back[0][3], *a_one,
        *[b[2] for b in back], *normed, *[b[0] for b in back], *[b[1] for b in back],
    )
    back_a = Chain(plane_sums((ga[0], ga[1]), (ga[2], ga[3]), whole, at))
    back_a.step(acc, *line.last)
    grad_in, small = call(
        input_body, [((tokens, width), F4), ((8, width), F4)], [], 6, 0,
        part, acc, p_own, g1, d_mixed, gains2, dq_gain, *[b[4] for b in back],
    )
    sums = Chain(sum_steps(small)).step()
    while back_a.value is None:
        deps = back_a.last
        back_a.step(*deps)
        line.step(*deps)
        sums.step(*deps)
    last_a = Chain(line_sums(back_a.value, whole, at, True)).step()
    sums.step(*last_a.last)
    last_a.finish()
    sums.finish()
    grad_a, grad_bc = last_a.value, line.finish()
    grad_b, grad_c = grad_bc[:, :width_b], grad_bc[:, width_b:]
    small = sums.value
    grad_g1, grad_b1, grad_g2, grad_b2 = small[0], small[1], small[2], small[3]
    grad_gq = small[4, :TILE].reshape(-1, HD).sum(axis=0)
    grad_gk = small[5, :TILE].reshape(-1, HD).sum(axis=0)

    rest = half + first
    grad_wu = jnp.concatenate([grad_b[:, :first], grad_b[:, rest:]], axis=1)
    return (
        result,
        back_home(grad_in)[0],
        grad_g1,
        grad_b1,
        grad_a[:, :half],
        grad_a[:, half : 2 * half],
        grad_a[:, 2 * half :],
        grad_gq,
        grad_gk,
        grad_b[:, first:rest].T,
        grad_g2,
        grad_b2,
        grad_wu,
        grad_c.T,
    )


def solution(mesh):
    rows = P("dp", None, ("row", "col"), None)
    inward = P(("dp", "row"), "col")
    outward = P("col", ("dp", "row"))
    return jax.shard_map(
        per_device,
        mesh=mesh,
        in_specs=(
            rows, P("dp", None, None), P(), P(), inward, inward, inward, P(), P(),
            outward, P(), P(), inward, outward, rows,
        ),
        out_specs=(
            rows, rows, P(), P(), inward, inward, inward, P(), P(),
            outward, P(), P(), inward, outward,
        ),
        check_vma=False,
    )
```

```python
import functools
import math

import jax
import jax.numpy as jnp
from jax import lax
from jax.experimental import pallas as pl
from jax.experimental.pallas import tpu as pltpu
from jax.sharding import PartitionSpec as P

HD = 64
LANES = 128
TILE = 256
EPSILON = 1e-06
BF = jnp.bfloat16
F4 = jnp.float32
VM = pl.BlockSpec(memory_space=pltpu.VMEM)


def ring_order(n):
    return list(range(0, n, 2)) + list(range(n - 1 - (n % 2), 0, -2))


def ring_place(r, n):
    return jnp.where(r % 2 == 0, r // 2, n - 1 - r // 2 - (n % 2) + (n % 2) * 1)


def ring_row(q, n):
    return jnp.where(2 * q < n, 2 * q, 2 * (n - 1 - q) + 1)


class Place:
    def __init__(self):
        n, m = lax.axis_size("row"), lax.axis_size("dp")
        place = ring_place(lax.axis_index("row"), n)
        me = lax.axis_index("dp")
        made = {("c",): lax.axis_index("col") == 0}
        for bit in range(m.bit_length() - 1):
            one = (me >> bit) & 1
            made["low", bit] = one == 0
            made["one", bit] = one
            made["zero", bit] = 1 - one
        for r in range(n):
            slot = (place - ring_order(n).index(r) + n) % n
            for k in range(n - 1):
                made["slot", r, k] = slot == k
        for r in range(n):
            for k in range(n - 1):
                made["far", r, k] = lax.axis_index("row") == r ^ k
        for k in range(n):
            made["pair", k] = lax.axis_index("row") ^ k
        for step in range(n):
            made["row", step] = ring_row((place - step + n) % n, n)
        names = list(made)
        self.made = dict(zip(names, lax.optimization_barrier(tuple(made.values()))))

    def __call__(self, *name):
        return self.made[name]


def index(x, i, axis=0, keepdims=False):
    return lax.dynamic_index_in_dim(
        x, i, axis, keepdims=keepdims, allow_negative_indices=False
    )


def hop(x, n):
    order = ring_order(n)
    pairs = [(order[i], order[(i + 1) % n]) for i in range(n)]
    return lax.ppermute(x, "row", pairs)


def swap_bit(x, axis, n, bit):
    return lax.ppermute(x, axis, [(i, i ^ (1 << bit)) for i in range(n)])


def swap_core(x):
    return lax.ppermute(x, "col", [(0, 1), (1, 0)])


def bit_orders(n):
    bits = list(range(n.bit_length() - 1))
    half = len(bits) // 2
    return bits, bits[half:] + bits[:half]


def regular(block):
    dp = lax.axis_size("dp")
    return dp & (dp - 1) == 0 and block % 16 == 0


def after(x, deps):
    if not deps:
        return x
    return lax.optimization_barrier((x, *deps))[0]


def all_after(xs, deps):
    if not deps:
        return tuple(xs)
    return lax.optimization_barrier((*xs, *deps))[: len(xs)]


class Chain:
    def __init__(self, steps):
        self.steps = steps
        self.last = ()
        self.value = None
        next(steps)

    def step(self, *deps):
        if self.value is None:
            try:
                self.last = self.steps.send(deps)
            except StopIteration as end:
                self.value = end.value
        return self

    def finish(self):
        while self.value is None:
            self.step()
        return self.value


def join_line(blocks, at, kind="slot"):
    n = len(blocks)
    parts = []
    for r in range(n):
        x = blocks[-1]
        for k in range(n - 1):
            x = jnp.where(at(kind, r, k), blocks[k], x)
        parts.append(x)
    return jnp.concatenate(parts, axis=0)


def straight(n):
    return n & (n - 1) == 0 and n <= 4


def line_steps(shard, at, at_once=False):
    deps = yield ()
    shard = after(shard, deps)
    if not regular(shard.shape[0]):
        return shard
    n = lax.axis_size("row")
    blocks = [shard]
    if at_once and straight(n):
        for k in range(1, n):
            pairs = [(i, i ^ k) for i in range(n)]
            blocks.append(lax.ppermute(shard, "row", pairs))
        deps = yield tuple(blocks[1:])
        blocks[1:] = all_after(blocks[1:], deps)
        return join_line(blocks, at, "far")
    for _ in range(n - 1):
        got = hop(blocks[-1], n)
        deps = yield (got,)
        blocks.append(after(got, deps))
    return join_line(blocks, at)


def plane_steps(parts, whole, at):
    deps = yield ()
    m = lax.axis_size("dp")
    parts = list(parts)
    if whole:
        both = lax.all_gather(
            jnp.concatenate(parts, axis=1), ("dp", "row"), axis=0, tiled=True
        )
        deps = yield (both,)
        both, cut = after(both, deps), parts[0].shape[1]
        parts = [both[:, :cut], both[:, cut:]]
    else:
        done = ([], [])
        for bits in zip(*bit_orders(m)):
            got = [swap_bit(x, "dp", m, bit) for x, bit in zip(parts, bits)]
            deps = yield tuple(got)
            got = all_after(got, deps)
            for i, bit in enumerate(bits):
                axis = sum(1 for b in done[i] if b > bit)
                low = at("low", bit)
                first = jnp.where(low, parts[i], got[i])
                second = jnp.where(low, got[i], parts[i])
                parts[i] = jnp.stack([first, second], axis=axis)
                done[i].append(bit)
        parts = [x.reshape(-1, x.shape[-1]) for x in parts]
    got = [swap_core(x) for x in parts]
    yield tuple(got)
    return (parts[0], got[0]), (parts[1], got[1])


def add_low(a, b):
    return (a.astype(F4) + b.astype(F4)).astype(BF)


def plane_sums(one, two, whole, at):
    m = lax.axis_size("dp")
    deps = yield ()
    got = [swap_core(x) for x in all_after((one[1], two[1]), deps)]
    deps = yield tuple(got)
    parts = [add_low(x[0], y) for x, y in zip((one, two), all_after(got, deps))]
    if whole:
        return jnp.concatenate(parts, axis=1)
    count = m.bit_length() - 1
    left = [list(range(count - 1, -1, -1)), list(range(count - 1, -1, -1))]
    parts = [x.reshape((2,) * count + (-1, x.shape[-1])) for x in parts]
    for bits in zip(*bit_orders(m)):
        got, keep = [], []
        for i, bit in enumerate(bits):
            axis = left[i].index(bit)
            got.append(swap_bit(index(parts[i], at("zero", bit), axis), "dp", m, bit))
            keep.append(index(parts[i], at("one", bit), axis))
            left[i].remove(bit)
        deps = yield tuple(got)
        parts = [add_low(x, y) for x, y in zip(keep, all_after(got, deps))]
    return jnp.concatenate(parts, axis=1)


def line_sums(both, whole, at, at_once=False):
    deps = yield ()
    both = after(both, deps)
    if whole:
        total = lax.psum_scatter(both, ("dp", "row"), scatter_dimension=0, tiled=True)
        yield (total,)
        return total.astype(F4)
    n = lax.axis_size("row")
    both = both.reshape(n, -1, both.shape[-1])
    if at_once and straight(n):
        got = [
            lax.ppermute(index(both, at("pair", k)), "row", [(i, i ^ k) for i in range(n)])
            for k in range(1, n)
        ]
        deps = yield tuple(got)
        total = index(both, at("pair", 0)).astype(F4)
        for x in all_after(got, deps):
            total = total + x.astype(F4)
        return total
    acc = index(both, at("row", 1))
    for step in range(n - 1):
        got = hop(acc, n)
        deps = yield (got,)
        got = after(got, deps)
        if step < n - 2:
            acc = add_low(index(both, at("row", step + 2)), got)
    return index(both, at("row", 0)).astype(F4) + got.astype(F4)


def sum_steps(x):
    deps = yield ()
    x = after(x, deps)
    for axis in ("dp", "row", "col"):
        n = lax.axis_size(axis)
        for bit in range(n.bit_length() - 1) if n & (n - 1) == 0 else (None,):
            got = lax.psum(x, axis) - x if bit is None else swap_bit(x, axis, n, bit)
            deps = yield (got,)
            x = x + after(got, deps)
    return x


def dot_nn(a, b):
    return jnp.dot(a, b, preferred_element_type=F4)


def dot_nt(a, b):
    return lax.dot_general(a, b, (((1,), (1,)), ((), ())), preferred_element_type=F4)


def dot_tn(a, b):
    return lax.dot_general(a, b, (((0,), (0,)), ((), ())), preferred_element_type=F4)


def mean_last(x):
    return jnp.mean(x, axis=-1, keepdims=True)


def centre(x):
    c = x - mean_last(x)
    return c, lax.rsqrt(mean_last(c * c) + EPSILON)


def group_matrix():
    i = lax.broadcasted_iota(jnp.int32, (TILE, TILE), 0) // HD
    j = lax.broadcasted_iota(jnp.int32, (TILE, TILE), 1) // HD
    return jnp.where(i == j, 1.0 / HD, 0.0).astype(BF)


def group_mean(x, matrix):
    high = x.astype(BF)
    low = (x - high.astype(F4)).astype(BF)
    return dot_nn(high, matrix) + dot_nn(low, matrix)


def head_norm(x, matrix):
    c = x - group_mean(x, matrix)
    return c, lax.rsqrt(group_mean(c * c, matrix) + EPSILON)


def low_mean(x, matrix):
    return dot_nn(x.astype(BF), matrix)


def head_norm_back(e, hat, rate, gain, matrix):
    t = e * gain
    hat, rate = hat.astype(F4), rate.astype(F4)
    d = rate * (t - low_mean(t, matrix) - hat * low_mean(t * hat, matrix))
    return d, e * hat


def fold_heads(x):
    return jnp.sum(x, axis=0, keepdims=True)


def padded(rows):
    return -(-rows // LANES) * LANES


def head_rows(columns):
    rows = columns.shape[0]
    pair = lax.broadcasted_iota(jnp.int32, (8, LANES), 0)
    at = lax.broadcasted_iota(jnp.int32, (8, LANES), 1)
    parts = []
    for s in (0, 1):
        sel = jnp.where(at == 2 * pair + s, 1.0, 0.0)
        parts.append(
            lax.dot_general(
                sel, columns, (((1,), (1,)), ((), ())),
                precision=lax.Precision.HIGHEST, preferred_element_type=F4,
            )
        )
    return parts, padded(rows)


def fold_lanes(x):
    return sum(x[:, i * HD : (i + 1) * HD] for i in range(TILE // HD))


def tiles(width):
    return width // TILE


def lane(i, width):
    return pl.ds(pl.multiple_of(i * width, width), width)


def call(body, outs, scratch, room, flops, *args, weight=4.0):
    size = sum(a.size * a.dtype.itemsize for a in args)
    size += sum(math.prod(s) * jnp.dtype(d).itemsize for s, d in outs)
    hold = sum(math.prod(s.shape) * jnp.dtype(s.dtype).itemsize for s in scratch)
    return pl.pallas_call(
        body,
        out_shape=[jax.ShapeDtypeStruct(s, d) for s, d in outs],
        in_specs=[VM] * len(args),
        out_specs=[VM] * len(outs),
        scratch_shapes=scratch,
        compiler_params=pltpu.CompilerParams(vmem_limit_bytes=hold + (room << 20)),
        cost_estimate=pl.CostEstimate(
            flops=int(flops * weight), bytes_accessed=int(size), transcendentals=0
        ),
    )(*args)


def pair_masks(rows):
    at = lax.broadcasted_iota(jnp.int32, (rows, LANES), 1)
    return (at < HD, at >= HD)


def pick(x, mask):
    return jnp.where(mask, x, jnp.zeros_like(x))


def write_rows(ref, columns):
    parts, step = head_rows(columns)
    ref[...] = jnp.zeros_like(ref)
    for s, x in enumerate(parts):
        ref[:, s * step : s * step + x.shape[1]] = x


def column(ref, h):
    at = lax.broadcasted_iota(jnp.int32, ref.shape, 1)
    return jnp.sum(jnp.where(at == h, ref[...], 0.0), axis=-1, keepdims=True)


def look_body(first, last, half, *refs):
    p, g1, b1, kg, ids, idk, a1o, a1x, a2o, a2x = refs[:10]
    idq = ids[: p.shape[0], :]
    refs = refs[10:]
    if first:
        qg, normed, k_hat, k_rate, k_low, v_low, out, total_out = refs[:8]
        q_hat, q_rate, q, bias, stat, k_raw, q_raw = refs[8:]
    else:
        q, acc, total_in, normed, k_hat, k_rate, k_low, v_low, out, total_out = refs[:10]
        bias, stat, k_raw = refs[10:]
    x = p[...].astype(F4)
    c, r = centre(x)
    n = (c * r * g1[...] + b1[...]).astype(BF)
    normed[...] = n
    head = 0 if first else half
    cut = a1o.shape[1]
    for s, (a1, a2) in enumerate(((a1o, a2o), (a1x, a2x))):
        at = s * half
        one = dot_nn(n, a1[:, head:])
        two = dot_nn(n, a2[...])
        if first:
            q_raw[:, at : at + half] = one[:, :half]
        k_raw[:, at : at + cut - half] = one[:, half - head :]
        k_raw[:, at + cut - half : at + half] = two[:, : 2 * half - cut]
        v_low[:, at : at + half] = two[:, 2 * half - cut :].astype(BF)
    matrix = group_matrix()
    for t in range(tiles(2 * half)):
        cols = slice(t * TILE, (t + 1) * TILE)
        c, r = head_norm(k_raw[:, cols], matrix)
        k_hat[:, cols] = (c * r).astype(BF)
        k_rate[:, cols] = r.astype(BF)
        k_low[:, cols] = (c * r * kg[...]).astype(BF)
        if first:
            c, r = head_norm(q_raw[:, cols], matrix)
            q_hat[:, cols] = (c * r).astype(BF)
            q_rate[:, cols] = r.astype(BF)
            q[:, cols] = (c * r * qg[...] * (float(HD) ** -0.5)).astype(BF)

    bias[...] = jnp.where(idq == idk[...], 0.0, -1e30)
    stat[...] = jnp.zeros_like(stat) if first else total_in[...]
    masks = pair_masks(p.shape[0])
    lanes = lax.broadcasted_iota(jnp.int32, stat.shape, 1)

    @pl.loop(0, 2 * half // LANES)
    def _(pair):
        cols = lane(pair, LANES)
        q_pair, k_pair, v_pair = q[:, cols], k_low[:, cols], v_low[:, cols]
        outs = []
        for s, mask in enumerate(masks):
            e = jnp.exp(dot_nt(pick(q_pair, mask), k_pair) + bias[...])
            total = jnp.sum(e, axis=-1, keepdims=True)
            got = dot_nn(e.astype(BF), v_pair)
            if not first:
                got = got + acc[:, cols]
            h = 2 * pair + s
            if last:
                total = total + column(stat, h)
                got = got * (1.0 / total)
                stat[...] = jnp.where(lanes == h, jnp.log(total), stat[...])
            else:
                stat[...] += jnp.where(lanes == h, total, 0.0)
            outs.append(got)
        out[:, cols] = jnp.where(masks[0], outs[0], outs[1]).astype(out.dtype)

    if last:
        write_rows(total_out, stat[...])
    else:
        total_out[...] = stat[...]


def look(first, last, p, g1, b1, qg, kg, idq, idk, parts, before):
    tokens, width = p.shape
    half = width // 2
    wide = (tokens, width)
    outs = [(wide, BF)] * 5
    outs += [(wide, BF if last else F4)]
    outs += [((8, 2 * padded(tokens)) if last else (tokens, LANES), F4)]
    if first:
        outs += [(wide, BF)] * 3
    flops = 2 * tokens * width * (width * (3 if first else 2) + 4 * tokens)
    body = functools.partial(look_body, first, last, half)
    scratch = [pltpu.VMEM((tokens, tokens), F4), pltpu.VMEM((tokens, LANES), F4)]
    scratch += [pltpu.VMEM(wide, F4)] * (2 if first else 1)
    extra = (qg,) if first else before
    return call(
        body, outs, scratch, 5, flops, p, g1, b1, kg, idq, idk, *parts, *extra
    )


ROOT = math.sqrt(2.0 / math.pi)
CUBE = 0.044715


def gelu_pair(u):
    square = u * u
    t = jnp.tanh(ROOT * u * (1.0 + CUBE * square))
    half = 0.5 * (1.0 + t)
    slope = half + 0.5 * u * (1.0 - t * t) * (ROOT * (1.0 + 3.0 * CUBE * square))
    return u * half, slope


def up_body(half, p, att, cot, g2, b2, b1o, b1x, b2o, b2x, *outs):
    mixed, n2, act, slope, g1o, g1x, g2o, g2x = outs
    first = b1o.shape[1]
    inner = first + b2o.shape[1] - half
    m = p[...].astype(F4)
    for s, part in enumerate((b2o, b2x)):
        m = m + dot_nt(att[:, s * half : (s + 1) * half], part[:, :half])
    mixed[...] = m
    c, r = centre(m)
    n2[...] = (c * r * g2[...] + b2[...]).astype(BF)
    for s, (one, two) in enumerate(((b1o, b2o), (b1x, b2x))):

        @pl.loop(0, tiles(first))
        def _(i):
            u = dot_nn(n2[...], one[:, lane(i, TILE)])
            to = pl.ds(pl.multiple_of(s * inner + i * TILE, TILE), TILE)
            a, d = gelu_pair(u)
            act[:, to] = a.astype(BF)
            slope[:, to] = d.astype(BF)

        rest = inner - first
        for i in range(tiles(rest)):
            u = dot_nn(n2[...], two[:, half + i * TILE : half + (i + 1) * TILE])
            to = slice(s * inner + first + i * TILE, s * inner + first + (i + 1) * TILE)
            a, d = gelu_pair(u)
            act[:, to] = a.astype(BF)
            slope[:, to] = d.astype(BF)
    mid = g1o.shape[1]
    for s, (one, two) in enumerate(((g1o, g2o), (g1x, g2x))):
        for base, out in ((s * inner, one), (s * inner + mid, two)):

            @pl.loop(0, tiles(mid))
            def _(i):
                frm = pl.ds(pl.multiple_of(base + i * TILE, TILE), TILE)
                out[:, lane(i, TILE)] = dot_tn(cot[...], act[:, frm]).astype(BF)


def slope_body(half, *refs):
    mixed, slope, att, cot, g2 = refs[:5]
    b1o, b1x, b2o, b2x, c1o, c1x, c2o, c2x = refs[5:13]
    d_up, d_mixed, d_att, delta, gains = refs[13:]
    first = b1o.shape[1]
    inner = first + b2o.shape[1] - half
    mid = c1o.shape[1]
    for s, (one, two) in enumerate(((c1o, c2o), (c1x, c2x))):
        at = s * inner
        for base, part in ((at, one), (at + mid, two)):

            @pl.loop(0, tiles(mid))
            def _(i):
                to = pl.ds(pl.multiple_of(base + i * TILE, TILE), TILE)
                d = dot_nn(cot[...], part[:, lane(i, TILE)])
                d_up[:, to] = (d * slope[:, to].astype(F4)).astype(BF)

    e = jnp.zeros(mixed.shape, F4)
    for s, (one, two) in enumerate(((b1o, b2o), (b1x, b2x))):
        at = s * inner
        e = e + dot_nt(d_up[:, at : at + first], one[...])
        e = e + dot_nt(d_up[:, at + first : at + inner], two[:, half:])
    c, r = centre(mixed[...])
    t = e * g2[...]
    d_mixed[...] = cot[...].astype(F4) + r * (
        t - mean_last(t) - c * (r * r) * mean_last(t * c)
    )
    gains[0:1, :] = jnp.sum(e * c * r, axis=0, keepdims=True)
    gains[1:2, :] = jnp.sum(e, axis=0, keepdims=True)
    d_branch = d_mixed[...].astype(BF)
    row = lax.broadcasted_iota(jnp.int32, (half, LANES), 0) // HD
    col = lax.broadcasted_iota(jnp.int32, (half, LANES), 1)
    sums = jnp.zeros((mixed.shape[0], LANES), F4)
    for s, part in enumerate((b2o, b2x)):
        cols = slice(s * half, (s + 1) * half)
        d = dot_nn(d_branch, part[:, :half]).astype(BF)
        d_att[:, cols] = d
        prod = d.astype(F4) * att[:, cols].astype(F4)
        high = prod.astype(BF)
        low = (prod - high.astype(F4)).astype(BF)
        sel = jnp.where(row + s * (half // HD) == col, 1.0, 0.0).astype(BF)
        sums = sums + dot_nn(high, sel) + dot_nn(low, sel)
    write_rows(delta, sums)


def inner_body(half, *refs):
    mixed, n2, act, att, d_up, d_mixed, c1o, c1x, c2o, c2x = refs[:10]
    result, h1o, h1x, h2o, h2x = refs[10:]
    first = h1o.shape[1]
    inner = first + h2o.shape[1] - half
    mid = c1o.shape[1]
    out = mixed[...]
    for s, (one, two) in enumerate(((c1o, c2o), (c1x, c2x))):
        at = s * inner
        out = out + dot_nt(act[:, at : at + mid], one[...])
        out = out + dot_nt(act[:, at + mid : at + inner], two[...])
    result[...] = out.astype(BF)
    d_branch = d_mixed[...].astype(BF)
    for s, (one, two) in enumerate(((h1o, h2o), (h1x, h2x))):
        at = s * inner
        two[:, :half] = dot_tn(d_branch, att[:, s * half : (s + 1) * half]).astype(BF)

        @pl.loop(0, tiles(first))
        def _(i):
            frm = pl.ds(pl.multiple_of(at + i * TILE, TILE), TILE)
            one[:, lane(i, TILE)] = dot_tn(n2[...], d_up[:, frm]).astype(BF)

        two[:, half:] = dot_tn(n2[...], d_up[:, at + first : at + inner]).astype(BF)


def back_body(half, j, *refs):
    q, k, v, d_att, stat, delta, idq, ids, k_hat, k_rate, kg = refs[:11]
    a1o, a1x, a2o, a2x = refs[11:15]
    dk_low, dv_low, dq, part, k_gain, bias, dk, q_cat, d_cat = refs[15:]
    tokens = q.shape[0]
    step = padded(tokens)
    bias[...] = jnp.where(ids[j * tokens : (j + 1) * tokens, :] == idq[...], 0.0, -1e30)
    q_cat[...] = jnp.zeros_like(q_cat)
    d_cat[...] = jnp.zeros_like(d_cat)
    masks = pair_masks(tokens)

    @pl.loop(0, q.shape[1] // LANES)
    def _(pair):
        cols = lane(pair, LANES)
        k_pair, v_pair = k[:, cols], v[:, cols]
        for s, mask in enumerate(masks):
            q_cat[s * step : s * step + tokens, :] = pick(q[:, cols], mask)
            d_cat[s * step : s * step + tokens, :] = pick(d_att[:, cols], mask)
        row = pl.ds(pair, 1)
        prob = jnp.exp(dot_nt(k_pair, q_cat[...]) + bias[...] - stat[row, :])
        d_prob = dot_nt(v_pair, d_cat[...])
        d_score = (prob * (d_prob - delta[row, :])).astype(BF)
        dv_low[:, cols] = dot_nn(prob.astype(BF), d_cat[...]).astype(BF)
        dk[:, cols] = dot_nn(d_score, q_cat[...])
        both = dot_tn(d_score, k_pair)
        dq[:, cols] = jnp.where(masks[0], both[:tokens], both[step : step + tokens])

    matrix = group_matrix()
    total = jnp.zeros((1, TILE), F4)
    for t in range(tiles(2 * half)):
        cols = slice(t * TILE, (t + 1) * TILE)
        d, g = head_norm_back(
            dk[:, cols], k_hat[:, cols], k_rate[:, cols], kg[...], matrix
        )
        dk_low[:, cols] = d.astype(BF)
        total = total + fold_heads(g)
    k_gain[...] = total
    cut = a1o.shape[1]
    e = jnp.zeros((tokens, 2 * half), F4)
    for s, (one, two) in enumerate(((a1o, a2o), (a1x, a2x))):
        at = s * half
        mid = at + cut - half
        e = e + dot_nt(dk_low[:, at:mid], one[:, half:])
        e = e + dot_nt(dk_low[:, mid : at + half], two[:, : 2 * half - cut])
        e = e + dot_nt(dv_low[:, at : at + half], two[:, 2 * half - cut :])
    part[...] = e.astype(part.dtype)


def back_block(
    weight, j, q, k, v, d_att, stat, delta, idq, ids, k_hat, k_rate, kg, parts
):
    tokens, width = q.shape
    wide, step = (tokens, width), padded(tokens)
    outs = [(wide, BF), (wide, BF), (wide, F4), (wide, F4 if j == 0 else BF)]
    outs += [((1, TILE), F4)]
    scratch = [pltpu.VMEM((tokens, 2 * step), F4), pltpu.VMEM(wide, F4)]
    scratch += [pltpu.VMEM((2 * step, LANES), BF)] * 2
    flops = 10 * tokens * tokens * width * 4 + 4 * tokens * width * width
    body = functools.partial(back_body, width // 2, j)
    return call(
        body, outs, scratch, 8, flops,
        q, k, v, d_att, stat, delta, idq, ids, k_hat, k_rate, kg, *parts,
        weight=weight,
    )


def weight_body(n, half, *refs):
    q_hat, q_rate, qg, own = refs[:4]
    a1o, a1x = refs[4:6]
    dqs, ns = refs[6 : 6 + n], refs[6 + n : 6 + 2 * n]
    dks, dvs = refs[6 + 2 * n : 6 + 3 * n], refs[6 + 3 * n : 6 + 4 * n]
    part, q_gain, g1o, g1x, g2o, g2x, dq_low, n_all, dk_all, dv_all = refs[6 + 4 * n :]
    tokens = q_hat.shape[0]
    matrix = group_matrix()
    total = jnp.zeros((1, TILE), F4)
    factor = float(HD) ** -0.5
    for t in range(tiles(2 * half)):
        cols = slice(t * TILE, (t + 1) * TILE)
        e = dqs[0][:, cols]
        for other in dqs[1:]:
            e = e + other[:, cols]
        d, g = head_norm_back(
            e * factor, q_hat[:, cols], q_rate[:, cols], qg[...], matrix
        )
        dq_low[:, cols] = d.astype(BF)
        total = total + fold_heads(g)
    q_gain[...] = total
    e = dot_nt(dq_low[:, :half], a1o[:, :half]) + dot_nt(dq_low[:, half:], a1x[:, :half])
    part[...] = own[...] + e
    for b in range(n):
        rows = slice(b * tokens, (b + 1) * tokens)
        n_all[rows, :] = ns[b][...]
        dk_all[rows, :] = dks[b][...]
        dv_all[rows, :] = dvs[b][...]
    cut = g1o.shape[1]
    for s, (one, two) in enumerate(((g1o, g2o), (g1x, g2x))):
        at = s * half
        mid = at + cut - half
        one[:, :half] = dot_tn(ns[0][...], dq_low[:, at : at + half]).astype(BF)
        one[:, half:] = dot_tn(n_all[...], dk_all[:, at:mid]).astype(BF)
        two[:, : 2 * half - cut] = dot_tn(n_all[...], dk_all[:, mid : at + half]).astype(BF)
        two[:, 2 * half - cut :] = dot_tn(n_all[...], dv_all[:, at : at + half]).astype(BF)


def input_body(own, rest, p, g1, d_mixed, second, query, *refs):
    keys, (out, small) = refs[:-2], refs[-2:]
    e = own[...] + rest[...].astype(F4)
    c, r = centre(p[...].astype(F4))
    hat = c * r
    t = e * g1[...]
    out[...] = d_mixed[...] + r * (t - mean_last(t) - hat * mean_last(t * hat))
    small[...] = jnp.zeros_like(small)
    small[0:1, :] = jnp.sum(e * hat, axis=0, keepdims=True)
    small[1:2, :] = jnp.sum(e, axis=0, keepdims=True)
    small[2:4, :] = second[...]
    small[4:5, :HD] = fold_lanes(query[...])
    total = keys[0][...]
    for x in keys[1:]:
        total = total + x[...]
    small[5:6, :HD] = fold_lanes(total)


def take_micro(x, c):
    mine = jnp.where(c0, x[0], x[1])
    other = jnp.where(c0, x[1], x[0])
    return mine, other


def per_device(
    patches,
    picture_ids,
    ln1_gain,
    ln1_bias,
    w_query,
    w_key,
    w_value,
    q_gain,
    k_gain,
    w_out,
    ln2_gain,
    ln2_bias,
    w_up,
    w_down,
    cotangent,
):
    n = lax.axis_size("row")
    at = Place()
    c0 = at("c")
    width = patches.shape[-1]
    half = w_query.shape[1]
    piece = patches.shape[2]
    tokens = 2 * piece
    inner = w_up.shape[1]

    cut_a = half + half * 2 // 3
    first = inner * 2 // 3
    mid = inner // 2
    width_b = inner + half
    whole = not regular(w_query.shape[0])
    chunk_a = jnp.concatenate([w_query, w_key, w_value], axis=1)
    chunk_b = jnp.concatenate([w_up[:, :first], w_out.T, w_up[:, first:]], axis=1)
    line_a = Chain(line_steps(chunk_a, at, True))
    line_b = Chain(line_steps(chunk_b, at))

    def back_home(x):
        lower, upper = x[:piece], x[piece:]
        keep = jnp.where(c0, lower, upper)
        got = swap_core(jnp.where(c0, upper, lower))
        whole = jnp.stack([jnp.where(c0, keep, got), jnp.where(c0, got, keep)])
        return whole[None], got

    def take(x):
        mine = jnp.where(c0, x[0], x[1])
        got = swap_core(jnp.where(c0, x[1], x[0]))
        return jnp.concatenate(
            [jnp.where(c0, mine, got), jnp.where(c0, got, mine)], axis=0
        )

    g1, b1 = ln1_gain[None], ln1_bias[None]
    g2, b2 = ln2_gain[None], ln2_bias[None]
    qg, kg = jnp.tile(q_gain, TILE // HD)[None], jnp.tile(k_gain, TILE // HD)[None]
    ids = jnp.where(c0, picture_ids[0, 0], picture_ids[0, 1]).reshape(n, tokens)
    id_blocks = [index(ids, at("row", j), keepdims=True) for j in range(n)]
    ids = jnp.concatenate(id_blocks, axis=1).reshape(n * tokens, 1)
    spare = jnp.full((1, padded(tokens) - tokens), -1, jnp.int32)
    idq = jnp.concatenate([id_blocks[0], spare] * 2, axis=1)
    ready = lax.optimization_barrier((g1, b1, g2, b2, qg, kg, ids, idq, *id_blocks))
    g1, b1, g2, b2, qg, kg, ids, idq, *id_blocks = ready

    line_a.step()
    p_own = take(patches[0])
    blocks = [p_own, hop(p_own, n)]
    got_a = line_a.last
    rows_a = line_a.step(*ready).finish()
    chain_a = Chain(plane_steps((rows_a[:, :cut_a], rows_a[:, cut_a:]), whole, at))
    chain_a.step()
    line_b.step(*got_a)
    chain_a.step()
    for _ in range(n - 2):
        line_b.step()
    got_b = line_b.last
    rows_b = line_b.finish()
    a_one, a_two = chain_a.finish()
    swap_a = chain_a.last
    a_parts = a_one + a_two
    cot = take(cotangent[0])
    line_c = Chain(line_steps(after(w_down.T, got_b), at)).step()
    chain_b = Chain(plane_steps((rows_b[:, :first], rows_b[:, first:]), whole, at))

    made, marks = [], []
    before = token = ()
    deps = got_b
    for j in range(n):
        if 0 < j < n - 1:
            blocks.append(hop(after(blocks[j], marks[-1] if j > 1 else got_b), n))
        if j in (0, 1, n - 1):
            chain_b.step(*token)
        if 0 < j < n - 1:
            line_c.step(*token)
        if j == n - 1:
            rows_c = line_c.finish()
            chain_c = Chain(plane_steps((rows_c[:, :mid], rows_c[:, mid:]), whole, at))
            chain_c.step()
        made.append(
            look(
                j == 0, j == n - 1, after(blocks[j], deps), g1, b1, qg, kg, ids,
                id_blocks[j], a_parts, before,
            )
        )
        if j == 0:
            q_hat, q_rate, q_low = made[0][7:]
        before = (q_low, *made[j][5:7])
        token = (made[j][6],)
        marks.append(token)
        deps = token + (chain_c.last if j == n - 1 else line_c.last)
        if j != 1 or n < 4:
            deps = deps + chain_b.last
    normed = [m[0] for m in made]
    k_hat, k_rate, k_low, v_low = [[m[i] for m in made] for i in (1, 2, 3, 4)]
    att, stat = made[-1][5:7]

    b_one, b_two = chain_b.finish()
    b_parts = b_one + b_two
    chain_c.step(*token)
    mixed, n2, act, slope, *gc = call(
        functools.partial(up_body, half),
        [((tokens, width), F4), ((tokens, width), BF)]
        + [((tokens, 2 * inner), BF)] * 2
        + [((width, mid), BF)] * 4,
        [], 6,
        2 * tokens * width * (width + 4 * inner),
        p_own, after(att, deps), cot, g2, b2, *b_parts,
    )
    c_one, c_two = chain_c.step(mixed).finish()
    c_parts = c_one + c_two

    back_c = Chain(plane_sums((gc[0], gc[1]), (gc[2], gc[3]), whole, at)).step()
    deps = back_c.last
    back_c.step()
    d_up, d_mixed, d_att, delta, gains2 = call(
        functools.partial(slope_body, half),
        [((tokens, 2 * inner), BF), ((tokens, width), F4), ((tokens, width), BF)]
        + [((8, 2 * padded(tokens)), F4), ((2, width), F4)],
        [], 9,
        2 * tokens * width * (width + 4 * inner),
        after(mixed, deps), slope, att, cot, g2, *b_parts, *c_parts,
    )
    back = [None] * n
    back_b = acc = None
    deps = (delta,)
    for turn, j in enumerate([*range(1, n), 0]):
        back[j] = back_block(
            0.1 if turn in (0, n - 1) else 4.0,
            j, q_low, k_low[j], v_low[j], after(d_att, deps), stat, delta, idq, ids,
            k_hat[j], k_rate[j], kg, a_parts,
        )
        token = back[j][4]
        deps = (token,)
        if turn != 1:
            deps = deps + back_c.last
            back_c.step(token)
        if back_b is not None and turn != n - 2:
            deps = deps + back_b.last
            back_b.step(token)
        if turn == 0:
            result, *gb = call(
                functools.partial(inner_body, half),
                [((tokens, width), BF)]
                + [((width, first), BF)] * 2
                + [((width, half + inner - first), BF)] * 2,
                [], 8,
                2 * tokens * width * (width + 4 * inner),
                mixed, n2, act, att, d_up, after(d_mixed, deps), *c_parts,
            )
            deps = (result,)
            result, got = back_home(result)
            back_b = Chain(plane_sums((gb[0], gb[1]), (gb[2], gb[3]), whole, at)).step()
        elif turn > 0:
            deps = deps + (got,)
        if j:
            part = back[j][3]
            if acc is None:
                acc = part
            else:
                deps = deps + (acc,)
                acc = add_low(part, acc)
            acc = hop(acc, n)
    deps = deps + (acc,)
    part, dq_gain, *ga = call(
        functools.partial(weight_body, n, half),
        [((tokens, width), F4), ((1, TILE), F4)]
        + [((width, cut_a), BF)] * 2
        + [((width, 3 * half - cut_a), BF)] * 2,
        [pltpu.VMEM((tokens, width), BF)] + [pltpu.VMEM((n * tokens, width), BF)] * 3,
        10,
        2 * tokens * width * width * (2 + 2 * n),
        after(q_hat, deps), q_rate, qg, back[0][3], *a_one,
        *[b[2] for b in back], *normed, *[b[0] for b in back], *[b[1] for b in back],
        weight=0.1,
    )
    back_a = Chain(plane_sums((ga[0], ga[1]), (ga[2], ga[3]), whole, at))
    back_a.step(acc, *back_b.last)
    sum_b, sum_c = back_b.step(dq_gain).finish(), back_c.finish()
    both = jnp.concatenate([sum_b, sum_c], axis=1)
    line = Chain(line_sums(both, whole, at)).step()
    grad_in, small = call(
        input_body, [((tokens, width), F4), ((8, width), F4)], [], 6, 0,
        part, acc, p_own, g1, d_mixed, gains2, dq_gain, *[b[4] for b in back],
    )
    sums = Chain(sum_steps(small)).step()
    while back_a.value is None:
        deps = back_a.last
        back_a.step(*deps)
        sums.step(*deps)
        line.step(*sums.last)
    last_a = Chain(line_sums(back_a.value, whole, at, True)).step()
    sums.step(*last_a.last)
    last_a.finish()
    sums.finish()
    grad_a, grad_bc = last_a.value, line.finish()
    grad_b, grad_c = grad_bc[:, :width_b], grad_bc[:, width_b:]
    small = sums.value
    grad_g1, grad_b1, grad_g2, grad_b2 = small[0], small[1], small[2], small[3]
    grad_gq, grad_gk = small[4, :HD], small[5, :HD]

    rest = half + first
    grad_wu = jnp.concatenate([grad_b[:, :first], grad_b[:, rest:]], axis=1)
    return (
        result,
        back_home(grad_in)[0],
        grad_g1,
        grad_b1,
        grad_a[:, :half],
        grad_a[:, half : 2 * half],
        grad_a[:, 2 * half :],
        grad_gq,
        grad_gk,
        grad_b[:, first:rest].T,
        grad_g2,
        grad_b2,
        grad_wu,
        grad_c.T,
    )


def solution(mesh):
    rows = P("dp", None, ("row", "col"), None)
    inward = P(("dp", "row"), "col")
    outward = P("col", ("dp", "row"))
    return jax.shard_map(
        per_device,
        mesh=mesh,
        in_specs=(
            rows, P("dp", None, None), P(), P(), inward, inward, inward, P(), P(),
            outward, P(), P(), inward, outward, rows,
        ),
        out_specs=(
            rows, rows, P(), P(), inward, inward, inward, P(), P(),
            outward, P(), P(), inward, outward,
        ),
        check_vma=False,
    )
```

```python
import functools
import math

import jax
import jax.numpy as jnp
from jax import lax
from jax.experimental import pallas as pl
from jax.experimental.pallas import tpu as pltpu
from jax.sharding import PartitionSpec as P

HD = 64
LANES = 128
TILE = 256
EPSILON = 1e-06
BF = jnp.bfloat16
F4 = jnp.float32
VM = pl.BlockSpec(memory_space=pltpu.VMEM)


def ring_order(n):
    return list(range(0, n, 2)) + list(range(n - 1 - (n % 2), 0, -2))


def ring_place(r, n):
    return jnp.where(r % 2 == 0, r // 2, n - 1 - r // 2 - (n % 2) + (n % 2) * 1)


def ring_row(q, n):
    return jnp.where(2 * q < n, 2 * q, 2 * (n - 1 - q) + 1)


class Place:
    def __init__(self):
        n, m = lax.axis_size("row"), lax.axis_size("dp")
        place = ring_place(lax.axis_index("row"), n)
        me = lax.axis_index("dp")
        made = {("c",): lax.axis_index("col") == 0}
        for bit in range(m.bit_length() - 1):
            one = (me >> bit) & 1
            made["low", bit] = one == 0
            made["one", bit] = one
            made["zero", bit] = 1 - one
        for r in range(n):
            slot = (place - ring_order(n).index(r) + n) % n
            for k in range(n - 1):
                made["slot", r, k] = slot == k
        for r in range(n):
            for k in range(n - 1):
                made["far", r, k] = lax.axis_index("row") == r ^ k
        for k in range(n):
            made["pair", k] = lax.axis_index("row") ^ k
        for step in range(n):
            made["row", step] = ring_row((place - step + n) % n, n)
        names = list(made)
        self.made = dict(zip(names, lax.optimization_barrier(tuple(made.values()))))

    def __call__(self, *name):
        return self.made[name]


def index(x, i, axis=0, keepdims=False):
    return lax.dynamic_index_in_dim(
        x, i, axis, keepdims=keepdims, allow_negative_indices=False
    )


def hop(x, n):
    order = ring_order(n)
    pairs = [(order[i], order[(i + 1) % n]) for i in range(n)]
    return lax.ppermute(x, "row", pairs)


def swap_bit(x, axis, n, bit):
    return lax.ppermute(x, axis, [(i, i ^ (1 << bit)) for i in range(n)])


def swap_core(x):
    return lax.ppermute(x, "col", [(0, 1), (1, 0)])


def bit_orders(n):
    bits = list(range(n.bit_length() - 1))
    half = len(bits) // 2
    return bits, bits[half:] + bits[:half]


def regular(block):
    dp = lax.axis_size("dp")
    return dp & (dp - 1) == 0 and block % 16 == 0


def after(x, deps):
    if not deps:
        return x
    return lax.optimization_barrier((x, *deps))[0]


def all_after(xs, deps):
    if not deps:
        return tuple(xs)
    return lax.optimization_barrier((*xs, *deps))[: len(xs)]


class Chain:
    def __init__(self, steps):
        self.steps = steps
        self.last = ()
        self.value = None
        next(steps)

    def step(self, *deps):
        if self.value is None:
            try:
                self.last = self.steps.send(deps)
            except StopIteration as end:
                self.value = end.value
        return self

    def finish(self):
        while self.value is None:
            self.step()
        return self.value


def join_line(blocks, at, kind="slot"):
    n = len(blocks)
    parts = []
    for r in range(n):
        x = blocks[-1]
        for k in range(n - 1):
            x = jnp.where(at(kind, r, k), blocks[k], x)
        parts.append(x)
    return jnp.concatenate(parts, axis=0)


def straight(n):
    return n & (n - 1) == 0 and n <= 4


def line_steps(shard, at, at_once=False):
    deps = yield ()
    shard = after(shard, deps)
    if not regular(shard.shape[0]):
        return shard
    n = lax.axis_size("row")
    blocks = [shard]
    if at_once and straight(n):
        for k in range(1, n):
            pairs = [(i, i ^ k) for i in range(n)]
            blocks.append(lax.ppermute(shard, "row", pairs))
        deps = yield tuple(blocks[1:])
        blocks[1:] = all_after(blocks[1:], deps)
        return join_line(blocks, at, "far")
    for _ in range(n - 1):
        got = hop(blocks[-1], n)
        deps = yield (got,)
        blocks.append(after(got, deps))
    return join_line(blocks, at)


def plane_steps(parts, whole, at):
    deps = yield ()
    m = lax.axis_size("dp")
    parts = list(parts)
    if whole:
        both = lax.all_gather(
            jnp.concatenate(parts, axis=1), ("dp", "row"), axis=0, tiled=True
        )
        deps = yield (both,)
        both, cut = after(both, deps), parts[0].shape[1]
        parts = [both[:, :cut], both[:, cut:]]
    else:
        done = ([], [])
        for bits in zip(*bit_orders(m)):
            got = [swap_bit(x, "dp", m, bit) for x, bit in zip(parts, bits)]
            deps = yield tuple(got)
            got = all_after(got, deps)
            for i, bit in enumerate(bits):
                axis = sum(1 for b in done[i] if b > bit)
                low = at("low", bit)
                first = jnp.where(low, parts[i], got[i])
                second = jnp.where(low, got[i], parts[i])
                parts[i] = jnp.stack([first, second], axis=axis)
                done[i].append(bit)
        parts = [x.reshape(-1, x.shape[-1]) for x in parts]
    got = [swap_core(x) for x in parts]
    yield tuple(got)
    return (parts[0], got[0]), (parts[1], got[1])


def add_low(a, b):
    return (a.astype(F4) + b.astype(F4)).astype(BF)


def plane_sums(one, two, whole, at):
    m = lax.axis_size("dp")
    deps = yield ()
    got = [swap_core(x) for x in all_after((one[1], two[1]), deps)]
    deps = yield tuple(got)
    parts = [add_low(x[0], y) for x, y in zip((one, two), all_after(got, deps))]
    if whole:
        return jnp.concatenate(parts, axis=1)
    count = m.bit_length() - 1
    left = [list(range(count - 1, -1, -1)), list(range(count - 1, -1, -1))]
    parts = [x.reshape((2,) * count + (-1, x.shape[-1])) for x in parts]
    for bits in zip(*bit_orders(m)):
        got, keep = [], []
        for i, bit in enumerate(bits):
            axis = left[i].index(bit)
            got.append(swap_bit(index(parts[i], at("zero", bit), axis), "dp", m, bit))
            keep.append(index(parts[i], at("one", bit), axis))
            left[i].remove(bit)
        deps = yield tuple(got)
        parts = [add_low(x, y) for x, y in zip(keep, all_after(got, deps))]
    return jnp.concatenate(parts, axis=1)


def line_sums(both, whole, at, at_once=False):
    deps = yield ()
    both = after(both, deps)
    if whole:
        total = lax.psum_scatter(both, ("dp", "row"), scatter_dimension=0, tiled=True)
        yield (total,)
        return total.astype(F4)
    n = lax.axis_size("row")
    both = both.reshape(n, -1, both.shape[-1])
    if at_once and straight(n):
        got = [
            lax.ppermute(index(both, at("pair", k)), "row", [(i, i ^ k) for i in range(n)])
            for k in range(1, n)
        ]
        deps = yield tuple(got)
        total = index(both, at("pair", 0)).astype(F4)
        for x in all_after(got, deps):
            total = total + x.astype(F4)
        return total
    acc = index(both, at("row", 1))
    for step in range(n - 1):
        got = hop(acc, n)
        deps = yield (got,)
        got = after(got, deps)
        if step < n - 2:
            acc = add_low(index(both, at("row", step + 2)), got)
    return index(both, at("row", 0)).astype(F4) + got.astype(F4)


def sum_steps(x):
    deps = yield ()
    x = after(x, deps)
    for axis in ("dp", "row", "col"):
        n = lax.axis_size(axis)
        for bit in range(n.bit_length() - 1) if n & (n - 1) == 0 else (None,):
            got = lax.psum(x, axis) - x if bit is None else swap_bit(x, axis, n, bit)
            deps = yield (got,)
            x = x + after(got, deps)
    return x


def dot_nn(a, b):
    return jnp.dot(a, b, preferred_element_type=F4)


def dot_nt(a, b):
    return lax.dot_general(a, b, (((1,), (1,)), ((), ())), preferred_element_type=F4)


def dot_tn(a, b):
    return lax.dot_general(a, b, (((0,), (0,)), ((), ())), preferred_element_type=F4)


def mean_last(x):
    return jnp.mean(x, axis=-1, keepdims=True)


def centre(x):
    c = x - mean_last(x)
    return c, lax.rsqrt(mean_last(c * c) + EPSILON)


def group_matrix():
    i = lax.broadcasted_iota(jnp.int32, (TILE, TILE), 0) // HD
    j = lax.broadcasted_iota(jnp.int32, (TILE, TILE), 1) // HD
    return jnp.where(i == j, 1.0 / HD, 0.0).astype(BF)


def group_mean(x, matrix):
    high = x.astype(BF)
    low = (x - high.astype(F4)).astype(BF)
    return dot_nn(high, matrix) + dot_nn(low, matrix)


def head_norm(x, matrix):
    c = x - group_mean(x, matrix)
    return c, lax.rsqrt(group_mean(c * c, matrix) + EPSILON)


def low_mean(x, matrix):
    return dot_nn(x.astype(BF), matrix)


def head_norm_back(e, hat, rate, gain, matrix):
    t = e * gain
    hat, rate = hat.astype(F4), rate.astype(F4)
    d = rate * (t - low_mean(t, matrix) - hat * low_mean(t * hat, matrix))
    return d, e * hat


def fold_heads(x):
    return jnp.sum(x, axis=0, keepdims=True)


def padded(rows):
    return -(-rows // LANES) * LANES


def head_rows(columns):
    rows = columns.shape[0]
    pair = lax.broadcasted_iota(jnp.int32, (8, LANES), 0)
    at = lax.broadcasted_iota(jnp.int32, (8, LANES), 1)
    parts = []
    for s in (0, 1):
        sel = jnp.where(at == 2 * pair + s, 1.0, 0.0)
        parts.append(
            lax.dot_general(
                sel, columns, (((1,), (1,)), ((), ())),
                precision=lax.Precision.HIGHEST, preferred_element_type=F4,
            )
        )
    return parts, padded(rows)


def fold_lanes(x):
    return sum(x[:, i * HD : (i + 1) * HD] for i in range(TILE // HD))


def tiles(width):
    return width // TILE


def lane(i, width):
    return pl.ds(pl.multiple_of(i * width, width), width)


def call(body, outs, scratch, room, flops, *args, weight=4.0):
    size = sum(a.size * a.dtype.itemsize for a in args)
    size += sum(math.prod(s) * jnp.dtype(d).itemsize for s, d in outs)
    hold = sum(math.prod(s.shape) * jnp.dtype(s.dtype).itemsize for s in scratch)
    return pl.pallas_call(
        body,
        out_shape=[jax.ShapeDtypeStruct(s, d) for s, d in outs],
        in_specs=[VM] * len(args),
        out_specs=[VM] * len(outs),
        scratch_shapes=scratch,
        compiler_params=pltpu.CompilerParams(vmem_limit_bytes=hold + (room << 20)),
        cost_estimate=pl.CostEstimate(
            flops=int(flops * weight), bytes_accessed=int(size), transcendentals=0
        ),
    )(*args)


def pair_masks(rows):
    at = lax.broadcasted_iota(jnp.int32, (rows, LANES), 1)
    return (at < HD, at >= HD)


def pick(x, mask):
    return jnp.where(mask, x, jnp.zeros_like(x))


def write_rows(ref, columns):
    parts, step = head_rows(columns)
    ref[...] = jnp.zeros_like(ref)
    for s, x in enumerate(parts):
        ref[:, s * step : s * step + x.shape[1]] = x


def column(ref, h):
    at = lax.broadcasted_iota(jnp.int32, ref.shape, 1)
    return jnp.sum(jnp.where(at == h, ref[...], 0.0), axis=-1, keepdims=True)


def look_body(first, last, half, *refs):
    p, g1, b1, kg, ids, idk, a1o, a1x, a2o, a2x = refs[:10]
    idq = ids[: p.shape[0], :]
    refs = refs[10:]
    if first:
        qg, normed, k_hat, k_rate, k_low, v_low, out, total_out = refs[:8]
        q_hat, q_rate, q, bias, stat, k_raw, q_raw = refs[8:]
    else:
        q, acc, total_in, normed, k_hat, k_rate, k_low, v_low, out, total_out = refs[:10]
        bias, stat, k_raw = refs[10:]
    x = p[...].astype(F4)
    c, r = centre(x)
    n = (c * r * g1[...] + b1[...]).astype(BF)
    normed[...] = n
    head = 0 if first else half
    cut = a1o.shape[1]
    for s, (a1, a2) in enumerate(((a1o, a2o), (a1x, a2x))):
        at = s * half
        one = dot_nn(n, a1[:, head:])
        two = dot_nn(n, a2[...])
        if first:
            q_raw[:, at : at + half] = one[:, :half]
        k_raw[:, at : at + cut - half] = one[:, half - head :]
        k_raw[:, at + cut - half : at + half] = two[:, : 2 * half - cut]
        v_low[:, at : at + half] = two[:, 2 * half - cut :].astype(BF)
    matrix = group_matrix()
    for t in range(tiles(2 * half)):
        cols = slice(t * TILE, (t + 1) * TILE)
        c, r = head_norm(k_raw[:, cols], matrix)
        k_hat[:, cols] = (c * r).astype(BF)
        k_rate[:, cols] = r.astype(BF)
        k_low[:, cols] = (c * r * kg[...]).astype(BF)
        if first:
            c, r = head_norm(q_raw[:, cols], matrix)
            q_hat[:, cols] = (c * r).astype(BF)
            q_rate[:, cols] = r.astype(BF)
            q[:, cols] = (c * r * qg[...] * (float(HD) ** -0.5)).astype(BF)

    bias[...] = jnp.where(idq == idk[...], 0.0, -1e30)
    stat[...] = jnp.zeros_like(stat) if first else total_in[...]
    masks = pair_masks(p.shape[0])
    lanes = lax.broadcasted_iota(jnp.int32, stat.shape, 1)

    @pl.loop(0, 2 * half // LANES)
    def _(pair):
        cols = lane(pair, LANES)
        q_pair, k_pair, v_pair = q[:, cols], k_low[:, cols], v_low[:, cols]
        outs = []
        for s, mask in enumerate(masks):
            e = jnp.exp(dot_nt(pick(q_pair, mask), k_pair) + bias[...])
            total = jnp.sum(e, axis=-1, keepdims=True)
            got = dot_nn(e.astype(BF), v_pair)
            if not first:
                got = got + acc[:, cols]
            h = 2 * pair + s
            if last:
                total = total + column(stat, h)
                got = got * (1.0 / total)
                stat[...] = jnp.where(lanes == h, jnp.log(total), stat[...])
            else:
                stat[...] += jnp.where(lanes == h, total, 0.0)
            outs.append(got)
        out[:, cols] = jnp.where(masks[0], outs[0], outs[1]).astype(out.dtype)

    if last:
        write_rows(total_out, stat[...])
    else:
        total_out[...] = stat[...]


def look(weight, first, last, p, g1, b1, qg, kg, idq, idk, parts, before):
    tokens, width = p.shape
    half = width // 2
    wide = (tokens, width)
    outs = [(wide, BF)] * 5
    outs += [(wide, BF if last else F4)]
    outs += [((8, 2 * padded(tokens)) if last else (tokens, LANES), F4)]
    if first:
        outs += [(wide, BF)] * 3
    flops = 2 * tokens * width * (width * (3 if first else 2) + 4 * tokens)
    body = functools.partial(look_body, first, last, half)
    scratch = [pltpu.VMEM((tokens, tokens), F4), pltpu.VMEM((tokens, LANES), F4)]
    scratch += [pltpu.VMEM(wide, F4)] * (2 if first else 1)
    extra = (qg,) if first else before
    return call(
        body, outs, scratch, 5, flops, p, g1, b1, kg, idq, idk, *parts, *extra,
        weight=weight,
    )


ROOT = math.sqrt(2.0 / math.pi)
CUBE = 0.044715


def gelu_pair(u):
    square = u * u
    t = jnp.tanh(ROOT * u * (1.0 + CUBE * square))
    half = 0.5 * (1.0 + t)
    slope = half + 0.5 * u * (1.0 - t * t) * (ROOT * (1.0 + 3.0 * CUBE * square))
    return u * half, slope


def up_body(half, p, att, cot, g2, b2, b1o, b1x, b2o, b2x, *outs):
    mixed, n2, act, slope, g1o, g1x, g2o, g2x = outs
    first = b1o.shape[1]
    inner = first + b2o.shape[1] - half
    m = p[...].astype(F4)
    for s, part in enumerate((b2o, b2x)):
        m = m + dot_nt(att[:, s * half : (s + 1) * half], part[:, :half])
    mixed[...] = m
    c, r = centre(m)
    n2[...] = (c * r * g2[...] + b2[...]).astype(BF)
    for s, (one, two) in enumerate(((b1o, b2o), (b1x, b2x))):

        @pl.loop(0, tiles(first))
        def _(i):
            u = dot_nn(n2[...], one[:, lane(i, TILE)])
            to = pl.ds(pl.multiple_of(s * inner + i * TILE, TILE), TILE)
            a, d = gelu_pair(u)
            act[:, to] = a.astype(BF)
            slope[:, to] = d.astype(BF)

        rest = inner - first
        for i in range(tiles(rest)):
            u = dot_nn(n2[...], two[:, half + i * TILE : half + (i + 1) * TILE])
            to = slice(s * inner + first + i * TILE, s * inner + first + (i + 1) * TILE)
            a, d = gelu_pair(u)
            act[:, to] = a.astype(BF)
            slope[:, to] = d.astype(BF)
    mid = g1o.shape[1]
    for s, (one, two) in enumerate(((g1o, g2o), (g1x, g2x))):
        for base, out in ((s * inner, one), (s * inner + mid, two)):

            @pl.loop(0, tiles(mid))
            def _(i):
                frm = pl.ds(pl.multiple_of(base + i * TILE, TILE), TILE)
                out[:, lane(i, TILE)] = dot_tn(cot[...], act[:, frm]).astype(BF)


def slope_body(half, *refs):
    mixed, slope, att, cot, g2 = refs[:5]
    b1o, b1x, b2o, b2x, c1o, c1x, c2o, c2x = refs[5:13]
    d_up, d_mixed, d_att, delta, gains = refs[13:]
    first = b1o.shape[1]
    inner = first + b2o.shape[1] - half
    mid = c1o.shape[1]
    for s, (one, two) in enumerate(((c1o, c2o), (c1x, c2x))):
        at = s * inner
        for base, part in ((at, one), (at + mid, two)):

            @pl.loop(0, tiles(mid))
            def _(i):
                to = pl.ds(pl.multiple_of(base + i * TILE, TILE), TILE)
                d = dot_nn(cot[...], part[:, lane(i, TILE)])
                d_up[:, to] = (d * slope[:, to].astype(F4)).astype(BF)

    e = jnp.zeros(mixed.shape, F4)
    for s, (one, two) in enumerate(((b1o, b2o), (b1x, b2x))):
        at = s * inner
        e = e + dot_nt(d_up[:, at : at + first], one[...])
        e = e + dot_nt(d_up[:, at + first : at + inner], two[:, half:])
    c, r = centre(mixed[...])
    t = e * g2[...]
    d_mixed[...] = cot[...].astype(F4) + r * (
        t - mean_last(t) - c * (r * r) * mean_last(t * c)
    )
    gains[0:1, :] = jnp.sum(e * c * r, axis=0, keepdims=True)
    gains[1:2, :] = jnp.sum(e, axis=0, keepdims=True)
    d_branch = d_mixed[...].astype(BF)
    row = lax.broadcasted_iota(jnp.int32, (half, LANES), 0) // HD
    col = lax.broadcasted_iota(jnp.int32, (half, LANES), 1)
    sums = jnp.zeros((mixed.shape[0], LANES), F4)
    for s, part in enumerate((b2o, b2x)):
        cols = slice(s * half, (s + 1) * half)
        d = dot_nn(d_branch, part[:, :half]).astype(BF)
        d_att[:, cols] = d
        prod = d.astype(F4) * att[:, cols].astype(F4)
        high = prod.astype(BF)
        low = (prod - high.astype(F4)).astype(BF)
        sel = jnp.where(row + s * (half // HD) == col, 1.0, 0.0).astype(BF)
        sums = sums + dot_nn(high, sel) + dot_nn(low, sel)
    write_rows(delta, sums)


def inner_body(half, *refs):
    mixed, n2, act, att, d_up, d_mixed, c1o, c1x, c2o, c2x = refs[:10]
    result, h1o, h1x, h2o, h2x = refs[10:]
    first = h1o.shape[1]
    inner = first + h2o.shape[1] - half
    mid = c1o.shape[1]
    out = mixed[...]
    for s, (one, two) in enumerate(((c1o, c2o), (c1x, c2x))):
        at = s * inner
        out = out + dot_nt(act[:, at : at + mid], one[...])
        out = out + dot_nt(act[:, at + mid : at + inner], two[...])
    result[...] = out.astype(BF)
    d_branch = d_mixed[...].astype(BF)
    for s, (one, two) in enumerate(((h1o, h2o), (h1x, h2x))):
        at = s * inner
        two[:, :half] = dot_tn(d_branch, att[:, s * half : (s + 1) * half]).astype(BF)

        @pl.loop(0, tiles(first))
        def _(i):
            frm = pl.ds(pl.multiple_of(at + i * TILE, TILE), TILE)
            one[:, lane(i, TILE)] = dot_tn(n2[...], d_up[:, frm]).astype(BF)

        two[:, half:] = dot_tn(n2[...], d_up[:, at + first : at + inner]).astype(BF)


def back_body(half, j, *refs):
    q, k, v, d_att, stat, delta, idq, ids, k_hat, k_rate, kg = refs[:11]
    a1o, a1x, a2o, a2x = refs[11:15]
    dk_low, dv_low, dq, part, k_gain, bias, dk, q_cat, d_cat = refs[15:]
    tokens = q.shape[0]
    step = padded(tokens)
    bias[...] = jnp.where(ids[j * tokens : (j + 1) * tokens, :] == idq[...], 0.0, -1e30)
    q_cat[...] = jnp.zeros_like(q_cat)
    d_cat[...] = jnp.zeros_like(d_cat)
    masks = pair_masks(tokens)

    @pl.loop(0, q.shape[1] // LANES)
    def _(pair):
        cols = lane(pair, LANES)
        k_pair, v_pair = k[:, cols], v[:, cols]
        for s, mask in enumerate(masks):
            q_cat[s * step : s * step + tokens, :] = pick(q[:, cols], mask)
            d_cat[s * step : s * step + tokens, :] = pick(d_att[:, cols], mask)
        row = pl.ds(pair, 1)
        prob = jnp.exp(dot_nt(k_pair, q_cat[...]) + bias[...] - stat[row, :])
        d_prob = dot_nt(v_pair, d_cat[...])
        d_score = (prob * (d_prob - delta[row, :])).astype(BF)
        dv_low[:, cols] = dot_nn(prob.astype(BF), d_cat[...]).astype(BF)
        dk[:, cols] = dot_nn(d_score, q_cat[...])
        both = dot_tn(d_score, k_pair)
        dq[:, cols] = jnp.where(masks[0], both[:tokens], both[step : step + tokens])

    matrix = group_matrix()
    total = jnp.zeros((1, TILE), F4)
    for t in range(tiles(2 * half)):
        cols = slice(t * TILE, (t + 1) * TILE)
        d, g = head_norm_back(
            dk[:, cols], k_hat[:, cols], k_rate[:, cols], kg[...], matrix
        )
        dk_low[:, cols] = d.astype(BF)
        total = total + fold_heads(g)
    k_gain[...] = total
    cut = a1o.shape[1]
    e = jnp.zeros((tokens, 2 * half), F4)
    for s, (one, two) in enumerate(((a1o, a2o), (a1x, a2x))):
        at = s * half
        mid = at + cut - half
        e = e + dot_nt(dk_low[:, at:mid], one[:, half:])
        e = e + dot_nt(dk_low[:, mid : at + half], two[:, : 2 * half - cut])
        e = e + dot_nt(dv_low[:, at : at + half], two[:, 2 * half - cut :])
    part[...] = e.astype(part.dtype)


def back_block(
    weight, j, q, k, v, d_att, stat, delta, idq, ids, k_hat, k_rate, kg, parts
):
    tokens, width = q.shape
    wide, step = (tokens, width), padded(tokens)
    outs = [(wide, BF), (wide, BF), (wide, F4), (wide, F4 if j == 0 else BF)]
    outs += [((1, TILE), F4)]
    scratch = [pltpu.VMEM((tokens, 2 * step), F4), pltpu.VMEM(wide, F4)]
    scratch += [pltpu.VMEM((2 * step, LANES), BF)] * 2
    flops = 10 * tokens * tokens * width * 4 + 4 * tokens * width * width
    body = functools.partial(back_body, width // 2, j)
    return call(
        body, outs, scratch, 8, flops,
        q, k, v, d_att, stat, delta, idq, ids, k_hat, k_rate, kg, *parts,
        weight=weight,
    )


def weight_body(n, half, *refs):
    q_hat, q_rate, qg, own = refs[:4]
    a1o, a1x = refs[4:6]
    dqs, ns = refs[6 : 6 + n], refs[6 + n : 6 + 2 * n]
    dks, dvs = refs[6 + 2 * n : 6 + 3 * n], refs[6 + 3 * n : 6 + 4 * n]
    part, q_gain, g1o, g1x, g2o, g2x, dq_low, n_all, dk_all, dv_all = refs[6 + 4 * n :]
    tokens = q_hat.shape[0]
    matrix = group_matrix()
    total = jnp.zeros((1, TILE), F4)
    factor = float(HD) ** -0.5
    for t in range(tiles(2 * half)):
        cols = slice(t * TILE, (t + 1) * TILE)
        e = dqs[0][:, cols]
        for other in dqs[1:]:
            e = e + other[:, cols]
        d, g = head_norm_back(
            e * factor, q_hat[:, cols], q_rate[:, cols], qg[...], matrix
        )
        dq_low[:, cols] = d.astype(BF)
        total = total + fold_heads(g)
    q_gain[...] = total
    e = dot_nt(dq_low[:, :half], a1o[:, :half]) + dot_nt(dq_low[:, half:], a1x[:, :half])
    part[...] = own[...] + e
    for b in range(n):
        rows = slice(b * tokens, (b + 1) * tokens)
        n_all[rows, :] = ns[b][...]
        dk_all[rows, :] = dks[b][...]
        dv_all[rows, :] = dvs[b][...]
    cut = g1o.shape[1]
    for s, (one, two) in enumerate(((g1o, g2o), (g1x, g2x))):
        at = s * half
        mid = at + cut - half
        one[:, :half] = dot_tn(ns[0][...], dq_low[:, at : at + half]).astype(BF)
        one[:, half:] = dot_tn(n_all[...], dk_all[:, at:mid]).astype(BF)
        two[:, : 2 * half - cut] = dot_tn(n_all[...], dk_all[:, mid : at + half]).astype(BF)
        two[:, 2 * half - cut :] = dot_tn(n_all[...], dv_all[:, at : at + half]).astype(BF)


def input_body(own, rest, p, g1, d_mixed, second, query, *refs):
    keys, (out, small) = refs[:-2], refs[-2:]
    e = own[...] + rest[...].astype(F4)
    c, r = centre(p[...].astype(F4))
    hat = c * r
    t = e * g1[...]
    out[...] = d_mixed[...] + r * (t - mean_last(t) - hat * mean_last(t * hat))
    small[...] = jnp.zeros_like(small)
    small[0:1, :] = jnp.sum(e * hat, axis=0, keepdims=True)
    small[1:2, :] = jnp.sum(e, axis=0, keepdims=True)
    small[2:4, :] = second[...]
    small[4:5, :HD] = fold_lanes(query[...])
    total = keys[0][...]
    for x in keys[1:]:
        total = total + x[...]
    small[5:6, :HD] = fold_lanes(total)


def take_micro(x, c):
    mine = jnp.where(c0, x[0], x[1])
    other = jnp.where(c0, x[1], x[0])
    return mine, other


def per_device(
    patches,
    picture_ids,
    ln1_gain,
    ln1_bias,
    w_query,
    w_key,
    w_value,
    q_gain,
    k_gain,
    w_out,
    ln2_gain,
    ln2_bias,
    w_up,
    w_down,
    cotangent,
):
    n = lax.axis_size("row")
    at = Place()
    c0 = at("c")
    width = patches.shape[-1]
    half = w_query.shape[1]
    piece = patches.shape[2]
    tokens = 2 * piece
    inner = w_up.shape[1]

    cut_a = half + half * 2 // 3
    first = inner * 2 // 3
    mid = inner // 2
    width_b = inner + half
    whole = not regular(w_query.shape[0])
    chunk_a = jnp.concatenate([w_query, w_key, w_value], axis=1)
    chunk_b = jnp.concatenate([w_up[:, :first], w_out.T, w_up[:, first:]], axis=1)
    line_a = Chain(line_steps(chunk_a, at, True))
    line_b = Chain(line_steps(chunk_b, at))

    def back_home(x):
        lower, upper = x[:piece], x[piece:]
        keep = jnp.where(c0, lower, upper)
        got = swap_core(jnp.where(c0, upper, lower))
        whole = jnp.stack([jnp.where(c0, keep, got), jnp.where(c0, got, keep)])
        return whole[None], got

    def take(x):
        mine = jnp.where(c0, x[0], x[1])
        got = swap_core(jnp.where(c0, x[1], x[0]))
        return jnp.concatenate(
            [jnp.where(c0, mine, got), jnp.where(c0, got, mine)], axis=0
        )

    g1, b1 = ln1_gain[None], ln1_bias[None]
    g2, b2 = ln2_gain[None], ln2_bias[None]
    qg, kg = jnp.tile(q_gain, TILE // HD)[None], jnp.tile(k_gain, TILE // HD)[None]
    ids = jnp.where(c0, picture_ids[0, 0], picture_ids[0, 1]).reshape(n, tokens)
    id_blocks = [index(ids, at("row", j), keepdims=True) for j in range(n)]
    ids = jnp.concatenate(id_blocks, axis=1).reshape(n * tokens, 1)
    spare = jnp.full((1, padded(tokens) - tokens), -1, jnp.int32)
    idq = jnp.concatenate([id_blocks[0], spare] * 2, axis=1)
    ready = lax.optimization_barrier((g1, b1, g2, b2, qg, kg, ids, idq, *id_blocks))
    g1, b1, g2, b2, qg, kg, ids, idq, *id_blocks = ready

    line_a.step()
    p_own = take(patches[0])
    blocks = [p_own, hop(p_own, n)]
    got_a = line_a.last
    rows_a = line_a.step(*ready).finish()
    chain_a = Chain(plane_steps((rows_a[:, :cut_a], rows_a[:, cut_a:]), whole, at))
    chain_a.step()
    line_b.step(*got_a)
    chain_a.step()
    for _ in range(n - 2):
        line_b.step()
    got_b = line_b.last
    rows_b = line_b.finish()
    a_one, a_two = chain_a.finish()
    swap_a = chain_a.last
    a_parts = a_one + a_two
    cot = take(cotangent[0])
    line_c = Chain(line_steps(w_down.T, at, True))
    chain_b = Chain(plane_steps((rows_b[:, :first], rows_b[:, first:]), whole, at))

    made, marks = [], []
    before = token = ()
    deps = got_b
    for j in range(n):
        if 0 < j < n - 1:
            blocks.append(hop(after(blocks[j], marks[-1] if j > 1 else got_b), n))
        if j in (0, 1, n - 1):
            chain_b.step(*token)
        if j == 1:
            line_c.step(*token)
        if j == n - 1:
            rows_c = line_c.finish()
            chain_c = Chain(plane_steps((rows_c[:, :mid], rows_c[:, mid:]), whole, at))
            chain_c.step()
        made.append(
            look(
                0.1 if j == n - 2 else 4.0,
                j == 0, j == n - 1, after(blocks[j], deps), g1, b1, qg, kg, ids,
                id_blocks[j], a_parts, before,
            )
        )
        if j == 0:
            q_hat, q_rate, q_low = made[0][7:]
        before = (q_low, *made[j][5:7])
        token = (made[j][6],)
        marks.append(token)
        deps = token + (chain_c.last if j == n - 1 else line_c.last)
        if j != 1 or n < 4:
            deps = deps + chain_b.last
    normed = [m[0] for m in made]
    k_hat, k_rate, k_low, v_low = [[m[i] for m in made] for i in (1, 2, 3, 4)]
    att, stat = made[-1][5:7]

    b_one, b_two = chain_b.finish()
    b_parts = b_one + b_two
    chain_c.step(*token)
    mixed, n2, act, slope, *gc = call(
        functools.partial(up_body, half),
        [((tokens, width), F4), ((tokens, width), BF)]
        + [((tokens, 2 * inner), BF)] * 2
        + [((width, mid), BF)] * 4,
        [], 6,
        2 * tokens * width * (width + 4 * inner),
        p_own, after(att, deps), cot, g2, b2, *b_parts,
    )
    c_one, c_two = chain_c.step(mixed).finish()
    c_parts = c_one + c_two

    back_c = Chain(plane_sums((gc[0], gc[1]), (gc[2], gc[3]), whole, at)).step()
    deps = back_c.last
    back_c.step()
    d_up, d_mixed, d_att, delta, gains2 = call(
        functools.partial(slope_body, half),
        [((tokens, 2 * inner), BF), ((tokens, width), F4), ((tokens, width), BF)]
        + [((8, 2 * padded(tokens)), F4), ((2, width), F4)],
        [], 9,
        2 * tokens * width * (width + 4 * inner),
        after(mixed, deps), slope, att, cot, g2, *b_parts, *c_parts,
    )
    back = [None] * n
    back_b = acc = None
    deps = (delta,)
    for turn, j in enumerate([*range(1, n), 0]):
        back[j] = back_block(
            0.1 if turn in (0, n - 1) else 4.0,
            j, q_low, k_low[j], v_low[j], after(d_att, deps), stat, delta, idq, ids,
            k_hat[j], k_rate[j], kg, a_parts,
        )
        token = back[j][4]
        deps = (token,)
        if turn != 1:
            deps = deps + back_c.last
            back_c.step(token)
        if back_b is not None and turn != n - 2:
            deps = deps + back_b.last
            back_b.step(token)
        if turn == 0:
            result, *gb = call(
                functools.partial(inner_body, half),
                [((tokens, width), BF)]
                + [((width, first), BF)] * 2
                + [((width, half + inner - first), BF)] * 2,
                [], 8,
                2 * tokens * width * (width + 4 * inner),
                mixed, n2, act, att, d_up, after(d_mixed, deps), *c_parts,
            )
            deps = (result,)
            result, got = back_home(result)
            back_b = Chain(plane_sums((gb[0], gb[1]), (gb[2], gb[3]), whole, at)).step()
        elif turn > 0:
            deps = deps + (got,)
        if j:
            part = back[j][3]
            if acc is None:
                acc = part
            else:
                deps = deps + (acc,)
                acc = add_low(part, acc)
            acc = hop(acc, n)
    deps = deps + (acc,)
    part, dq_gain, *ga = call(
        functools.partial(weight_body, n, half),
        [((tokens, width), F4), ((1, TILE), F4)]
        + [((width, cut_a), BF)] * 2
        + [((width, 3 * half - cut_a), BF)] * 2,
        [pltpu.VMEM((tokens, width), BF)] + [pltpu.VMEM((n * tokens, width), BF)] * 3,
        10,
        2 * tokens * width * width * (2 + 2 * n),
        after(q_hat, deps), q_rate, qg, back[0][3], *a_one,
        *[b[2] for b in back], *normed, *[b[0] for b in back], *[b[1] for b in back],
        weight=0.1,
    )
    back_a = Chain(plane_sums((ga[0], ga[1]), (ga[2], ga[3]), whole, at))
    back_a.step(acc, *back_b.last)
    sum_b, sum_c = back_b.step(dq_gain).finish(), back_c.finish()
    both = jnp.concatenate([sum_b, sum_c], axis=1)
    line = Chain(line_sums(both, whole, at)).step()
    grad_in, small = call(
        input_body, [((tokens, width), F4), ((8, width), F4)], [], 6, 0,
        part, acc, p_own, g1, d_mixed, gains2, dq_gain, *[b[4] for b in back],
    )
    sums = Chain(sum_steps(small)).step()
    while back_a.value is None:
        deps = back_a.last
        back_a.step(*deps)
        sums.step(*deps)
        line.step(*sums.last)
    last_a = Chain(line_sums(back_a.value, whole, at, True)).step()
    sums.step(*last_a.last)
    last_a.finish()
    sums.finish()
    grad_a, grad_bc = last_a.value, line.finish()
    grad_b, grad_c = grad_bc[:, :width_b], grad_bc[:, width_b:]
    small = sums.value
    grad_g1, grad_b1, grad_g2, grad_b2 = small[0], small[1], small[2], small[3]
    grad_gq, grad_gk = small[4, :HD], small[5, :HD]

    rest = half + first
    grad_wu = jnp.concatenate([grad_b[:, :first], grad_b[:, rest:]], axis=1)
    return (
        result,
        back_home(grad_in)[0],
        grad_g1,
        grad_b1,
        grad_a[:, :half],
        grad_a[:, half : 2 * half],
        grad_a[:, 2 * half :],
        grad_gq,
        grad_gk,
        grad_b[:, first:rest].T,
        grad_g2,
        grad_b2,
        grad_wu,
        grad_c.T,
    )


def solution(mesh):
    rows = P("dp", None, ("row", "col"), None)
    inward = P(("dp", "row"), "col")
    outward = P("col", ("dp", "row"))
    return jax.shard_map(
        per_device,
        mesh=mesh,
        in_specs=(
            rows, P("dp", None, None), P(), P(), inward, inward, inward, P(), P(),
            outward, P(), P(), inward, outward, rows,
        ),
        out_specs=(
            rows, rows, P(), P(), inward, inward, inward, P(), P(),
            outward, P(), P(), inward, outward,
        ),
        check_vma=False,
    )
```

```python
import functools
import math

import jax
import jax.numpy as jnp
from jax import lax
from jax.experimental import pallas as pl
from jax.experimental.pallas import tpu as pltpu
from jax.sharding import PartitionSpec as P

HD = 64
LANES = 128
TILE = 256
EPSILON = 1e-06
BF = jnp.bfloat16
F4 = jnp.float32
VM = pl.BlockSpec(memory_space=pltpu.VMEM)


def ring_order(n):
    return list(range(0, n, 2)) + list(range(n - 1 - (n % 2), 0, -2))


def ring_place(r, n):
    return jnp.where(r % 2 == 0, r // 2, n - 1 - r // 2 - (n % 2) + (n % 2) * 1)


def ring_row(q, n):
    return jnp.where(2 * q < n, 2 * q, 2 * (n - 1 - q) + 1)


class Place:
    def __init__(self):
        n, m = lax.axis_size("row"), lax.axis_size("dp")
        place = ring_place(lax.axis_index("row"), n)
        me = lax.axis_index("dp")
        made = {("c",): lax.axis_index("col") == 0}
        for bit in range(m.bit_length() - 1):
            one = (me >> bit) & 1
            made["low", bit] = one == 0
            made["one", bit] = one
            made["zero", bit] = 1 - one
        for r in range(n):
            slot = (place - ring_order(n).index(r) + n) % n
            for k in range(n - 1):
                made["slot", r, k] = slot == k
        for r in range(n):
            for k in range(n - 1):
                made["far", r, k] = lax.axis_index("row") == r ^ k
        for k in range(n):
            made["pair", k] = lax.axis_index("row") ^ k
        for step in range(n):
            made["row", step] = ring_row((place - step + n) % n, n)
        names = list(made)
        self.made = dict(zip(names, lax.optimization_barrier(tuple(made.values()))))

    def __call__(self, *name):
        return self.made[name]


def index(x, i, axis=0, keepdims=False):
    return lax.dynamic_index_in_dim(
        x, i, axis, keepdims=keepdims, allow_negative_indices=False
    )


def hop(x, n):
    order = ring_order(n)
    pairs = [(order[i], order[(i + 1) % n]) for i in range(n)]
    return lax.ppermute(x, "row", pairs)


def swap_bit(x, axis, n, bit):
    return lax.ppermute(x, axis, [(i, i ^ (1 << bit)) for i in range(n)])


def swap_core(x):
    return lax.ppermute(x, "col", [(0, 1), (1, 0)])


def bit_orders(n):
    bits = list(range(n.bit_length() - 1))
    half = len(bits) // 2
    return bits, bits[half:] + bits[:half]


def regular(block):
    dp = lax.axis_size("dp")
    return dp & (dp - 1) == 0 and block % 16 == 0


def after(x, deps):
    if not deps:
        return x
    return lax.optimization_barrier((x, *deps))[0]


def all_after(xs, deps):
    if not deps:
        return tuple(xs)
    return lax.optimization_barrier((*xs, *deps))[: len(xs)]


class Chain:
    def __init__(self, steps):
        self.steps = steps
        self.last = ()
        self.value = None
        next(steps)

    def step(self, *deps):
        if self.value is None:
            try:
                self.last = self.steps.send(deps)
            except StopIteration as end:
                self.value = end.value
        return self

    def finish(self):
        while self.value is None:
            self.step()
        return self.value


def join_line(blocks, at, kind="slot"):
    n = len(blocks)
    parts = []
    for r in range(n):
        x = blocks[-1]
        for k in range(n - 1):
            x = jnp.where(at(kind, r, k), blocks[k], x)
        parts.append(x)
    return jnp.concatenate(parts, axis=0)


def straight(n):
    return n & (n - 1) == 0 and n <= 4


def line_steps(shard, at, at_once=False):
    deps = yield ()
    shard = after(shard, deps)
    if not regular(shard.shape[0]):
        return shard
    n = lax.axis_size("row")
    blocks = [shard]
    if at_once and straight(n):
        for k in range(1, n):
            pairs = [(i, i ^ k) for i in range(n)]
            blocks.append(lax.ppermute(shard, "row", pairs))
        deps = yield tuple(blocks[1:])
        blocks[1:] = all_after(blocks[1:], deps)
        return join_line(blocks, at, "far")
    for _ in range(n - 1):
        got = hop(blocks[-1], n)
        deps = yield (got,)
        blocks.append(after(got, deps))
    return join_line(blocks, at)


def plane_steps(parts, whole, at):
    deps = yield ()
    m = lax.axis_size("dp")
    parts = list(parts)
    if whole:
        both = lax.all_gather(
            jnp.concatenate(parts, axis=1), ("dp", "row"), axis=0, tiled=True
        )
        deps = yield (both,)
        both, cut = after(both, deps), parts[0].shape[1]
        parts = [both[:, :cut], both[:, cut:]]
    else:
        done = ([], [])
        for bits in zip(*bit_orders(m)):
            got = [swap_bit(x, "dp", m, bit) for x, bit in zip(parts, bits)]
            deps = yield tuple(got)
            got = all_after(got, deps)
            for i, bit in enumerate(bits):
                axis = sum(1 for b in done[i] if b > bit)
                low = at("low", bit)
                first = jnp.where(low, parts[i], got[i])
                second = jnp.where(low, got[i], parts[i])
                parts[i] = jnp.stack([first, second], axis=axis)
                done[i].append(bit)
        parts = [x.reshape(-1, x.shape[-1]) for x in parts]
    got = [swap_core(x) for x in parts]
    yield tuple(got)
    return (parts[0], got[0]), (parts[1], got[1])


def add_low(a, b):
    return (a.astype(F4) + b.astype(F4)).astype(BF)


def plane_sums(one, two, whole, at):
    m = lax.axis_size("dp")
    deps = yield ()
    got = [swap_core(x) for x in all_after((one[1], two[1]), deps)]
    deps = yield tuple(got)
    parts = [add_low(x[0], y) for x, y in zip((one, two), all_after(got, deps))]
    if whole:
        return jnp.concatenate(parts, axis=1)
    count = m.bit_length() - 1
    left = [list(range(count - 1, -1, -1)), list(range(count - 1, -1, -1))]
    parts = [x.reshape((2,) * count + (-1, x.shape[-1])) for x in parts]
    for bits in zip(*bit_orders(m)):
        got, keep = [], []
        for i, bit in enumerate(bits):
            axis = left[i].index(bit)
            got.append(swap_bit(index(parts[i], at("zero", bit), axis), "dp", m, bit))
            keep.append(index(parts[i], at("one", bit), axis))
            left[i].remove(bit)
        deps = yield tuple(got)
        parts = [add_low(x, y) for x, y in zip(keep, all_after(got, deps))]
    return jnp.concatenate(parts, axis=1)


def line_sums(both, whole, at, at_once=False):
    deps = yield ()
    both = after(both, deps)
    if whole:
        total = lax.psum_scatter(both, ("dp", "row"), scatter_dimension=0, tiled=True)
        yield (total,)
        return total.astype(F4)
    n = lax.axis_size("row")
    both = both.reshape(n, -1, both.shape[-1])
    if at_once and straight(n):
        got = [
            lax.ppermute(index(both, at("pair", k)), "row", [(i, i ^ k) for i in range(n)])
            for k in range(1, n)
        ]
        deps = yield tuple(got)
        total = index(both, at("pair", 0)).astype(F4)
        for x in all_after(got, deps):
            total = total + x.astype(F4)
        return total
    acc = index(both, at("row", 1))
    for step in range(n - 1):
        got = hop(acc, n)
        deps = yield (got,)
        got = after(got, deps)
        if step < n - 2:
            acc = add_low(index(both, at("row", step + 2)), got)
    return index(both, at("row", 0)).astype(F4) + got.astype(F4)


def sum_steps(x):
    deps = yield ()
    x = after(x, deps)
    for axis in ("dp", "row", "col"):
        n = lax.axis_size(axis)
        for bit in range(n.bit_length() - 1) if n & (n - 1) == 0 else (None,):
            got = lax.psum(x, axis) - x if bit is None else swap_bit(x, axis, n, bit)
            deps = yield (got,)
            x = x + after(got, deps)
    return x


def dot_nn(a, b):
    return jnp.dot(a, b, preferred_element_type=F4)


def dot_nt(a, b):
    return lax.dot_general(a, b, (((1,), (1,)), ((), ())), preferred_element_type=F4)


def dot_tn(a, b):
    return lax.dot_general(a, b, (((0,), (0,)), ((), ())), preferred_element_type=F4)


def mean_last(x):
    return jnp.mean(x, axis=-1, keepdims=True)


def centre(x):
    c = x - mean_last(x)
    return c, lax.rsqrt(mean_last(c * c) + EPSILON)


def group_matrix():
    i = lax.broadcasted_iota(jnp.int32, (TILE, TILE), 0) // HD
    j = lax.broadcasted_iota(jnp.int32, (TILE, TILE), 1) // HD
    return jnp.where(i == j, 1.0 / HD, 0.0).astype(BF)


def group_mean(x, matrix):
    high = x.astype(BF)
    low = (x - high.astype(F4)).astype(BF)
    return dot_nn(high, matrix) + dot_nn(low, matrix)


def head_norm(x, matrix):
    c = x - group_mean(x, matrix)
    return c, lax.rsqrt(group_mean(c * c, matrix) + EPSILON)


def low_mean(x, matrix):
    return dot_nn(x.astype(BF), matrix)


def head_norm_back(e, hat, rate, gain, matrix):
    t = e * gain
    hat, rate = hat.astype(F4), rate.astype(F4)
    d = rate * (t - low_mean(t, matrix) - hat * low_mean(t * hat, matrix))
    return d, e * hat


def fold_heads(x):
    return jnp.sum(x, axis=0, keepdims=True)


def padded(rows):
    return -(-rows // LANES) * LANES


def head_rows(columns):
    rows = columns.shape[0]
    pair = lax.broadcasted_iota(jnp.int32, (8, LANES), 0)
    at = lax.broadcasted_iota(jnp.int32, (8, LANES), 1)
    parts = []
    for s in (0, 1):
        sel = jnp.where(at == 2 * pair + s, 1.0, 0.0)
        parts.append(
            lax.dot_general(
                sel, columns, (((1,), (1,)), ((), ())),
                precision=lax.Precision.HIGHEST, preferred_element_type=F4,
            )
        )
    return parts, padded(rows)


def fold_lanes(x):
    return sum(x[:, i * HD : (i + 1) * HD] for i in range(TILE // HD))


def tiles(width):
    return width // TILE


def lane(i, width):
    return pl.ds(pl.multiple_of(i * width, width), width)


def call(body, outs, scratch, room, flops, *args, weight=4.0):
    size = sum(a.size * a.dtype.itemsize for a in args)
    size += sum(math.prod(s) * jnp.dtype(d).itemsize for s, d in outs)
    hold = sum(math.prod(s.shape) * jnp.dtype(s.dtype).itemsize for s in scratch)
    return pl.pallas_call(
        body,
        out_shape=[jax.ShapeDtypeStruct(s, d) for s, d in outs],
        in_specs=[VM] * len(args),
        out_specs=[VM] * len(outs),
        scratch_shapes=scratch,
        compiler_params=pltpu.CompilerParams(vmem_limit_bytes=hold + (room << 20)),
        cost_estimate=pl.CostEstimate(
            flops=int(flops * weight), bytes_accessed=int(size), transcendentals=0
        ),
    )(*args)


def pair_masks(rows):
    at = lax.broadcasted_iota(jnp.int32, (rows, LANES), 1)
    return (at < HD, at >= HD)


def pick(x, mask):
    return jnp.where(mask, x, jnp.zeros_like(x))


def write_rows(ref, columns):
    parts, step = head_rows(columns)
    ref[...] = jnp.zeros_like(ref)
    for s, x in enumerate(parts):
        ref[:, s * step : s * step + x.shape[1]] = x


def column(ref, h):
    at = lax.broadcasted_iota(jnp.int32, ref.shape, 1)
    return jnp.sum(jnp.where(at == h, ref[...], 0.0), axis=-1, keepdims=True)


def look_body(first, last, half, *refs):
    p, g1, b1, kg, ids, idk, a1o, a1x, a2o, a2x = refs[:10]
    idq = ids[: p.shape[0], :]
    refs = refs[10:]
    if first:
        qg, normed, k_hat, k_rate, k_low, v_low, out, total_out = refs[:8]
        q_hat, q_rate, q, bias, stat, k_raw, q_raw = refs[8:]
    else:
        q, acc, total_in, normed, k_hat, k_rate, k_low, v_low, out, total_out = refs[:10]
        bias, stat, k_raw = refs[10:]
    x = p[...].astype(F4)
    c, r = centre(x)
    n = (c * r * g1[...] + b1[...]).astype(BF)
    normed[...] = n
    head = 0 if first else half
    cut = a1o.shape[1]
    for s, (a1, a2) in enumerate(((a1o, a2o), (a1x, a2x))):
        at = s * half
        one = dot_nn(n, a1[:, head:])
        two = dot_nn(n, a2[...])
        if first:
            q_raw[:, at : at + half] = one[:, :half]
        k_raw[:, at : at + cut - half] = one[:, half - head :]
        k_raw[:, at + cut - half : at + half] = two[:, : 2 * half - cut]
        v_low[:, at : at + half] = two[:, 2 * half - cut :].astype(BF)
    matrix = group_matrix()
    for t in range(tiles(2 * half)):
        cols = slice(t * TILE, (t + 1) * TILE)
        c, r = head_norm(k_raw[:, cols], matrix)
        k_hat[:, cols] = (c * r).astype(BF)
        k_rate[:, cols] = r.astype(BF)
        k_low[:, cols] = (c * r * kg[...]).astype(BF)
        if first:
            c, r = head_norm(q_raw[:, cols], matrix)
            q_hat[:, cols] = (c * r).astype(BF)
            q_rate[:, cols] = r.astype(BF)
            q[:, cols] = (c * r * qg[...] * (float(HD) ** -0.5)).astype(BF)

    bias[...] = jnp.where(idq == idk[...], 0.0, -1e30)
    stat[...] = jnp.zeros_like(stat) if first else total_in[...]
    masks = pair_masks(p.shape[0])
    lanes = lax.broadcasted_iota(jnp.int32, stat.shape, 1)

    @pl.loop(0, 2 * half // LANES)
    def _(pair):
        cols = lane(pair, LANES)
        q_pair, k_pair, v_pair = q[:, cols], k_low[:, cols], v_low[:, cols]
        outs = []
        for s, mask in enumerate(masks):
            e = jnp.exp(dot_nt(pick(q_pair, mask), k_pair) + bias[...])
            total = jnp.sum(e, axis=-1, keepdims=True)
            got = dot_nn(e.astype(BF), v_pair)
            if not first:
                got = got + acc[:, cols]
            h = 2 * pair + s
            if last:
                total = total + column(stat, h)
                got = got * (1.0 / total)
                stat[...] = jnp.where(lanes == h, jnp.log(total), stat[...])
            else:
                stat[...] += jnp.where(lanes == h, total, 0.0)
            outs.append(got)
        out[:, cols] = jnp.where(masks[0], outs[0], outs[1]).astype(out.dtype)

    if last:
        write_rows(total_out, stat[...])
    else:
        total_out[...] = stat[...]


def look(weight, first, last, p, g1, b1, qg, kg, idq, idk, parts, before):
    tokens, width = p.shape
    half = width // 2
    wide = (tokens, width)
    outs = [(wide, BF)] * 5
    outs += [(wide, BF if last else F4)]
    outs += [((8, 2 * padded(tokens)) if last else (tokens, LANES), F4)]
    if first:
        outs += [(wide, BF)] * 3
    flops = 2 * tokens * width * (width * (3 if first else 2) + 4 * tokens)
    body = functools.partial(look_body, first, last, half)
    scratch = [pltpu.VMEM((tokens, tokens), F4), pltpu.VMEM((tokens, LANES), F4)]
    scratch += [pltpu.VMEM(wide, F4)] * (2 if first else 1)
    extra = (qg,) if first else before
    return call(
        body, outs, scratch, 5, flops, p, g1, b1, kg, idq, idk, *parts, *extra,
        weight=weight,
    )


ROOT = math.sqrt(2.0 / math.pi)
CUBE = 0.044715


def gelu_pair(u):
    square = u * u
    t = jnp.tanh(ROOT * u * (1.0 + CUBE * square))
    half = 0.5 * (1.0 + t)
    slope = half + 0.5 * u * (1.0 - t * t) * (ROOT * (1.0 + 3.0 * CUBE * square))
    return u * half, slope


def up_body(half, p, att, cot, g2, b2, b1o, b1x, b2o, b2x, *outs):
    mixed, n2, act, slope, g1o, g1x, g2o, g2x = outs
    first = b1o.shape[1]
    inner = first + b2o.shape[1] - half
    m = p[...].astype(F4)
    for s, part in enumerate((b2o, b2x)):
        m = m + dot_nt(att[:, s * half : (s + 1) * half], part[:, :half])
    mixed[...] = m
    c, r = centre(m)
    n2[...] = (c * r * g2[...] + b2[...]).astype(BF)
    for s, (one, two) in enumerate(((b1o, b2o), (b1x, b2x))):

        @pl.loop(0, tiles(first))
        def _(i):
            u = dot_nn(n2[...], one[:, lane(i, TILE)])
            to = pl.ds(pl.multiple_of(s * inner + i * TILE, TILE), TILE)
            a, d = gelu_pair(u)
            act[:, to] = a.astype(BF)
            slope[:, to] = d.astype(BF)

        rest = inner - first
        for i in range(tiles(rest)):
            u = dot_nn(n2[...], two[:, half + i * TILE : half + (i + 1) * TILE])
            to = slice(s * inner + first + i * TILE, s * inner + first + (i + 1) * TILE)
            a, d = gelu_pair(u)
            act[:, to] = a.astype(BF)
            slope[:, to] = d.astype(BF)
    mid = g1o.shape[1]
    for s, (one, two) in enumerate(((g1o, g2o), (g1x, g2x))):
        for base, out in ((s * inner, one), (s * inner + mid, two)):

            @pl.loop(0, tiles(mid))
            def _(i):
                frm = pl.ds(pl.multiple_of(base + i * TILE, TILE), TILE)
                out[:, lane(i, TILE)] = dot_tn(cot[...], act[:, frm]).astype(BF)


def slope_body(half, *refs):
    mixed, slope, att, cot, g2 = refs[:5]
    b1o, b1x, b2o, b2x, c1o, c1x, c2o, c2x = refs[5:13]
    d_up, d_mixed, d_att, delta, gains = refs[13:]
    first = b1o.shape[1]
    inner = first + b2o.shape[1] - half
    mid = c1o.shape[1]
    for s, (one, two) in enumerate(((c1o, c2o), (c1x, c2x))):
        at = s * inner
        for base, part in ((at, one), (at + mid, two)):

            @pl.loop(0, tiles(mid))
            def _(i):
                to = pl.ds(pl.multiple_of(base + i * TILE, TILE), TILE)
                d = dot_nn(cot[...], part[:, lane(i, TILE)])
                d_up[:, to] = (d * slope[:, to].astype(F4)).astype(BF)

    e = jnp.zeros(mixed.shape, F4)
    for s, (one, two) in enumerate(((b1o, b2o), (b1x, b2x))):
        at = s * inner
        e = e + dot_nt(d_up[:, at : at + first], one[...])
        e = e + dot_nt(d_up[:, at + first : at + inner], two[:, half:])
    c, r = centre(mixed[...])
    t = e * g2[...]
    d_mixed[...] = cot[...].astype(F4) + r * (
        t - mean_last(t) - c * (r * r) * mean_last(t * c)
    )
    gains[0:1, :] = jnp.sum(e * c * r, axis=0, keepdims=True)
    gains[1:2, :] = jnp.sum(e, axis=0, keepdims=True)
    d_branch = d_mixed[...].astype(BF)
    row = lax.broadcasted_iota(jnp.int32, (half, LANES), 0) // HD
    col = lax.broadcasted_iota(jnp.int32, (half, LANES), 1)
    sums = jnp.zeros((mixed.shape[0], LANES), F4)
    for s, part in enumerate((b2o, b2x)):
        cols = slice(s * half, (s + 1) * half)
        d = dot_nn(d_branch, part[:, :half]).astype(BF)
        d_att[:, cols] = d
        prod = d.astype(F4) * att[:, cols].astype(F4)
        high = prod.astype(BF)
        low = (prod - high.astype(F4)).astype(BF)
        sel = jnp.where(row + s * (half // HD) == col, 1.0, 0.0).astype(BF)
        sums = sums + dot_nn(high, sel) + dot_nn(low, sel)
    write_rows(delta, sums)


def inner_body(half, *refs):
    mixed, n2, act, att, d_up, d_mixed, c1o, c1x, c2o, c2x = refs[:10]
    result, h1o, h1x, h2o, h2x = refs[10:]
    first = h1o.shape[1]
    inner = first + h2o.shape[1] - half
    mid = c1o.shape[1]
    out = mixed[...]
    for s, (one, two) in enumerate(((c1o, c2o), (c1x, c2x))):
        at = s * inner
        out = out + dot_nt(act[:, at : at + mid], one[...])
        out = out + dot_nt(act[:, at + mid : at + inner], two[...])
    result[...] = out.astype(BF)
    d_branch = d_mixed[...].astype(BF)
    for s, (one, two) in enumerate(((h1o, h2o), (h1x, h2x))):
        at = s * inner
        two[:, :half] = dot_tn(d_branch, att[:, s * half : (s + 1) * half]).astype(BF)

        @pl.loop(0, tiles(first))
        def _(i):
            frm = pl.ds(pl.multiple_of(at + i * TILE, TILE), TILE)
            one[:, lane(i, TILE)] = dot_tn(n2[...], d_up[:, frm]).astype(BF)

        two[:, half:] = dot_tn(n2[...], d_up[:, at + first : at + inner]).astype(BF)


def back_body(half, j, *refs):
    q, k, v, d_att, stat, delta, idq, ids, k_hat, k_rate, kg = refs[:11]
    a1o, a1x, a2o, a2x = refs[11:15]
    dk_low, dv_low, dq, part, k_gain, bias, dk, q_cat, d_cat = refs[15:]
    tokens = q.shape[0]
    step = padded(tokens)
    bias[...] = jnp.where(ids[j * tokens : (j + 1) * tokens, :] == idq[...], 0.0, -1e30)
    q_cat[...] = jnp.zeros_like(q_cat)
    d_cat[...] = jnp.zeros_like(d_cat)
    masks = pair_masks(tokens)

    @pl.loop(0, q.shape[1] // LANES)
    def _(pair):
        cols = lane(pair, LANES)
        k_pair, v_pair = k[:, cols], v[:, cols]
        for s, mask in enumerate(masks):
            q_cat[s * step : s * step + tokens, :] = pick(q[:, cols], mask)
            d_cat[s * step : s * step + tokens, :] = pick(d_att[:, cols], mask)
        row = pl.ds(pair, 1)
        prob = jnp.exp(dot_nt(k_pair, q_cat[...]) + bias[...] - stat[row, :])
        d_prob = dot_nt(v_pair, d_cat[...])
        d_score = (prob * (d_prob - delta[row, :])).astype(BF)
        dv_low[:, cols] = dot_nn(prob.astype(BF), d_cat[...]).astype(BF)
        dk[:, cols] = dot_nn(d_score, q_cat[...])
        both = dot_tn(d_score, k_pair)
        dq[:, cols] = jnp.where(masks[0], both[:tokens], both[step : step + tokens])

    matrix = group_matrix()
    total = jnp.zeros((1, TILE), F4)
    for t in range(tiles(2 * half)):
        cols = slice(t * TILE, (t + 1) * TILE)
        d, g = head_norm_back(
            dk[:, cols], k_hat[:, cols], k_rate[:, cols], kg[...], matrix
        )
        dk_low[:, cols] = d.astype(BF)
        total = total + fold_heads(g)
    k_gain[...] = total
    cut = a1o.shape[1]
    e = jnp.zeros((tokens, 2 * half), F4)
    for s, (one, two) in enumerate(((a1o, a2o), (a1x, a2x))):
        at = s * half
        mid = at + cut - half
        e = e + dot_nt(dk_low[:, at:mid], one[:, half:])
        e = e + dot_nt(dk_low[:, mid : at + half], two[:, : 2 * half - cut])
        e = e + dot_nt(dv_low[:, at : at + half], two[:, 2 * half - cut :])
    part[...] = e.astype(part.dtype)


def back_block(
    weight, j, q, k, v, d_att, stat, delta, idq, ids, k_hat, k_rate, kg, parts
):
    tokens, width = q.shape
    wide, step = (tokens, width), padded(tokens)
    outs = [(wide, BF), (wide, BF), (wide, F4), (wide, F4 if j == 0 else BF)]
    outs += [((1, TILE), F4)]
    scratch = [pltpu.VMEM((tokens, 2 * step), F4), pltpu.VMEM(wide, F4)]
    scratch += [pltpu.VMEM((2 * step, LANES), BF)] * 2
    flops = 10 * tokens * tokens * width * 4 + 4 * tokens * width * width
    body = functools.partial(back_body, width // 2, j)
    return call(
        body, outs, scratch, 8, flops,
        q, k, v, d_att, stat, delta, idq, ids, k_hat, k_rate, kg, *parts,
        weight=weight,
    )


def weight_body(n, half, *refs):
    q_hat, q_rate, qg, own = refs[:4]
    a1o, a1x = refs[4:6]
    dqs, ns = refs[6 : 6 + n], refs[6 + n : 6 + 2 * n]
    dks, dvs = refs[6 + 2 * n : 6 + 3 * n], refs[6 + 3 * n : 6 + 4 * n]
    part, q_gain, g1o, g1x, g2o, g2x, dq_low, n_all, dk_all, dv_all = refs[6 + 4 * n :]
    tokens = q_hat.shape[0]
    matrix = group_matrix()
    total = jnp.zeros((1, TILE), F4)
    factor = float(HD) ** -0.5
    for t in range(tiles(2 * half)):
        cols = slice(t * TILE, (t + 1) * TILE)
        e = dqs[0][:, cols]
        for other in dqs[1:]:
            e = e + other[:, cols]
        d, g = head_norm_back(
            e * factor, q_hat[:, cols], q_rate[:, cols], qg[...], matrix
        )
        dq_low[:, cols] = d.astype(BF)
        total = total + fold_heads(g)
    q_gain[...] = total
    e = dot_nt(dq_low[:, :half], a1o[:, :half]) + dot_nt(dq_low[:, half:], a1x[:, :half])
    part[...] = own[...] + e
    for b in range(n):
        rows = slice(b * tokens, (b + 1) * tokens)
        n_all[rows, :] = ns[b][...]
        dk_all[rows, :] = dks[b][...]
        dv_all[rows, :] = dvs[b][...]
    cut = g1o.shape[1]
    for s, (one, two) in enumerate(((g1o, g2o), (g1x, g2x))):
        at = s * half
        mid = at + cut - half
        one[:, :half] = dot_tn(ns[0][...], dq_low[:, at : at + half]).astype(BF)
        one[:, half:] = dot_tn(n_all[...], dk_all[:, at:mid]).astype(BF)
        two[:, : 2 * half - cut] = dot_tn(n_all[...], dk_all[:, mid : at + half]).astype(BF)
        two[:, 2 * half - cut :] = dot_tn(n_all[...], dv_all[:, at : at + half]).astype(BF)


def input_body(own, rest, p, g1, d_mixed, second, query, *refs):
    keys, (out, small) = refs[:-2], refs[-2:]
    e = own[...] + rest[...].astype(F4)
    c, r = centre(p[...].astype(F4))
    hat = c * r
    t = e * g1[...]
    out[...] = d_mixed[...] + r * (t - mean_last(t) - hat * mean_last(t * hat))
    small[...] = jnp.zeros_like(small)
    small[0:1, :] = jnp.sum(e * hat, axis=0, keepdims=True)
    small[1:2, :] = jnp.sum(e, axis=0, keepdims=True)
    small[2:4, :] = second[...]
    small[4:5, :HD] = fold_lanes(query[...])
    total = keys[0][...]
    for x in keys[1:]:
        total = total + x[...]
    small[5:6, :HD] = fold_lanes(total)


def take_micro(x, c):
    mine = jnp.where(c0, x[0], x[1])
    other = jnp.where(c0, x[1], x[0])
    return mine, other


def per_device(
    patches,
    picture_ids,
    ln1_gain,
    ln1_bias,
    w_query,
    w_key,
    w_value,
    q_gain,
    k_gain,
    w_out,
    ln2_gain,
    ln2_bias,
    w_up,
    w_down,
    cotangent,
):
    n = lax.axis_size("row")
    at = Place()
    c0 = at("c")
    width = patches.shape[-1]
    half = w_query.shape[1]
    piece = patches.shape[2]
    tokens = 2 * piece
    inner = w_up.shape[1]

    cut_a = half + half * 2 // 3
    first = inner * 2 // 3
    mid = inner // 2
    width_b = inner + half
    whole = not regular(w_query.shape[0])
    chunk_a = jnp.concatenate([w_query, w_key, w_value], axis=1)
    chunk_b = jnp.concatenate([w_up[:, :first], w_out.T, w_up[:, first:]], axis=1)
    line_a = Chain(line_steps(chunk_a, at, True))
    line_b = Chain(line_steps(chunk_b, at))

    def back_home(x):
        lower, upper = x[:piece], x[piece:]
        keep = jnp.where(c0, lower, upper)
        got = swap_core(jnp.where(c0, upper, lower))
        whole = jnp.stack([jnp.where(c0, keep, got), jnp.where(c0, got, keep)])
        return whole[None], got

    def take(x):
        mine = jnp.where(c0, x[0], x[1])
        got = swap_core(jnp.where(c0, x[1], x[0]))
        return jnp.concatenate(
            [jnp.where(c0, mine, got), jnp.where(c0, got, mine)], axis=0
        )

    g1, b1 = ln1_gain[None], ln1_bias[None]
    g2, b2 = ln2_gain[None], ln2_bias[None]
    qg, kg = jnp.tile(q_gain, TILE // HD)[None], jnp.tile(k_gain, TILE // HD)[None]
    ids = jnp.where(c0, picture_ids[0, 0], picture_ids[0, 1]).reshape(n, tokens)
    id_blocks = [index(ids, at("row", j), keepdims=True) for j in range(n)]
    ids = jnp.concatenate(id_blocks, axis=1).reshape(n * tokens, 1)
    spare = jnp.full((1, padded(tokens) - tokens), -1, jnp.int32)
    idq = jnp.concatenate([id_blocks[0], spare] * 2, axis=1)
    ready = lax.optimization_barrier((g1, b1, g2, b2, qg, kg, ids, idq, *id_blocks))
    g1, b1, g2, b2, qg, kg, ids, idq, *id_blocks = ready

    line_a.step()
    p_own = take(patches[0])
    blocks = [p_own, hop(p_own, n)]
    got_a = line_a.last
    rows_a = line_a.step(*ready).finish()
    chain_a = Chain(plane_steps((rows_a[:, :cut_a], rows_a[:, cut_a:]), whole, at))
    chain_a.step()
    line_b.step(*got_a)
    chain_a.step()
    for _ in range(n - 2):
        line_b.step()
    got_b = line_b.last
    rows_b = line_b.finish()
    a_one, a_two = chain_a.finish()
    swap_a = chain_a.last
    a_parts = a_one + a_two
    cot = take(cotangent[0])
    line_c = Chain(line_steps(w_down.T, at, True))
    chain_b = Chain(plane_steps((rows_b[:, :first], rows_b[:, first:]), whole, at))

    made, marks = [], []
    before = token = ()
    deps = got_b
    for j in range(n):
        if 0 < j < n - 1:
            blocks.append(hop(after(blocks[j], marks[-1] if j > 1 else got_b), n))
        if j in (0, 1, n - 1):
            chain_b.step(*token)
        if j == 1:
            line_c.step(*token)
        if j == n - 1:
            rows_c = line_c.finish()
            chain_c = Chain(plane_steps((rows_c[:, :mid], rows_c[:, mid:]), whole, at))
            chain_c.step()
        made.append(
            look(
                0.1 if 0 < j < n - 1 else 4.0,
                j == 0, j == n - 1, after(blocks[j], deps), g1, b1, qg, kg, ids,
                id_blocks[j], a_parts, before,
            )
        )
        if j == 0:
            q_hat, q_rate, q_low = made[0][7:]
        before = (q_low, *made[j][5:7])
        token = (made[j][6],)
        marks.append(token)
        deps = token + (chain_c.last if j == n - 1 else line_c.last)
        if j != 1 or n < 4:
            deps = deps + chain_b.last
    normed = [m[0] for m in made]
    k_hat, k_rate, k_low, v_low = [[m[i] for m in made] for i in (1, 2, 3, 4)]
    att, stat = made[-1][5:7]

    b_one, b_two = chain_b.finish()
    b_parts = b_one + b_two
    chain_c.step(*token)
    mixed, n2, act, slope, *gc = call(
        functools.partial(up_body, half),
        [((tokens, width), F4), ((tokens, width), BF)]
        + [((tokens, 2 * inner), BF)] * 2
        + [((width, mid), BF)] * 4,
        [], 6,
        2 * tokens * width * (width + 4 * inner),
        p_own, after(att, deps), cot, g2, b2, *b_parts,
    )
    c_one, c_two = chain_c.step(mixed).finish()
    c_parts = c_one + c_two

    back_c = Chain(plane_sums((gc[0], gc[1]), (gc[2], gc[3]), whole, at)).step()
    deps = back_c.last
    back_c.step()
    d_up, d_mixed, d_att, delta, gains2 = call(
        functools.partial(slope_body, half),
        [((tokens, 2 * inner), BF), ((tokens, width), F4), ((tokens, width), BF)]
        + [((8, 2 * padded(tokens)), F4), ((2, width), F4)],
        [], 9,
        2 * tokens * width * (width + 4 * inner),
        after(mixed, deps), slope, att, cot, g2, *b_parts, *c_parts,
    )
    back = [None] * n
    back_b = acc = None
    deps = (delta,)
    for turn, j in enumerate([*range(1, n), 0]):
        back[j] = back_block(
            0.1 if turn in (0, n - 1) else 4.0,
            j, q_low, k_low[j], v_low[j], after(d_att, deps), stat, delta, idq, ids,
            k_hat[j], k_rate[j], kg, a_parts,
        )
        token = back[j][4]
        deps = (token,)
        if turn != 1:
            deps = deps + back_c.last
            back_c.step(token)
        if back_b is not None and turn != n - 2:
            deps = deps + back_b.last
            back_b.step(token)
        if turn == 0:
            result, *gb = call(
                functools.partial(inner_body, half),
                [((tokens, width), BF)]
                + [((width, first), BF)] * 2
                + [((width, half + inner - first), BF)] * 2,
                [], 8,
                2 * tokens * width * (width + 4 * inner),
                mixed, n2, act, att, d_up, after(d_mixed, deps), *c_parts,
            )
            deps = (result,)
            result, got = back_home(result)
            back_b = Chain(plane_sums((gb[0], gb[1]), (gb[2], gb[3]), whole, at)).step()
        elif turn > 0:
            deps = deps + (got,)
        if j:
            part = back[j][3]
            if acc is None:
                acc = part
            else:
                deps = deps + (acc,)
                acc = add_low(part, acc)
            acc = hop(acc, n)
    deps = deps + (acc,)
    part, dq_gain, *ga = call(
        functools.partial(weight_body, n, half),
        [((tokens, width), F4), ((1, TILE), F4)]
        + [((width, cut_a), BF)] * 2
        + [((width, 3 * half - cut_a), BF)] * 2,
        [pltpu.VMEM((tokens, width), BF)] + [pltpu.VMEM((n * tokens, width), BF)] * 3,
        10,
        2 * tokens * width * width * (2 + 2 * n),
        after(q_hat, deps), q_rate, qg, back[0][3], *a_one,
        *[b[2] for b in back], *normed, *[b[0] for b in back], *[b[1] for b in back],
        weight=0.1,
    )
    back_a = Chain(plane_sums((ga[0], ga[1]), (ga[2], ga[3]), whole, at))
    back_a.step(acc, *back_b.last)
    sum_b, sum_c = back_b.step(dq_gain).finish(), back_c.finish()
    both = jnp.concatenate([sum_b, sum_c], axis=1)
    line = Chain(line_sums(both, whole, at)).step()
    grad_in, small = call(
        input_body, [((tokens, width), F4), ((8, width), F4)], [], 6, 0,
        part, acc, p_own, g1, d_mixed, gains2, dq_gain, *[b[4] for b in back],
    )
    sums = Chain(sum_steps(small)).step()
    while back_a.value is None:
        deps = back_a.last
        back_a.step(*deps)
        sums.step(*deps)
        line.step(*sums.last)
    last_a = Chain(line_sums(back_a.value, whole, at, True)).step()
    sums.step(*last_a.last)
    last_a.finish()
    sums.finish()
    grad_a, grad_bc = last_a.value, line.finish()
    grad_b, grad_c = grad_bc[:, :width_b], grad_bc[:, width_b:]
    small = sums.value
    grad_g1, grad_b1, grad_g2, grad_b2 = small[0], small[1], small[2], small[3]
    grad_gq, grad_gk = small[4, :HD], small[5, :HD]

    rest = half + first
    grad_wu = jnp.concatenate([grad_b[:, :first], grad_b[:, rest:]], axis=1)
    return (
        result,
        back_home(grad_in)[0],
        grad_g1,
        grad_b1,
        grad_a[:, :half],
        grad_a[:, half : 2 * half],
        grad_a[:, 2 * half :],
        grad_gq,
        grad_gk,
        grad_b[:, first:rest].T,
        grad_g2,
        grad_b2,
        grad_wu,
        grad_c.T,
    )


def solution(mesh):
    rows = P("dp", None, ("row", "col"), None)
    inward = P(("dp", "row"), "col")
    outward = P("col", ("dp", "row"))
    return jax.shard_map(
        per_device,
        mesh=mesh,
        in_specs=(
            rows, P("dp", None, None), P(), P(), inward, inward, inward, P(), P(),
            outward, P(), P(), inward, outward, rows,
        ),
        out_specs=(
            rows, rows, P(), P(), inward, inward, inward, P(), P(),
            outward, P(), P(), inward, outward,
        ),
        check_vma=False,
    )
```
